32 devices in a mesh: shard: 4 (over z), ctx: 4 (over y, x), tp: 2 (over core).
Axes of the slice: x: 2, y: 2, z: 4, core: 2. Of those that a mesh axis runs over, the one named last changes fastest.
Arguments:
- tokens: bfloat16 [2, 4, 4096, 512], P(None, 'shard', 'ctx'), may hold values from -6 to 6
- cotangent: bfloat16 [2, 4, 4096, 512], P(None, 'shard', 'ctx'), may hold values from -6 to 6
- w_query: bfloat16 [512, 512], P('shard', 'tp'), may hold values from -0.25 to 0.25
- w_key: bfloat16 [512, 512], P('shard', 'tp'), may hold values from -0.25 to 0.25
- w_value: bfloat16 [512, 512], P('shard', 'tp'), may hold values from -0.25 to 0.25
- w_out: bfloat16 [512, 512], P('tp', 'shard'), may hold values from -6 to 6
- w_up: bfloat16 [512, 2048], P('shard', 'tp'), may hold values from -0.25 to 0.25
- w_down: bfloat16 [2048, 512], P('tp', 'shard'), may hold values from -0.125 to 0.125
- b_query: bfloat16 [8, 64], P('tp', 'shard'), may hold values from -3 to 3
- b_value: bfloat16 [8, 64], P('tp', 'shard'), may hold values from -3 to 3
- b_up: bfloat16 [8, 256], P('tp', 'shard'), may hold values from -3 to 3
- b_out: bfloat16 [512], P('shard'), may hold values from -3 to 3
- b_down: bfloat16 [512], P('shard'), may hold values from -3 to 3
- gain_attn: bfloat16 [512], P('shard'), may hold values from 0.099609375 to 1.8984375
- shift_attn: bfloat16 [512], P('shard'), may hold values from -3 to 3
- gain_ffn: bfloat16 [512], P('shard'), may hold values from 0.099609375 to 1.8984375
- shift_ffn: bfloat16 [512], P('shard'), may hold values from -3 to 3
Outputs:
- output: bfloat16 [2, 4, 4096, 512], P(None, 'shard', 'ctx')
- grad_tokens: bfloat16 [2, 4, 4096, 512], P(None, 'shard', 'ctx')
- grad_w_query: float32 [512, 512], P('shard', 'tp')
- grad_w_key: float32 [512, 512], P('shard', 'tp')
- grad_w_value: float32 [512, 512], P('shard', 'tp')
- grad_w_out: float32 [512, 512], P('tp', 'shard')
- grad_w_up: float32 [512, 2048], P('shard', 'tp')
- grad_w_down: float32 [2048, 512], P('tp', 'shard')
- grad_b_query: float32 [8, 64], P('tp', 'shard')
- grad_b_value: float32 [8, 64], P('tp', 'shard')
- grad_b_up: float32 [8, 256], P('tp', 'shard')
- grad_b_out: float32 [512], P('shard')
- grad_b_down: float32 [512], P('shard')
- grad_gain_attn: float32 [512], P('shard')
- grad_shift_attn: float32 [512], P('shard')
- grad_gain_ffn: float32 [512], P('shard')
- grad_shift_ffn: float32 [512], P('shard')
The draws below stay inside these ranges and needn't reach their ends.
All inputs are finite; a program needn't handle non-finite values.
Results may differ from the reference program's by a relative error of at most 0.017.
Values may be sent and summed in bfloat16 or wider, within the bound.
A program may use at most 256 MiB of HBM per device.

```python
import jax
import jax.numpy as jnp
from jax import lax

D = 512
HEADS = 8
HD = 64
FF = 2048
MICRO = 2
LENGTH = 4096
BATCH = 4


def levels(stream_key, extent, pieces, smallest, high):
    def one(dim, shards_of):
        heights = jax.random.uniform(jax.random.fold_in(jax.random.fold_in(stream_key, 6), dim), (shards_of,), jnp.float32, smallest / len(pieces), high / len(pieces))
        return jnp.repeat(jnp.exp(heights), extent[dim] // shards_of).reshape((-1,) + (1,) * (len(extent) - dim - 1))

    level = one(*pieces[0])
    for cut in pieces[1:]:
        level = level * one(*cut)
    return level


def bell_draw(stream_key, extent, deviation, bound, pieces=(), kind=jnp.bfloat16):
    level = levels(stream_key, extent, pieces, -0.22, 0.18) if pieces else 1.0
    array = jax.random.normal(stream_key, extent, jnp.float32) * deviation * level
    return jnp.minimum(jnp.maximum(array, -bound), bound).astype(kind)


def setup_inputs(seed: int = 0) -> dict:
    keys = jax.random.split(jax.random.key(seed), 18)
    tokens = bell_draw(keys[0], (MICRO, BATCH, LENGTH, D), 1.0, 6.0, ((1, 4), (2, 4)))
    cotangent = bell_draw(keys[1], (MICRO, BATCH, LENGTH, D), 1.0, 6.0, ((1, 4), (2, 4)))
    w_query = bell_draw(keys[2], (D, D), D ** -0.5, 0.25, ((0, 4), (1, 2)))
    w_key = bell_draw(keys[3], (D, D), D ** -0.5, 0.25, ((0, 4), (1, 2)))
    w_value = bell_draw(keys[4], (D, D), D ** -0.5, 0.25, ((0, 4), (1, 2)))
    w_out = bell_draw(keys[5], (D, D), (max(1, D * 8 // LENGTH)) ** -0.5, 6.0, ((0, 2), (1, 4)))
    w_up = bell_draw(keys[6], (D, FF), D ** -0.5, 0.25, ((0, 4), (1, 2)))
    w_down = bell_draw(keys[7], (FF, D), FF ** -0.5, 0.125, ((0, 2), (1, 4)))
    b_query = bell_draw(keys[8], (HEADS, HD), 0.5, 3.0, ((0, 2), (1, 4)))
    b_value = bell_draw(keys[9], (HEADS, HD), 0.5, 3.0, ((0, 2), (1, 4)))
    b_up = bell_draw(keys[10], (HEADS, FF // HEADS), 0.5, 3.0, ((0, 2), (1, 4)))
    b_out = bell_draw(keys[11], (D,), 0.5, 3.0, ((0, 4),))
    b_down = bell_draw(keys[12], (D,), 0.5, 3.0, ((0, 4),))
    gain_attn = jnp.clip(1.0 + 0.18 * jax.random.normal(keys[13], (D,), jnp.float32), 0.099609375, 1.8984375).astype(jnp.bfloat16)
    shift_attn = bell_draw(keys[14], (D,), 0.5, 3.0, ((0, 4),))
    gain_ffn = jnp.clip(1.0 + 0.18 * jax.random.normal(keys[15], (D,), jnp.float32), 0.099609375, 1.8984375).astype(jnp.bfloat16)
    shift_ffn = bell_draw(keys[16], (D,), 0.5, 3.0, ((0, 4),))
    return {"tokens": tokens, "cotangent": cotangent, "w_query": w_query, "w_key": w_key, "w_value": w_value, "w_out": w_out, "w_up": w_up, "w_down": w_down, "b_query": b_query, "b_value": b_value, "b_up": b_up, "b_out": b_out, "b_down": b_down, "gain_attn": gain_attn, "shift_attn": shift_attn, "gain_ffn": gain_ffn, "shift_ffn": shift_ffn}


@jax.custom_vjp
def low(v):
    return lax.optimization_barrier(v.astype(jnp.bfloat16)).astype(jnp.float32)

@jax.custom_vjp
def low_back(v):
    return v

def low_keep(v):
    return (low(v), None)

def low_pass(kept, grad):
    return (grad,)

def back_keep(v):
    return (v, None)

def back_low(kept, grad):
    return (low(grad),)
low.defvjp(low_keep, low_pass)
low_back.defvjp(back_keep, back_low)
norm_eps = 1e-05
highest = lax.Precision.HIGHEST

def layer_norm(values, gain, shift):
    average = lax.optimization_barrier(jnp.mean(values, axis=-1, keepdims=True))
    centred = values - average
    variance = lax.optimization_barrier(jnp.mean(centred * centred, axis=-1, keepdims=True))
    return centred * lax.rsqrt(variance + norm_eps) * gain + shift

def matmul(left, right):
    return jnp.dot(left, right, precision=highest)

def add_terms(first_term, second_term):
    return first_term + second_term

def forward(params, sequence):
    w_query, w_key, w_value, w_out, w_up, w_down, b_query, b_value, b_up, b_out, b_down, gain_attn, shift_attn, gain_ffn, shift_ffn = params
    length_here = sequence.shape[0]
    normed_one = low(layer_norm(sequence, gain_attn, shift_attn))
    query_rows = low(low_back(matmul(normed_one, w_query) + b_query.reshape(-1)))
    key_rows = low(low_back(matmul(normed_one, w_key)))
    value_rows = low(low_back(matmul(normed_one, w_value) + b_value.reshape(-1)))
    key_heads = key_rows.reshape(length_here, HEADS, HD)
    value_heads = value_rows.reshape(length_here, HEADS, HD)
    block_rows = min(512, length_here)
    query_blocks = query_rows.reshape(length_here // block_rows, block_rows, HEADS, HD)
    score_scale = 1.0 / HD ** 0.5

    def attend(query_block):
        raw_scores = jnp.einsum('qhd,khd->hqk', query_block, key_heads, precision=highest)
        scores = low_back(raw_scores * score_scale)
        attn_weights = low(jax.nn.softmax(scores, axis=-1))
        return jnp.einsum('hqk,khd->qhd', attn_weights, value_heads, precision=highest)
    mixed_rows = lax.map(jax.checkpoint(attend), query_blocks).reshape(length_here, HEADS * HD)
    mixed_rows = low(low_back(mixed_rows))
    attended = low_back(matmul(mixed_rows, w_out) + b_out)
    middle = sequence + attended
    normed_two = low(layer_norm(middle, gain_ffn, shift_ffn))
    pre_active = low_back(matmul(normed_two, w_up) + b_up.reshape(-1))
    active = low(jax.nn.gelu(pre_active, approximate=False))
    ffn_out = low_back(matmul(active, w_down) + b_down)
    return middle + ffn_out

def reference(tokens, cotangent, w_query, w_key, w_value, w_out, w_up, w_down, b_query, b_value, b_up, b_out, b_down, gain_attn, shift_attn, gain_ffn, shift_ffn):
    params = tuple((param.astype(jnp.float32) for param in (w_query, w_key, w_value, w_out, w_up, w_down, b_query, b_value, b_up, b_out, b_down, gain_attn, shift_attn, gain_ffn, shift_ffn)))
    inputs = tokens.astype(jnp.float32).reshape(-1, LENGTH, D)
    upstreams = cotangent.astype(jnp.float32).reshape(-1, LENGTH, D)

    def one_sequence(running, sequence_pair):
        sequence, upstream = sequence_pair
        result, pullback = jax.vjp(forward, params, sequence)
        grad_params, grad_input = pullback(upstream)
        return (jax.tree.map(add_terms, running, grad_params), (result, grad_input))
    zeros = jax.tree.map(jnp.zeros_like, params)
    totals, (results, grad_inputs) = lax.scan(one_sequence, zeros, (inputs, upstreams))
    shape_out = tokens.shape
    return (results.reshape(shape_out).astype(jnp.bfloat16), grad_inputs.reshape(shape_out).astype(jnp.bfloat16), totals[0], totals[1], totals[2], totals[3], totals[4], totals[5], totals[6], totals[7], totals[8], totals[9], totals[10], totals[11], totals[12], totals[13], totals[14])
```

```python
import functools
import math

import jax
import jax.numpy as jnp
from jax import lax
from jax.experimental import pallas as pl
from jax.experimental.pallas import tpu as pltpu
from jax.sharding import PartitionSpec as P

F32 = jnp.float32
BF16 = jnp.bfloat16
MESH = pl.DeviceIdType.MESH
norm_eps = 1e-05
LOG2E = math.log2(math.e)
VMEM_LIMIT = 60 * 2**20


def dot_nn(left, right):
    return lax.dot_general(left, right, (((1,), (0,)), ((), ())), preferred_element_type=F32)


def dot_nt(left, right):
    return lax.dot_general(left, right, (((1,), (1,)), ((), ())), preferred_element_type=F32)


def dot_tn(left, right):
    return lax.dot_general(left, right, (((0,), (0,)), ((), ())), preferred_element_type=F32)


def unit_norm(values):
    average = jnp.mean(values, axis=-1, keepdims=True)
    centred = values - average
    variance = jnp.mean(centred * centred, axis=-1, keepdims=True)
    inverse = lax.rsqrt(variance + norm_eps)
    return centred * inverse, inverse


def norm_back(grad_normed, unit_vals, inverse, gain):
    scaled = grad_normed * gain
    return inverse * (
        scaled
        - jnp.mean(scaled, axis=-1, keepdims=True)
        - unit_vals * jnp.mean(scaled * unit_vals, axis=-1, keepdims=True)
    )


def column_sum(values):
    return jnp.sum(values, axis=0, keepdims=True)


def full_spec(shape):
    return pl.BlockSpec(shape, lambda *_: (0,) * len(shape))


def params(limit=VMEM_LIMIT, **others):
    return pltpu.CompilerParams(vmem_limit_bytes=limit, **others)


def gather_kernel(ns, nc, w_ref, small_ref, x_ref, w_out, small_out, x_out, *sems):
    w_send, w_recv, s_send, s_recv, x_send, x_recv, wt_send, wt_recv, st_send, st_recv, xt_send, xt_recv, local = sems
    s = lax.axis_index("shard")
    c = lax.axis_index("ctx")
    t = lax.axis_index("tp")
    other = 1 - t
    depth = w_ref.shape[1]
    half = x_ref.shape[0] // 2

    barrier = pltpu.get_barrier_semaphore()
    for d in range(1, ns):
        pl.semaphore_signal(barrier, inc=1, device_id={"shard": s ^ d}, device_id_type=MESH)
    for d in range(1, nc):
        pl.semaphore_signal(barrier, inc=1, device_id={"ctx": c ^ d}, device_id_type=MESH)
    pl.semaphore_signal(barrier, inc=1, device_id={"tp": other}, device_id_type=MESH)
    pl.semaphore_wait(barrier, ns + nc - 1)

    def w_rows(part, owner):
        return w_out.at[part, :, pl.ds(pl.multiple_of(owner * depth, depth), depth), :]

    def x_rows(which):
        return x_ref.at[pl.ds(pl.multiple_of(which * half, half), half), :]

    def send(source, target, send_sem, recv_sem, where):
        copy = pltpu.make_async_remote_copy(
            src_ref=source, dst_ref=target, send_sem=send_sem, recv_sem=recv_sem,
            device_id=where, device_id_type=MESH,
        )
        copy.start()
        return copy

    sent = []
    x_copies, w_copies, s_copies = {}, {}, {}
    for d in range(1, nc):
        x_copies[d] = send(x_rows(t), x_out.at[d, 0], x_send.at[d], x_recv.at[d], {"ctx": c ^ d})
    for d in range(1, ns):
        w_copies[d] = send(w_ref, w_rows(0, s), w_send.at[d], w_recv.at[d], {"shard": s ^ d})
        s_copies[d] = send(small_ref, small_out.at[0, s], s_send.at[d], s_recv.at[d], {"shard": s ^ d})
    last = [
        send(w_ref, w_rows(1, s), wt_send.at[0], wt_recv.at[0], {"tp": other}),
        send(small_ref, small_out.at[1, s], st_send.at[0], st_recv.at[0], {"tp": other}),
    ]
    locals_ = [
        pltpu.make_async_copy(w_ref, w_rows(0, s), local.at[0]),
        pltpu.make_async_copy(small_ref, small_out.at[0, s], local.at[1]),
        pltpu.make_async_copy(x_rows(t), x_out.at[0, 0], local.at[2]),
        pltpu.make_async_copy(x_rows(other), x_out.at[0, 1], local.at[3]),
    ]
    for copy in locals_:
        copy.start()
    for d in range(1, max(ns, nc)):
        if d < ns:
            w_copies[d].wait_recv()
            last.append(send(w_rows(0, s ^ d), w_rows(1, s ^ d), wt_send.at[d], wt_recv.at[d], {"tp": other}))
            s_copies[d].wait_recv()
            last.append(
                send(small_out.at[0, s ^ d], small_out.at[1, s ^ d], st_send.at[d], st_recv.at[d], {"tp": other})
            )
        if d < nc:
            x_copies[d].wait_recv()
            last.append(send(x_out.at[d, 0], x_out.at[d, 1], xt_send.at[d], xt_recv.at[d], {"tp": other}))
    for copies in (x_copies, w_copies, s_copies):
        for copy in copies.values():
            copy.wait_send()
    for copy in last:
        copy.wait()
    for copy in locals_:
        copy.wait()


def gather_first(w_stack, small, x_rows, ns, nc):
    kinds, depth, width = w_stack.shape
    length, features = x_rows.shape
    dma = pltpu.SemaphoreType.DMA
    return pl.pallas_call(
        functools.partial(gather_kernel, ns, nc),
        in_specs=[pl.BlockSpec(memory_space=pltpu.VMEM)] * 3,
        out_specs=[pl.BlockSpec(memory_space=pl.ANY)] * 3,
        out_shape=[
            jax.ShapeDtypeStruct((2, kinds, ns * depth, width), BF16),
            jax.ShapeDtypeStruct((2, ns) + small.shape, BF16),
            jax.ShapeDtypeStruct((nc, 2, length // 2, features), BF16),
        ],
        scratch_shapes=[dma((ns,)), dma((ns,)), dma((ns,)), dma((ns,)), dma((nc,)), dma((nc,))]
        + [dma((ns,)), dma((ns,)), dma((ns,)), dma((ns,)), dma((nc,)), dma((nc,)), dma((4,))],
        compiler_params=params(collective_id=0, has_side_effects=True),
        name="gather_first",
    )(w_stack, small, x_rows)


def front_kernel(x_ref, w_ref, gain_ref, shift_ref, bq_ref, bv_ref, n_ref, k_ref, v_ref, q_ref, *, q_scale):
    step = pl.program_id(0)
    unit, _ = unit_norm(x_ref[...].astype(F32))
    normed = (unit * gain_ref[...] + shift_ref[...]).astype(BF16)
    n_ref[...] = normed
    width = w_ref.shape[3]
    for part in range(2):
        cols = slice(part * width, (part + 1) * width)
        k_ref[:, cols] = dot_nn(normed, w_ref[part, 1]).astype(BF16)
        v_ref[:, cols] = (dot_nn(normed, w_ref[part, 2]) + bv_ref[:, cols]).astype(BF16)

    @pl.when(step == 0)
    def _():
        for part in range(2):
            cols = slice(part * width, (part + 1) * width)
            q_ref[:, cols] = ((dot_nn(normed, w_ref[part, 0]) + bq_ref[:, cols]) * q_scale).astype(BF16)


def front(x_all, weights, gain, shift, b_query, b_value, head_width):
    keys, features = x_all.shape
    block = keys // 8
    width = 2 * weights.shape[3]
    return pl.pallas_call(
        functools.partial(front_kernel, q_scale=LOG2E / math.sqrt(head_width)),
        grid=(8,),
        in_specs=[
            pl.BlockSpec((block, features), lambda i: (i, 0)),
            full_spec(weights.shape),
            full_spec((1, features)),
            full_spec((1, features)),
            full_spec((1, width)),
            full_spec((1, width)),
        ],
        out_specs=[
            pl.BlockSpec((block, features), lambda i: (i, 0)),
            pl.BlockSpec((block, width), lambda i: (i, 0)),
            pl.BlockSpec((block, width), lambda i: (i, 0)),
            full_spec((block, width)),
        ],
        out_shape=[
            jax.ShapeDtypeStruct((keys, features), BF16),
            jax.ShapeDtypeStruct((keys, width), BF16),
            jax.ShapeDtypeStruct((keys, width), BF16),
            jax.ShapeDtypeStruct((block, width), BF16),
        ],
        compiler_params=params(),
        cost_estimate=pl.CostEstimate(
            flops=4 * keys * features * width, bytes_accessed=8 * keys * features, transcendentals=keys
        ),
        name="front",
    )(x_all, weights, gain, shift, b_query, b_value)


def with_parts(lane, base, values, first, width):
    high = values.astype(BF16).astype(F32)
    rest = values - high
    middle = rest.astype(BF16).astype(F32)
    low = rest - middle
    extra = jnp.where(
        lane == first, high, jnp.where(lane == first + 1, middle, jnp.where(lane == first + 2, low, 0.0))
    )
    inside = (lane < width) if first else (lane >= width)
    return jnp.where(inside, base, extra)


def send(source, target, send_sem, recv_sem, where):
    return pltpu.make_async_remote_copy(
        src_ref=source, dst_ref=target, send_sem=send_sem, recv_sem=recv_sem, device_id=where, device_id_type=MESH
    )


def greet(counts):
    barrier = pltpu.get_barrier_semaphore()
    total = 0
    for name, count in counts:
        me = lax.axis_index(name)
        for d in range(1, count):
            pl.semaphore_signal(barrier, inc=1, device_id={name: me ^ d}, device_id_type=MESH)
            total += 1
    pl.semaphore_wait(barrier, total)


class Gather:

    def __init__(self, name, count, source, theirs, target, place, sems):
        self.name, self.count, self.source, self.theirs = name, count, source, theirs
        self.target, self.place = target, place
        self.out_sem, self.in_sem, self.cross_out, self.cross_in, self.local = sems
        self.me = lax.axis_index(name)

    def first(self, d):
        where = {self.name: self.me ^ d}
        return send(self.source, self.place(self.target, 0, self.me, d), self.out_sem.at[d], self.in_sem.at[d], where)

    def cross(self, d):
        where = {"tp": 1 - lax.axis_index("tp")}
        owner = self.me ^ d
        source = self.place(self.target, 0, owner, d) if d else self.source
        return send(source, self.place(self.target, 1, owner, d), self.cross_out.at[d], self.cross_in.at[d], where)

    def locals(self):
        copies = [pltpu.make_async_copy(self.source, self.place(self.target, 0, self.me, 0), self.local.at[0])]
        if self.theirs is not None:
            copies.append(pltpu.make_async_copy(self.theirs, self.place(self.target, 1, self.me, 0), self.local.at[1]))
        return copies

    def crossed(self):
        return range(0 if self.theirs is None else 1, self.count)

    def start(self):
        for d in range(1, self.count):
            self.first(d).start()
        for copy in self.locals():
            copy.start()
        if self.theirs is None:
            self.cross(0).start()

    def forward(self):
        for d in range(1, self.count):
            self.first(d).wait_recv()
            self.cross(d).start()

    def finish(self):
        for d in range(1, self.count):
            self.first(d).wait_send()
        for d in self.crossed():
            self.cross(d).wait()
        for copy in self.locals():
            copy.wait()


def place_rows(ref, part, owner, d):
    size = ref.shape[1] // lax.axis_size("shard")
    return ref.at[part, pl.ds(pl.multiple_of(owner * size, size), size), :]


def place_columns(ref, part, owner, d):
    size = ref.shape[2] // lax.axis_size("shard")
    return ref.at[part, :, pl.ds(pl.multiple_of(owner * size, size), size)]


def place_slot(ref, part, owner, d):
    return ref.at[part, owner]


def place_distance(ref, part, owner, d):
    return ref.at[d, part]


def gather_sems(count):
    dma = pltpu.SemaphoreType.DMA
    return [dma((count,)), dma((count,)), dma((count,)), dma((count,)), dma((2,))]


def attend_kernel(*refs, kc, width, plans):
    count = len(plans)
    q_ref, k_ref, v_ref = refs[:3]
    sources = refs[3 : 3 + count]
    o_ref, qx_ref = refs[3 + count : 5 + count]
    targets = refs[5 + count : 5 + 2 * count]
    scores = refs[5 + 2 * count]
    sems = refs[6 + 2 * count :]
    step = pl.program_id(0)
    last = pl.num_programs(0) - 1
    t = lax.axis_index("tp")

    def gathers(wanted):
        found = []
        for i, (name, number, place, split) in enumerate(plans):
            if name != wanted:
                continue
            source, theirs = sources[i], None
            if split:
                half = source.shape[0] // 2
                theirs = source.at[pl.ds(pl.multiple_of((1 - t) * half, half), half), :]
                source = source.at[pl.ds(pl.multiple_of(t * half, half), half), :]
            found.append(Gather(name, number, source, theirs, targets[i], place, sems[5 * i : 5 * i + 5]))
        return found

    counts = {name: number for name, number, _, _ in plans}

    @pl.when(step == 0)
    def _():
        greet([("tp", 2)] + list(counts.items()))
        for name in counts:
            for gather in gathers(name):
                gather.start()

    @pl.when(step == last)
    def _():
        for gather in gathers("ctx"):
            gather.forward()

    rows, lanes = q_ref.shape
    keys = k_ref.shape[0]
    lane = lax.broadcasted_iota(jnp.int32, (rows, lanes), 1)
    lane_v = lax.broadcasted_iota(jnp.int32, (kc, lanes), 1)
    q = q_ref[...].astype(F32)
    tops = []
    for h in range(2):
        inside = (lane < width) if h == 0 else (lane >= width)
        q_head = jnp.where(inside, q, 0.0).astype(BF16)
        top = None
        for i in range(keys // kc):
            part = dot_nt(k_ref[i * kc : (i + 1) * kc], q_head)
            scores[h, i * kc : (i + 1) * kc] = part
            here = jnp.max(part.reshape(kc // 8, 8, rows), axis=0)
            top = here if top is None else jnp.maximum(top, here)
        tops.append(jnp.max(top, axis=0, keepdims=True))
    outs = []
    for h in range(2):
        inside_v = (lane_v < width) if h == 0 else (lane_v >= width)
        total = jnp.zeros((lanes, rows), F32)
        for i in range(keys // kc):
            v_one = jnp.where(inside_v, v_ref[i * kc : (i + 1) * kc], jnp.ones((), BF16))
            exponent = jnp.exp2(scores[h, i * kc : (i + 1) * kc] - tops[h]).astype(BF16)
            total += dot_tn(v_one, exponent)
        first = width if h == 0 else 0
        log_total = tops[h] + jnp.log2(total[first : first + 1, :])
        total = total.T
        outs.append(total / pltpu.roll(total, width, 1))
        log_column = jnp.broadcast_to(log_total, (8, rows)).T[:, :1]
        qx_ref[:, h * lanes : (h + 1) * lanes] = with_parts(lane, q, -log_column, first, width).astype(BF16)
    o_ref[...] = jnp.where(lane < width, outs[0], outs[1]).astype(BF16)

    @pl.when(step == last)
    def _():
        for gather in gathers("shard"):
            gather.forward()
        for name in counts:
            for gather in gathers(name):
                gather.finish()


def attend_forward(q, k, v, width, plans, sources, shapes, number):
    rows, cols = q.shape
    keys = k.shape[0]
    lanes = 2 * width
    kc = 512
    anywhere = pl.BlockSpec(memory_space=pl.ANY)
    return pl.pallas_call(
        functools.partial(attend_kernel, kc=kc, width=width, plans=plans),
        grid=(cols // lanes,),
        in_specs=[
            pl.BlockSpec((rows, lanes), lambda j: (0, j)),
            pl.BlockSpec((keys, lanes), lambda j: (0, j)),
            pl.BlockSpec((keys, lanes), lambda j: (0, j)),
        ]
        + [anywhere] * len(plans),
        out_specs=[
            pl.BlockSpec((rows, lanes), lambda j: (0, j)),
            pl.BlockSpec((rows, 2 * lanes), lambda j: (0, j)),
        ]
        + [anywhere] * len(plans),
        out_shape=[
            jax.ShapeDtypeStruct((rows, cols), BF16),
            jax.ShapeDtypeStruct((rows, 2 * cols), BF16),
        ]
        + [jax.ShapeDtypeStruct(shape, BF16) for shape in shapes],
        scratch_shapes=[pltpu.VMEM((2, keys, rows), F32)]
        + [sem for plan in plans for sem in gather_sems(plan[1])],
        compiler_params=params(collective_id=number, has_side_effects=True),
        cost_estimate=pl.CostEstimate(
            flops=12 * rows * keys * cols, bytes_accessed=4 * keys * cols, transcendentals=rows * keys * cols // width
        ),
        name="attend_forward",
    )(q, k, v, *sources)


def attend_back_step(qx_ref, k_ref, v_ref, go_ref, o_ref, dq_ref, dk_ref, dv_ref, width):
    rows, lanes = o_ref.shape
    keys = k_ref.shape[0]
    lane = lax.broadcasted_iota(jnp.int32, (rows, lanes), 1)
    lane_k = lax.broadcasted_iota(jnp.int32, (keys, lanes), 1)
    one = jnp.ones((), BF16)
    grad_out = go_ref[...].astype(F32)
    both = grad_out * o_ref[...].astype(F32)
    grad_k, grad_v, grad_q = [], [], []
    for h in range(2):
        inside = (lane < width) if h == 0 else (lane >= width)
        inside_k = (lane_k < width) if h == 0 else (lane_k >= width)
        first = width if h == 0 else 0
        delta = jnp.sum(jnp.where(inside, both, 0.0), axis=1, keepdims=True)
        gx = with_parts(lane, grad_out, -delta, first, width).astype(BF16)
        kx = jnp.where(inside_k, k_ref[...], one)
        vx = jnp.where(inside_k, v_ref[...], one)
        qx = qx_ref[:, h * lanes : (h + 1) * lanes]
        prob = jnp.exp2(dot_nt(kx, qx))
        grad_v.append(dot_nn(prob.astype(BF16), gx))
        grad_score = (prob * dot_nt(vx, gx)).astype(BF16)
        grad_k.append(dot_nn(grad_score, qx))
        grad_q.append(dot_tn(kx, grad_score))
    dk_ref[...] = (jnp.where(lane_k < width, grad_k[0], grad_k[1]) * (1.0 / LOG2E)).astype(BF16)
    dv_ref[...] = jnp.where(lane_k < width, grad_v[0], grad_v[1]).astype(BF16)
    grad_both = jnp.concatenate([grad_q[0][:width], grad_q[1][width:]], axis=0)
    dq_ref[...] = (grad_both.T * (1.0 / math.sqrt(width))).astype(BF16)


def sum_rows(target, at, left, left_at, right, right_at, rows, chunk=64):
    def one(i, carry):
        here = pl.multiple_of(i * chunk, chunk)
        value = left[pl.ds(left_at + here, chunk), :].astype(F32) + right[pl.ds(right_at + here, chunk), :].astype(F32)
        target[pl.ds(at + here, chunk), :] = value.astype(target.dtype)
        return carry

    lax.fori_loop(0, rows // chunk, one, 0)


class Axis:

    def __init__(self, name, count, sems):
        self.name, self.count, self.sems = name, count, sems
        self.me = lax.axis_index(name)

    def copy(self, d, source, target):
        return send(source(self.me ^ d, d), target(self.me, d), self.sems[0].at[d], self.sems[1].at[d], {self.name: self.me ^ d})

    def start(self, source, target):
        for d in range(1, self.count):
            self.copy(d, source, target).start()

    def wait(self, source, target):
        for d in range(1, self.count):
            self.copy(d, source, target).wait()


def axis_sems(*counts):
    return [pltpu.SemaphoreType.DMA((count,)) for count in counts for _ in range(2)]


def cross(source, target, sems, i):
    return send(source, target, sems[0].at[i], sems[1].at[i], {"tp": 1 - lax.axis_index("tp")})


class RowSum:

    def __init__(self, dw_send, dw_own, extra, received, total, blocks, tp_sems, ctx):
        self.dw_send, self.dw_own, self.extra = dw_send, dw_own, extra
        self.received, self.total, self.blocks = received, total, blocks
        self.tp_sems, self.ctx = tp_sems, ctx
        self.main, self.more = dw_own.shape[0], extra.shape[1]
        self.size = (self.main + self.more) // ctx.count

    def crossing(self):
        return [
            cross(self.dw_send, self.received.at[pl.ds(0, self.main), :], self.tp_sems, 0),
            cross(self.extra.at[1], self.received.at[pl.ds(self.main, self.more), :], self.tp_sems, 1),
        ]

    def start(self):
        for copy in self.crossing():
            copy.start()

    def source(self, peer, d):
        return self.total.at[pl.ds(pl.multiple_of(peer * self.size, 16), self.size), :]

    def target(self, me, d):
        return self.blocks.at[d]

    def spread(self):
        for copy in self.crossing():
            copy.wait()
        sum_rows(self.total, 0, self.dw_own, 0, self.received, 0, self.main)
        sum_rows(self.total, self.main, self.extra.at[0], 0, self.received, self.main, self.more)
        self.ctx.start(self.source, self.target)

    def finish(self, out):
        self.ctx.wait(self.source, self.target)
        count, size, width = out.shape
        value = self.total[pl.ds(pl.multiple_of(self.ctx.me * self.size, 16), self.size), :].astype(F32)
        for d in range(1, self.ctx.count):
            value += self.blocks[d].astype(F32)
        for j in range(count):
            out[j] = value[:, j * width : (j + 1) * width].astype(out.dtype)


class ShardSum:

    def __init__(self, parts, received, blocks, shard, ctx):
        self.parts, self.received, self.blocks, self.shard, self.ctx = parts, received, blocks, shard, ctx

    def source(self, peer, d):
        return self.parts.at[peer]

    def target(self, me, d):
        return self.received.at[d]

    def start(self):
        self.shard.start(self.source, self.target)

    def mine(self, peer, d):
        return self.blocks.at[self.ctx.me]

    def theirs(self, me, d):
        return self.blocks.at[me]

    def spread(self):
        self.shard.wait(self.source, self.target)
        value = self.parts[self.shard.me].astype(F32)
        for d in range(1, self.shard.count):
            value += self.received[d].astype(F32)
        self.blocks[self.ctx.me] = value.astype(BF16)
        self.ctx.start(self.mine, self.theirs)

    def finish(self):
        self.ctx.wait(self.mine, self.theirs)


class InputSum:

    def __init__(self, dn_send, dn_own, received, total, blocks, tp_sems, ctx):
        self.dn_send, self.dn_own, self.received = dn_send, dn_own, received
        self.total, self.blocks, self.tp_sems, self.ctx = total, blocks, tp_sems, ctx

    def crossing(self, d):
        return cross(self.dn_send(d), self.received.at[d], self.tp_sems, d)

    def start(self):
        for d in reversed(range(self.ctx.count)):
            self.crossing(d).start()

    def source(self, peer, d):
        return self.total.at[d]

    def target(self, me, d):
        return self.blocks.at[d]

    def spread(self):
        for d in reversed(range(self.ctx.count)):
            self.crossing(d).wait()
            rows = self.received.shape[1]
            sum_rows(self.total.at[d], 0, self.dn_own(d), 0, self.received.at[d], 0, rows)
            if d:
                self.ctx.copy(d, self.source, self.target).start()

    def finish(self):
        self.ctx.wait(self.source, self.target)

    def rows(self, at, size):
        value = self.total[0, pl.ds(at, size), :].astype(F32)
        for d in range(1, self.ctx.count):
            value += self.blocks[d, pl.ds(at, size), :].astype(F32)
        return value


def attend_back_one(
    qx_ref, k_ref, v_ref, go_ref, o_ref, dw_all, dw_own, extra, out_half,
    dq_ref, dk_ref, dv_ref, dw_out, whole,
    received, total, blocks, tp_out, tp_in, ctx_out, ctx_in, whole_sems, *, width, nc,
):
    step = pl.program_id(0)
    last = pl.num_programs(0) - 1
    t = lax.axis_index("tp")
    rows = RowSum(dw_all.at[1], dw_own.at[0], extra, received, total, blocks, (tp_out, tp_in), Axis("ctx", nc, (ctx_out, ctx_in)))

    def whole_copies():
        return [
            cross(out_half, whole.at[:, t], (whole_sems, whole_sems.at[pl.ds(1, 1)]), 0),
            pltpu.make_async_copy(out_half, whole.at[:, t], whole_sems.at[2]),
        ]

    @pl.when(step == 0)
    def _():
        greet([("tp", 2), ("ctx", nc)])
        rows.start()
        for copy in whole_copies():
            copy.start()

    @pl.when(step == 1)
    def _():
        rows.spread()

    attend_back_step(qx_ref, k_ref, v_ref, go_ref, o_ref, dq_ref, dk_ref, dv_ref, width)

    @pl.when(step == last)
    def _():
        rows.finish(dw_out)
        for copy in whole_copies():
            copy.wait()


def attend_back_two(
    qx_ref, k_ref, v_ref, go_ref, o_ref, dw_parts, dn_all, dn_own,
    dq_ref, dk_ref, dv_ref, dw_done, dn_done,
    dw_received, dw_blocks, dn_received, dn_total, dn_blocks,
    z_out, z_in, back_out, back_in, tp_out, tp_in, ctx_out, ctx_in, *, width, nc, ns,
):
    step = pl.program_id(0)
    last = pl.num_programs(0) - 1
    weights = ShardSum(
        dw_parts, dw_received, dw_blocks, Axis("shard", ns, (z_out, z_in)), Axis("ctx", nc, (back_out, back_in))
    )
    inputs = InputSum(
        lambda d: dn_all.at[d, 1], lambda d: dn_own.at[d, 0], dn_received, dn_total, dn_blocks,
        (tp_out, tp_in), Axis("ctx", nc, (ctx_out, ctx_in)),
    )

    @pl.when(step == 0)
    def _():
        greet([("tp", 2), ("ctx", nc), ("shard", ns)])
        inputs.start()
        weights.start()

    @pl.when(step == 1)
    def _():
        inputs.spread()

    @pl.when(step == 2)
    def _():
        weights.spread()

    attend_back_step(qx_ref, k_ref, v_ref, go_ref, o_ref, dq_ref, dk_ref, dv_ref, width)

    @pl.when(step == last)
    def _():
        inputs.finish()
        weights.finish()
        dw_done[...] = dw_blocks[...]
        size = 64

        def one(i, carry):
            at = pl.multiple_of(i * size, size)
            dn_done[pl.ds(at, size), :] = inputs.rows(at, size)
            return carry

        lax.fori_loop(0, dn_done.shape[0] // size, one, 0)


def attend_back(kernel, qx, k, v, grad_mixed, mixed, width, micro, others, other_specs, out_shapes, out_specs, scratch, number):
    rows, cols = mixed.shape
    keys = k.shape[0]
    lanes = 2 * width
    return pl.pallas_call(
        functools.partial(kernel, width=width),
        grid=(cols // lanes,),
        in_specs=[
            pl.BlockSpec((rows, 2 * lanes), lambda j: (0, j)),
            pl.BlockSpec((keys, lanes), lambda j: (0, j)),
            pl.BlockSpec((keys, lanes), lambda j: (0, j)),
            pl.BlockSpec((rows, lanes), lambda j: (micro, j)),
            pl.BlockSpec((rows, lanes), lambda j: (0, j)),
        ]
        + other_specs,
        out_specs=[
            pl.BlockSpec((rows, lanes), lambda j: (0, j)),
            pl.BlockSpec((keys, lanes), lambda j: (0, j)),
            pl.BlockSpec((keys, lanes), lambda j: (0, j)),
        ]
        + out_specs,
        out_shape=[
            jax.ShapeDtypeStruct((rows, cols), BF16),
            jax.ShapeDtypeStruct((keys, cols), BF16),
            jax.ShapeDtypeStruct((keys, cols), BF16),
        ]
        + out_shapes,
        scratch_shapes=scratch,
        compiler_params=params(collective_id=number, has_side_effects=True),
        cost_estimate=pl.CostEstimate(
            flops=30 * rows * keys * cols, bytes_accessed=8 * keys * cols, transcendentals=rows * keys * cols // width
        ),
        name="attend_back",
    )(qx, k, v, grad_mixed, mixed, *others)


def once(shape, index=None):
    place = index or (0,) * len(shape)
    return pl.BlockSpec(shape, lambda *_: place, pipeline_mode=pl.Buffered(1))


def attend_back_rows(qx, k, v, grad_mixed, mixed, width, micro, dw, extra, out, ns, nc):
    main, features = dw.shape[1:]
    rows = main + extra.shape[1]
    anywhere = pl.BlockSpec(memory_space=pl.ANY)
    block = (nc, rows // nc, features)
    parts = (ns, rows // nc, features // ns)
    micros, half, _ = out.shape
    return attend_back(
        functools.partial(attend_back_one, nc=nc), qx, k, v, grad_mixed, mixed, width, micro,
        [dw, dw, extra, out],
        [anywhere, once((1, main, features)), once(extra.shape), anywhere],
        [jax.ShapeDtypeStruct(parts, BF16), jax.ShapeDtypeStruct((micros, 2, half, features), BF16)],
        [full_spec(parts), anywhere],
        [
            pltpu.VMEM((rows, features), BF16), pltpu.VMEM((rows, features), BF16), pltpu.VMEM(block, BF16),
            *axis_sems(2, nc), pltpu.SemaphoreType.DMA((3,)),
        ],
        3,
    )


def attend_back_inputs(qx, k, v, grad_mixed, mixed, width, micro, dw_parts, dn, ns, nc):
    _, size, part = dw_parts.shape
    half, features = dn.shape[2:]
    anywhere = pl.BlockSpec(memory_space=pl.ANY)
    block = pltpu.VMEM((nc, half, features), BF16)
    return attend_back(
        functools.partial(attend_back_two, nc=nc, ns=ns), qx, k, v, grad_mixed, mixed, width, micro,
        [dw_parts, dn, dn],
        [once(dw_parts.shape), anywhere, once((nc, 1, half, features))],
        [jax.ShapeDtypeStruct((nc, size, part), BF16), jax.ShapeDtypeStruct((half, features), F32)],
        [full_spec((nc, size, part)), full_spec((half, features))],
        [
            pltpu.VMEM(dw_parts.shape, BF16), pltpu.VMEM((nc, size, part), BF16), block, block, block,
            *axis_sems(ns, nc, nc, nc),
        ],
        4,
    )


def ffn_kernel(
    x_ref, o_ref, g_ref, w_out, w_up, w_down, bup_ref, vec_ref,
    out_ref, gm_ref, gx_ref, dw_ref, dup_ref, dvec_ref, dw_acc,
):
    step = pl.program_id(0)
    steps = pl.num_programs(0)
    b_out, b_down, gain, shift = (vec_ref[i : i + 1, :] for i in range(4))
    hw = w_out.shape[1]
    hidden = w_up.shape[2]

    @pl.when(step == 0)
    def _():
        dw_acc[...] = jnp.zeros_like(dw_acc)
        dup_ref[...] = jnp.zeros_like(dup_ref)
        dvec_ref[...] = jnp.zeros_like(dvec_ref)

    mixed = o_ref[...]
    grad_b = g_ref[...]
    grad = grad_b.astype(F32)
    attended = dot_nn(mixed[:, :hw], w_out[0]) + dot_nn(mixed[:, hw:], w_out[1])
    middle = x_ref[...].astype(F32) + (attended + b_out)
    unit, inverse = unit_norm(middle)
    normed = (unit * gain + shift).astype(BF16)
    ffn_out = jnp.zeros_like(middle)
    grad_normed = jnp.zeros_like(middle)
    for part in range(2):
        pre = dot_nn(normed, w_up[part]) + bup_ref[part]
        gate = 0.5 + 0.5 * lax.erf(pre * math.sqrt(0.5))
        active = (pre * gate).astype(BF16)
        ffn_out += dot_nn(active, w_down[part])
        slope = gate + pre * jnp.exp(pre * pre * -0.5) * (1.0 / math.sqrt(2.0 * math.pi))
        grad_pre_f = dot_nt(grad_b, w_down[part]) * slope
        grad_pre = grad_pre_f.astype(BF16)
        dup_ref[part] += column_sum(grad_pre.astype(F32))
        grad_normed += dot_nt(grad_pre, w_up[part])
        dw_acc[part, hw : hw + hidden] += dot_tn(active, grad_b)
        dw_acc[part, hw + hidden :] += dot_tn(grad_pre, normed)
    out_ref[...] = (middle + (ffn_out + b_down)).astype(BF16)
    grad_middle = grad + norm_back(grad_normed, unit, inverse, gain)
    gm_ref[...] = grad_middle
    grad_att = grad_middle.astype(BF16)
    dvec_ref[0:1] += column_sum(grad_att.astype(F32))
    dvec_ref[1:2] += column_sum(grad)
    dvec_ref[2:3] += column_sum(grad_normed * unit)
    dvec_ref[3:4] += column_sum(grad_normed)
    for part in range(2):
        cols = slice(part * hw, (part + 1) * hw)
        gx_ref[:, cols] = dot_nt(grad_att, w_out[part]).astype(BF16)
        dw_acc[part, :hw] += dot_tn(mixed[:, cols], grad_att)

    @pl.when(step == steps - 1)
    def _():
        dw_ref[...] = dw_acc[...].astype(BF16)


def feed_forward(x, mixed, grad, w_out, w_up, w_down, b_up, vectors):
    rows, features = x.shape
    block = 256
    hw, hidden = w_out.shape[1], w_up.shape[2]
    total = hw + 2 * hidden
    row_spec = pl.BlockSpec((block, features), lambda i: (i, 0))

    def fixed(shape):
        return pl.BlockSpec(shape, lambda i: (0,) * len(shape), pipeline_mode=pl.Buffered(1))

    return pl.pallas_call(
        ffn_kernel,
        grid=(rows // block,),
        in_specs=[row_spec] * 3
        + [fixed(w.shape) for w in (w_out, w_up, w_down)]
        + [fixed(b_up.shape), fixed(vectors.shape)],
        out_specs=[row_spec] * 3
        + [full_spec((2, total, features)), full_spec((2, 1, hidden)), full_spec((8, features))],
        out_shape=[
            jax.ShapeDtypeStruct((rows, features), BF16),
            jax.ShapeDtypeStruct((rows, features), F32),
            jax.ShapeDtypeStruct((rows, 2 * hw), BF16),
            jax.ShapeDtypeStruct((2, total, features), BF16),
            jax.ShapeDtypeStruct((2, 1, hidden), F32),
            jax.ShapeDtypeStruct((8, features), F32),
        ],
        scratch_shapes=[pltpu.VMEM((2, total, features), F32)],
        compiler_params=params(),
        cost_estimate=pl.CostEstimate(
            flops=12 * rows * total * features, bytes_accessed=20 * total * features, transcendentals=4 * rows * hidden
        ),
        name="feed_forward",
    )(x, mixed, grad, w_out, w_up, w_down, b_up, vectors)


def back_kernel(x_ref, n_ref, dk_ref, dv_ref, dq_ref, w_ref, dw_start, db_start, dn_ref, dw_ref, db_ref, dw_acc):
    step = pl.program_id(0)
    width = w_ref.shape[3]
    normed = n_ref[...]
    unit, _ = unit_norm(x_ref[...].astype(F32))
    total = jnp.zeros(n_ref.shape, F32)

    @pl.when(step == 0)
    def _():
        dw_acc[...] = dw_start[...]
        db_ref[...] = db_start[...]
        query = jnp.zeros(n_ref.shape, F32)
        grad = dq_ref[...]
        for part in range(2):
            cols = slice(part * width, (part + 1) * width)
            dw_acc[part, 0] += dot_tn(grad[:, cols], normed)
            query += dot_nt(grad[:, cols], w_ref[part, 0])
        db_ref[0:1] += column_sum(grad.astype(F32))
        db_ref[2:3] += column_sum(query * unit)
        db_ref[3:4] += column_sum(query)
        dn_ref[...] = query.astype(BF16)

    for kind, ref in ((1, dk_ref), (2, dv_ref)):
        for part in range(2):
            cols = slice(part * width, (part + 1) * width)
            grad = ref[:, cols]
            total += dot_nt(grad, w_ref[part, kind])
            dw_acc[part, kind] += dot_tn(grad, normed)
    db_ref[1:2] += column_sum(dv_ref[...].astype(F32))
    db_ref[2:3] += column_sum(total * unit)
    db_ref[3:4] += column_sum(total)

    @pl.when(step == 0)
    def _():
        dn_ref[...] = (total + dn_ref[...].astype(F32)).astype(BF16)

    @pl.when(step > 0)
    def _():
        dn_ref[...] = total.astype(BF16)

    @pl.when(step == pl.num_programs(0) - 1)
    def _():
        dw_ref[...] = dw_acc[...].astype(dw_ref.dtype)


def project_back(x_all, normed, dq, dk, dv, weights, dw_start, db_start, kind):
    keys, features = normed.shape
    block = keys // 8
    width = weights.shape[3]
    stack = (2, 3, width, features)
    return pl.pallas_call(
        back_kernel,
        grid=(8,),
        in_specs=[
            pl.BlockSpec((block, features), lambda i: (i, 0)),
            pl.BlockSpec((block, features), lambda i: (i, 0)),
            pl.BlockSpec((block, 2 * width), lambda i: (i, 0)),
            pl.BlockSpec((block, 2 * width), lambda i: (i, 0)),
            once((block, 2 * width)),
            once(weights.shape),
            once(stack),
            once((8, 2 * width)),
        ],
        out_specs=[
            pl.BlockSpec((block, features), lambda i: (i, 0)),
            full_spec(stack),
            full_spec((8, 2 * width)),
        ],
        out_shape=[
            jax.ShapeDtypeStruct((keys, features), BF16),
            jax.ShapeDtypeStruct(stack, kind),
            jax.ShapeDtypeStruct((8, 2 * width), F32),
        ],
        scratch_shapes=[pltpu.VMEM(stack, F32)],
        compiler_params=params(),
        cost_estimate=pl.CostEstimate(
            flops=16 * keys * features * width, bytes_accessed=8 * keys * features, transcendentals=0
        ),
        name="project_back",
    )(x_all, normed, dk, dv, dq, weights, dw_start, db_start)


def last_kernel(
    dn_ref, dw_ref, extra_ref, dn_first, x_ref, gm_ref, gain_ref,
    grad_ref, blocks_ref,
    w_received, w_total, w_blocks, z_parts, z_received, dn_received, dn_total, dn_blocks,
    wtp_out, wtp_in, wctx_out, wctx_in, z_out, z_in, back_out, back_in, tp_out, tp_in, ctx_out, ctx_in,
    row_out, row_in, *, ns, nc,
):
    t = lax.axis_index("tp")
    micros, _, half, _ = grad_ref.shape
    rows = RowSum(
        dw_ref.at[1], dw_ref.at[0], extra_ref, w_received, w_total, w_blocks, (wtp_out, wtp_in),
        Axis("ctx", nc, (wctx_out, wctx_in)),
    )
    weights = ShardSum(
        z_parts, z_received, blocks_ref, Axis("shard", ns, (z_out, z_in)), Axis("ctx", nc, (back_out, back_in))
    )
    inputs = InputSum(
        lambda d: dn_ref.at[d, 1], lambda d: dn_ref.at[d, 0], dn_received, dn_total, dn_blocks,
        (tp_out, tp_in), Axis("ctx", nc, (ctx_out, ctx_in)),
    )

    def row(micro):
        return cross(grad_ref.at[micro, t], grad_ref.at[micro, t], (row_out, row_in), micro)

    def finish_rows(micro, grad_rows):
        size = 64

        def one(i, carry):
            at = pl.multiple_of(i * size, size)
            unit, inverse = unit_norm(x_ref[micro, pl.ds(at, size), :].astype(F32))
            value = gm_ref[micro, pl.ds(at, size), :] + norm_back(grad_rows(at, size), unit, inverse, gain_ref[...])
            grad_ref[micro, t, pl.ds(at, size), :] = value.astype(BF16)
            return carry

        lax.fori_loop(0, half // size, one, 0)
        row(micro).start()

    greet([("tp", 2), ("ctx", nc), ("shard", ns)])
    rows.start()
    inputs.start()
    rows.spread()
    inputs.spread()
    for micro in range(micros - 1):
        finish_rows(micro, lambda at, size: dn_first[micro, pl.ds(at, size), :])
    rows.finish(z_parts)
    weights.start()
    weights.spread()
    inputs.finish()
    finish_rows(micros - 1, inputs.rows)
    weights.finish()
    for micro in range(micros):
        row(micro).wait()


def last_sums(dn, dw, extra, dn_first, x, grad_middle, gain, ns, nc):
    main, features = dw.shape[1:]
    rows = main + extra.shape[1]
    micros, half, _ = x.shape
    size, part = rows // nc, features // ns
    block = pltpu.VMEM((nc, half, features), BF16)
    return pl.pallas_call(
        functools.partial(last_kernel, ns=ns, nc=nc),
        in_specs=[pl.BlockSpec(memory_space=pltpu.VMEM)] * 7,
        out_specs=[pl.BlockSpec(memory_space=pltpu.VMEM)] * 2,
        out_shape=[
            jax.ShapeDtypeStruct((micros, 2, half, features), BF16),
            jax.ShapeDtypeStruct((nc, size, part), BF16),
        ],
        scratch_shapes=[
            pltpu.VMEM((rows, features), BF16), pltpu.VMEM((rows, features), BF16), pltpu.VMEM((nc, size, features), BF16),
            pltpu.VMEM((ns, size, part), BF16), pltpu.VMEM((ns, size, part), BF16), block, block, block,
            *axis_sems(2, nc, ns, nc, nc, nc, micros),
        ],
        compiler_params=params(collective_id=5, has_side_effects=True),
        name="last_sums",
    )(dn, dw, extra, dn_first, x, grad_middle, gain)


def pad_rows(rows, multiple):
    extra = -rows.shape[0] % multiple
    return jnp.concatenate([rows, jnp.zeros((extra,) + rows.shape[1:], rows.dtype)]) if extra else rows


def body(
    tokens, cotangent, w_query, w_key, w_value, w_out, w_up, w_down,
    b_query, b_value, b_up, b_out, b_down, gain_attn, shift_attn, gain_ffn, shift_ffn,
):
    ns, nc = lax.axis_size("shard"), lax.axis_size("ctx")
    t = lax.axis_index("tp")
    micros, _, length, features = tokens.shape
    half = length // 2
    heads, head_part = b_query.shape
    head_width = head_part * ns
    up_part = b_up.shape[1]
    feature_part = b_out.shape[0]

    smalls = [b_query, b_value, b_up, b_out, b_down, gain_attn, shift_attn, gain_ffn, shift_ffn]
    flat = jnp.concatenate([v.reshape(-1) for v in smalls])
    small = jnp.pad(flat, (0, -flat.shape[0] % 2048)).reshape(-1, 128)
    w_all, small_all, x_first = gather_first(
        jnp.stack([w_query, w_key, w_value]), small, tokens[0, 0], ns, nc
    )
    small_all = small_all.reshape(2, ns, -1)
    offset = 0
    vectors = []
    for v in smalls:
        vectors.append(small_all[:, :, offset : offset + v.size])
        offset += v.size

    def by_head(v, part):
        return v.reshape(2, ns, heads, part).transpose(0, 2, 1, 3).reshape(2, heads * part * ns).astype(F32)

    def plain(v):
        return v[0].reshape(1, features).astype(F32)

    bq = by_head(vectors[0], head_part).reshape(1, -1)
    bv = by_head(vectors[1], head_part).reshape(1, -1)
    bup = by_head(vectors[2], up_part)[:, None, :]
    v_out, v_down, g_one, s_one, g_two, s_two = (plain(v) for v in vectors[3:])

    mine = lax.dynamic_slice_in_dim(tokens[:, 0], t * half, half, 1)
    grad_mine = lax.dynamic_slice_in_dim(cotangent[:, 0], t * half, half, 1)
    keys = 2 * nc * half
    aligned = feature_part % 128 == 0
    column_place = place_columns if aligned else place_slot

    def column_shape(w):
        return (2, w.shape[0], features) if aligned else (2, ns) + w.shape

    def whole_columns(w):
        if not aligned:
            w = w.transpose(0, 2, 1, 3).reshape(2, w.shape[2], features)
        return w

    plans = [
        (("ctx", nc, place_distance, True), ("shard", ns, place_rows, False), ("shard", ns, column_place, False)),
        (("shard", ns, column_place, False),),
    ]
    sources = [(tokens[1, 0], w_up, w_out), (w_down,)]
    shapes = [
        ((nc, 2, half, features), (2, features, w_up.shape[1]), column_shape(w_out)),
        (column_shape(w_down),),
    ]
    x_alls = [x_first.reshape(keys, features), None]
    saved = []
    arrived = []
    for micro in range(micros):
        normed, k, v, q = front(x_alls[micro], w_all, g_one, s_one, bq, bv, head_width)
        mixed, qx, *more = attend_forward(
            q, k, v, head_width, plans[micro], sources[micro], shapes[micro], micro + 1
        )
        if micro == 0:
            x_alls[1] = more.pop(0).reshape(keys, features)
        arrived += more
        saved.append((normed, k, v, qx, mixed))
    wu, wo, wd = arrived[0], whole_columns(arrived[1]), whole_columns(arrived[2])

    out, grad_middle, grad_mixed, dw, dup, dvec = feed_forward(
        mine.reshape(-1, features),
        jnp.concatenate([entry[4] for entry in saved]),
        grad_mine.reshape(-1, features),
        wo, wu, wd, bup, jnp.concatenate([v_out, v_down, g_two, s_two] * 2),
    )

    def spread(v, part):
        return v.reshape(heads, ns, part).transpose(1, 0, 2).reshape(ns, -1)

    def as_rows(v):
        count = v.shape[1] // feature_part
        return v.reshape(ns, count, feature_part).transpose(1, 0, 2).reshape(count, features)

    extra = jnp.stack(
        [pad_rows(jnp.concatenate([dvec[:4], as_rows(spread(dup[part, 0], up_part))]), 16 * nc) for part in range(2)]
    ).astype(BF16)

    width = heads * head_width
    normed, k, v, qx, mixed = saved[0]
    dq, dk, dv, dw_parts, output = attend_back_rows(
        qx, k, v, grad_mixed, mixed, head_width, 0, dw, extra, out.reshape(micros, half, features), ns, nc
    )
    start_dw = jnp.zeros((2, 3, width, features), F32)
    start_db = jnp.zeros((8, 2 * width), F32)
    dn, dw_now, db_now = project_back(x_alls[0], normed, dq, dk, dv, w_all, start_dw, start_db, F32)
    normed, k, v, qx, mixed = saved[1]
    dq, dk, dv, dw_done, dn_first = attend_back_inputs(
        qx, k, v, grad_mixed, mixed, head_width, 1, dw_parts, dn.reshape(nc, 2, half, features), ns, nc
    )
    dn, dw_now, db_now = project_back(x_alls[1], normed, dq, dk, dv, w_all, dw_now, db_now, BF16)

    extras = []
    for part in range(2):
        cols = slice(part * width, (part + 1) * width)
        biases = jnp.concatenate([spread(db_now[0, cols], head_part), spread(db_now[1, cols], head_part)], axis=1)
        extras.append(pad_rows(jnp.concatenate([db_now[2:4], as_rows(biases)]), 16 * nc))
    grad_tokens, attn_done = last_sums(
        dn.reshape(nc, 2, half, features), dw_now.reshape(2, 3 * width, features), jnp.stack(extras).astype(BF16),
        dn_first[None], mine, grad_middle.reshape(micros, half, features), g_one, ns, nc,
    )

    output = output.reshape(micros, 1, length, features)
    grad_tokens = grad_tokens.reshape(micros, 1, length, features)
    done_ffn = dw_done.reshape(-1, feature_part).astype(F32)
    done_attn = attn_done.reshape(-1, feature_part).astype(F32)
    hidden = heads * up_part * ns
    g_out, g_down, g_up = done_ffn[:width], done_ffn[width : width + hidden], done_ffn[width + hidden : width + 2 * hidden]
    tail = done_ffn[width + 2 * hidden :]
    g_query, g_key, g_value = (done_attn[i * width : (i + 1) * width].T for i in range(3))
    tail_attn = done_attn[3 * width :]
    g_bup = tail[4:].reshape(-1)[: heads * up_part].reshape(heads, up_part)
    g_heads = tail_attn[2:].reshape(-1)
    g_bq = g_heads[: heads * head_part].reshape(heads, head_part)
    g_bv = g_heads[heads * head_part : 2 * heads * head_part].reshape(heads, head_part)
    return (
        output, grad_tokens, g_query, g_key, g_value, g_out, g_up.T, g_down, g_bq, g_bv, g_bup,
        tail[0], tail[1], tail_attn[0], tail_attn[1], tail[2], tail[3],
    )


def solution(mesh):
    wide, tall = P("shard", "tp"), P("tp", "shard")
    rows, vector = P(None, "shard", "ctx", None), P("shard")
    weights = (wide, wide, wide, tall, wide, tall)
    return jax.shard_map(
        body,
        mesh=mesh,
        in_specs=(rows, rows) + weights + (tall,) * 3 + (vector,) * 6,
        out_specs=(rows, rows) + weights + (tall,) * 3 + (vector,) * 6,
        check_vma=False,
    )
```

```python
import functools
import math

import jax
import jax.numpy as jnp
from jax import lax
from jax.experimental import pallas as pl
from jax.experimental.pallas import tpu as pltpu
from jax.sharding import PartitionSpec as P

F32 = jnp.float32
BF16 = jnp.bfloat16
MESH = pl.DeviceIdType.MESH
norm_eps = 1e-05
LOG2E = math.log2(math.e)
VMEM_LIMIT = 60 * 2**20


def dot_nn(left, right):
    return lax.dot_general(left, right, (((1,), (0,)), ((), ())), preferred_element_type=F32)


def dot_nt(left, right):
    return lax.dot_general(left, right, (((1,), (1,)), ((), ())), preferred_element_type=F32)


def dot_tn(left, right):
    return lax.dot_general(left, right, (((0,), (0,)), ((), ())), preferred_element_type=F32)


def unit_norm(values):
    average = jnp.mean(values, axis=-1, keepdims=True)
    centred = values - average
    variance = jnp.mean(centred * centred, axis=-1, keepdims=True)
    inverse = lax.rsqrt(variance + norm_eps)
    return centred * inverse, inverse


def norm_back(grad_normed, unit_vals, inverse, gain):
    scaled = grad_normed * gain
    return inverse * (
        scaled
        - jnp.mean(scaled, axis=-1, keepdims=True)
        - unit_vals * jnp.mean(scaled * unit_vals, axis=-1, keepdims=True)
    )


def column_sum(values):
    return jnp.sum(values, axis=0, keepdims=True)


def full_spec(shape):
    return pl.BlockSpec(shape, lambda *_: (0,) * len(shape))


def params(limit=VMEM_LIMIT, **others):
    return pltpu.CompilerParams(vmem_limit_bytes=limit, **others)


def once(shape, index=None):
    place = index or (0,) * len(shape)
    return pl.BlockSpec(shape, lambda *_: place, pipeline_mode=pl.Buffered(1))


def send(source, target, send_sem, recv_sem, where):
    return pltpu.make_async_remote_copy(
        src_ref=source, dst_ref=target, send_sem=send_sem, recv_sem=recv_sem, device_id=where, device_id_type=MESH
    )


def gather_kernel(ns, nc, wq_ref, wk_ref, wv_ref, small_ref, x_block, w_out, small_out, x_out, *sems):
    w_send, w_recv, s_send, s_recv, x_send, x_recv, wt_send, wt_recv, st_send, st_recv, xt_send, xt_recv, local = sems
    w_refs = (wq_ref, wk_ref, wv_ref)
    kinds = range(3)
    x_ref = x_block.at[0, 0]
    s = lax.axis_index("shard")
    c = lax.axis_index("ctx")
    t = lax.axis_index("tp")
    other = 1 - t
    depth = wq_ref.shape[0]
    half = x_ref.shape[0] // 2

    barrier = pltpu.get_barrier_semaphore()
    for d in range(1, ns):
        pl.semaphore_signal(barrier, inc=1, device_id={"shard": s ^ d}, device_id_type=MESH)
    for d in range(1, nc):
        pl.semaphore_signal(barrier, inc=1, device_id={"ctx": c ^ d}, device_id_type=MESH)
    pl.semaphore_signal(barrier, inc=1, device_id={"tp": other}, device_id_type=MESH)
    pl.semaphore_wait(barrier, ns + nc - 1)

    def w_rows(part, kind, owner):
        return w_out.at[part, kind, pl.ds(pl.multiple_of(owner * depth, depth), depth), :]

    def x_rows(which):
        return x_ref.at[pl.ds(pl.multiple_of(which * half, half), half), :]

    def begin(source, target, send_sem, recv_sem, where):
        copy = send(source, target, send_sem, recv_sem, where)
        copy.start()
        return copy

    x_copies, w_copies, s_copies = {}, {}, {}
    for d in range(1, nc):
        x_copies[d] = begin(x_rows(t), x_out.at[d, 0], x_send.at[d], x_recv.at[d], {"ctx": c ^ d})
    for d in range(1, ns):
        for k in kinds:
            w_copies[d, k] = begin(
                w_refs[k], w_rows(0, k, s), w_send.at[k, d], w_recv.at[k, d], {"shard": s ^ d}
            )
        s_copies[d] = begin(small_ref, small_out.at[0, s], s_send.at[d], s_recv.at[d], {"shard": s ^ d})
    last = [begin(w_refs[k], w_rows(1, k, s), wt_send.at[k, 0], wt_recv.at[k, 0], {"tp": other}) for k in kinds]
    last.append(begin(small_ref, small_out.at[1, s], st_send.at[0], st_recv.at[0], {"tp": other}))
    locals_ = [pltpu.make_async_copy(w_refs[k], w_rows(0, k, s), local.at[k]) for k in kinds]
    locals_ += [
        pltpu.make_async_copy(small_ref, small_out.at[0, s], local.at[3]),
        pltpu.make_async_copy(x_rows(t), x_out.at[0, 0], local.at[4]),
        pltpu.make_async_copy(x_rows(other), x_out.at[0, 1], local.at[5]),
    ]
    for copy in locals_:
        copy.start()
    for d in range(1, max(ns, nc)):
        if d < ns:
            for k in kinds:
                w_copies[d, k].wait_recv()
                last.append(
                    begin(
                        w_rows(0, k, s ^ d), w_rows(1, k, s ^ d), wt_send.at[k, d], wt_recv.at[k, d], {"tp": other}
                    )
                )
            s_copies[d].wait_recv()
            last.append(
                begin(small_out.at[0, s ^ d], small_out.at[1, s ^ d], st_send.at[d], st_recv.at[d], {"tp": other})
            )
        if d < nc:
            x_copies[d].wait_recv()
            last.append(begin(x_out.at[d, 0], x_out.at[d, 1], xt_send.at[d], xt_recv.at[d], {"tp": other}))
    for copies in (x_copies, w_copies, s_copies):
        for copy in copies.values():
            copy.wait_send()
    for copy in last:
        copy.wait()
    for copy in locals_:
        copy.wait()


def gather_first(weights, small, tokens, ns, nc):
    depth, width = weights[0].shape
    length, features = tokens.shape[2:]
    dma = pltpu.SemaphoreType.DMA
    vmem = pl.BlockSpec(memory_space=pltpu.VMEM)
    return pl.pallas_call(
        functools.partial(gather_kernel, ns, nc),
        grid=(1,),
        in_specs=[vmem] * 4 + [once((1, 1, length, features))],
        out_specs=[pl.BlockSpec(memory_space=pl.ANY)] * 3,
        out_shape=[
            jax.ShapeDtypeStruct((2, 3, ns * depth, width), BF16),
            jax.ShapeDtypeStruct((2, ns) + small.shape, BF16),
            jax.ShapeDtypeStruct((nc, 2, length // 2, features), BF16),
        ],
        scratch_shapes=[dma((3, ns)), dma((3, ns)), dma((ns,)), dma((ns,)), dma((nc,)), dma((nc,))]
        + [dma((3, ns)), dma((3, ns)), dma((ns,)), dma((ns,)), dma((nc,)), dma((nc,)), dma((6,))],
        compiler_params=params(collective_id=0, has_side_effects=True),
        name="gather_first",
    )(*weights, small, tokens)


def front_kernel(x_ref, w_ref, vec_ref, bias_ref, n_ref, k_ref, v_ref, q_ref, *, q_scale):
    step = pl.program_id(0)
    gain, shift = vec_ref[2:3], vec_ref[3:4]
    width = w_ref.shape[3]
    size = x_ref.shape[0] // 4
    for i in range(4):
        rows = slice(i * size, (i + 1) * size)
        unit, _ = unit_norm(x_ref[rows].astype(F32))
        normed = (unit * gain + shift).astype(BF16)
        n_ref[rows] = normed
        for part in range(2):
            cols = slice(part * width, (part + 1) * width)
            k_ref[rows, cols] = dot_nn(normed, w_ref[part, 1]).astype(BF16)
            v_ref[rows, cols] = (dot_nn(normed, w_ref[part, 2]) + bias_ref[1:2, cols]).astype(BF16)

    @pl.when(step == 0)
    def _():
        normed = n_ref[: q_ref.shape[0]]
        for part in range(2):
            cols = slice(part * width, (part + 1) * width)
            q_ref[:, cols] = ((dot_nn(normed, w_ref[part, 0]) + bias_ref[0:1, cols]) * q_scale).astype(BF16)


def front(x_all, weights, vectors, biases, head_width, half):
    keys, features = x_all.shape
    block = 2 * half
    width = 2 * weights.shape[3]
    return pl.pallas_call(
        functools.partial(front_kernel, q_scale=LOG2E / math.sqrt(head_width)),
        grid=(keys // block,),
        in_specs=[
            pl.BlockSpec((block, features), lambda i: (i, 0)),
            once(weights.shape),
            once(vectors.shape),
            once(biases.shape),
        ],
        out_specs=[
            pl.BlockSpec((block, features), lambda i: (i, 0)),
            pl.BlockSpec((block, width), lambda i: (i, 0)),
            pl.BlockSpec((block, width), lambda i: (i, 0)),
            full_spec((half, width)),
        ],
        out_shape=[
            jax.ShapeDtypeStruct((keys, features), BF16),
            jax.ShapeDtypeStruct((keys, width), BF16),
            jax.ShapeDtypeStruct((keys, width), BF16),
            jax.ShapeDtypeStruct((half, width), BF16),
        ],
        compiler_params=params(),
        cost_estimate=pl.CostEstimate(
            flops=4 * keys * features * width, bytes_accessed=8 * keys * features, transcendentals=keys
        ),
        name="front",
    )(x_all, weights, vectors, biases)


def with_parts(lane, base, values, first, width):
    high = values.astype(BF16).astype(F32)
    rest = values - high
    middle = rest.astype(BF16).astype(F32)
    low = rest - middle
    extra = jnp.where(
        lane == first, high, jnp.where(lane == first + 1, middle, jnp.where(lane == first + 2, low, 0.0))
    )
    inside = (lane < width) if first else (lane >= width)
    return jnp.where(inside, base, extra)


def greet(counts):
    barrier = pltpu.get_barrier_semaphore()
    total = 0
    for name, count in counts:
        me = lax.axis_index(name)
        for d in range(1, count):
            pl.semaphore_signal(barrier, inc=1, device_id={name: me ^ d}, device_id_type=MESH)
            total += 1
    pl.semaphore_wait(barrier, total)


class Gather:

    def __init__(self, name, count, source, theirs, target, place, sems):
        self.name, self.count, self.source, self.theirs = name, count, source, theirs
        self.target, self.place = target, place
        self.out_sem, self.in_sem, self.cross_out, self.cross_in, self.local = sems
        self.me = lax.axis_index(name)

    def first(self, d):
        where = {self.name: self.me ^ d}
        return send(self.source, self.place(self.target, 0, self.me, d), self.out_sem.at[d], self.in_sem.at[d], where)

    def cross(self, d):
        where = {"tp": 1 - lax.axis_index("tp")}
        owner = self.me ^ d
        source = self.place(self.target, 0, owner, d) if d else self.source
        return send(source, self.place(self.target, 1, owner, d), self.cross_out.at[d], self.cross_in.at[d], where)

    def locals(self):
        copies = [pltpu.make_async_copy(self.source, self.place(self.target, 0, self.me, 0), self.local.at[0])]
        if self.theirs is not None:
            copies.append(pltpu.make_async_copy(self.theirs, self.place(self.target, 1, self.me, 0), self.local.at[1]))
        return copies

    def crossed(self):
        return range(0 if self.theirs is None else 1, self.count)

    def start(self):
        for d in range(1, self.count):
            self.first(d).start()
        for copy in self.locals():
            copy.start()
        if self.theirs is None:
            self.cross(0).start()

    def forward(self):
        for d in range(1, self.count):
            self.first(d).wait_recv()
            self.cross(d).start()

    def finish(self):
        for d in range(1, self.count):
            self.first(d).wait_send()
        for d in self.crossed():
            self.cross(d).wait()
        for copy in self.locals():
            copy.wait()


def place_rows(ref, part, owner, d):
    size = ref.shape[1] // lax.axis_size("shard")
    return ref.at[part, pl.ds(pl.multiple_of(owner * size, size), size), :]


def place_columns(ref, part, owner, d):
    size = ref.shape[2] // lax.axis_size("shard")
    return ref.at[part, :, pl.ds(pl.multiple_of(owner * size, size), size)]


def place_slot(ref, part, owner, d):
    return ref.at[part, owner]


def place_distance(ref, part, owner, d):
    return ref.at[d, part]


def gather_sems(count):
    dma = pltpu.SemaphoreType.DMA
    return [dma((count,)), dma((count,)), dma((count,)), dma((count,)), dma((2,))]


def attend_kernel(*refs, kc, width, plans):
    count = len(plans)
    q_ref, k_ref, v_ref = refs[:3]
    sources = refs[3 : 3 + count]
    o_ref, qx_ref = refs[3 + count : 5 + count]
    targets = refs[5 + count : 5 + 2 * count]
    scores = refs[5 + 2 * count]
    sems = refs[6 + 2 * count :]
    step = pl.program_id(0)
    last = pl.num_programs(0) - 1
    t = lax.axis_index("tp")

    def gathers(wanted):
        found = []
        for i, (name, number, place, split) in enumerate(plans):
            if name != wanted:
                continue
            source, theirs = sources[i], None
            if split:
                source = source.at[0, 0]
                half = source.shape[0] // 2
                theirs = source.at[pl.ds(pl.multiple_of((1 - t) * half, half), half), :]
                source = source.at[pl.ds(pl.multiple_of(t * half, half), half), :]
            found.append(Gather(name, number, source, theirs, targets[i], place, sems[5 * i : 5 * i + 5]))
        return found

    counts = {name: number for name, number, _, _ in plans}

    @pl.when(step == 0)
    def _():
        greet([("tp", 2)] + list(counts.items()))
        for name in counts:
            for gather in gathers(name):
                gather.start()

    @pl.when(step == last)
    def _():
        for gather in gathers("ctx"):
            gather.forward()

    rows, lanes = q_ref.shape
    keys = k_ref.shape[0]
    lane = lax.broadcasted_iota(jnp.int32, (rows, lanes), 1)
    lane_v = lax.broadcasted_iota(jnp.int32, (kc, lanes), 1)
    q = q_ref[...].astype(F32)
    tops = []
    for h in range(2):
        inside = (lane < width) if h == 0 else (lane >= width)
        q_head = jnp.where(inside, q, 0.0).astype(BF16)
        top = None
        for i in range(keys // kc):
            part = dot_nt(k_ref[i * kc : (i + 1) * kc], q_head)
            scores[h, i * kc : (i + 1) * kc] = part
            here = jnp.max(part.reshape(kc // 8, 8, rows), axis=0)
            top = here if top is None else jnp.maximum(top, here)
        tops.append(jnp.max(top, axis=0, keepdims=True))
    outs = []
    for h in range(2):
        inside_v = (lane_v < width) if h == 0 else (lane_v >= width)
        total = jnp.zeros((lanes, rows), F32)
        for i in range(keys // kc):
            v_one = jnp.where(inside_v, v_ref[i * kc : (i + 1) * kc], jnp.ones((), BF16))
            exponent = jnp.exp2(scores[h, i * kc : (i + 1) * kc] - tops[h]).astype(BF16)
            total += dot_tn(v_one, exponent)
        first = width if h == 0 else 0
        log_total = tops[h] + jnp.log2(total[first : first + 1, :])
        total = total.T
        outs.append(total / pltpu.roll(total, width, 1))
        log_column = jnp.broadcast_to(log_total, (8, rows)).T[:, :1]
        qx_ref[:, h * lanes : (h + 1) * lanes] = with_parts(lane, q, -log_column, first, width).astype(BF16)
    o_ref[...] = jnp.where(lane < width, outs[0], outs[1]).astype(BF16)

    @pl.when(step == last)
    def _():
        for gather in gathers("shard"):
            gather.forward()
        for name in counts:
            for gather in gathers(name):
                gather.finish()


def attend_forward(q, k, v, width, plans, sources, source_specs, shapes, number):
    rows, cols = q.shape
    keys = k.shape[0]
    lanes = 2 * width
    kc = 512
    anywhere = pl.BlockSpec(memory_space=pl.ANY)
    return pl.pallas_call(
        functools.partial(attend_kernel, kc=kc, width=width, plans=plans),
        grid=(cols // lanes,),
        in_specs=[
            pl.BlockSpec((rows, lanes), lambda j: (0, j)),
            pl.BlockSpec((keys, lanes), lambda j: (0, j)),
            pl.BlockSpec((keys, lanes), lambda j: (0, j)),
        ]
        + source_specs,
        out_specs=[
            pl.BlockSpec((rows, lanes), lambda j: (0, j)),
            pl.BlockSpec((rows, 2 * lanes), lambda j: (0, j)),
        ]
        + [anywhere] * len(plans),
        out_shape=[
            jax.ShapeDtypeStruct((rows, cols), BF16),
            jax.ShapeDtypeStruct((rows, 2 * cols), BF16),
        ]
        + [jax.ShapeDtypeStruct(shape, BF16) for shape in shapes],
        scratch_shapes=[pltpu.VMEM((2, keys, rows), F32)]
        + [sem for plan in plans for sem in gather_sems(plan[1])],
        compiler_params=params(collective_id=number, has_side_effects=True),
        cost_estimate=pl.CostEstimate(
            flops=12 * rows * keys * cols, bytes_accessed=4 * keys * cols, transcendentals=rows * keys * cols // width
        ),
        name="attend_forward",
    )(q, k, v, *sources)


def attend_back_step(qx_ref, k_ref, v_ref, go_ref, o_ref, dq_ref, dk_ref, dv_ref, width):
    rows, lanes = o_ref.shape
    keys = k_ref.shape[0]
    lane = lax.broadcasted_iota(jnp.int32, (rows, lanes), 1)
    lane_k = lax.broadcasted_iota(jnp.int32, (keys, lanes), 1)
    one = jnp.ones((), BF16)
    grad_out = go_ref[...].astype(F32)
    both = grad_out * o_ref[...].astype(F32)
    grad_k, grad_v, grad_q = [], [], []
    for h in range(2):
        inside = (lane < width) if h == 0 else (lane >= width)
        inside_k = (lane_k < width) if h == 0 else (lane_k >= width)
        first = width if h == 0 else 0
        delta = jnp.sum(jnp.where(inside, both, 0.0), axis=1, keepdims=True)
        gx = with_parts(lane, grad_out, -delta, first, width).astype(BF16)
        kx = jnp.where(inside_k, k_ref[...], one)
        vx = jnp.where(inside_k, v_ref[...], one)
        qx = qx_ref[:, h * lanes : (h + 1) * lanes]
        prob = jnp.exp2(dot_nt(kx, qx))
        grad_v.append(dot_nn(prob.astype(BF16), gx))
        grad_score = (prob * dot_nt(vx, gx)).astype(BF16)
        grad_k.append(dot_nn(grad_score, qx))
        grad_q.append(dot_tn(kx, grad_score))
    dk_ref[...] = (jnp.where(lane_k < width, grad_k[0], grad_k[1]) * (1.0 / LOG2E)).astype(BF16)
    dv_ref[...] = jnp.where(lane_k < width, grad_v[0], grad_v[1]).astype(BF16)
    grad_both = jnp.concatenate([grad_q[0][:width], grad_q[1][width:]], axis=0)
    dq_ref[...] = (grad_both.T * (1.0 / math.sqrt(width))).astype(BF16)


def sum_rows(target, at, left, left_at, right, right_at, rows, chunk=64):
    def one(i, carry):
        here = pl.multiple_of(i * chunk, chunk)
        value = left[pl.ds(left_at + here, chunk), :].astype(F32) + right[pl.ds(right_at + here, chunk), :].astype(F32)
        target[pl.ds(at + here, chunk), :] = value.astype(target.dtype)
        return carry

    lax.fori_loop(0, rows // chunk, one, 0)


class Axis:

    def __init__(self, name, count, sems):
        self.name, self.count, self.sems = name, count, sems
        self.me = lax.axis_index(name)

    def copy(self, d, source, target):
        return send(source(self.me ^ d, d), target(self.me, d), self.sems[0].at[d], self.sems[1].at[d], {self.name: self.me ^ d})

    def start(self, source, target):
        for d in range(1, self.count):
            self.copy(d, source, target).start()

    def wait(self, source, target):
        for d in range(1, self.count):
            self.copy(d, source, target).wait()


def axis_sems(*counts):
    return [pltpu.SemaphoreType.DMA((count,)) for count in counts for _ in range(2)]


def cross(source, target, sems, i):
    return send(source, target, sems[0].at[i], sems[1].at[i], {"tp": 1 - lax.axis_index("tp")})


class RowSum:

    def __init__(self, dw_send, dw_own, extra, received, total, blocks, tp_sems, ctx):
        self.dw_send, self.dw_own, self.extra = dw_send, dw_own, extra
        self.received, self.total, self.blocks = received, total, blocks
        self.tp_sems, self.ctx = tp_sems, ctx
        self.main, self.more = dw_own.shape[0], extra.shape[1]
        self.size = (self.main + self.more) // ctx.count

    def crossing(self):
        return [
            cross(self.dw_send, self.received.at[pl.ds(0, self.main), :], self.tp_sems, 0),
            cross(self.extra.at[1], self.received.at[pl.ds(self.main, self.more), :], self.tp_sems, 1),
        ]

    def start(self):
        for copy in self.crossing():
            copy.start()

    def source(self, peer, d):
        return self.total.at[pl.ds(pl.multiple_of(peer * self.size, 16), self.size), :]

    def target(self, me, d):
        return self.blocks.at[d]

    def spread(self):
        for copy in self.crossing():
            copy.wait()
        sum_rows(self.total, 0, self.dw_own, 0, self.received, 0, self.main)
        sum_rows(self.total, self.main, self.extra.at[0], 0, self.received, self.main, self.more)
        self.ctx.start(self.source, self.target)

    def finish(self, out):
        self.ctx.wait(self.source, self.target)
        count, size, width = out.shape
        value = self.total[pl.ds(pl.multiple_of(self.ctx.me * self.size, 16), self.size), :].astype(F32)
        for d in range(1, self.ctx.count):
            value += self.blocks[d].astype(F32)
        for j in range(count):
            out[j] = value[:, j * width : (j + 1) * width].astype(out.dtype)


class ShardSum:

    def __init__(self, parts, received, blocks, shard, ctx):
        self.parts, self.received, self.blocks, self.shard, self.ctx = parts, received, blocks, shard, ctx

    def source(self, peer, d):
        return self.parts.at[peer]

    def target(self, me, d):
        return self.received.at[d]

    def start(self):
        self.shard.start(self.source, self.target)

    def mine(self, peer, d):
        return self.blocks.at[self.ctx.me]

    def theirs(self, me, d):
        return self.blocks.at[me]

    def spread(self):
        self.shard.wait(self.source, self.target)
        value = self.parts[self.shard.me].astype(F32)
        for d in range(1, self.shard.count):
            value += self.received[d].astype(F32)
        self.blocks[self.ctx.me] = value.astype(BF16)
        self.ctx.start(self.mine, self.theirs)

    def finish(self):
        self.ctx.wait(self.mine, self.theirs)


class InputSum:

    def __init__(self, dn_send, dn_own, received, total, blocks, tp_sems, ctx):
        self.dn_send, self.dn_own, self.received = dn_send, dn_own, received
        self.total, self.blocks, self.tp_sems, self.ctx = total, blocks, tp_sems, ctx

    def crossing(self, d):
        return cross(self.dn_send(d), self.received.at[d], self.tp_sems, d)

    def start(self):
        for d in reversed(range(self.ctx.count)):
            self.crossing(d).start()

    def source(self, peer, d):
        return self.total.at[d]

    def target(self, me, d):
        return self.blocks.at[d]

    def spread(self):
        for d in reversed(range(self.ctx.count)):
            self.crossing(d).wait()
            rows = self.received.shape[1]
            sum_rows(self.total.at[d], 0, self.dn_own(d), 0, self.received.at[d], 0, rows)
            if d:
                self.ctx.copy(d, self.source, self.target).start()

    def finish(self):
        self.ctx.wait(self.source, self.target)

    def rows(self, at, size):
        value = self.total[0, pl.ds(at, size), :].astype(F32)
        for d in range(1, self.ctx.count):
            value += self.blocks[d, pl.ds(at, size), :].astype(F32)
        return value


def attend_back_one(
    qx_ref, k_ref, v_ref, go_ref, o_ref, dw_all, dw_own, extra, out_half,
    dq_ref, dk_ref, dv_ref, dw_out, whole,
    received, total, blocks, tp_out, tp_in, ctx_out, ctx_in, whole_sems, *, width, nc,
):
    step = pl.program_id(0)
    last = pl.num_programs(0) - 1
    t = lax.axis_index("tp")
    rows = RowSum(dw_all.at[1], dw_own.at[0], extra, received, total, blocks, (tp_out, tp_in), Axis("ctx", nc, (ctx_out, ctx_in)))

    def whole_copies():
        return [
            cross(out_half, whole.at[:, t], (whole_sems, whole_sems.at[pl.ds(1, 1)]), 0),
            pltpu.make_async_copy(out_half, whole.at[:, t], whole_sems.at[2]),
        ]

    @pl.when(step == 0)
    def _():
        greet([("tp", 2), ("ctx", nc)])
        rows.start()
        for copy in whole_copies():
            copy.start()

    @pl.when(step == 1)
    def _():
        rows.spread()

    attend_back_step(qx_ref, k_ref, v_ref, go_ref, o_ref, dq_ref, dk_ref, dv_ref, width)

    @pl.when(step == last)
    def _():
        rows.finish(dw_out)
        for copy in whole_copies():
            copy.wait()


def attend_back_two(
    qx_ref, k_ref, v_ref, go_ref, o_ref, dw_parts, dn_all, dn_own,
    dq_ref, dk_ref, dv_ref, dw_done, dn_done,
    dw_received, dw_blocks, dn_received, dn_total, dn_blocks,
    z_out, z_in, back_out, back_in, tp_out, tp_in, ctx_out, ctx_in, *, width, nc, ns,
):
    step = pl.program_id(0)
    last = pl.num_programs(0) - 1
    weights = ShardSum(
        dw_parts, dw_received, dw_blocks, Axis("shard", ns, (z_out, z_in)), Axis("ctx", nc, (back_out, back_in))
    )
    inputs = InputSum(
        lambda d: dn_all.at[d, 1], lambda d: dn_own.at[d, 0], dn_received, dn_total, dn_blocks,
        (tp_out, tp_in), Axis("ctx", nc, (ctx_out, ctx_in)),
    )

    @pl.when(step == 0)
    def _():
        greet([("tp", 2), ("ctx", nc), ("shard", ns)])
        inputs.start()
        weights.start()

    @pl.when(step == 1)
    def _():
        inputs.spread()

    @pl.when(step == 2)
    def _():
        weights.spread()

    attend_back_step(qx_ref, k_ref, v_ref, go_ref, o_ref, dq_ref, dk_ref, dv_ref, width)

    @pl.when(step == last)
    def _():
        inputs.finish()
        weights.finish()
        dw_done[...] = dw_blocks[...]
        size = 64

        def one(i, carry):
            at = pl.multiple_of(i * size, size)
            dn_done[pl.ds(at, size), :] = inputs.rows(at, size)
            return carry

        lax.fori_loop(0, dn_done.shape[0] // size, one, 0)


def attend_back(kernel, qx, k, v, grad_mixed, mixed, width, micro, others, other_specs, out_shapes, out_specs, scratch, number):
    rows, cols = mixed.shape
    keys = k.shape[0]
    lanes = 2 * width
    return pl.pallas_call(
        functools.partial(kernel, width=width),
        grid=(cols // lanes,),
        in_specs=[
            pl.BlockSpec((rows, 2 * lanes), lambda j: (0, j)),
            pl.BlockSpec((keys, lanes), lambda j: (0, j)),
            pl.BlockSpec((keys, lanes), lambda j: (0, j)),
            pl.BlockSpec((rows, lanes), lambda j: (micro, j)),
            pl.BlockSpec((rows, lanes), lambda j: (0, j)),
        ]
        + other_specs,
        out_specs=[
            pl.BlockSpec((rows, lanes), lambda j: (0, j)),
            pl.BlockSpec((keys, lanes), lambda j: (0, j)),
            pl.BlockSpec((keys, lanes), lambda j: (0, j)),
        ]
        + out_specs,
        out_shape=[
            jax.ShapeDtypeStruct((rows, cols), BF16),
            jax.ShapeDtypeStruct((keys, cols), BF16),
            jax.ShapeDtypeStruct((keys, cols), BF16),
        ]
        + out_shapes,
        scratch_shapes=scratch,
        compiler_params=params(collective_id=number, has_side_effects=True),
        cost_estimate=pl.CostEstimate(
            flops=30 * rows * keys * cols, bytes_accessed=8 * keys * cols, transcendentals=rows * keys * cols // width
        ),
        name="attend_back",
    )(qx, k, v, grad_mixed, mixed, *others)


def attend_back_rows(qx, k, v, grad_mixed, mixed, width, micro, dw, extra, out, ns, nc):
    main, features = dw.shape[1:]
    rows = main + extra.shape[1]
    anywhere = pl.BlockSpec(memory_space=pl.ANY)
    block = (nc, rows // nc, features)
    parts = (ns, rows // nc, features // ns)
    micros, half, _ = out.shape
    return attend_back(
        functools.partial(attend_back_one, nc=nc), qx, k, v, grad_mixed, mixed, width, micro,
        [dw, dw, extra, out],
        [anywhere, once((1, main, features)), once(extra.shape), once(out.shape)],
        [jax.ShapeDtypeStruct(parts, BF16), jax.ShapeDtypeStruct((micros, 2, half, features), BF16)],
        [full_spec(parts), anywhere],
        [
            pltpu.VMEM((rows, features), BF16), pltpu.VMEM((rows, features), BF16), pltpu.VMEM(block, BF16),
            *axis_sems(2, nc), pltpu.SemaphoreType.DMA((3,)),
        ],
        3,
    )


def attend_back_inputs(qx, k, v, grad_mixed, mixed, width, micro, dw_parts, dn, ns, nc):
    _, size, part = dw_parts.shape
    half, features = dn.shape[2:]
    anywhere = pl.BlockSpec(memory_space=pl.ANY)
    block = pltpu.VMEM((nc, half, features), BF16)
    return attend_back(
        functools.partial(attend_back_two, nc=nc, ns=ns), qx, k, v, grad_mixed, mixed, width, micro,
        [dw_parts, dn, dn],
        [once(dw_parts.shape), anywhere, once((nc, 1, half, features))],
        [jax.ShapeDtypeStruct((nc, size, part), BF16), jax.ShapeDtypeStruct((half, features), F32)],
        [full_spec((nc, size, part)), full_spec((half, features))],
        [
            pltpu.VMEM(dw_parts.shape, BF16), pltpu.VMEM((nc, size, part), BF16), block, block, block,
            *axis_sems(ns, nc, nc, nc),
        ],
        4,
    )


def ffn_kernel(
    where_ref, x_ref, o0_ref, o1_ref, g_ref, w_out, w_up, w_down, bup_ref, vec_ref,
    out_ref, gm_ref, gx_ref, dw_ref, dup_ref, dvec_ref, dw_acc,
):
    step = pl.program_id(0)
    steps = pl.num_programs(0)
    b_out, b_down, gain, shift = (vec_ref[i : i + 1, :] for i in (0, 1, 4, 5))
    hw = w_out.shape[1]
    hidden = w_up.shape[2]

    @pl.when(step == 0)
    def _():
        dw_acc[...] = jnp.zeros_like(dw_acc)
        dup_ref[...] = jnp.zeros_like(dup_ref)
        dvec_ref[...] = jnp.zeros_like(dvec_ref)

    mixed = jnp.where(2 * step < steps, o0_ref[...], o1_ref[...])
    grad_b = g_ref[0, 0]
    grad = grad_b.astype(F32)
    attended = dot_nn(mixed[:, :hw], w_out[0]) + dot_nn(mixed[:, hw:], w_out[1])
    middle = x_ref[0, 0].astype(F32) + (attended + b_out)
    unit, inverse = unit_norm(middle)
    normed = (unit * gain + shift).astype(BF16)
    ffn_out = jnp.zeros_like(middle)
    grad_normed = jnp.zeros_like(middle)
    for part in range(2):
        pre = dot_nn(normed, w_up[part]) + bup_ref[part]
        gate = 0.5 + 0.5 * lax.erf(pre * math.sqrt(0.5))
        active = (pre * gate).astype(BF16)
        ffn_out += dot_nn(active, w_down[part])
        slope = gate + pre * jnp.exp(pre * pre * -0.5) * (1.0 / math.sqrt(2.0 * math.pi))
        grad_pre_f = dot_nt(grad_b, w_down[part]) * slope
        grad_pre = grad_pre_f.astype(BF16)
        dup_ref[part] += column_sum(grad_pre.astype(F32))
        grad_normed += dot_nt(grad_pre, w_up[part])
        dw_acc[part, hw : hw + hidden] += dot_tn(active, grad_b)
        dw_acc[part, hw + hidden :] += dot_tn(grad_pre, normed)
    out_ref[...] = (middle + (ffn_out + b_down)).astype(BF16)
    grad_middle = grad + norm_back(grad_normed, unit, inverse, gain)
    gm_ref[...] = grad_middle
    grad_att = grad_middle.astype(BF16)
    dvec_ref[0:1] += column_sum(grad_att.astype(F32))
    dvec_ref[1:2] += column_sum(grad)
    dvec_ref[2:3] += column_sum(grad_normed * unit)
    dvec_ref[3:4] += column_sum(grad_normed)
    for part in range(2):
        cols = slice(part * hw, (part + 1) * hw)
        gx_ref[:, cols] = dot_nt(grad_att, w_out[part]).astype(BF16)
        dw_acc[part, :hw] += dot_tn(mixed[:, cols], grad_att)

    @pl.when(step == steps - 1)
    def _():
        dw_ref[...] = dw_acc[...].astype(BF16)


def feed_forward(tokens, mixed, cotangent, w_out, w_up, w_down, b_up, vectors, where):
    micros, _, length, features = tokens.shape
    block = 256
    half = length // 2
    each = half // block
    rows = micros * half
    hw, hidden = w_out.shape[1], w_up.shape[2]
    total = hw + 2 * hidden
    row_spec = pl.BlockSpec((block, features), lambda i, t: (i, 0))
    input_spec = pl.BlockSpec((1, 1, block, features), lambda i, t: (i // each, 0, t[0] * each + i % each, 0))
    return pl.pallas_call(
        ffn_kernel,
        grid_spec=pltpu.PrefetchScalarGridSpec(
            num_scalar_prefetch=1,
            grid=(rows // block,),
            in_specs=[
                input_spec,
                pl.BlockSpec((block, 2 * hw), lambda i, t: (jnp.minimum(i, each - 1), 0)),
                pl.BlockSpec((block, 2 * hw), lambda i, t: (jnp.maximum(i - each, 0), 0)),
                input_spec,
            ]
            + [once(w.shape) for w in (w_out, w_up, w_down)]
            + [once(b_up.shape), once(vectors.shape)],
            out_specs=[row_spec] * 3
            + [full_spec((2, total, features)), full_spec((2, 1, hidden)), full_spec((8, features))],
            scratch_shapes=[pltpu.VMEM((2, total, features), F32)],
        ),
        out_shape=[
            jax.ShapeDtypeStruct((rows, features), BF16),
            jax.ShapeDtypeStruct((rows, features), F32),
            jax.ShapeDtypeStruct((rows, 2 * hw), BF16),
            jax.ShapeDtypeStruct((2, total, features), BF16),
            jax.ShapeDtypeStruct((2, 1, hidden), F32),
            jax.ShapeDtypeStruct((8, features), F32),
        ],
        compiler_params=params(),
        cost_estimate=pl.CostEstimate(
            flops=12 * rows * total * features, bytes_accessed=20 * total * features, transcendentals=4 * rows * hidden
        ),
        name="feed_forward",
    )(where, tokens, *mixed, cotangent, w_out, w_up, w_down, b_up, vectors)


def back_kernel(x_ref, n_ref, dk_ref, dv_ref, dq_ref, w_ref, *refs):
    starts, (dn_ref, dw_ref, db_ref, dw_acc) = refs[:-4], refs[-4:]
    step = pl.program_id(0)
    width = w_ref.shape[3]
    normed = n_ref[...]
    unit, _ = unit_norm(x_ref[...].astype(F32))
    total = jnp.zeros(n_ref.shape, F32)

    @pl.when(step == 0)
    def _():
        dw_acc[...] = starts[0][...] if starts else jnp.zeros_like(dw_acc)
        db_ref[...] = starts[1][...] if starts else jnp.zeros_like(db_ref)
        query = jnp.zeros(n_ref.shape, F32)
        grad = dq_ref[...]
        for part in range(2):
            cols = slice(part * width, (part + 1) * width)
            dw_acc[part, 0] += dot_tn(grad[:, cols], normed)
            query += dot_nt(grad[:, cols], w_ref[part, 0])
        db_ref[0:1] += column_sum(grad.astype(F32))
        db_ref[2:3] += column_sum(query * unit)
        db_ref[3:4] += column_sum(query)
        dn_ref[...] = query.astype(BF16)

    for kind, ref in ((1, dk_ref), (2, dv_ref)):
        for part in range(2):
            cols = slice(part * width, (part + 1) * width)
            grad = ref[:, cols]
            total += dot_nt(grad, w_ref[part, kind])
            dw_acc[part, kind] += dot_tn(grad, normed)
    db_ref[1:2] += column_sum(dv_ref[...].astype(F32))
    db_ref[2:3] += column_sum(total * unit)
    db_ref[3:4] += column_sum(total)

    @pl.when(step == 0)
    def _():
        dn_ref[...] = (total + dn_ref[...].astype(F32)).astype(BF16)

    @pl.when(step > 0)
    def _():
        dn_ref[...] = total.astype(BF16)

    @pl.when(step == pl.num_programs(0) - 1)
    def _():
        dw_ref[...] = dw_acc[...].astype(dw_ref.dtype)


def project_back(x_all, normed, dq, dk, dv, weights, starts, kind):
    keys, features = normed.shape
    block = keys // 8
    width = weights.shape[3]
    stack = (2, 3, width, features)
    return pl.pallas_call(
        back_kernel,
        grid=(8,),
        in_specs=[
            pl.BlockSpec((block, features), lambda i: (i, 0)),
            pl.BlockSpec((block, features), lambda i: (i, 0)),
            pl.BlockSpec((block, 2 * width), lambda i: (i, 0)),
            pl.BlockSpec((block, 2 * width), lambda i: (i, 0)),
            once((block, 2 * width)),
            once(weights.shape),
        ]
        + [once(start.shape) for start in starts],
        out_specs=[
            pl.BlockSpec((block, features), lambda i: (i, 0)),
            full_spec(stack),
            full_spec((8, 2 * width)),
        ],
        out_shape=[
            jax.ShapeDtypeStruct((keys, features), BF16),
            jax.ShapeDtypeStruct(stack, kind),
            jax.ShapeDtypeStruct((8, 2 * width), F32),
        ],
        scratch_shapes=[pltpu.VMEM(stack, F32)],
        compiler_params=params(),
        cost_estimate=pl.CostEstimate(
            flops=16 * keys * features * width, bytes_accessed=8 * keys * features, transcendentals=0
        ),
        name="project_back",
    )(x_all, normed, dk, dv, dq, weights, *starts)


def last_kernel(
    dn_ref, dw_ref, extra_ref, dn_first, x_ref, gm_ref, gain_ref,
    grad_ref, blocks_ref,
    w_received, w_total, w_blocks, z_parts, z_received, dn_received, dn_total, dn_blocks,
    wtp_out, wtp_in, wctx_out, wctx_in, z_out, z_in, back_out, back_in, tp_out, tp_in, ctx_out, ctx_in,
    row_out, row_in, *, ns, nc,
):
    t = lax.axis_index("tp")
    micros, _, half, _ = grad_ref.shape
    rows = RowSum(
        dw_ref.at[1], dw_ref.at[0], extra_ref, w_received, w_total, w_blocks, (wtp_out, wtp_in),
        Axis("ctx", nc, (wctx_out, wctx_in)),
    )
    weights = ShardSum(
        z_parts, z_received, blocks_ref, Axis("shard", ns, (z_out, z_in)), Axis("ctx", nc, (back_out, back_in))
    )
    inputs = InputSum(
        lambda d: dn_ref.at[d, 1], lambda d: dn_ref.at[d, 0], dn_received, dn_total, dn_blocks,
        (tp_out, tp_in), Axis("ctx", nc, (ctx_out, ctx_in)),
    )

    def row(micro):
        return cross(grad_ref.at[micro, t], grad_ref.at[micro, t], (row_out, row_in), micro)

    def finish_rows(micro, grad_rows):
        size = 64

        def one(i, carry):
            at = pl.multiple_of(i * size, size)
            unit, inverse = unit_norm(x_ref[micro, 0, pl.ds(t * half + at, size), :].astype(F32))
            value = gm_ref[micro, pl.ds(at, size), :] + norm_back(grad_rows(at, size), unit, inverse, gain_ref[2:3])
            grad_ref[micro, t, pl.ds(at, size), :] = value.astype(BF16)
            return carry

        lax.fori_loop(0, half // size, one, 0)
        row(micro).start()

    greet([("tp", 2), ("ctx", nc), ("shard", ns)])
    rows.start()
    inputs.start()
    rows.spread()
    inputs.spread()
    for micro in range(micros - 1):
        finish_rows(micro, lambda at, size: dn_first[micro, pl.ds(at, size), :])
    rows.finish(z_parts)
    weights.start()
    weights.spread()
    inputs.finish()
    finish_rows(micros - 1, inputs.rows)
    weights.finish()
    for micro in range(micros):
        row(micro).wait()


def last_sums(dn, dw, extra, dn_first, x, grad_middle, gain, ns, nc):
    main, features = dw.shape[1:]
    rows = main + extra.shape[1]
    micros, half, _ = grad_middle.shape
    size, part = rows // nc, features // ns
    block = pltpu.VMEM((nc, half, features), BF16)
    return pl.pallas_call(
        functools.partial(last_kernel, ns=ns, nc=nc),
        in_specs=[pl.BlockSpec(memory_space=pltpu.VMEM)] * 7,
        out_specs=[pl.BlockSpec(memory_space=pltpu.VMEM)] * 2,
        out_shape=[
            jax.ShapeDtypeStruct((micros, 2, half, features), BF16),
            jax.ShapeDtypeStruct((nc, size, part), BF16),
        ],
        scratch_shapes=[
            pltpu.VMEM((rows, features), BF16), pltpu.VMEM((rows, features), BF16), pltpu.VMEM((nc, size, features), BF16),
            pltpu.VMEM((ns, size, part), BF16), pltpu.VMEM((ns, size, part), BF16), block, block, block,
            *axis_sems(2, nc, ns, nc, nc, nc, micros),
        ],
        compiler_params=params(collective_id=5, has_side_effects=True),
        name="last_sums",
    )(dn, dw, extra, dn_first, x, grad_middle, gain)


def pad_rows(rows, multiple):
    extra = -rows.shape[0] % multiple
    return jnp.concatenate([rows, jnp.zeros((extra,) + rows.shape[1:], rows.dtype)]) if extra else rows


def body(
    tokens, cotangent, w_query, w_key, w_value, w_out, w_up, w_down,
    b_query, b_value, b_up, b_out, b_down, gain_attn, shift_attn, gain_ffn, shift_ffn,
):
    ns, nc = lax.axis_size("shard"), lax.axis_size("ctx")
    t = lax.axis_index("tp")
    micros, _, length, features = tokens.shape
    half = length // 2
    heads, head_part = b_query.shape
    head_width = head_part * ns
    up_part = b_up.shape[1]
    feature_part = b_out.shape[0]

    smalls = [b_query, b_value, b_up, b_out, b_down, gain_attn, shift_attn, gain_ffn, shift_ffn]
    flat = jnp.concatenate([v.reshape(-1) for v in smalls])
    small = jnp.pad(flat, (0, -flat.shape[0] % 2048)).reshape(-1, 128)
    w_all, small_all, x_first = gather_first((w_query, w_key, w_value), small, tokens, ns, nc)
    small_all = small_all.reshape(2, ns, -1)
    bias_size, up_size = b_query.size, b_up.size
    biases = small_all[:, :, : 2 * bias_size].reshape(2, ns, 2, heads, head_part)
    biases = biases.transpose(2, 0, 3, 1, 4).reshape(2, 2 * heads * head_width).astype(F32)
    bup = small_all[:, :, 2 * bias_size : 2 * bias_size + up_size].reshape(2, ns, heads, up_part)
    bup = bup.transpose(0, 2, 1, 3).reshape(2, 1, heads * up_part * ns).astype(F32)
    at = 2 * bias_size + up_size
    vectors = small_all[0, :, at : at + 6 * feature_part].reshape(ns, 6, feature_part)
    vectors = vectors.transpose(1, 0, 2).reshape(6, features).astype(F32)
    keys = 2 * nc * half
    aligned = feature_part % 128 == 0
    column_place = place_columns if aligned else place_slot

    def column_shape(w):
        return (2, w.shape[0], features) if aligned else (2, ns) + w.shape

    def whole_columns(w):
        if not aligned:
            w = w.transpose(0, 2, 1, 3).reshape(2, w.shape[2], features)
        return w

    plans = [
        (("ctx", nc, place_distance, True), ("shard", ns, place_rows, False), ("shard", ns, column_place, False)),
        (("shard", ns, column_place, False),),
    ]
    sources = [(tokens, w_up, w_out), (w_down,)]
    specs = [
        [once((1, 1, length, features), (1, 0, 0, 0)), once(w_up.shape), once(w_out.shape)],
        [once(w_down.shape)],
    ]
    shapes = [
        ((nc, 2, half, features), (2, features, w_up.shape[1]), column_shape(w_out)),
        (column_shape(w_down),),
    ]
    x_alls = [x_first.reshape(keys, features), None]
    saved = []
    arrived = []
    for micro in range(micros):
        normed, k, v, q = front(x_alls[micro], w_all, vectors, biases, head_width, half)
        mixed, qx, *more = attend_forward(
            q, k, v, head_width, plans[micro], sources[micro], specs[micro], shapes[micro], micro + 1
        )
        if micro == 0:
            x_alls[1] = more.pop(0).reshape(keys, features)
        arrived += more
        saved.append((normed, k, v, qx, mixed))
    wu, wo, wd = arrived[0], whole_columns(arrived[1]), whole_columns(arrived[2])

    out, grad_middle, grad_mixed, dw, dup, dvec = feed_forward(
        tokens, [entry[4] for entry in saved], cotangent, wo, wu, wd, bup, vectors, jnp.full((1,), t, jnp.int32)
    )

    def spread(v, part):
        return v.reshape(heads, ns, part).transpose(1, 0, 2).reshape(ns, -1)

    def as_rows(v):
        count = v.shape[1] // feature_part
        return v.reshape(ns, count, feature_part).transpose(1, 0, 2).reshape(count, features)

    extra = jnp.stack(
        [pad_rows(jnp.concatenate([dvec[:4], as_rows(spread(dup[part, 0], up_part))]), 16 * nc) for part in range(2)]
    ).astype(BF16)

    width = heads * head_width
    normed, k, v, qx, mixed = saved[0]
    dq, dk, dv, dw_parts, output = attend_back_rows(
        qx, k, v, grad_mixed, mixed, head_width, 0, dw, extra, out.reshape(micros, half, features), ns, nc
    )
    dn, dw_now, db_now = project_back(x_alls[0], normed, dq, dk, dv, w_all, (), F32)
    normed, k, v, qx, mixed = saved[1]
    dq, dk, dv, dw_done, dn_first = attend_back_inputs(
        qx, k, v, grad_mixed, mixed, head_width, 1, dw_parts, dn.reshape(nc, 2, half, features), ns, nc
    )
    dn, dw_now, db_now = project_back(x_alls[1], normed, dq, dk, dv, w_all, (dw_now, db_now), BF16)

    extras = []
    for part in range(2):
        cols = slice(part * width, (part + 1) * width)
        biases = jnp.concatenate([spread(db_now[0, cols], head_part), spread(db_now[1, cols], head_part)], axis=1)
        extras.append(pad_rows(jnp.concatenate([db_now[2:4], as_rows(biases)]), 16 * nc))
    grad_tokens, attn_done = last_sums(
        dn.reshape(nc, 2, half, features), dw_now.reshape(2, 3 * width, features), jnp.stack(extras).astype(BF16),
        dn_first[None], tokens, grad_middle.reshape(micros, half, features), vectors, ns, nc,
    )

    output = output.reshape(micros, 1, length, features)
    grad_tokens = grad_tokens.reshape(micros, 1, length, features)
    done_ffn = dw_done.reshape(-1, feature_part).astype(F32)
    done_attn = attn_done.reshape(-1, feature_part).astype(F32)
    hidden = heads * up_part * ns
    g_out, g_down, g_up = done_ffn[:width], done_ffn[width : width + hidden], done_ffn[width + hidden : width + 2 * hidden]
    tail = done_ffn[width + 2 * hidden :]
    g_query, g_key, g_value = (done_attn[i * width : (i + 1) * width].T for i in range(3))
    tail_attn = done_attn[3 * width :]
    g_bup = tail[4:].reshape(-1)[: heads * up_part].reshape(heads, up_part)
    g_heads = tail_attn[2:].reshape(-1)
    g_bq = g_heads[: heads * head_part].reshape(heads, head_part)
    g_bv = g_heads[heads * head_part : 2 * heads * head_part].reshape(heads, head_part)
    return (
        output, grad_tokens, g_query, g_key, g_value, g_out, g_up.T, g_down, g_bq, g_bv, g_bup,
        tail[0], tail[1], tail_attn[0], tail_attn[1], tail[2], tail[3],
    )


def solution(mesh):
    wide, tall = P("shard", "tp"), P("tp", "shard")
    rows, vector = P(None, "shard", "ctx", None), P("shard")
    weights = (wide, wide, wide, tall, wide, tall)
    return jax.shard_map(
        body,
        mesh=mesh,
        in_specs=(rows, rows) + weights + (tall,) * 3 + (vector,) * 6,
        out_specs=(rows, rows) + weights + (tall,) * 3 + (vector,) * 6,
        check_vma=False,
    )
```

```python
import functools
import math

import jax
import jax.numpy as jnp
from jax import lax
from jax.experimental import pallas as pl
from jax.experimental.pallas import tpu as pltpu
from jax.sharding import PartitionSpec as P

F32 = jnp.float32
BF16 = jnp.bfloat16
MESH = pl.DeviceIdType.MESH
norm_eps = 1e-05
LOG2E = math.log2(math.e)
VMEM_LIMIT = 60 * 2**20


def dot_nn(left, right):
    return lax.dot_general(left, right, (((1,), (0,)), ((), ())), preferred_element_type=F32)


def dot_nt(left, right):
    return lax.dot_general(left, right, (((1,), (1,)), ((), ())), preferred_element_type=F32)


def dot_tn(left, right):
    return lax.dot_general(left, right, (((0,), (0,)), ((), ())), preferred_element_type=F32)


def unit_norm(values):
    average = jnp.mean(values, axis=-1, keepdims=True)
    centred = values - average
    variance = jnp.mean(centred * centred, axis=-1, keepdims=True)
    inverse = lax.rsqrt(variance + norm_eps)
    return centred * inverse, inverse


def norm_back(grad_normed, unit_vals, inverse, gain):
    scaled = grad_normed * gain
    return inverse * (
        scaled
        - jnp.mean(scaled, axis=-1, keepdims=True)
        - unit_vals * jnp.mean(scaled * unit_vals, axis=-1, keepdims=True)
    )


def column_sum(values):
    return jnp.sum(values, axis=0, keepdims=True)


def full_spec(shape):
    return pl.BlockSpec(shape, lambda *_: (0,) * len(shape))


def params(limit=VMEM_LIMIT, **others):
    return pltpu.CompilerParams(vmem_limit_bytes=limit, **others)


def once(shape, index=None):
    place = index or (0,) * len(shape)
    return pl.BlockSpec(shape, lambda *_: place, pipeline_mode=pl.Buffered(1))


def send(source, target, send_sem, recv_sem, where):
    return pltpu.make_async_remote_copy(
        src_ref=source, dst_ref=target, send_sem=send_sem, recv_sem=recv_sem, device_id=where, device_id_type=MESH
    )


def gather_kernel(ns, nc, wq_ref, wk_ref, wv_ref, small_ref, x_block, w_out, small_out, x_out, *sems):
    w_send, w_recv, s_send, s_recv, x_send, x_recv, wt_send, wt_recv, st_send, st_recv, xt_send, xt_recv, local = sems
    w_refs = (wq_ref, wk_ref, wv_ref)
    kinds = range(3)
    x_ref = x_block.at[0, 0]
    s = lax.axis_index("shard")
    c = lax.axis_index("ctx")
    t = lax.axis_index("tp")
    other = 1 - t
    depth = wq_ref.shape[0]
    half = x_ref.shape[0] // 2

    barrier = pltpu.get_barrier_semaphore()
    for d in range(1, ns):
        pl.semaphore_signal(barrier, inc=1, device_id={"shard": s ^ d}, device_id_type=MESH)
    for d in range(1, nc):
        pl.semaphore_signal(barrier, inc=1, device_id={"ctx": c ^ d}, device_id_type=MESH)
    pl.semaphore_signal(barrier, inc=1, device_id={"tp": other}, device_id_type=MESH)
    pl.semaphore_wait(barrier, ns + nc - 1)

    def w_rows(part, kind, owner):
        return w_out.at[part, kind, pl.ds(pl.multiple_of(owner * depth, depth), depth), :]

    def x_rows(which):
        return x_ref.at[pl.ds(pl.multiple_of(which * half, half), half), :]

    def begin(source, target, send_sem, recv_sem, where):
        copy = send(source, target, send_sem, recv_sem, where)
        copy.start()
        return copy

    x_copies, w_copies, s_copies = {}, {}, {}
    for d in range(1, nc):
        x_copies[d] = begin(x_rows(t), x_out.at[d, 0], x_send.at[d], x_recv.at[d], {"ctx": c ^ d})
    for d in range(1, ns):
        for k in kinds:
            w_copies[d, k] = begin(
                w_refs[k], w_rows(0, k, s), w_send.at[k, d], w_recv.at[k, d], {"shard": s ^ d}
            )
        s_copies[d] = begin(small_ref, small_out.at[0, s], s_send.at[d], s_recv.at[d], {"shard": s ^ d})
    last = [begin(w_refs[k], w_rows(1, k, s), wt_send.at[k, 0], wt_recv.at[k, 0], {"tp": other}) for k in kinds]
    last.append(begin(small_ref, small_out.at[1, s], st_send.at[0], st_recv.at[0], {"tp": other}))
    locals_ = [pltpu.make_async_copy(w_refs[k], w_rows(0, k, s), local.at[k]) for k in kinds]
    locals_ += [
        pltpu.make_async_copy(small_ref, small_out.at[0, s], local.at[3]),
        pltpu.make_async_copy(x_rows(t), x_out.at[0, 0], local.at[4]),
        pltpu.make_async_copy(x_rows(other), x_out.at[0, 1], local.at[5]),
    ]
    for copy in locals_:
        copy.start()
    for d in range(1, max(ns, nc)):
        if d < ns:
            for k in kinds:
                w_copies[d, k].wait_recv()
                last.append(
                    begin(
                        w_rows(0, k, s ^ d), w_rows(1, k, s ^ d), wt_send.at[k, d], wt_recv.at[k, d], {"tp": other}
                    )
                )
            s_copies[d].wait_recv()
            last.append(
                begin(small_out.at[0, s ^ d], small_out.at[1, s ^ d], st_send.at[d], st_recv.at[d], {"tp": other})
            )
        if d < nc:
            x_copies[d].wait_recv()
            last.append(begin(x_out.at[d, 0], x_out.at[d, 1], xt_send.at[d], xt_recv.at[d], {"tp": other}))
    for copies in (x_copies, w_copies, s_copies):
        for copy in copies.values():
            copy.wait_send()
    for copy in last:
        copy.wait()
    for copy in locals_:
        copy.wait()


def gather_first(weights, small, tokens, ns, nc):
    depth, width = weights[0].shape
    length, features = tokens.shape[2:]
    dma = pltpu.SemaphoreType.DMA
    vmem = pl.BlockSpec(memory_space=pltpu.VMEM)
    return pl.pallas_call(
        functools.partial(gather_kernel, ns, nc),
        grid=(1,),
        in_specs=[vmem] * 4 + [once((1, 1, length, features))],
        out_specs=[pl.BlockSpec(memory_space=pl.ANY)] * 3,
        out_shape=[
            jax.ShapeDtypeStruct((2, 3, ns * depth, width), BF16),
            jax.ShapeDtypeStruct((2, ns) + small.shape, BF16),
            jax.ShapeDtypeStruct((nc, 2, length // 2, features), BF16),
        ],
        scratch_shapes=[dma((3, ns)), dma((3, ns)), dma((ns,)), dma((ns,)), dma((nc,)), dma((nc,))]
        + [dma((3, ns)), dma((3, ns)), dma((ns,)), dma((ns,)), dma((nc,)), dma((nc,)), dma((6,))],
        compiler_params=params(collective_id=0, has_side_effects=True),
        name="gather_first",
    )(*weights, small, tokens)


def front_kernel(x_ref, w_ref, vec_ref, bias_ref, n_ref, k_ref, v_ref, q_ref, *, q_scale):
    step = pl.program_id(0)
    gain, shift = vec_ref[2:3], vec_ref[3:4]
    width = w_ref.shape[3]
    size = x_ref.shape[0] // 4
    for i in range(4):
        rows = slice(i * size, (i + 1) * size)
        unit, _ = unit_norm(x_ref[rows].astype(F32))
        normed = (unit * gain + shift).astype(BF16)
        n_ref[rows] = normed
        for part in range(2):
            cols = slice(part * width, (part + 1) * width)
            k_ref[rows, cols] = dot_nn(normed, w_ref[part, 1]).astype(BF16)
            v_ref[rows, cols] = (dot_nn(normed, w_ref[part, 2]) + bias_ref[1:2, cols]).astype(BF16)

    @pl.when(step == 0)
    def _():
        normed = n_ref[: q_ref.shape[0]]
        for part in range(2):
            cols = slice(part * width, (part + 1) * width)
            q_ref[:, cols] = ((dot_nn(normed, w_ref[part, 0]) + bias_ref[0:1, cols]) * q_scale).astype(BF16)


def front(x_all, weights, vectors, biases, head_width, half):
    keys, features = x_all.shape
    block = 2 * half
    width = 2 * weights.shape[3]
    return pl.pallas_call(
        functools.partial(front_kernel, q_scale=LOG2E / math.sqrt(head_width)),
        grid=(keys // block,),
        in_specs=[
            pl.BlockSpec((block, features), lambda i: (i, 0)),
            once(weights.shape),
            once(vectors.shape),
            once(biases.shape),
        ],
        out_specs=[
            pl.BlockSpec((block, features), lambda i: (i, 0)),
            pl.BlockSpec((block, width), lambda i: (i, 0)),
            pl.BlockSpec((block, width), lambda i: (i, 0)),
            full_spec((half, width)),
        ],
        out_shape=[
            jax.ShapeDtypeStruct((keys, features), BF16),
            jax.ShapeDtypeStruct((keys, width), BF16),
            jax.ShapeDtypeStruct((keys, width), BF16),
            jax.ShapeDtypeStruct((half, width), BF16),
        ],
        compiler_params=params(),
        cost_estimate=pl.CostEstimate(
            flops=4 * keys * features * width, bytes_accessed=8 * keys * features, transcendentals=keys
        ),
        name="front",
    )(x_all, weights, vectors, biases)


def with_parts(lane, base, values, first, width):
    high = values.astype(BF16).astype(F32)
    rest = values - high
    middle = rest.astype(BF16).astype(F32)
    low = rest - middle
    extra = jnp.where(
        lane == first, high, jnp.where(lane == first + 1, middle, jnp.where(lane == first + 2, low, 0.0))
    )
    inside = (lane < width) if first else (lane >= width)
    return jnp.where(inside, base, extra)


def greet(counts):
    barrier = pltpu.get_barrier_semaphore()
    total = 0
    for name, count in counts:
        me = lax.axis_index(name)
        for d in range(1, count):
            pl.semaphore_signal(barrier, inc=1, device_id={name: me ^ d}, device_id_type=MESH)
            total += 1
    pl.semaphore_wait(barrier, total)


class Gather:

    def __init__(self, name, count, source, theirs, target, place, sems):
        self.name, self.count, self.source, self.theirs = name, count, source, theirs
        self.target, self.place = target, place
        self.out_sem, self.in_sem, self.cross_out, self.cross_in, self.local = sems
        self.me = lax.axis_index(name)

    def first(self, d):
        where = {self.name: self.me ^ d}
        return send(self.source, self.place(self.target, 0, self.me, d), self.out_sem.at[d], self.in_sem.at[d], where)

    def cross(self, d):
        where = {"tp": 1 - lax.axis_index("tp")}
        owner = self.me ^ d
        source = self.place(self.target, 0, owner, d) if d else self.source
        return send(source, self.place(self.target, 1, owner, d), self.cross_out.at[d], self.cross_in.at[d], where)

    def locals(self):
        copies = [pltpu.make_async_copy(self.source, self.place(self.target, 0, self.me, 0), self.local.at[0])]
        if self.theirs is not None:
            copies.append(pltpu.make_async_copy(self.theirs, self.place(self.target, 1, self.me, 0), self.local.at[1]))
        return copies

    def crossed(self):
        return range(0 if self.theirs is None else 1, self.count)

    def start(self):
        for d in range(1, self.count):
            self.first(d).start()
        for copy in self.locals():
            copy.start()
        if self.theirs is None:
            self.cross(0).start()

    def forward(self):
        for d in range(1, self.count):
            self.first(d).wait_recv()
            self.cross(d).start()

    def finish(self):
        for d in range(1, self.count):
            self.first(d).wait_send()
        for d in self.crossed():
            self.cross(d).wait()
        for copy in self.locals():
            copy.wait()


def place_rows(ref, part, owner, d):
    size = ref.shape[1] // lax.axis_size("shard")
    return ref.at[part, pl.ds(pl.multiple_of(owner * size, size), size), :]


def place_columns(ref, part, owner, d):
    size = ref.shape[2] // lax.axis_size("shard")
    return ref.at[part, :, pl.ds(pl.multiple_of(owner * size, size), size)]


def place_slot(ref, part, owner, d):
    return ref.at[part, owner]


def place_distance(ref, part, owner, d):
    return ref.at[d, part]


def gather_sems(count):
    dma = pltpu.SemaphoreType.DMA
    return [dma((count,)), dma((count,)), dma((count,)), dma((count,)), dma((2,))]


def attend_kernel(*refs, kc, width, plans):
    count = len(plans)
    q_ref, k_ref, v_ref = refs[:3]
    sources = refs[3 : 3 + count]
    o_ref, qx_ref = refs[3 + count : 5 + count]
    targets = refs[5 + count : 5 + 2 * count]
    scores = refs[5 + 2 * count]
    sems = refs[6 + 2 * count :]
    step = pl.program_id(0)
    last = pl.num_programs(0) - 1
    t = lax.axis_index("tp")

    def gathers(wanted):
        found = []
        for i, (name, number, place, split) in enumerate(plans):
            if name != wanted:
                continue
            source, theirs = sources[i], None
            if split:
                source = source.at[0, 0]
                half = source.shape[0] // 2
                theirs = source.at[pl.ds(pl.multiple_of((1 - t) * half, half), half), :]
                source = source.at[pl.ds(pl.multiple_of(t * half, half), half), :]
            found.append(Gather(name, number, source, theirs, targets[i], place, sems[5 * i : 5 * i + 5]))
        return found

    counts = {name: number for name, number, _, _ in plans}

    @pl.when(step == 0)
    def _():
        greet([("tp", 2)] + list(counts.items()))
        for name in counts:
            for gather in gathers(name):
                gather.start()

    @pl.when(step == last)
    def _():
        for gather in gathers("ctx"):
            gather.forward()

    rows, lanes = q_ref.shape
    keys = k_ref.shape[0]
    lane = lax.broadcasted_iota(jnp.int32, (rows, lanes), 1)
    lane_v = lax.broadcasted_iota(jnp.int32, (kc, lanes), 1)
    q = q_ref[...].astype(F32)
    tops = []
    for h in range(2):
        inside = (lane < width) if h == 0 else (lane >= width)
        q_head = jnp.where(inside, q, 0.0).astype(BF16)
        top = None
        for i in range(keys // kc):
            part = dot_nt(k_ref[i * kc : (i + 1) * kc], q_head)
            scores[h, i * kc : (i + 1) * kc] = part
            here = jnp.max(part.reshape(kc // 8, 8, rows), axis=0)
            top = here if top is None else jnp.maximum(top, here)
        tops.append(jnp.max(top, axis=0, keepdims=True))
    outs = []
    for h in range(2):
        inside_v = (lane_v < width) if h == 0 else (lane_v >= width)
        total = jnp.zeros((lanes, rows), F32)
        for i in range(keys // kc):
            v_one = jnp.where(inside_v, v_ref[i * kc : (i + 1) * kc], jnp.ones((), BF16))
            exponent = jnp.exp2(scores[h, i * kc : (i + 1) * kc] - tops[h]).astype(BF16)
            total += dot_tn(v_one, exponent)
        first = width if h == 0 else 0
        log_total = tops[h] + jnp.log2(total[first : first + 1, :])
        total = total.T
        outs.append(total / pltpu.roll(total, width, 1))
        log_column = jnp.broadcast_to(log_total, (8, rows)).T[:, :1]
        qx_ref[:, h * lanes : (h + 1) * lanes] = with_parts(lane, q, -log_column, first, width).astype(BF16)
    o_ref[...] = jnp.where(lane < width, outs[0], outs[1]).astype(BF16)

    @pl.when(step == last)
    def _():
        for gather in gathers("shard"):
            gather.forward()
        for name in counts:
            for gather in gathers(name):
                gather.finish()


def attend_forward(q, k, v, width, plans, sources, source_specs, shapes, number):
    rows, cols = q.shape
    keys = k.shape[0]
    lanes = 2 * width
    kc = 512
    anywhere = pl.BlockSpec(memory_space=pl.ANY)
    return pl.pallas_call(
        functools.partial(attend_kernel, kc=kc, width=width, plans=plans),
        grid=(cols // lanes,),
        in_specs=[
            pl.BlockSpec((rows, lanes), lambda j: (0, j)),
            pl.BlockSpec((keys, lanes), lambda j: (0, j)),
            pl.BlockSpec((keys, lanes), lambda j: (0, j)),
        ]
        + source_specs,
        out_specs=[
            pl.BlockSpec((rows, lanes), lambda j: (0, j)),
            pl.BlockSpec((rows, 2 * lanes), lambda j: (0, j)),
        ]
        + [anywhere] * len(plans),
        out_shape=[
            jax.ShapeDtypeStruct((rows, cols), BF16),
            jax.ShapeDtypeStruct((rows, 2 * cols), BF16),
        ]
        + [jax.ShapeDtypeStruct(shape, BF16) for shape in shapes],
        scratch_shapes=[pltpu.VMEM((2, keys, rows), F32)]
        + [sem for plan in plans for sem in gather_sems(plan[1])],
        compiler_params=params(collective_id=number, has_side_effects=True),
        cost_estimate=pl.CostEstimate(
            flops=12 * rows * keys * cols, bytes_accessed=4 * keys * cols, transcendentals=rows * keys * cols // width
        ),
        name="attend_forward",
    )(q, k, v, *sources)


def sum_rows(target, at, left, left_at, right, right_at, rows, chunk=64):
    def one(i, carry):
        here = pl.multiple_of(i * chunk, chunk)
        value = left[pl.ds(left_at + here, chunk), :].astype(F32) + right[pl.ds(right_at + here, chunk), :].astype(F32)
        target[pl.ds(at + here, chunk), :] = value.astype(target.dtype)
        return carry

    lax.fori_loop(0, rows // chunk, one, 0)


class Axis:

    def __init__(self, name, count, sems):
        self.name, self.count, self.sems = name, count, sems
        self.me = lax.axis_index(name)

    def copy(self, d, source, target):
        return send(source(self.me ^ d, d), target(self.me, d), self.sems[0].at[d], self.sems[1].at[d], {self.name: self.me ^ d})

    def start(self, source, target):
        for d in range(1, self.count):
            self.copy(d, source, target).start()

    def wait(self, source, target):
        for d in range(1, self.count):
            self.copy(d, source, target).wait()


def axis_sems(*counts):
    return [pltpu.SemaphoreType.DMA((count,)) for count in counts for _ in range(2)]


def cross(source, target, sems, i):
    return send(source, target, sems[0].at[i], sems[1].at[i], {"tp": 1 - lax.axis_index("tp")})


class RowSum:

    def __init__(self, dw_send, dw_own, extra, received, total, blocks, tp_sems, ctx):
        self.dw_send, self.dw_own, self.extra = dw_send, dw_own, extra
        self.received, self.total, self.blocks = received, total, blocks
        self.tp_sems, self.ctx = tp_sems, ctx
        self.main, self.more = dw_own.shape[0], extra.shape[1]
        self.size = (self.main + self.more) // ctx.count

    def crossing(self):
        return [
            cross(self.dw_send, self.received.at[pl.ds(0, self.main), :], self.tp_sems, 0),
            cross(self.extra.at[1], self.received.at[pl.ds(self.main, self.more), :], self.tp_sems, 1),
        ]

    def start(self):
        for copy in self.crossing():
            copy.start()

    def source(self, peer, d):
        return self.total.at[pl.ds(pl.multiple_of(peer * self.size, 16), self.size), :]

    def target(self, me, d):
        return self.blocks.at[d]

    def spread(self):
        for copy in self.crossing():
            copy.wait()
        sum_rows(self.total, 0, self.dw_own, 0, self.received, 0, self.main)
        sum_rows(self.total, self.main, self.extra.at[0], 0, self.received, self.main, self.more)
        self.ctx.start(self.source, self.target)

    def finish(self, out):
        self.ctx.wait(self.source, self.target)
        count, size, width = out.shape
        value = self.total[pl.ds(pl.multiple_of(self.ctx.me * self.size, 16), self.size), :].astype(F32)
        for d in range(1, self.ctx.count):
            value += self.blocks[d].astype(F32)
        for j in range(count):
            out[j] = value[:, j * width : (j + 1) * width].astype(out.dtype)


class ShardSum:

    def __init__(self, parts, received, blocks, shard, ctx):
        self.parts, self.received, self.blocks, self.shard, self.ctx = parts, received, blocks, shard, ctx

    def source(self, peer, d):
        return self.parts.at[peer]

    def target(self, me, d):
        return self.received.at[d]

    def start(self):
        self.shard.start(self.source, self.target)

    def mine(self, peer, d):
        return self.blocks.at[self.ctx.me]

    def theirs(self, me, d):
        return self.blocks.at[me]

    def spread(self):
        self.shard.wait(self.source, self.target)
        value = self.parts[self.shard.me].astype(F32)
        for d in range(1, self.shard.count):
            value += self.received[d].astype(F32)
        self.blocks[self.ctx.me] = value.astype(BF16)
        self.ctx.start(self.mine, self.theirs)

    def finish(self):
        self.ctx.wait(self.mine, self.theirs)


class InputSum:

    def __init__(self, dn_send, dn_own, received, total, blocks, tp_sems, ctx):
        self.dn_send, self.dn_own, self.received = dn_send, dn_own, received
        self.total, self.blocks, self.tp_sems, self.ctx = total, blocks, tp_sems, ctx

    def crossing(self, d):
        return cross(self.dn_send(d), self.received.at[d], self.tp_sems, d)

    def source(self, peer, d):
        return self.total.at[d]

    def target(self, me, d):
        return self.blocks.at[d]

    def spread_one(self, d):
        self.crossing(d).wait()
        sum_rows(self.total.at[d], 0, self.dn_own(d), 0, self.received.at[d], 0, self.received.shape[1])
        if d:
            self.ctx.copy(d, self.source, self.target).start()

    def finish(self):
        self.ctx.wait(self.source, self.target)

    def rows(self, at, size):
        value = self.total[0, pl.ds(at, size), :].astype(F32)
        for d in range(1, self.ctx.count):
            value += self.blocks[d, pl.ds(at, size), :].astype(F32)
        return value


def attend_back_step(refs, scratch, starts, width):
    qx_ref, k_ref, v_ref, go_ref, o_ref, n_ref, x_ref, w_ref = refs
    gx_all, dq_acc, dn_acc, dw_acc, db_ref, sums_ref = scratch
    i, j = pl.program_id(0), pl.program_id(1)
    last_block, last_pair = pl.num_programs(0) - 1, pl.num_programs(1) - 1
    rows, lanes = o_ref.shape
    keys = k_ref.shape[0]
    lane = lax.broadcasted_iota(jnp.int32, (rows, lanes), 1)
    lane_k = lax.broadcasted_iota(jnp.int32, (keys, lanes), 1)
    one = jnp.ones((), BF16)

    @pl.when(i == 0)
    def _():
        grad_out = go_ref[...].astype(F32)
        both = grad_out * o_ref[...].astype(F32)
        for h in range(2):
            inside = (lane < width) if h == 0 else (lane >= width)
            delta = jnp.sum(jnp.where(inside, both, 0.0), axis=1, keepdims=True)
            gx_all[j, h] = with_parts(lane, grad_out, -delta, width if h == 0 else 0, width).astype(BF16)
        dq_acc[j] = jnp.zeros(dq_acc.shape[1:], F32)
        dw_acc[j] = starts[0][j] if starts else jnp.zeros(dw_acc.shape[1:], F32)
        db_ref[j] = starts[1][j] if starts else jnp.zeros(db_ref.shape[1:], F32)

    @pl.when((i == 0) & (j == 0))
    def _():
        sums_ref[...] = starts[2][...] if starts else jnp.zeros_like(sums_ref)

    @pl.when(j == 0)
    def _():
        dn_acc[...] = jnp.zeros_like(dn_acc)

    grad_k, grad_v, grad_q = [], [], []
    for h in range(2):
        inside_k = (lane_k < width) if h == 0 else (lane_k >= width)
        kx = jnp.where(inside_k, k_ref[...], one)
        vx = jnp.where(inside_k, v_ref[...], one)
        qx = qx_ref[:, h * lanes : (h + 1) * lanes]
        gx = gx_all[j, h]
        prob = jnp.exp2(dot_nt(kx, qx))
        grad_v.append(dot_nn(prob.astype(BF16), gx))
        grad_score = (prob * dot_nt(vx, gx)).astype(BF16)
        grad_k.append(dot_nn(grad_score, qx))
        grad_q.append(dot_tn(kx, grad_score))
    dk = (jnp.where(lane_k < width, grad_k[0], grad_k[1]) * (1.0 / LOG2E)).astype(BF16)
    dv = jnp.where(lane_k < width, grad_v[0], grad_v[1]).astype(BF16)
    dq_acc[j] += jnp.concatenate([grad_q[0][:width], grad_q[1][width:]], axis=0)
    both = jnp.concatenate([dk, dv], axis=1)
    weights = jnp.concatenate([w_ref[0, 1], w_ref[0, 2]], axis=1)
    dn_acc[...] += dot_nt(both, weights)
    grad_w = dot_tn(both, n_ref[...])
    dw_acc[j, 1] += grad_w[:lanes]
    dw_acc[j, 2] += grad_w[lanes:]
    db_ref[j, 1:2] += column_sum(dv.astype(F32))

    @pl.when(i == last_block)
    def _():
        dq = (dq_acc[j].T * (1.0 / math.sqrt(width))).astype(BF16)
        dn_acc[:rows] += dot_nt(dq, w_ref[0, 0])
        dw_acc[j, 0] += dot_tn(dq, n_ref[:rows])
        db_ref[j, 0:1] += column_sum(dq.astype(F32))

    @pl.when(j == last_pair)
    def _():
        unit, _ = unit_norm(x_ref[...].astype(F32))
        sums_ref[0:1] += column_sum(dn_acc[...] * unit)
        sums_ref[1:2] += column_sum(dn_acc[...])


def attend_back_kernel(*refs, width, nc, ns, hosted, hosted_counts, started):
    i, j = pl.program_id(0), pl.program_id(1)
    last_pair = pl.num_programs(1) - 1
    n_in, n_out, n_scratch = hosted_counts
    at = 8
    base = refs[:at]
    starts = refs[at : at + 3] if started else ()
    at += 3 if started else 0
    extra_in, at = refs[at : at + n_in], at + n_in
    (dw_ref, db_ref, sums_ref, dn_done), at = refs[at : at + 4], at + 4
    extra_out, at = refs[at : at + n_out], at + n_out
    gx_all, dq_acc, dn_acc, dw_acc, dn_sent, dn_received, dn_total, dn_blocks, tp_out, tp_in, ctx_out, ctx_in = refs[at : at + 12]
    extra_scratch = refs[at + 12 :]
    inputs = InputSum(
        lambda d: dn_sent.at[d, 1], lambda d: dn_sent.at[d, 0], dn_received, dn_total, dn_blocks,
        (tp_out, tp_in), Axis("ctx", nc, (ctx_out, ctx_in)),
    )
    guest = hosted(extra_in, extra_out, extra_scratch, nc, ns)

    @pl.when((i == 0) & (j == 0))
    def _():
        greet(guest.peers)
        guest.begin()

    @pl.when((i == 1) & (j == 0))
    def _():
        guest.middle()

    for d in range(1, nc):

        @pl.when((i == nc - d) & (j == 0))
        def _(d=d):
            inputs.crossing(d).start()

        @pl.when((i == nc - d) & (j == last_pair - 1))
        def _(d=d):
            inputs.spread_one(d)

    attend_back_step(
        base, (gx_all, dq_acc, dn_acc, dw_acc, db_ref, sums_ref), starts, width
    )

    @pl.when(j == last_pair)
    def _():
        half = dn_acc.shape[0] // 2
        for part in range(2):
            dn_sent[nc - 1 - i, part] = dn_acc[part * half : (part + 1) * half].astype(BF16)

    @pl.when((i == nc - 1) & (j == last_pair))
    def _():
        dw_ref[...] = dw_acc[...].astype(dw_ref.dtype)
        inputs.crossing(0).start()
        guest.end()
        inputs.spread_one(0)
        inputs.finish()
        size = 64

        def one(r, carry):
            here = pl.multiple_of(r * size, size)
            dn_done[pl.ds(here, size), :] = inputs.rows(here, size)
            return carry

        lax.fori_loop(0, dn_done.shape[0] // size, one, 0)


class HostRows:

    def __init__(self, ins, outs, scratch, nc, ns):
        dw_all, dw_own, extra, out_half = ins
        self.dw_out, whole = outs
        received, total, blocks, tp_out, tp_in, ctx_out, ctx_in, sems = scratch
        t = lax.axis_index("tp")
        self.rows = RowSum(
            dw_all.at[1], dw_own.at[0], extra, received, total, blocks, (tp_out, tp_in), Axis("ctx", nc, (ctx_out, ctx_in))
        )
        self.copies = lambda: [
            cross(out_half, whole.at[:, t], (sems, sems.at[pl.ds(1, 1)]), 0),
            pltpu.make_async_copy(out_half, whole.at[:, t], sems.at[2]),
        ]
        self.peers = [("tp", 2), ("ctx", nc)]

    def begin(self):
        self.rows.start()
        for copy in self.copies():
            copy.start()

    def middle(self):
        self.rows.spread()

    def end(self):
        self.rows.finish(self.dw_out)
        for copy in self.copies():
            copy.wait()


class HostShards:

    def __init__(self, ins, outs, scratch, nc, ns):
        (self.done,) = outs
        received, self.blocks, z_out, z_in, back_out, back_in = scratch
        self.sums = ShardSum(
            ins[0], received, self.blocks, Axis("shard", ns, (z_out, z_in)), Axis("ctx", nc, (back_out, back_in))
        )
        self.peers = [("tp", 2), ("ctx", nc), ("shard", ns)]

    def begin(self):
        self.sums.start()

    def middle(self):
        self.sums.spread()

    def end(self):
        self.sums.finish()
        self.done[...] = self.blocks[...]


def attend_back(
    hosted, entry, grad_mixed, x_all, weights, width, micro, starts, kind, ins, in_specs, outs, out_specs, scratch, number, ns, nc
):
    normed, k, v, qx, mixed = entry
    rows, cols = mixed.shape
    keys, features = normed.shape
    lanes = 2 * width
    pairs = cols // lanes
    size = keys // nc
    each = pairs // 2
    stack = (pairs, 3, lanes, features)
    block = pltpu.VMEM((nc, rows, features), BF16)

    def key_block(shape, column):
        return pl.BlockSpec(shape, lambda i, j: (nc - 1 - i, j if column else 0))

    return pl.pallas_call(
        functools.partial(
            attend_back_kernel, width=width, nc=nc, ns=ns, hosted=hosted,
            hosted_counts=(len(ins), len(outs), len(scratch)), started=bool(starts),
        ),
        grid=(nc, pairs),
        in_specs=[
            pl.BlockSpec((rows, 2 * lanes), lambda i, j: (0, j)),
            key_block((size, lanes), True),
            key_block((size, lanes), True),
            pl.BlockSpec((rows, lanes), lambda i, j: (micro, j)),
            pl.BlockSpec((rows, lanes), lambda i, j: (0, j)),
            key_block((size, features), False),
            key_block((size, features), False),
            pl.BlockSpec((1, 3, features, lanes), lambda i, j: (j // each, 0, 0, j % each)),
        ]
        + [once(start.shape) for start in starts]
        + in_specs,
        out_specs=[full_spec(stack), full_spec((pairs, 8, lanes)), full_spec((8, features)), full_spec((rows, features))]
        + out_specs,
        out_shape=[
            jax.ShapeDtypeStruct(stack, kind),
            jax.ShapeDtypeStruct((pairs, 8, lanes), F32),
            jax.ShapeDtypeStruct((8, features), F32),
            jax.ShapeDtypeStruct((rows, features), F32),
        ]
        + outs,
        scratch_shapes=[
            pltpu.VMEM((pairs, 2, rows, lanes), BF16),
            pltpu.VMEM((pairs, lanes, rows), F32),
            pltpu.VMEM((size, features), F32),
            pltpu.VMEM(stack, F32),
            pltpu.VMEM((nc, 2, rows, features), BF16),
            block, block, block,
            *axis_sems(nc, nc),
        ]
        + scratch,
        compiler_params=params(collective_id=number, has_side_effects=True),
        cost_estimate=pl.CostEstimate(
            flops=30 * rows * keys * cols, bytes_accessed=8 * keys * cols, transcendentals=rows * keys * cols // width
        ),
        name="attend_back",
    )(qx, k, v, grad_mixed, mixed, normed, x_all, weights, *starts, *ins)


def attend_back_rows(entry, grad_mixed, x_all, weights, width, dw, extra, out, ns, nc):
    main, features = dw.shape[1:]
    rows = main + extra.shape[1]
    block = (nc, rows // nc, features)
    parts = (ns, rows // nc, features // ns)
    micros, half, _ = out.shape
    anywhere = pl.BlockSpec(memory_space=pl.ANY)
    return attend_back(
        HostRows, entry, grad_mixed, x_all, weights, width, 0, (), F32,
        [dw, dw, extra, out],
        [anywhere, once((1, main, features)), once(extra.shape), once(out.shape)],
        [jax.ShapeDtypeStruct(parts, BF16), jax.ShapeDtypeStruct((micros, 2, half, features), BF16)],
        [full_spec(parts), anywhere],
        [
            pltpu.VMEM((rows, features), BF16), pltpu.VMEM((rows, features), BF16), pltpu.VMEM(block, BF16),
            *axis_sems(2, nc), pltpu.SemaphoreType.DMA((3,)),
        ],
        3, ns, nc,
    )


def attend_back_shards(entry, grad_mixed, x_all, weights, width, starts, dw_parts, ns, nc):
    _, size, part = dw_parts.shape
    return attend_back(
        HostShards, entry, grad_mixed, x_all, weights, width, 1, starts, BF16,
        [dw_parts], [once(dw_parts.shape)],
        [jax.ShapeDtypeStruct((nc, size, part), BF16)], [full_spec((nc, size, part))],
        [pltpu.VMEM(dw_parts.shape, BF16), pltpu.VMEM((nc, size, part), BF16), *axis_sems(ns, nc)],
        4, ns, nc,
    )


def ffn_kernel(
    where_ref, x_ref, o0_ref, o1_ref, g_ref, w_out, w_up, w_down, bup_ref, vec_ref,
    out_ref, gm_ref, gx_ref, dw_ref, dup_ref, dvec_ref, dw_acc,
):
    step = pl.program_id(0)
    steps = pl.num_programs(0)
    b_out, b_down, gain, shift = (vec_ref[i : i + 1, :] for i in (0, 1, 4, 5))
    hw = w_out.shape[1]
    hidden = w_up.shape[2]

    @pl.when(step == 0)
    def _():
        dw_acc[...] = jnp.zeros_like(dw_acc)
        dup_ref[...] = jnp.zeros_like(dup_ref)
        dvec_ref[...] = jnp.zeros_like(dvec_ref)

    mixed = jnp.where(2 * step < steps, o0_ref[...], o1_ref[...])
    grad_b = g_ref[0, 0]
    grad = grad_b.astype(F32)
    attended = dot_nn(mixed[:, :hw], w_out[0]) + dot_nn(mixed[:, hw:], w_out[1])
    middle = x_ref[0, 0].astype(F32) + (attended + b_out)
    unit, inverse = unit_norm(middle)
    normed = (unit * gain + shift).astype(BF16)
    ffn_out = jnp.zeros_like(middle)
    grad_normed = jnp.zeros_like(middle)
    for part in range(2):
        pre = dot_nn(normed, w_up[part]) + bup_ref[part]
        gate = 0.5 + 0.5 * lax.erf(pre * math.sqrt(0.5))
        active = (pre * gate).astype(BF16)
        ffn_out += dot_nn(active, w_down[part])
        slope = gate + pre * jnp.exp(pre * pre * -0.5) * (1.0 / math.sqrt(2.0 * math.pi))
        grad_pre_f = dot_nt(grad_b, w_down[part]) * slope
        grad_pre = grad_pre_f.astype(BF16)
        dup_ref[part] += column_sum(grad_pre.astype(F32))
        grad_normed += dot_nt(grad_pre, w_up[part])
        dw_acc[part, hw : hw + hidden] += dot_tn(active, grad_b)
        dw_acc[part, hw + hidden :] += dot_tn(grad_pre, normed)
    out_ref[...] = (middle + (ffn_out + b_down)).astype(BF16)
    grad_middle = grad + norm_back(grad_normed, unit, inverse, gain)
    gm_ref[...] = grad_middle
    grad_att = grad_middle.astype(BF16)
    dvec_ref[0:1] += column_sum(grad_att.astype(F32))
    dvec_ref[1:2] += column_sum(grad)
    dvec_ref[2:3] += column_sum(grad_normed * unit)
    dvec_ref[3:4] += column_sum(grad_normed)
    for part in range(2):
        cols = slice(part * hw, (part + 1) * hw)
        gx_ref[:, cols] = dot_nt(grad_att, w_out[part]).astype(BF16)
        dw_acc[part, :hw] += dot_tn(mixed[:, cols], grad_att)

    @pl.when(step == steps - 1)
    def _():
        dw_ref[...] = dw_acc[...].astype(BF16)


def feed_forward(tokens, mixed, cotangent, w_out, w_up, w_down, b_up, vectors, where):
    micros, _, length, features = tokens.shape
    block = 256
    half = length // 2
    each = half // block
    rows = micros * half
    hw, hidden = w_out.shape[1], w_up.shape[2]
    total = hw + 2 * hidden
    row_spec = pl.BlockSpec((block, features), lambda i, t: (i, 0))
    input_spec = pl.BlockSpec((1, 1, block, features), lambda i, t: (i // each, 0, t[0] * each + i % each, 0))
    return pl.pallas_call(
        ffn_kernel,
        grid_spec=pltpu.PrefetchScalarGridSpec(
            num_scalar_prefetch=1,
            grid=(rows // block,),
            in_specs=[
                input_spec,
                pl.BlockSpec((block, 2 * hw), lambda i, t: (jnp.minimum(i, each - 1), 0)),
                pl.BlockSpec((block, 2 * hw), lambda i, t: (jnp.maximum(i - each, 0), 0)),
                input_spec,
            ]
            + [once(w.shape) for w in (w_out, w_up, w_down)]
            + [once(b_up.shape), once(vectors.shape)],
            out_specs=[row_spec] * 3
            + [full_spec((2, total, features)), full_spec((2, 1, hidden)), full_spec((8, features))],
            scratch_shapes=[pltpu.VMEM((2, total, features), F32)],
        ),
        out_shape=[
            jax.ShapeDtypeStruct((rows, features), BF16),
            jax.ShapeDtypeStruct((rows, features), F32),
            jax.ShapeDtypeStruct((rows, 2 * hw), BF16),
            jax.ShapeDtypeStruct((2, total, features), BF16),
            jax.ShapeDtypeStruct((2, 1, hidden), F32),
            jax.ShapeDtypeStruct((8, features), F32),
        ],
        compiler_params=params(),
        cost_estimate=pl.CostEstimate(
            flops=12 * rows * total * features, bytes_accessed=20 * total * features, transcendentals=4 * rows * hidden
        ),
        name="feed_forward",
    )(where, tokens, *mixed, cotangent, w_out, w_up, w_down, b_up, vectors)


def last_kernel(
    dw_ref, extra_ref, dn0_ref, dn1_ref, x_ref, gm_ref, vec_ref,
    grad_ref, blocks_ref,
    w_received, w_total, w_blocks, z_parts, z_received,
    wtp_out, wtp_in, wctx_out, wctx_in, z_out, z_in, back_out, back_in, row_out, row_in, *, ns, nc,
):
    t = lax.axis_index("tp")
    half = grad_ref.shape[2]
    rows = RowSum(
        dw_ref.at[1], dw_ref.at[0], extra_ref, w_received, w_total, w_blocks, (wtp_out, wtp_in),
        Axis("ctx", nc, (wctx_out, wctx_in)),
    )
    weights = ShardSum(
        z_parts, z_received, blocks_ref, Axis("shard", ns, (z_out, z_in)), Axis("ctx", nc, (back_out, back_in))
    )

    def row(micro):
        return cross(grad_ref.at[micro, t], grad_ref.at[micro, t], (row_out, row_in), micro)

    def finish_rows(micro, dn_ref):
        size = 64

        def one(i, carry):
            at = pl.multiple_of(i * size, size)
            unit, inverse = unit_norm(x_ref[micro, 0, pl.ds(t * half + at, size), :].astype(F32))
            value = gm_ref[micro, pl.ds(at, size), :] + norm_back(
                dn_ref[pl.ds(at, size), :], unit, inverse, vec_ref[2:3]
            )
            grad_ref[micro, t, pl.ds(at, size), :] = value.astype(BF16)
            return carry

        lax.fori_loop(0, half // size, one, 0)
        row(micro).start()

    greet([("tp", 2), ("ctx", nc), ("shard", ns)])
    rows.start()
    rows.spread()
    finish_rows(0, dn0_ref)
    rows.finish(z_parts)
    weights.start()
    finish_rows(1, dn1_ref)
    weights.spread()
    weights.finish()
    for micro in range(2):
        row(micro).wait()


def last_sums(dw, extra, dn, x, grad_middle, vectors, ns, nc):
    main, features = dw.shape[1:]
    rows = main + extra.shape[1]
    micros, half, _ = grad_middle.shape
    size, part = rows // nc, features // ns
    return pl.pallas_call(
        functools.partial(last_kernel, ns=ns, nc=nc),
        in_specs=[pl.BlockSpec(memory_space=pltpu.VMEM)] * 7,
        out_specs=[pl.BlockSpec(memory_space=pltpu.VMEM)] * 2,
        out_shape=[
            jax.ShapeDtypeStruct((micros, 2, half, features), BF16),
            jax.ShapeDtypeStruct((nc, size, part), BF16),
        ],
        scratch_shapes=[
            pltpu.VMEM((rows, features), BF16), pltpu.VMEM((rows, features), BF16), pltpu.VMEM((nc, size, features), BF16),
            pltpu.VMEM((ns, size, part), BF16), pltpu.VMEM((ns, size, part), BF16),
            *axis_sems(2, nc, ns, nc, micros),
        ],
        compiler_params=params(collective_id=5, has_side_effects=True),
        name="last_sums",
    )(dw, extra, *dn, x, grad_middle, vectors)


def pad_rows(rows, multiple):
    extra = -rows.shape[0] % multiple
    return jnp.concatenate([rows, jnp.zeros((extra,) + rows.shape[1:], rows.dtype)]) if extra else rows


def body(
    tokens, cotangent, w_query, w_key, w_value, w_out, w_up, w_down,
    b_query, b_value, b_up, b_out, b_down, gain_attn, shift_attn, gain_ffn, shift_ffn,
):
    ns, nc = lax.axis_size("shard"), lax.axis_size("ctx")
    t = lax.axis_index("tp")
    micros, _, length, features = tokens.shape
    half = length // 2
    heads, head_part = b_query.shape
    head_width = head_part * ns
    up_part = b_up.shape[1]
    feature_part = b_out.shape[0]

    smalls = [b_query, b_value, b_up, b_out, b_down, gain_attn, shift_attn, gain_ffn, shift_ffn]
    flat = jnp.concatenate([v.reshape(-1) for v in smalls])
    small = jnp.pad(flat, (0, -flat.shape[0] % 2048)).reshape(-1, 128)
    w_all, small_all, x_first = gather_first((w_query, w_key, w_value), small, tokens, ns, nc)
    small_all = small_all.reshape(2, ns, -1)
    bias_size, up_size = b_query.size, b_up.size
    biases = small_all[:, :, : 2 * bias_size].reshape(2, ns, 2, heads, head_part)
    biases = biases.transpose(2, 0, 3, 1, 4).reshape(2, 2 * heads * head_width).astype(F32)
    bup = small_all[:, :, 2 * bias_size : 2 * bias_size + up_size].reshape(2, ns, heads, up_part)
    bup = bup.transpose(0, 2, 1, 3).reshape(2, 1, heads * up_part * ns).astype(F32)
    at = 2 * bias_size + up_size
    vectors = small_all[0, :, at : at + 6 * feature_part].reshape(ns, 6, feature_part)
    vectors = vectors.transpose(1, 0, 2).reshape(6, features).astype(F32)
    keys = 2 * nc * half
    aligned = feature_part % 128 == 0
    column_place = place_columns if aligned else place_slot

    def column_shape(w):
        return (2, w.shape[0], features) if aligned else (2, ns) + w.shape

    def whole_columns(w):
        if not aligned:
            w = w.transpose(0, 2, 1, 3).reshape(2, w.shape[2], features)
        return w

    plans = [
        (("ctx", nc, place_distance, True), ("shard", ns, place_rows, False), ("shard", ns, column_place, False)),
        (("shard", ns, column_place, False),),
    ]
    sources = [(tokens, w_up, w_out), (w_down,)]
    specs = [
        [once((1, 1, length, features), (1, 0, 0, 0)), once(w_up.shape), once(w_out.shape)],
        [once(w_down.shape)],
    ]
    shapes = [
        ((nc, 2, half, features), (2, features, w_up.shape[1]), column_shape(w_out)),
        (column_shape(w_down),),
    ]
    x_alls = [x_first.reshape(keys, features), None]
    saved = []
    arrived = []
    for micro in range(micros):
        normed, k, v, q = front(x_alls[micro], w_all, vectors, biases, head_width, half)
        mixed, qx, *more = attend_forward(
            q, k, v, head_width, plans[micro], sources[micro], specs[micro], shapes[micro], micro + 1
        )
        if micro == 0:
            x_alls[1] = more.pop(0).reshape(keys, features)
        arrived += more
        saved.append((normed, k, v, qx, mixed))
    wu, wo, wd = arrived[0], whole_columns(arrived[1]), whole_columns(arrived[2])

    out, grad_middle, grad_mixed, dw, dup, dvec = feed_forward(
        tokens, [entry[4] for entry in saved], cotangent, wo, wu, wd, bup, vectors, jnp.full((1,), t, jnp.int32)
    )

    def spread(v, part):
        return v.reshape(heads, ns, part).transpose(1, 0, 2).reshape(ns, -1)

    def as_rows(v):
        count = v.shape[1] // feature_part
        return v.reshape(ns, count, feature_part).transpose(1, 0, 2).reshape(count, features)

    extra = jnp.stack(
        [pad_rows(jnp.concatenate([dvec[:4], as_rows(spread(dup[part, 0], up_part))]), 16 * nc) for part in range(2)]
    ).astype(BF16)

    width = heads * head_width
    *starts, dn_first, dw_parts, output = attend_back_rows(
        saved[0], grad_mixed, x_alls[0], w_all, head_width, dw, extra, out.reshape(micros, half, features), ns, nc
    )
    dw_now, db_now, sums, dn_second, dw_done = attend_back_shards(
        saved[1], grad_mixed, x_alls[1], w_all, head_width, starts, dw_parts, ns, nc
    )

    db_now = db_now[:, :2].reshape(2, -1, 2, 2 * head_width).transpose(0, 2, 1, 3).reshape(2, 2, width)
    extras = []
    for part in range(2):
        biases = jnp.concatenate([spread(db_now[part, 0], head_part), spread(db_now[part, 1], head_part)], axis=1)
        extras.append(pad_rows(jnp.concatenate([sums[:2], as_rows(biases)]), 16 * nc))
    grad_tokens, attn_done = last_sums(
        dw_now.reshape(2, 3 * width, features), jnp.stack(extras).astype(BF16),
        (dn_first, dn_second), tokens, grad_middle.reshape(micros, half, features), vectors, ns, nc,
    )

    output = output.reshape(micros, 1, length, features)
    grad_tokens = grad_tokens.reshape(micros, 1, length, features)
    done_ffn = dw_done.reshape(-1, feature_part).astype(F32)
    done_attn = attn_done.reshape(-1, feature_part).astype(F32)
    hidden = heads * up_part * ns
    g_out, g_down, g_up = done_ffn[:width], done_ffn[width : width + hidden], done_ffn[width + hidden : width + 2 * hidden]
    tail = done_ffn[width + 2 * hidden :]
    by_kind = done_attn[: 3 * width].reshape(-1, 3, 2 * head_width, feature_part)
    g_query, g_key, g_value = (by_kind[:, i].reshape(width, feature_part).T for i in range(3))
    tail_attn = done_attn[3 * width :]
    g_bup = tail[4:].reshape(-1)[: heads * up_part].reshape(heads, up_part)
    g_heads = tail_attn[2:].reshape(-1)
    g_bq = g_heads[: heads * head_part].reshape(heads, head_part)
    g_bv = g_heads[heads * head_part : 2 * heads * head_part].reshape(heads, head_part)
    return (
        output, grad_tokens, g_query, g_key, g_value, g_out, g_up.T, g_down, g_bq, g_bv, g_bup,
        tail[0], tail[1], tail_attn[0], tail_attn[1], tail[2], tail[3],
    )


def solution(mesh):
    wide, tall = P("shard", "tp"), P("tp", "shard")
    rows, vector = P(None, "shard", "ctx", None), P("shard")
    weights = (wide, wide, wide, tall, wide, tall)
    return jax.shard_map(
        body,
        mesh=mesh,
        in_specs=(rows, rows) + weights + (tall,) * 3 + (vector,) * 6,
        out_specs=(rows, rows) + weights + (tall,) * 3 + (vector,) * 6,
        check_vma=False,
    )
```

```python
import functools
import math

import jax
import jax.numpy as jnp
from jax import lax
from jax.experimental import pallas as pl
from jax.experimental.pallas import tpu as pltpu
from jax.sharding import PartitionSpec as P

F32 = jnp.float32
BF16 = jnp.bfloat16
MESH = pl.DeviceIdType.MESH
norm_eps = 1e-05
LOG2E = math.log2(math.e)
VMEM_LIMIT = 60 * 2**20


def dot_nn(left, right):
    return lax.dot_general(left, right, (((1,), (0,)), ((), ())), preferred_element_type=F32)


def dot_nt(left, right):
    return lax.dot_general(left, right, (((1,), (1,)), ((), ())), preferred_element_type=F32)


def dot_tn(left, right):
    return lax.dot_general(left, right, (((0,), (0,)), ((), ())), preferred_element_type=F32)


def unit_norm(values):
    average = jnp.mean(values, axis=-1, keepdims=True)
    centred = values - average
    variance = jnp.mean(centred * centred, axis=-1, keepdims=True)
    inverse = lax.rsqrt(variance + norm_eps)
    return centred * inverse, inverse


def norm_back(grad_normed, unit_vals, inverse, gain):
    scaled = grad_normed * gain
    return inverse * (
        scaled
        - jnp.mean(scaled, axis=-1, keepdims=True)
        - unit_vals * jnp.mean(scaled * unit_vals, axis=-1, keepdims=True)
    )


def column_sum(values):
    return jnp.sum(values, axis=0, keepdims=True)


def full_spec(shape):
    return pl.BlockSpec(shape, lambda *_: (0,) * len(shape))


def params(limit=VMEM_LIMIT, **others):
    return pltpu.CompilerParams(vmem_limit_bytes=limit, **others)


def once(shape, index=None):
    place = index or (0,) * len(shape)
    return pl.BlockSpec(shape, lambda *_: place, pipeline_mode=pl.Buffered(1))


def send(source, target, send_sem, recv_sem, where):
    return pltpu.make_async_remote_copy(
        src_ref=source, dst_ref=target, send_sem=send_sem, recv_sem=recv_sem, device_id=where, device_id_type=MESH
    )


def greet_first(counts):
    barrier = pltpu.get_barrier_semaphore()
    for name, count in counts:
        me = lax.axis_index(name)
        for d in range(1, count):
            pl.semaphore_signal(barrier, inc=1, device_id={name: me ^ d}, device_id_type=MESH)


def greet_wait(counts):
    pl.semaphore_wait(pltpu.get_barrier_semaphore(), sum(count - 1 for _, count in counts))


def greet(counts):
    greet_first(counts)
    greet_wait(counts)


class Gather:

    def __init__(self, name, count, source, theirs, target, place, sems):
        self.name, self.count, self.source, self.theirs = name, count, source, theirs
        self.target, self.place = target, place
        self.out_sem, self.in_sem, self.cross_out, self.cross_in, self.local = sems
        self.me = lax.axis_index(name)

    def first(self, d):
        where = {self.name: self.me ^ d}
        return send(self.source, self.place(self.target, 0, self.me, d), self.out_sem.at[d], self.in_sem.at[d], where)

    def cross(self, d):
        where = {"tp": 1 - lax.axis_index("tp")}
        owner = self.me ^ d
        source = self.place(self.target, 0, owner, d) if d else self.source
        return send(source, self.place(self.target, 1, owner, d), self.cross_out.at[d], self.cross_in.at[d], where)

    def locals(self):
        copies = [pltpu.make_async_copy(self.source, self.place(self.target, 0, self.me, 0), self.local.at[0])]
        if self.theirs is not None:
            copies.append(pltpu.make_async_copy(self.theirs, self.place(self.target, 1, self.me, 0), self.local.at[1]))
        return copies

    def crossed(self):
        return range(0 if self.theirs is None else 1, self.count)

    def start(self, late=0):
        for d in range(1, self.count - late):
            self.first(d).start()
        for copy in self.locals():
            copy.start()
        if self.theirs is None:
            self.cross(0).start()

    def forward(self, distances=None):
        for d in distances or range(1, self.count):
            self.first(d).wait_recv()
            self.cross(d).start()

    def finish(self):
        for d in range(1, self.count):
            self.first(d).wait_send()
        for d in self.crossed():
            self.cross(d).wait()
        for copy in self.locals():
            copy.wait()


def place_rows(ref, part, owner, d):
    size = ref.shape[1] // lax.axis_size("shard")
    return ref.at[part, pl.ds(pl.multiple_of(owner * size, size), size), :]


def place_columns(ref, part, owner, d):
    size = ref.shape[2] // lax.axis_size("shard")
    return ref.at[part, :, pl.ds(pl.multiple_of(owner * size, size), size)]


def place_slot(ref, part, owner, d):
    return ref.at[part, owner]


def place_distance(ref, part, owner, d):
    return ref.at[d, part]


def gather_sems(count):
    dma = pltpu.SemaphoreType.DMA
    return [dma((count,)), dma((count,)), dma((count,)), dma((count,)), dma((2,))]


def gather_kernel(ns, nc, wq_ref, wk_ref, wv_ref, x_block, *refs):
    tables, (w_out, small_out, x_out, small_ref), sems = refs[:-17], refs[-17:-13], refs[-13:]
    w_send, w_recv, s_send, s_recv, x_send, x_recv, wt_send, wt_recv, st_send, st_recv, xt_send, xt_recv, local = sems
    w_refs = (wq_ref, wk_ref, wv_ref)
    kinds = range(3)
    x_ref = x_block.at[0, 0]
    s = lax.axis_index("shard")
    c = lax.axis_index("ctx")
    t = lax.axis_index("tp")
    other = 1 - t
    depth = wq_ref.shape[0]
    half = x_ref.shape[0] // 2

    peers = [("tp", 2), ("ctx", nc), ("shard", ns)]
    greet_first(peers)
    small_ref[...] = jnp.zeros_like(small_ref)
    row = 0
    for table in tables:
        count, lanes = table.shape
        small_ref[row : row + count, :lanes] = table[...].astype(F32)
        row += count
    greet_wait(peers)

    def w_rows(part, kind, owner):
        return w_out.at[part, kind, pl.ds(pl.multiple_of(owner * depth, depth), depth), :]

    def x_rows(which):
        return x_ref.at[pl.ds(pl.multiple_of(which * half, half), half), :]

    def begin(source, target, send_sem, recv_sem, where):
        copy = send(source, target, send_sem, recv_sem, where)
        copy.start()
        return copy

    x_copies, w_copies, s_copies = {}, {}, {}
    size = half // 2

    def x_part(d, h):
        return x_out.at[d, 0, pl.ds(h * size, size), :]

    def x_begin(source, d, h, to):
        copy = begin(source, x_part(d, h), x_send.at[d, h], x_recv.at[d, h], {"ctx": c ^ to})
        x_copies[d, h] = copy

    relayed = nc == 4
    for h in range(2):
        for d in range(1, 3 if relayed else nc):
            part = h if d % 2 else 1 - h
            source = x_ref.at[pl.ds(pl.multiple_of(t * half + part * size, size), size), :]
            x_begin(source, d, part, d)
    for d in range(1, ns):
        for k in kinds:
            w_copies[d, k] = begin(
                w_refs[k], w_rows(0, k, s), w_send.at[k, d], w_recv.at[k, d], {"shard": s ^ d}
            )
        s_copies[d] = begin(small_ref, small_out.at[0, s], s_send.at[d], s_recv.at[d], {"shard": s ^ d})
    last = [begin(w_refs[k], w_rows(1, k, s), wt_send.at[k, 0], wt_recv.at[k, 0], {"tp": other}) for k in kinds]
    last.append(begin(small_ref, small_out.at[1, s], st_send.at[0], st_recv.at[0], {"tp": other}))
    locals_ = [pltpu.make_async_copy(w_refs[k], w_rows(0, k, s), local.at[k]) for k in kinds]
    locals_ += [
        pltpu.make_async_copy(small_ref, small_out.at[0, s], local.at[3]),
        pltpu.make_async_copy(x_rows(t), x_out.at[0, 0], local.at[4]),
        pltpu.make_async_copy(x_rows(other), x_out.at[0, 1], local.at[5]),
    ]
    for copy in locals_:
        copy.start()
    if relayed:
        x_copies[1, 0].wait_recv()
        x_begin(x_part(1, 0), 3, 0, 2)
        x_copies[2, 1].wait_recv()
        x_begin(x_part(2, 1), 3, 1, 1)
    waited = {(1, 0), (2, 1)} if relayed else set()
    for d in range(1, max(ns, nc)):
        if d < ns:
            for k in kinds:
                w_copies[d, k].wait_recv()
                last.append(
                    begin(
                        w_rows(0, k, s ^ d), w_rows(1, k, s ^ d), wt_send.at[k, d], wt_recv.at[k, d], {"tp": other}
                    )
                )
            s_copies[d].wait_recv()
            last.append(
                begin(small_out.at[0, s ^ d], small_out.at[1, s ^ d], st_send.at[d], st_recv.at[d], {"tp": other})
            )
        if d < nc:
            for h in range(2):
                if (d, h) not in waited:
                    x_copies[d, h].wait_recv()
            last.append(begin(x_out.at[d, 0], x_out.at[d, 1], xt_send.at[d], xt_recv.at[d], {"tp": other}))
    for copies in (x_copies, w_copies, s_copies):
        for copy in copies.values():
            copy.wait_send()
    for copy in last:
        copy.wait()
    for copy in locals_:
        copy.wait()


def gather_first(weights, tables, tokens, ns, nc):
    depth, width = weights[0].shape
    length, features = tokens.shape[2:]
    rows = -(-sum(table.shape[0] for table in tables) // 8) * 8
    lanes = -(-max(table.shape[1] for table in tables) // 128) * 128
    dma = pltpu.SemaphoreType.DMA
    vmem = pl.BlockSpec(memory_space=pltpu.VMEM)
    return pl.pallas_call(
        functools.partial(gather_kernel, ns, nc),
        grid=(1,),
        in_specs=[vmem] * 3 + [once((1, 1, length, features))] + [vmem] * len(tables),
        out_specs=[pl.BlockSpec(memory_space=pl.ANY)] * 3,
        out_shape=[
            jax.ShapeDtypeStruct((2, 3, ns * depth, width), BF16),
            jax.ShapeDtypeStruct((2, ns, rows, lanes), F32),
            jax.ShapeDtypeStruct((nc, 2, length // 2, features), BF16),
        ],
        scratch_shapes=[pltpu.VMEM((rows, lanes), F32)]
        + [dma((3, ns)), dma((3, ns)), dma((ns,)), dma((ns,)), dma((nc, 2)), dma((nc, 2))]
        + [dma((3, ns)), dma((3, ns)), dma((ns,)), dma((ns,)), dma((nc,)), dma((nc,)), dma((6,))],
        compiler_params=params(collective_id=0, has_side_effects=True),
        name="gather_first",
    )(*weights, tokens, *tables)


def project_rows(x, w_ref, vec_ref, bias_ref, n_ref, k_ref, v_ref):
    gain, shift = vec_ref[2:3], vec_ref[3:4]
    width = w_ref.shape[3]
    size = n_ref.shape[0] // 4
    for i in range(4):
        rows = slice(i * size, (i + 1) * size)
        unit, _ = unit_norm(x(i, size).astype(F32))
        normed = (unit * gain + shift).astype(BF16)
        n_ref[rows] = normed
        for part in range(2):
            cols = slice(part * width, (part + 1) * width)
            k_ref[rows, cols] = dot_nn(normed, w_ref[part, 1]).astype(BF16)
            v_ref[rows, cols] = (dot_nn(normed, w_ref[part, 2]) + bias_ref[1:2, cols]).astype(BF16)


def project_query(w_ref, bias_ref, n_ref, q_ref, q_scale):
    width = w_ref.shape[3]
    normed = n_ref[: q_ref.shape[0]]
    for part in range(2):
        cols = slice(part * width, (part + 1) * width)
        q_ref[:, cols] = ((dot_nn(normed, w_ref[part, 0]) + bias_ref[0:1, cols]) * q_scale).astype(BF16)


def front_kernel(
    x_ref, w_ref, vec_ref, bias_ref, guest_ref, n_ref, k_ref, v_ref, q_ref, guest_all, *sems, q_scale, ns, place, size
):
    step = pl.program_id(0)
    gather = Gather("shard", ns, guest_ref.at[pl.ds(0, size), :], None, guest_all, place, sems)

    peers = [("tp", 2), ("shard", ns)]

    @pl.when(step == 0)
    def _():
        greet_first(peers)

    @pl.when(step == 1)
    def _():
        greet_wait(peers)
        gather.start()

    project_rows(lambda i, size: x_ref[i * size : (i + 1) * size], w_ref, vec_ref, bias_ref, n_ref, k_ref, v_ref)

    @pl.when(step == 0)
    def _():
        project_query(w_ref, bias_ref, n_ref, q_ref, q_scale)

    @pl.when(step == pl.num_programs(0) - 1)
    def _():
        gather.forward()
        gather.finish()


def front(x_all, weights, vectors, biases, head_width, half, guest, guest_rows, guest_shape, ns, place, number):
    keys, features = x_all.shape
    block = 2 * half
    width = 2 * weights.shape[3]
    scale = LOG2E / math.sqrt(head_width)
    return pl.pallas_call(
        functools.partial(front_kernel, q_scale=scale, ns=ns, place=place, size=guest_rows),
        grid=(keys // block,),
        in_specs=[
            pl.BlockSpec((block, features), lambda i: (i, 0)),
            once(weights.shape),
            once(vectors.shape),
            once(biases.shape),
            once(guest.shape),
        ],
        out_specs=[
            pl.BlockSpec((block, features), lambda i: (i, 0)),
            pl.BlockSpec((block, width), lambda i: (i, 0)),
            pl.BlockSpec((block, width), lambda i: (i, 0)),
            full_spec((half, width)),
            pl.BlockSpec(memory_space=pl.ANY),
        ],
        out_shape=[
            jax.ShapeDtypeStruct((keys, features), BF16),
            jax.ShapeDtypeStruct((keys, width), BF16),
            jax.ShapeDtypeStruct((keys, width), BF16),
            jax.ShapeDtypeStruct((half, width), BF16),
            jax.ShapeDtypeStruct(guest_shape, BF16),
        ],
        scratch_shapes=gather_sems(ns),
        compiler_params=params(collective_id=number, has_side_effects=True),
        cost_estimate=pl.CostEstimate(
            flops=4 * keys * features * width, bytes_accessed=8 * keys * features, transcendentals=keys
        ),
        name="front",
    )(x_all, weights, vectors, biases, guest)


def with_parts(lane, base, values, first, width):
    high = values.astype(BF16).astype(F32)
    rest = values - high
    middle = rest.astype(BF16).astype(F32)
    low = rest - middle
    extra = jnp.where(
        lane == first, high, jnp.where(lane == first + 1, middle, jnp.where(lane == first + 2, low, 0.0))
    )
    inside = (lane < width) if first else (lane >= width)
    return jnp.where(inside, base, extra)


def attend_kernel(*refs, kc, width, plans):
    count = len(plans)
    q_ref, k_ref, v_ref = refs[:3]
    sources = refs[3 : 3 + count]
    o_ref, qx_ref = refs[3 + count : 5 + count]
    targets = refs[5 + count : 5 + 2 * count]
    scores = refs[5 + 2 * count]
    sems = refs[6 + 2 * count :]
    step = pl.program_id(0)
    last = pl.num_programs(0) - 1
    t = lax.axis_index("tp")

    def gathers(wanted):
        found = []
        for i, (name, number, place, split, start) in enumerate(plans):
            if name != wanted:
                continue
            source, theirs = sources[i], None
            if split:
                source = source.at[0, 0]
                half = source.shape[0] // 2
                theirs = source.at[pl.ds(pl.multiple_of((1 - t) * half, half), half), :]
                source = source.at[pl.ds(pl.multiple_of(t * half, half), half), :]
            elif start:
                source = source.at[pl.ds(start, source.shape[0] - start), :]
            found.append(Gather(name, number, source, theirs, targets[i], place, sems[5 * i : 5 * i + 5]))
        return found

    counts = {name: number for name, number, *_ in plans}

    peers = [("tp", 2)] + list(counts.items())
    far = counts.get("ctx", 1) - 1

    @pl.when(step == 0)
    def _():
        greet_first(peers)


    rows, lanes = q_ref.shape
    keys = k_ref.shape[0]
    lane = lax.broadcasted_iota(jnp.int32, (rows, lanes), 1)
    lane_v = lax.broadcasted_iota(jnp.int32, (kc, lanes), 1)
    q = q_ref[...].astype(F32)
    tops = []
    for h in range(2):
        inside = (lane < width) if h == 0 else (lane >= width)
        q_head = jnp.where(inside, q, 0.0).astype(BF16)
        top = None
        for i in range(keys // kc):
            part = dot_nt(k_ref[i * kc : (i + 1) * kc], q_head)
            scores[h, i * kc : (i + 1) * kc] = part
            here = jnp.max(part.reshape(kc // 8, 8, rows), axis=0)
            top = here if top is None else jnp.maximum(top, here)
        tops.append(jnp.max(top, axis=0, keepdims=True))

    @pl.when(step == 0)
    def _():
        greet_wait(peers)
        for gather in gathers("shard"):
            gather.start()
        for gather in gathers("ctx"):
            gather.start(1)

    @pl.when(step == 2)
    def _():
        for gather in gathers("ctx"):
            gather.first(far).start()
            gather.forward(range(1, far))

    @pl.when(step == last)
    def _():
        for gather in gathers("shard"):
            if not far:
                gather.forward()

    outs = []
    for h in range(2):
        inside_v = (lane_v < width) if h == 0 else (lane_v >= width)
        total = jnp.zeros((lanes, rows), F32)
        for i in range(keys // kc):
            v_one = jnp.where(inside_v, v_ref[i * kc : (i + 1) * kc], jnp.ones((), BF16))
            exponent = jnp.exp2(scores[h, i * kc : (i + 1) * kc] - tops[h]).astype(BF16)
            total += dot_tn(v_one, exponent)
        first = width if h == 0 else 0
        log_total = tops[h] + jnp.log2(total[first : first + 1, :])
        total = total.T
        outs.append(total / pltpu.roll(total, width, 1))
        log_column = jnp.broadcast_to(log_total, (8, rows)).T[:, :1]
        qx_ref[:, h * lanes : (h + 1) * lanes] = with_parts(lane, q, -log_column, first, width).astype(BF16)
    o_ref[...] = jnp.where(lane < width, outs[0], outs[1]).astype(BF16)

    @pl.when(step == last)
    def _():
        if far:
            for gather in gathers("shard"):
                gather.forward()
            for gather in gathers("ctx"):
                gather.forward([far])
        for name in counts:
            for gather in gathers(name):
                gather.finish()


def attend_forward(q, k, v, width, plans, sources, source_specs, shapes, number):
    rows, cols = q.shape
    keys = k.shape[0]
    lanes = 2 * width
    kc = 512
    anywhere = pl.BlockSpec(memory_space=pl.ANY)
    return pl.pallas_call(
        functools.partial(attend_kernel, kc=kc, width=width, plans=plans),
        grid=(cols // lanes,),
        in_specs=[
            pl.BlockSpec((rows, lanes), lambda j: (0, j)),
            pl.BlockSpec((keys, lanes), lambda j: (0, j)),
            pl.BlockSpec((keys, lanes), lambda j: (0, j)),
        ]
        + source_specs,
        out_specs=[
            pl.BlockSpec((rows, lanes), lambda j: (0, j)),
            pl.BlockSpec((rows, 2 * lanes), lambda j: (0, j)),
        ]
        + [anywhere] * len(plans),
        out_shape=[
            jax.ShapeDtypeStruct((rows, cols), BF16),
            jax.ShapeDtypeStruct((rows, 2 * cols), BF16),
        ]
        + [jax.ShapeDtypeStruct(shape, BF16) for shape in shapes],
        scratch_shapes=[pltpu.VMEM((2, keys, rows), F32)]
        + [sem for plan in plans for sem in gather_sems(plan[1])],
        compiler_params=params(collective_id=number, has_side_effects=True),
        cost_estimate=pl.CostEstimate(
            flops=12 * rows * keys * cols, bytes_accessed=4 * keys * cols, transcendentals=rows * keys * cols // width
        ),
        name="attend_forward",
    )(q, k, v, *sources)


def sum_rows(target, at, left, left_at, right, right_at, rows, chunk=64):
    def one(i, carry):
        here = pl.multiple_of(i * chunk, chunk)
        value = left[pl.ds(left_at + here, chunk), :].astype(F32) + right[pl.ds(right_at + here, chunk), :].astype(F32)
        target[pl.ds(at + here, chunk), :] = value.astype(target.dtype)
        return carry

    lax.fori_loop(0, rows // chunk, one, 0)


class Axis:

    def __init__(self, name, count, sems):
        self.name, self.count, self.sems = name, count, sems
        self.me = lax.axis_index(name)

    def copy(self, d, source, target):
        return send(source(self.me ^ d, d), target(self.me, d), self.sems[0].at[d], self.sems[1].at[d], {self.name: self.me ^ d})

    def start(self, source, target):
        for d in range(1, self.count):
            self.copy(d, source, target).start()

    def wait(self, source, target):
        for d in range(1, self.count):
            self.copy(d, source, target).wait()


def axis_sems(*counts):
    return [pltpu.SemaphoreType.DMA((count,)) for count in counts for _ in range(2)]


def cross(source, target, sems, i):
    return send(source, target, sems[0].at[i], sems[1].at[i], {"tp": 1 - lax.axis_index("tp")})


class RowSum:

    def __init__(self, dw_send, dw_own, extra, received, total, blocks, tp_sems, ctx):
        self.dw_send, self.dw_own, self.extra = dw_send, dw_own, extra
        self.received, self.total, self.blocks = received, total, blocks
        self.tp_sems, self.ctx = tp_sems, ctx
        self.main, self.more = dw_own.shape[0], extra.shape[1]
        self.size = (self.main + self.more) // ctx.count

    def crossing(self):
        return [
            cross(self.dw_send, self.received.at[pl.ds(0, self.main), :], self.tp_sems, 0),
            cross(self.extra.at[1], self.received.at[pl.ds(self.main, self.more), :], self.tp_sems, 1),
        ]

    def start(self):
        for copy in self.crossing():
            copy.start()

    def source(self, peer, d):
        return self.total.at[pl.ds(pl.multiple_of(peer * self.size, 16), self.size), :]

    def target(self, me, d):
        return self.blocks.at[d]

    def spread(self):
        for copy in self.crossing():
            copy.wait()
        sum_rows(self.total, 0, self.dw_own, 0, self.received, 0, self.main)
        sum_rows(self.total, self.main, self.extra.at[0], 0, self.received, self.main, self.more)
        self.ctx.start(self.source, self.target)

    def finish(self, out):
        self.ctx.wait(self.source, self.target)
        count, size, width = out.shape
        value = self.total[pl.ds(pl.multiple_of(self.ctx.me * self.size, 16), self.size), :].astype(F32)
        for d in range(1, self.ctx.count):
            value += self.blocks[d].astype(F32)
        for j in range(count):
            out[j] = value[:, j * width : (j + 1) * width].astype(out.dtype)


class ShardSum:

    def __init__(self, parts, received, blocks, shard, ctx):
        self.parts, self.received, self.blocks, self.shard, self.ctx = parts, received, blocks, shard, ctx

    def source(self, peer, d):
        return self.parts.at[peer]

    def target(self, me, d):
        return self.received.at[d]

    def start(self):
        self.shard.start(self.source, self.target)

    def mine(self, peer, d):
        return self.blocks.at[self.ctx.me]

    def theirs(self, me, d):
        return self.blocks.at[me]

    def spread(self):
        self.shard.wait(self.source, self.target)
        value = self.parts[self.shard.me].astype(F32)
        for d in range(1, self.shard.count):
            value += self.received[d].astype(F32)
        self.blocks[self.ctx.me] = value.astype(BF16)
        self.ctx.start(self.mine, self.theirs)

    def finish(self):
        self.ctx.wait(self.mine, self.theirs)


class InputSum:

    def __init__(self, dn_send, dn_own, received, total, blocks, tp_sems, ctx):
        self.dn_send, self.dn_own, self.received = dn_send, dn_own, received
        self.total, self.blocks, self.tp_sems, self.ctx = total, blocks, tp_sems, ctx

    def crossing(self, d):
        return cross(self.dn_send(d), self.received.at[d], self.tp_sems, d)

    def source(self, peer, d):
        return self.total.at[d]

    def target(self, me, d):
        return self.blocks.at[d]

    def spread_one(self, d):
        self.crossing(d).wait()
        sum_rows(self.total.at[d], 0, self.dn_own(d), 0, self.received.at[d], 0, self.received.shape[1])
        self.ctx.copy(d, self.source, self.target).start()

    def finish(self):
        self.ctx.wait(self.source, self.target)

    def rows(self, own, at, size):
        value = own[pl.ds(at, size), :]
        for d in range(1, self.ctx.count):
            value += self.blocks[d, pl.ds(at, size), :].astype(F32)
        return value


def attend_back_step(refs, scratch, starts, width):
    qx_ref, k_ref, v_ref, go_ref, o_ref, n_ref, x_ref, w_ref = refs
    gx_all, dq_acc, dn_acc, dw_acc, db_ref, sums_ref = scratch
    i, j = pl.program_id(0), pl.program_id(1)
    last_block, last_pair = pl.num_programs(0) - 1, pl.num_programs(1) - 1
    rows, lanes = o_ref.shape
    keys = k_ref.shape[0]
    lane = lax.broadcasted_iota(jnp.int32, (rows, lanes), 1)
    lane_k = lax.broadcasted_iota(jnp.int32, (keys, lanes), 1)
    one = jnp.ones((), BF16)

    @pl.when(i == 0)
    def _():
        grad_out = go_ref[...].astype(F32)
        both = grad_out * o_ref[...].astype(F32)
        for h in range(2):
            inside = (lane < width) if h == 0 else (lane >= width)
            delta = jnp.sum(jnp.where(inside, both, 0.0), axis=1, keepdims=True)
            gx_all[j, h] = with_parts(lane, grad_out, -delta, width if h == 0 else 0, width).astype(BF16)
        dq_acc[j] = jnp.zeros(dq_acc.shape[1:], F32)
        dw_acc[j] = starts[0][j] if starts else jnp.zeros(dw_acc.shape[1:], F32)
        db_ref[j] = starts[1][j] if starts else jnp.zeros(db_ref.shape[1:], F32)

    @pl.when((i == 0) & (j == 0))
    def _():
        sums_ref[...] = starts[2][...] if starts else jnp.zeros_like(sums_ref)

    @pl.when(j == 0)
    def _():
        dn_acc[...] = jnp.zeros_like(dn_acc)

    grad_k, grad_v, grad_q = [], [], []
    for h in range(2):
        inside_k = (lane_k < width) if h == 0 else (lane_k >= width)
        kx = jnp.where(inside_k, k_ref[...], one)
        vx = jnp.where(inside_k, v_ref[...], one)
        qx = qx_ref[:, h * lanes : (h + 1) * lanes]
        gx = gx_all[j, h]
        prob = jnp.exp2(dot_nt(kx, qx))
        grad_v.append(dot_nn(prob.astype(BF16), gx))
        grad_score = (prob * dot_nt(vx, gx)).astype(BF16)
        grad_k.append(dot_nn(grad_score, qx))
        grad_q.append(dot_tn(kx, grad_score))
    dk = (jnp.where(lane_k < width, grad_k[0], grad_k[1]) * (1.0 / LOG2E)).astype(BF16)
    dv = jnp.where(lane_k < width, grad_v[0], grad_v[1]).astype(BF16)
    dq_acc[j] += jnp.concatenate([grad_q[0][:width], grad_q[1][width:]], axis=0)
    both = jnp.concatenate([dk, dv], axis=1)
    weights = jnp.concatenate([w_ref[0, 1], w_ref[0, 2]], axis=1)
    dn_acc[...] += dot_nt(both, weights)
    grad_w = dot_tn(both, n_ref[...])
    dw_acc[j, 1] += grad_w[:lanes]
    dw_acc[j, 2] += grad_w[lanes:]
    db_ref[j, 1:2] += column_sum(dv.astype(F32))

    @pl.when(i == last_block)
    def _():
        dq = (dq_acc[j].T * (1.0 / math.sqrt(width))).astype(BF16)
        dn_acc[:rows] += dot_nt(dq, w_ref[0, 0])
        dw_acc[j, 0] += dot_tn(dq, n_ref[:rows])
        db_ref[j, 0:1] += column_sum(dq.astype(F32))

    @pl.when(j == last_pair)
    def _():
        unit, _ = unit_norm(x_ref[...].astype(F32))
        sums_ref[0:1] += column_sum(dn_acc[...] * unit)
        sums_ref[1:2] += column_sum(dn_acc[...])


def attend_back_kernel(*refs, width, nc, ns, hosted, hosted_counts, started):
    i, j = pl.program_id(0), pl.program_id(1)
    last_pair = pl.num_programs(1) - 1
    n_in, n_out, n_scratch = hosted_counts
    at = 8
    base = refs[:at]
    starts = refs[at : at + 3] if started else ()
    at += 3 if started else 0
    extra_in, at = refs[at : at + n_in], at + n_in
    (dw_ref, db_ref, sums_ref, dn_done, dn_other), at = refs[at : at + 5], at + 5
    extra_out, at = refs[at : at + n_out], at + n_out
    gx_all, dq_acc, dn_acc, dw_acc, dn_sent, dn_received, dn_total, dn_blocks, tp_out, tp_in, ctx_out, ctx_in = refs[at : at + 12]
    extra_scratch = refs[at + 12 :]
    inputs = InputSum(
        lambda d: dn_sent.at[d, 1], lambda d: dn_sent.at[d, 0], dn_received, dn_total, dn_blocks,
        (tp_out, tp_in), Axis("ctx", nc, (ctx_out, ctx_in)),
    )
    guest = hosted(extra_in, extra_out, extra_scratch, nc, ns)

    @pl.when((i == 0) & (j == 0))
    def _():
        greet_first(guest.peers)

    @pl.when((i == 0) & (j == 1))
    def _():
        greet_wait(guest.peers)
        guest.begin()

    @pl.when((i == 1) & (j == 0))
    def _():
        guest.middle()

    for d in range(1, nc):

        @pl.when((i == nc - d) & (j == 0))
        def _(d=d):
            inputs.crossing(d).start()

        @pl.when((i == nc - d) & (j == 1))
        def _(d=d):
            inputs.spread_one(d)

    attend_back_step(
        base, (gx_all, dq_acc, dn_acc, dw_acc, db_ref, sums_ref), starts, width
    )

    half = dn_acc.shape[0] // 2

    @pl.when((j == last_pair) & (i < nc - 1))
    def _():
        for part in range(2):
            dn_sent[nc - 1 - i, part] = dn_acc[part * half : (part + 1) * half].astype(BF16)

    @pl.when((i == nc - 1) & (j == last_pair))
    def _():
        dw_ref[...] = dw_acc[...].astype(dw_ref.dtype)
        dn_other[...] = dn_acc[half:].astype(BF16)
        guest.end()
        inputs.finish()
        size = 64

        def one(r, carry):
            here = pl.multiple_of(r * size, size)
            dn_done[pl.ds(here, size), :] = inputs.rows(dn_acc, here, size)
            return carry

        lax.fori_loop(0, half // size, one, 0)


class HostRows:

    def __init__(self, ins, outs, scratch, nc, ns):
        dw_all, dw_own, extra, out_half = ins
        self.dw_out, whole = outs
        received, total, blocks, tp_out, tp_in, ctx_out, ctx_in, sems = scratch
        t = lax.axis_index("tp")
        self.rows = RowSum(
            dw_all.at[1], dw_own.at[0], extra, received, total, blocks, (tp_out, tp_in), Axis("ctx", nc, (ctx_out, ctx_in))
        )
        self.copies = lambda: [
            cross(out_half, whole.at[:, t], (sems, sems.at[pl.ds(1, 1)]), 0),
            pltpu.make_async_copy(out_half, whole.at[:, t], sems.at[2]),
        ]
        self.peers = [("tp", 2), ("ctx", nc)]

    def begin(self):
        self.rows.start()
        for copy in self.copies():
            copy.start()

    def middle(self):
        self.rows.spread()

    def end(self):
        self.rows.finish(self.dw_out)
        for copy in self.copies():
            copy.wait()


class HostShards:

    def __init__(self, ins, outs, scratch, nc, ns):
        (self.done,) = outs
        received, self.blocks, z_out, z_in, back_out, back_in = scratch
        self.sums = ShardSum(
            ins[0], received, self.blocks, Axis("shard", ns, (z_out, z_in)), Axis("ctx", nc, (back_out, back_in))
        )
        self.peers = [("tp", 2), ("ctx", nc), ("shard", ns)]

    def begin(self):
        self.sums.start()

    def middle(self):
        self.sums.spread()

    def end(self):
        self.sums.finish()
        self.done[...] = self.blocks[...]


def attend_back(
    hosted, entry, grad_mixed, x_all, weights, width, micro, starts, kind, ins, in_specs, outs, out_specs, scratch, number, ns, nc
):
    normed, k, v, qx, mixed = entry
    rows, cols = mixed.shape
    keys, features = normed.shape
    lanes = 2 * width
    pairs = cols // lanes
    size = keys // nc
    each = pairs // 2
    stack = (pairs, 3, lanes, features)
    block = pltpu.VMEM((nc, rows, features), BF16)

    def key_block(shape, column):
        return pl.BlockSpec(shape, lambda i, j: (nc - 1 - i, j if column else 0))

    return pl.pallas_call(
        functools.partial(
            attend_back_kernel, width=width, nc=nc, ns=ns, hosted=hosted,
            hosted_counts=(len(ins), len(outs), len(scratch)), started=bool(starts),
        ),
        grid=(nc, pairs),
        in_specs=[
            pl.BlockSpec((rows, 2 * lanes), lambda i, j: (0, j)),
            key_block((size, lanes), True),
            key_block((size, lanes), True),
            pl.BlockSpec((rows, lanes), lambda i, j: (micro, j)),
            pl.BlockSpec((rows, lanes), lambda i, j: (0, j)),
            key_block((size, features), False),
            key_block((size, features), False),
            pl.BlockSpec((1, 3, features, lanes), lambda i, j: (j // each, 0, 0, j % each)),
        ]
        + [once(value.shape) for value in starts]
        + in_specs,
        out_specs=[full_spec(stack), full_spec((pairs, 8, lanes)), full_spec((8, features))]
        + [full_spec((rows, features))] * 2
        + out_specs,
        out_shape=[
            jax.ShapeDtypeStruct(stack, kind),
            jax.ShapeDtypeStruct((pairs, 8, lanes), F32),
            jax.ShapeDtypeStruct((8, features), F32),
            jax.ShapeDtypeStruct((rows, features), F32),
            jax.ShapeDtypeStruct((rows, features), BF16),
        ]
        + outs,
        scratch_shapes=[
            pltpu.VMEM((pairs, 2, rows, lanes), BF16),
            pltpu.VMEM((pairs, lanes, rows), F32),
            pltpu.VMEM((size, features), F32),
            pltpu.VMEM(stack, F32),
            pltpu.VMEM((nc, 2, rows, features), BF16),
            block, block, block,
            *axis_sems(nc, nc),
        ]
        + scratch,
        compiler_params=params(collective_id=number, has_side_effects=True),
        cost_estimate=pl.CostEstimate(
            flops=30 * rows * keys * cols, bytes_accessed=8 * keys * cols, transcendentals=rows * keys * cols // width
        ),
        name="attend_back",
    )(qx, k, v, grad_mixed, mixed, normed, x_all, weights, *starts, *ins)


def attend_back_rows(entry, grad_mixed, x_all, weights, width, dw, extra, out, ns, nc):
    main, features = dw.shape[1:]
    rows = main + extra.shape[1]
    block = (nc, rows // nc, features)
    parts = (ns, rows // nc, features // ns)
    micros, half, _ = out.shape
    anywhere = pl.BlockSpec(memory_space=pl.ANY)
    return attend_back(
        HostRows, entry, grad_mixed, x_all, weights, width, 0, (), F32,
        [dw, dw, extra, out],
        [anywhere, once((1, main, features)), once(extra.shape), once(out.shape)],
        [jax.ShapeDtypeStruct(parts, BF16), jax.ShapeDtypeStruct((micros, 2, half, features), BF16)],
        [full_spec(parts), anywhere],
        [
            pltpu.VMEM((rows, features), BF16), pltpu.VMEM((rows, features), BF16), pltpu.VMEM(block, BF16),
            *axis_sems(2, nc), pltpu.SemaphoreType.DMA((3,)),
        ],
        3, ns, nc,
    )


def attend_back_shards(entry, grad_mixed, x_all, weights, width, starts, dw_parts, ns, nc):
    _, size, part = dw_parts.shape
    return attend_back(
        HostShards, entry, grad_mixed, x_all, weights, width, 1, starts, BF16,
        [dw_parts], [once(dw_parts.shape)],
        [jax.ShapeDtypeStruct((nc, size, part), BF16)], [full_spec((nc, size, part))],
        [pltpu.VMEM(dw_parts.shape, BF16), pltpu.VMEM((nc, size, part), BF16), *axis_sems(ns, nc)],
        4, ns, nc,
    )


def ffn_kernel(
    where_ref, x_ref, o0_ref, o1_ref, g_ref, w_out, w_up, down_first, down_rest, bup_ref, vec_ref,
    out_ref, gm_ref, gx_ref, dw_ref, dup_ref, dvec_ref, dw_acc, w_down,
):
    step = pl.program_id(0)
    steps = pl.num_programs(0)
    b_out, b_down, gain, shift = (vec_ref[i : i + 1, :] for i in (0, 1, 4, 5))
    hw = w_out.shape[1]
    hidden = w_up.shape[2]

    @pl.when(step == 0)
    def _():
        split = down_first.shape[1]
        w_down[:, :split] = down_first[...]
        w_down[:, split:] = down_rest[...]
        dw_acc[...] = jnp.zeros_like(dw_acc)
        dup_ref[...] = jnp.zeros_like(dup_ref)
        dvec_ref[...] = jnp.zeros_like(dvec_ref)

    mixed = jnp.where(2 * step < steps, o0_ref[...], o1_ref[...])
    grad_b = g_ref[0, 0]
    grad = grad_b.astype(F32)
    attended = dot_nn(mixed[:, :hw], w_out[0]) + dot_nn(mixed[:, hw:], w_out[1])
    middle = x_ref[0, 0].astype(F32) + (attended + b_out)
    unit, inverse = unit_norm(middle)
    normed = (unit * gain + shift).astype(BF16)
    ffn_out = jnp.zeros_like(middle)
    grad_normed = jnp.zeros_like(middle)
    for part in range(2):
        pre = dot_nn(normed, w_up[part]) + bup_ref[part]
        gate = 0.5 + 0.5 * lax.erf(pre * math.sqrt(0.5))
        active = (pre * gate).astype(BF16)
        ffn_out += dot_nn(active, w_down[part])
        slope = gate + pre * jnp.exp(pre * pre * -0.5) * (1.0 / math.sqrt(2.0 * math.pi))
        grad_pre_f = dot_nt(grad_b, w_down[part]) * slope
        grad_pre = grad_pre_f.astype(BF16)
        dup_ref[part] += column_sum(grad_pre.astype(F32))
        grad_normed += dot_nt(grad_pre, w_up[part])
        dw_acc[part, hw : hw + hidden] += dot_tn(active, grad_b)
        dw_acc[part, hw + hidden :] += dot_tn(grad_pre, normed)
    out_ref[...] = (middle + (ffn_out + b_down)).astype(BF16)
    grad_middle = grad + norm_back(grad_normed, unit, inverse, gain)
    gm_ref[...] = grad_middle
    grad_att = grad_middle.astype(BF16)
    dvec_ref[0:1] += column_sum(grad_att.astype(F32))
    dvec_ref[1:2] += column_sum(grad)
    dvec_ref[2:3] += column_sum(grad_normed * unit)
    dvec_ref[3:4] += column_sum(grad_normed)
    for part in range(2):
        cols = slice(part * hw, (part + 1) * hw)
        gx_ref[:, cols] = dot_nt(grad_att, w_out[part]).astype(BF16)
        dw_acc[part, :hw] += dot_tn(mixed[:, cols], grad_att)

    @pl.when(step == steps - 1)
    def _():
        dw_ref[...] = dw_acc[...].astype(BF16)


def feed_forward(tokens, mixed, cotangent, w_out, w_up, down_first, down_rest, b_up, vectors, where):
    micros, _, length, features = tokens.shape
    block = 256
    half = length // 2
    each = half // block
    rows = micros * half
    hw, hidden = w_out.shape[1], w_up.shape[2]
    total = hw + 2 * hidden
    row_spec = pl.BlockSpec((block, features), lambda i, t: (i, 0))
    input_spec = pl.BlockSpec((1, 1, block, features), lambda i, t: (i // each, 0, t[0] * each + i % each, 0))
    return pl.pallas_call(
        ffn_kernel,
        grid_spec=pltpu.PrefetchScalarGridSpec(
            num_scalar_prefetch=1,
            grid=(rows // block,),
            in_specs=[
                input_spec,
                pl.BlockSpec((block, 2 * hw), lambda i, t: (jnp.minimum(i, each - 1), 0)),
                pl.BlockSpec((block, 2 * hw), lambda i, t: (jnp.maximum(i - each, 0), 0)),
                input_spec,
            ]
            + [once(w.shape) for w in (w_out, w_up, down_first, down_rest)]
            + [once(b_up.shape), once(vectors.shape)],
            out_specs=[row_spec] * 3
            + [full_spec((2, total, features)), full_spec((2, 1, hidden)), full_spec((8, features))],
            scratch_shapes=[pltpu.VMEM((2, total, features), F32), pltpu.VMEM((2, hidden, features), BF16)],
        ),
        out_shape=[
            jax.ShapeDtypeStruct((rows, features), BF16),
            jax.ShapeDtypeStruct((rows, features), F32),
            jax.ShapeDtypeStruct((rows, 2 * hw), BF16),
            jax.ShapeDtypeStruct((2, total, features), BF16),
            jax.ShapeDtypeStruct((2, 1, hidden), F32),
            jax.ShapeDtypeStruct((8, features), F32),
        ],
        compiler_params=params(),
        cost_estimate=pl.CostEstimate(
            flops=12 * rows * total * features, bytes_accessed=20 * total * features, transcendentals=4 * rows * hidden
        ),
        name="feed_forward",
    )(where, tokens, *mixed, cotangent, w_out, w_up, down_first, down_rest, b_up, vectors)


def last_kernel(
    dw_ref, extra_ref, dn0_ref, dn1_ref, other0_ref, other1_ref, x_ref, gm_ref, vec_ref,
    grad_ref, blocks_ref,
    dn_received, w_received, w_total, w_blocks, z_parts, z_received,
    dn_out, dn_in, wtp_out, wtp_in, wctx_out, wctx_in, z_out, z_in, back_out, back_in, row_out, row_in, *, ns, nc,
):
    t = lax.axis_index("tp")
    half = grad_ref.shape[2]
    rows = RowSum(
        dw_ref.at[1], dw_ref.at[0], extra_ref, w_received, w_total, w_blocks, (wtp_out, wtp_in),
        Axis("ctx", nc, (wctx_out, wctx_in)),
    )
    weights = ShardSum(
        z_parts, z_received, blocks_ref, Axis("shard", ns, (z_out, z_in)), Axis("ctx", nc, (back_out, back_in))
    )

    def row(micro):
        return cross(grad_ref.at[micro, t], grad_ref.at[micro, t], (row_out, row_in), micro)

    others = [cross(ref, dn_received.at[m], (dn_out, dn_in), m) for m, ref in enumerate((other0_ref, other1_ref))]

    def finish_rows(micro, dn_ref):
        size = 64
        others[micro].wait()

        def one(i, carry):
            at = pl.multiple_of(i * size, size)
            unit, inverse = unit_norm(x_ref[micro, 0, pl.ds(t * half + at, size), :].astype(F32))
            value = gm_ref[micro, pl.ds(at, size), :] + norm_back(
                dn_ref[pl.ds(at, size), :] + dn_received[micro, pl.ds(at, size), :].astype(F32),
                unit, inverse, vec_ref[2:3],
            )
            grad_ref[micro, t, pl.ds(at, size), :] = value.astype(BF16)
            return carry

        lax.fori_loop(0, half // size, one, 0)
        row(micro).start()

    greet([("tp", 2), ("ctx", nc), ("shard", ns)])
    rows.start()
    for copy in others:
        copy.start()
    rows.spread()
    finish_rows(0, dn0_ref)
    rows.finish(z_parts)
    weights.start()
    finish_rows(1, dn1_ref)
    weights.spread()
    weights.finish()
    for micro in range(2):
        row(micro).wait()


def last_sums(dw, extra, dn, x, grad_middle, vectors, ns, nc):
    main, features = dw.shape[1:]
    rows = main + extra.shape[1]
    micros, half, _ = grad_middle.shape
    size, part = rows // nc, features // ns
    return pl.pallas_call(
        functools.partial(last_kernel, ns=ns, nc=nc),
        in_specs=[pl.BlockSpec(memory_space=pltpu.VMEM)] * 9,
        out_specs=[pl.BlockSpec(memory_space=pltpu.VMEM)] * 2,
        out_shape=[
            jax.ShapeDtypeStruct((micros, 2, half, features), BF16),
            jax.ShapeDtypeStruct((nc, size, part), BF16),
        ],
        scratch_shapes=[
            pltpu.VMEM((micros, half, features), BF16),
            pltpu.VMEM((rows, features), BF16), pltpu.VMEM((rows, features), BF16), pltpu.VMEM((nc, size, features), BF16),
            pltpu.VMEM((ns, size, part), BF16), pltpu.VMEM((ns, size, part), BF16),
            *axis_sems(micros, 2, nc, ns, nc, micros),
        ],
        compiler_params=params(collective_id=5, has_side_effects=True),
        name="last_sums",
    )(dw, extra, *dn, x, grad_middle, vectors)


def results_kernel(out_ref, grad_ref, ffn_ref, attn_ref, *refs, heads, head_part, up_part):
    (out, grad_tokens, g_query, g_key, g_value, g_out, g_up, g_down, g_bq, g_bv, g_bup, *vectors) = refs
    out[...] = out_ref[...]
    grad_tokens[...] = grad_ref[...]
    width, lanes = g_out.shape
    hidden = g_down.shape[0]
    pair = 2 * width // heads

    def values(ref, at, size):
        return ref[at : at + size, :].astype(F32)

    @pl.when(pl.program_id(0) == 0)
    def _():
        g_out[...] = values(ffn_ref, 0, width)
        g_down[...] = values(ffn_ref, width, hidden)
        g_up[...] = values(ffn_ref, width + hidden, hidden).T
        for i in range(heads // 2):
            for kind, ref in enumerate((g_query, g_key, g_value)):
                ref[:, i * pair : (i + 1) * pair] = values(attn_ref, (3 * i + kind) * pair, pair).T
        tail = values(ffn_ref, width + 2 * hidden, 16)
        tail_attn = values(attn_ref, 3 * width, 16)
        rows = (tail[0], tail[1], tail_attn[0], tail_attn[1], tail[2], tail[3])
        for ref, row in zip(vectors, rows):
            ref[...] = row
        for h in range(heads):
            at = h * up_part
            g_bup[h : h + 1] = tail[4 + at // lanes : 5 + at // lanes, at % lanes : at % lanes + up_part]
            for start, ref in ((0, g_bq), (heads * head_part, g_bv)):
                at = start + h * head_part
                ref[h : h + 1] = tail_attn[2 + at // lanes : 3 + at // lanes, at % lanes : at % lanes + head_part]


def write_results(output, grad_tokens, done_ffn, done_attn, shapes, heads, head_part, up_part):
    micros, length, features = output.shape
    steps = 4
    rows = pl.BlockSpec((micros, length // steps, features), lambda i: (0, i, 0))
    return pl.pallas_call(
        functools.partial(results_kernel, heads=heads, head_part=head_part, up_part=up_part),
        grid=(steps,),
        in_specs=[rows, rows, once(done_ffn.shape), once(done_attn.shape)],
        out_specs=[rows, rows] + [full_spec(shape) for shape in shapes],
        out_shape=[jax.ShapeDtypeStruct(output.shape, BF16)] * 2 + [jax.ShapeDtypeStruct(shape, F32) for shape in shapes],
        compiler_params=params(),
        name="results",
    )(output, grad_tokens, done_ffn, done_attn)


def pad_rows(rows, multiple):
    extra = -rows.shape[0] % multiple
    return jnp.concatenate([rows, jnp.zeros((extra,) + rows.shape[1:], rows.dtype)]) if extra else rows


def body(
    tokens, cotangent, w_query, w_key, w_value, w_out, w_up, w_down,
    b_query, b_value, b_up, b_out, b_down, gain_attn, shift_attn, gain_ffn, shift_ffn,
):
    ns, nc = lax.axis_size("shard"), lax.axis_size("ctx")
    t = lax.axis_index("tp")
    micros, _, length, features = tokens.shape
    half = length // 2
    heads, head_part = b_query.shape
    head_width = head_part * ns
    up_part = b_up.shape[1]
    feature_part = b_out.shape[0]

    tables = [b_query, b_value, b_up] + [v[None] for v in (b_out, b_down, gain_attn, shift_attn, gain_ffn, shift_ffn)]
    w_all, small_all, x_first = gather_first((w_query, w_key, w_value), tables, tokens, ns, nc)

    def by_head(row, part):
        table = small_all[:, :, row : row + heads, :part].transpose(0, 2, 1, 3)
        return table.reshape(2, heads * part * ns)

    biases = jnp.stack([by_head(0, head_part).reshape(-1), by_head(heads, head_part).reshape(-1)])
    bup = by_head(2 * heads, up_part)[:, None]
    vectors = small_all[0, :, 3 * heads : 3 * heads + 6, :feature_part].transpose(1, 0, 2)
    vectors = vectors.reshape(6, features)
    keys = 2 * nc * half
    aligned = feature_part % 128 == 0
    column_place = place_columns if aligned else place_slot

    def column_shape(w, rows):
        return (2, rows, features) if aligned else (2, ns, rows, w.shape[1])

    def whole_columns(w):
        if not aligned:
            w = w.transpose(0, 2, 1, 3).reshape(2, w.shape[2], features)
        return w

    ahead = w_down.shape[0] // 4
    plans = [
        (("ctx", nc, place_distance, True, 0), ("shard", ns, place_rows, False, 0)),
        (("shard", ns, column_place, False, ahead),),
    ]
    sources = [(tokens, w_up), (w_down,)]
    specs = [
        [once((1, 1, length, features), (1, 0, 0, 0)), once(w_up.shape)],
        [once(w_down.shape)],
    ]
    shapes = [
        ((nc, 2, half, features), (2, features, w_up.shape[1])),
        (column_shape(w_down, w_down.shape[0] - ahead),),
    ]
    guests = [(w_out, w_out.shape[0]), (w_down, ahead)]
    x_alls = [x_first.reshape(keys, features), None]
    saved = []
    arrived = []
    for micro in range(micros):
        guest, guest_rows = guests[micro]
        normed, k, v, q, early = front(
            x_alls[micro], w_all, vectors, biases, head_width, half, guest, guest_rows,
            column_shape(guest, guest_rows), ns, column_place, 6 + micro,
        )
        mixed, qx, *more = attend_forward(
            q, k, v, head_width, plans[micro], sources[micro], specs[micro], shapes[micro], micro + 1
        )
        if micro == 0:
            x_alls[1] = more.pop(0).reshape(keys, features)
        arrived += [early] + more
        saved.append((normed, k, v, qx, mixed))
    wo, wu, down_first, down_rest = arrived
    wo, down_first, down_rest = whole_columns(wo), whole_columns(down_first), whole_columns(down_rest)

    out, grad_middle, grad_mixed, dw, dup, dvec = feed_forward(
        tokens, [entry[4] for entry in saved], cotangent, wo, wu, down_first, down_rest, bup, vectors, jnp.full((1,), t, jnp.int32)
    )

    def spread(v, part):
        return v.reshape(heads, ns, part).transpose(1, 0, 2).reshape(ns, -1)

    def as_rows(v):
        count = v.shape[1] // feature_part
        return v.reshape(ns, count, feature_part).transpose(1, 0, 2).reshape(count, features)

    extra = jnp.stack(
        [pad_rows(jnp.concatenate([dvec[:4], as_rows(spread(dup[part, 0], up_part))]), 16 * nc) for part in range(2)]
    ).astype(BF16)

    width = heads * head_width
    *starts, dn_first, other_first, dw_parts, output = attend_back_rows(
        saved[0], grad_mixed, x_alls[0], w_all, head_width, dw, extra, out.reshape(micros, half, features), ns, nc
    )
    dw_now, db_now, sums, dn_second, other_second, dw_done = attend_back_shards(
        saved[1], grad_mixed, x_alls[1], w_all, head_width, starts, dw_parts, ns, nc
    )

    db_now = db_now[:, :2].reshape(2, -1, 2, 2 * head_width).transpose(0, 2, 1, 3).reshape(2, 2, width)
    extras = []
    for part in range(2):
        biases = jnp.concatenate([spread(db_now[part, 0], head_part), spread(db_now[part, 1], head_part)], axis=1)
        extras.append(pad_rows(jnp.concatenate([sums[:2], as_rows(biases)]), 16 * nc))
    grad_tokens, attn_done = last_sums(
        dw_now.reshape(2, 3 * width, features), jnp.stack(extras).astype(BF16),
        (dn_first, dn_second, other_first, other_second), tokens, grad_middle.reshape(micros, half, features), vectors, ns, nc,
    )

    if aligned:
        weights = (w_query, w_key, w_value, w_out, w_up, w_down, b_query, b_value, b_up)
        shapes = [v.shape for v in weights] + [(feature_part,)] * 6
        output, grad_tokens, *grads = write_results(
            output.reshape(micros, length, features), grad_tokens.reshape(micros, length, features),
            dw_done.reshape(-1, feature_part), attn_done.reshape(-1, feature_part), shapes, heads, head_part, up_part,
        )
        g_query, g_key, g_value, g_out, g_up, g_down, g_bq, g_bv, g_bup, *others = grads
        return (output[:, None], grad_tokens[:, None], g_query, g_key, g_value, g_out, g_up, g_down, g_bq, g_bv, g_bup, *others)
    output = output.reshape(micros, 1, length, features)
    grad_tokens = grad_tokens.reshape(micros, 1, length, features)
    done_ffn = dw_done.reshape(-1, feature_part).astype(F32)
    done_attn = attn_done.reshape(-1, feature_part).astype(F32)
    hidden = heads * up_part * ns
    g_out, g_down, g_up = done_ffn[:width], done_ffn[width : width + hidden], done_ffn[width + hidden : width + 2 * hidden]
    tail = done_ffn[width + 2 * hidden :]
    by_kind = done_attn[: 3 * width].reshape(-1, 3, 2 * head_width, feature_part)
    g_query, g_key, g_value = (by_kind[:, i].reshape(width, feature_part).T for i in range(3))
    tail_attn = done_attn[3 * width :]
    g_bup = tail[4:].reshape(-1)[: heads * up_part].reshape(heads, up_part)
    g_heads = tail_attn[2:].reshape(-1)
    g_bq = g_heads[: heads * head_part].reshape(heads, head_part)
    g_bv = g_heads[heads * head_part : 2 * heads * head_part].reshape(heads, head_part)
    return (
        output, grad_tokens, g_query, g_key, g_value, g_out, g_up.T, g_down, g_bq, g_bv, g_bup,
        tail[0], tail[1], tail_attn[0], tail_attn[1], tail[2], tail[3],
    )


def solution(mesh):
    wide, tall = P("shard", "tp"), P("tp", "shard")
    rows, vector = P(None, "shard", "ctx", None), P("shard")
    weights = (wide, wide, wide, tall, wide, tall)
    return jax.shard_map(
        body,
        mesh=mesh,
        in_specs=(rows, rows) + weights + (tall,) * 3 + (vector,) * 6,
        out_specs=(rows, rows) + weights + (tall,) * 3 + (vector,) * 6,
        check_vma=False,
    )
```

```python
import functools
import math

import jax
import jax.numpy as jnp
from jax import lax
from jax.experimental import pallas as pl
from jax.experimental.pallas import tpu as pltpu
from jax.sharding import PartitionSpec as P

F32 = jnp.float32
BF16 = jnp.bfloat16
MESH = pl.DeviceIdType.MESH
norm_eps = 1e-05
LOG2E = math.log2(math.e)
VMEM_LIMIT = 60 * 2**20


def dot_nn(left, right):
    return lax.dot_general(left, right, (((1,), (0,)), ((), ())), preferred_element_type=F32)


def dot_nt(left, right):
    return lax.dot_general(left, right, (((1,), (1,)), ((), ())), preferred_element_type=F32)


def dot_tn(left, right):
    return lax.dot_general(left, right, (((0,), (0,)), ((), ())), preferred_element_type=F32)


def unit_norm(values):
    average = jnp.mean(values, axis=-1, keepdims=True)
    centred = values - average
    variance = jnp.mean(centred * centred, axis=-1, keepdims=True)
    inverse = lax.rsqrt(variance + norm_eps)
    return centred * inverse, inverse


def norm_back(grad_normed, unit_vals, inverse, gain):
    scaled = grad_normed * gain
    return inverse * (
        scaled
        - jnp.mean(scaled, axis=-1, keepdims=True)
        - unit_vals * jnp.mean(scaled * unit_vals, axis=-1, keepdims=True)
    )


def column_sum(values):
    return jnp.sum(values, axis=0, keepdims=True)


def full_spec(shape):
    return pl.BlockSpec(shape, lambda *_: (0,) * len(shape))


def params(limit=VMEM_LIMIT, **others):
    return pltpu.CompilerParams(vmem_limit_bytes=limit, **others)


def once(shape, index=None):
    place = index or (0,) * len(shape)
    return pl.BlockSpec(shape, lambda *_: place, pipeline_mode=pl.Buffered(1))


def send(source, target, send_sem, recv_sem, where):
    return pltpu.make_async_remote_copy(
        src_ref=source, dst_ref=target, send_sem=send_sem, recv_sem=recv_sem, device_id=where, device_id_type=MESH
    )


def greet_first(counts):
    barrier = pltpu.get_barrier_semaphore()
    for name, count in counts:
        me = lax.axis_index(name)
        for d in range(1, count):
            pl.semaphore_signal(barrier, inc=1, device_id={name: me ^ d}, device_id_type=MESH)


def greet_wait(counts):
    pl.semaphore_wait(pltpu.get_barrier_semaphore(), sum(count - 1 for _, count in counts))


def greet(counts):
    greet_first(counts)
    greet_wait(counts)


class Gather:

    def __init__(self, name, count, source, theirs, target, place, sems):
        self.name, self.count, self.source, self.theirs = name, count, source, theirs
        self.target, self.place = target, place
        self.out_sem, self.in_sem, self.cross_out, self.cross_in, self.local = sems
        self.me = lax.axis_index(name)

    def first(self, d):
        where = {self.name: self.me ^ d}
        return send(self.source, self.place(self.target, 0, self.me, d), self.out_sem.at[d], self.in_sem.at[d], where)

    def cross(self, d):
        where = {"tp": 1 - lax.axis_index("tp")}
        owner = self.me ^ d
        source = self.place(self.target, 0, owner, d) if d else self.source
        return send(source, self.place(self.target, 1, owner, d), self.cross_out.at[d], self.cross_in.at[d], where)

    def locals(self):
        copies = [pltpu.make_async_copy(self.source, self.place(self.target, 0, self.me, 0), self.local.at[0])]
        if self.theirs is not None:
            copies.append(pltpu.make_async_copy(self.theirs, self.place(self.target, 1, self.me, 0), self.local.at[1]))
        return copies

    def crossed(self):
        return range(0 if self.theirs is None else 1, self.count)

    def start(self, late=0):
        for d in range(1, self.count - late):
            self.first(d).start()
        for copy in self.locals():
            copy.start()
        if self.theirs is None:
            self.cross(0).start()

    def forward(self, distances=None):
        for d in distances or range(1, self.count):
            self.first(d).wait_recv()
            self.cross(d).start()

    def relay(self, h):
        size = self.target.shape[2] // 2
        rows = pl.ds(h * size, size)
        i = (3, 0)[h]
        where = {self.name: self.me ^ (2 - h)}
        return send(
            self.target.at[1 + h, 0, rows, :], self.target.at[3, 0, rows, :], self.out_sem.at[i], self.in_sem.at[i], where
        )

    def forward_relayed(self):
        for h in range(2):
            self.relay(h).wait_recv()
        self.cross(3).start()

    def finish(self, relayed=False):
        for d in range(1, 3 if relayed else self.count):
            self.first(d).wait_send()
        for h in range(2 if relayed else 0):
            self.relay(h).wait_send()
        for d in self.crossed():
            self.cross(d).wait()
        for copy in self.locals():
            copy.wait()


def place_rows(ref, part, owner, d):
    size = ref.shape[1] // lax.axis_size("shard")
    return ref.at[part, pl.ds(pl.multiple_of(owner * size, size), size), :]


def place_columns(ref, part, owner, d):
    size = ref.shape[2] // lax.axis_size("shard")
    return ref.at[part, :, pl.ds(pl.multiple_of(owner * size, size), size)]


def place_slot(ref, part, owner, d):
    return ref.at[part, owner]


def place_distance(ref, part, owner, d):
    return ref.at[d, part]


def gather_sems(count):
    dma = pltpu.SemaphoreType.DMA
    return [dma((count,)), dma((count,)), dma((count,)), dma((count,)), dma((2,))]


def gather_kernel(ns, nc, place, wq_ref, wk_ref, wv_ref, wo_ref, x_block, *refs):
    tables, (w_out, wo_out, small_out, x_out, small_ref), sems = refs[:-18], refs[-18:-13], refs[-13:]
    w_send, w_recv, s_send, s_recv, x_send, x_recv, wt_send, wt_recv, st_send, st_recv, xt_send, xt_recv, local = sems
    w_refs = (wq_ref, wk_ref, wv_ref, wo_ref)
    kinds = range(4)
    x_ref = x_block.at[0, 0]
    s = lax.axis_index("shard")
    c = lax.axis_index("ctx")
    t = lax.axis_index("tp")
    other = 1 - t
    depth = wq_ref.shape[0]
    half = x_ref.shape[0] // 2

    peers = [("tp", 2), ("ctx", nc), ("shard", ns)]
    greet_first(peers)
    small_ref[...] = jnp.zeros_like(small_ref)
    row = 0
    for table in tables:
        count, lanes = table.shape
        small_ref[row : row + count, :lanes] = table[...].astype(F32)
        row += count
    greet_wait(peers)

    def w_rows(part, kind, owner):
        if kind == 3:
            return place(wo_out, part, owner, 0)
        return w_out.at[part, kind, pl.ds(pl.multiple_of(owner * depth, depth), depth), :]

    def x_rows(which):
        return x_ref.at[pl.ds(pl.multiple_of(which * half, half), half), :]

    def begin(source, target, send_sem, recv_sem, where):
        copy = send(source, target, send_sem, recv_sem, where)
        copy.start()
        return copy

    x_copies, w_copies, s_copies = {}, {}, {}
    size = half // 2

    def x_part(d, h):
        return x_out.at[d, 0, pl.ds(h * size, size), :]

    def x_begin(source, d, h, to):
        copy = begin(source, x_part(d, h), x_send.at[d, h], x_recv.at[d, h], {"ctx": c ^ to})
        x_copies[d, h] = copy

    relayed = nc == 4
    for h in range(2):
        for d in range(1, 3 if relayed else nc):
            part = h if d % 2 else 1 - h
            source = x_ref.at[pl.ds(pl.multiple_of(t * half + part * size, size), size), :]
            x_begin(source, d, part, d)
    for d in range(1, ns):
        for k in kinds:
            w_copies[d, k] = begin(
                w_refs[k], w_rows(0, k, s), w_send.at[k, d], w_recv.at[k, d], {"shard": s ^ d}
            )
        s_copies[d] = begin(small_ref, small_out.at[0, s], s_send.at[d], s_recv.at[d], {"shard": s ^ d})
    last = [begin(w_refs[k], w_rows(1, k, s), wt_send.at[k, 0], wt_recv.at[k, 0], {"tp": other}) for k in kinds]
    last.append(begin(small_ref, small_out.at[1, s], st_send.at[0], st_recv.at[0], {"tp": other}))
    locals_ = [pltpu.make_async_copy(w_refs[k], w_rows(0, k, s), local.at[k]) for k in kinds]
    locals_ += [
        pltpu.make_async_copy(small_ref, small_out.at[0, s], local.at[4]),
        pltpu.make_async_copy(x_rows(t), x_out.at[0, 0], local.at[5]),
        pltpu.make_async_copy(x_rows(other), x_out.at[0, 1], local.at[6]),
    ]
    for copy in locals_:
        copy.start()
    if relayed:
        x_copies[1, 0].wait_recv()
        x_begin(x_part(1, 0), 3, 0, 2)
        x_copies[2, 1].wait_recv()
        x_begin(x_part(2, 1), 3, 1, 1)
    waited = {(1, 0), (2, 1)} if relayed else set()
    for d in range(1, max(ns, nc)):
        if d < ns:
            for k in kinds:
                w_copies[d, k].wait_recv()
                last.append(
                    begin(
                        w_rows(0, k, s ^ d), w_rows(1, k, s ^ d), wt_send.at[k, d], wt_recv.at[k, d], {"tp": other}
                    )
                )
            s_copies[d].wait_recv()
            last.append(
                begin(small_out.at[0, s ^ d], small_out.at[1, s ^ d], st_send.at[d], st_recv.at[d], {"tp": other})
            )
        if d < nc:
            for h in range(2):
                if (d, h) not in waited:
                    x_copies[d, h].wait_recv()
            last.append(begin(x_out.at[d, 0], x_out.at[d, 1], xt_send.at[d], xt_recv.at[d], {"tp": other}))
    for copies in (x_copies, w_copies, s_copies):
        for copy in copies.values():
            copy.wait_send()
    for copy in last:
        copy.wait()
    for copy in locals_:
        copy.wait()


def gather_first(weights, tables, tokens, place, shape, ns, nc):
    depth, width = weights[0].shape
    length, features = tokens.shape[2:]
    rows = -(-sum(table.shape[0] for table in tables) // 8) * 8
    lanes = -(-max(table.shape[1] for table in tables) // 128) * 128
    dma = pltpu.SemaphoreType.DMA
    vmem = pl.BlockSpec(memory_space=pltpu.VMEM)
    return pl.pallas_call(
        functools.partial(gather_kernel, ns, nc, place),
        grid=(1,),
        in_specs=[vmem] * 4 + [once((1, 1, length, features))] + [vmem] * len(tables),
        out_specs=[pl.BlockSpec(memory_space=pl.ANY)] * 4,
        out_shape=[
            jax.ShapeDtypeStruct((2, 3, ns * depth, width), BF16),
            jax.ShapeDtypeStruct(shape, BF16),
            jax.ShapeDtypeStruct((2, ns, rows, lanes), F32),
            jax.ShapeDtypeStruct((nc, 2, length // 2, features), BF16),
        ],
        scratch_shapes=[pltpu.VMEM((rows, lanes), F32)]
        + [dma((4, ns)), dma((4, ns)), dma((ns,)), dma((ns,)), dma((nc, 2)), dma((nc, 2))]
        + [dma((4, ns)), dma((4, ns)), dma((ns,)), dma((ns,)), dma((nc,)), dma((nc,)), dma((7,))],
        compiler_params=params(collective_id=0, has_side_effects=True),
        name="gather_first",
    )(*weights, tokens, *tables)


def project_rows(x, w_ref, vec_ref, bias_ref, n_ref, k_ref, v_ref):
    gain, shift = vec_ref[2:3], vec_ref[3:4]
    width = w_ref.shape[3]
    size = n_ref.shape[0] // 4
    for i in range(4):
        rows = slice(i * size, (i + 1) * size)
        unit, _ = unit_norm(x(i, size).astype(F32))
        normed = (unit * gain + shift).astype(BF16)
        n_ref[rows] = normed
        for part in range(2):
            cols = slice(part * width, (part + 1) * width)
            k_ref[rows, cols] = dot_nn(normed, w_ref[part, 1]).astype(BF16)
            v_ref[rows, cols] = (dot_nn(normed, w_ref[part, 2]) + bias_ref[1:2, cols]).astype(BF16)


def project_query(w_ref, bias_ref, n_ref, q_ref, q_scale):
    width = w_ref.shape[3]
    normed = n_ref[: q_ref.shape[0]]
    for part in range(2):
        cols = slice(part * width, (part + 1) * width)
        q_ref[:, cols] = ((dot_nn(normed, w_ref[part, 0]) + bias_ref[0:1, cols]) * q_scale).astype(BF16)


def front_kernel(
    x_ref, w_ref, vec_ref, bias_ref, guest_ref, n_ref, k_ref, v_ref, q_ref, guest_all, *sems, q_scale, ns, place, size
):
    step = pl.program_id(0)
    part = guest_ref.at[:, pl.ds(0, size)] if place is place_rows else guest_ref.at[pl.ds(0, size), :]
    gather = Gather("shard", ns, part, None, guest_all, place, sems)

    peers = [("tp", 2), ("shard", ns)]

    @pl.when(step == 0)
    def _():
        greet_first(peers)

    @pl.when(step == 1)
    def _():
        greet_wait(peers)
        gather.start()

    project_rows(lambda i, size: x_ref[i * size : (i + 1) * size], w_ref, vec_ref, bias_ref, n_ref, k_ref, v_ref)

    @pl.when(step == 0)
    def _():
        project_query(w_ref, bias_ref, n_ref, q_ref, q_scale)

    @pl.when(step == pl.num_programs(0) - 1)
    def _():
        gather.forward()
        gather.finish()


def front(x_all, weights, vectors, biases, head_width, half, guest, guest_rows, guest_shape, ns, place, number):
    keys, features = x_all.shape
    block = 2 * half
    width = 2 * weights.shape[3]
    scale = LOG2E / math.sqrt(head_width)
    return pl.pallas_call(
        functools.partial(front_kernel, q_scale=scale, ns=ns, place=place, size=guest_rows),
        grid=(keys // block,),
        in_specs=[
            pl.BlockSpec((block, features), lambda i: (i, 0)),
            once(weights.shape),
            once(vectors.shape),
            once(biases.shape),
            once(guest.shape),
        ],
        out_specs=[
            pl.BlockSpec((block, features), lambda i: (i, 0)),
            pl.BlockSpec((block, width), lambda i: (i, 0)),
            pl.BlockSpec((block, width), lambda i: (i, 0)),
            full_spec((half, width)),
            pl.BlockSpec(memory_space=pl.ANY),
        ],
        out_shape=[
            jax.ShapeDtypeStruct((keys, features), BF16),
            jax.ShapeDtypeStruct((keys, width), BF16),
            jax.ShapeDtypeStruct((keys, width), BF16),
            jax.ShapeDtypeStruct((half, width), BF16),
            jax.ShapeDtypeStruct(guest_shape, BF16),
        ],
        scratch_shapes=gather_sems(ns),
        compiler_params=params(collective_id=number, has_side_effects=True),
        cost_estimate=pl.CostEstimate(
            flops=4 * keys * features * width, bytes_accessed=8 * keys * features, transcendentals=keys
        ),
        name="front",
    )(x_all, weights, vectors, biases, guest)


def with_parts(lane, base, values, first, width):
    high = values.astype(BF16).astype(F32)
    rest = values - high
    middle = rest.astype(BF16).astype(F32)
    low = rest - middle
    extra = jnp.where(
        lane == first, high, jnp.where(lane == first + 1, middle, jnp.where(lane == first + 2, low, 0.0))
    )
    inside = (lane < width) if first else (lane >= width)
    return jnp.where(inside, base, extra)


def attend_kernel(*refs, kc, width, plans):
    count = len(plans)
    q_ref, k_ref, v_ref = refs[:3]
    sources = refs[3 : 3 + count]
    o_ref, qx_ref = refs[3 + count : 5 + count]
    targets = refs[5 + count : 5 + 2 * count]
    scores = refs[5 + 2 * count]
    sems = refs[6 + 2 * count :]
    step = pl.program_id(0)
    last = pl.num_programs(0) - 1
    t = lax.axis_index("tp")

    def gathers(wanted):
        found = []
        for i, (name, number, place, split, start) in enumerate(plans):
            if name != wanted:
                continue
            source, theirs = sources[i], None
            if split:
                source = source.at[0, 0]
                half = source.shape[0] // 2
                theirs = source.at[pl.ds(pl.multiple_of((1 - t) * half, half), half), :]
                source = source.at[pl.ds(pl.multiple_of(t * half, half), half), :]
            elif start and place is place_rows:
                source = source.at[:, pl.ds(start, source.shape[1] - start)]
            elif start:
                source = source.at[pl.ds(start, source.shape[0] - start), :]
            found.append(Gather(name, number, source, theirs, targets[i], place, sems[5 * i : 5 * i + 5]))
        return found

    counts = {name: number for name, number, *_ in plans}

    peers = [("tp", 2)] + list(counts.items())
    far = counts.get("ctx", 1) - 1
    relayed = far == 3

    @pl.when(step == 0)
    def _():
        greet_first(peers)


    rows, lanes = q_ref.shape
    keys = k_ref.shape[0]
    lane = lax.broadcasted_iota(jnp.int32, (rows, lanes), 1)
    lane_v = lax.broadcasted_iota(jnp.int32, (kc, lanes), 1)
    q = q_ref[...].astype(F32)
    tops = []
    for h in range(2):
        inside = (lane < width) if h == 0 else (lane >= width)
        q_head = jnp.where(inside, q, 0.0).astype(BF16)
        top = None
        for i in range(keys // kc):
            part = dot_nt(k_ref[i * kc : (i + 1) * kc], q_head)
            scores[h, i * kc : (i + 1) * kc] = part
            here = jnp.max(part.reshape(kc // 8, 8, rows), axis=0)
            top = here if top is None else jnp.maximum(top, here)
        tops.append(jnp.max(top, axis=0, keepdims=True))

    @pl.when(step == 0)
    def _():
        greet_wait(peers)
        for gather in gathers("shard"):
            gather.start()
        for gather in gathers("ctx"):
            gather.start(1)

    @pl.when(step == 2)
    def _():
        for gather in gathers("ctx"):
            if not relayed:
                gather.first(far).start()
            gather.forward(range(1, far))
            for h in range(2 if relayed else 0):
                gather.relay(h).start()

    @pl.when(step == last)
    def _():
        for gather in gathers("shard"):
            if not far:
                gather.forward()

    outs = []
    for h in range(2):
        inside_v = (lane_v < width) if h == 0 else (lane_v >= width)
        total = jnp.zeros((lanes, rows), F32)
        for i in range(keys // kc):
            v_one = jnp.where(inside_v, v_ref[i * kc : (i + 1) * kc], jnp.ones((), BF16))
            exponent = jnp.exp2(scores[h, i * kc : (i + 1) * kc] - tops[h]).astype(BF16)
            total += dot_tn(v_one, exponent)
        first = width if h == 0 else 0
        log_total = tops[h] + jnp.log2(total[first : first + 1, :])
        total = total.T
        outs.append(total / pltpu.roll(total, width, 1))
        log_column = jnp.broadcast_to(log_total, (8, rows)).T[:, :1]
        qx_ref[:, h * lanes : (h + 1) * lanes] = with_parts(lane, q, -log_column, first, width).astype(BF16)
    o_ref[...] = jnp.where(lane < width, outs[0], outs[1]).astype(BF16)

    @pl.when(step == last)
    def _():
        if far:
            for gather in gathers("shard"):
                gather.forward()
            for gather in gathers("ctx"):
                if relayed:
                    gather.forward_relayed()
                else:
                    gather.forward([far])
        for name in counts:
            for gather in gathers(name):
                gather.finish(relayed and name == "ctx")


def attend_forward(q, k, v, width, plans, sources, source_specs, shapes, number):
    rows, cols = q.shape
    keys = k.shape[0]
    lanes = 2 * width
    kc = 512
    anywhere = pl.BlockSpec(memory_space=pl.ANY)
    return pl.pallas_call(
        functools.partial(attend_kernel, kc=kc, width=width, plans=plans),
        grid=(cols // lanes,),
        in_specs=[
            pl.BlockSpec((rows, lanes), lambda j: (0, j)),
            pl.BlockSpec((keys, lanes), lambda j: (0, j)),
            pl.BlockSpec((keys, lanes), lambda j: (0, j)),
        ]
        + source_specs,
        out_specs=[
            pl.BlockSpec((rows, lanes), lambda j: (0, j)),
            pl.BlockSpec((rows, 2 * lanes), lambda j: (0, j)),
        ]
        + [anywhere] * len(plans),
        out_shape=[
            jax.ShapeDtypeStruct((rows, cols), BF16),
            jax.ShapeDtypeStruct((rows, 2 * cols), BF16),
        ]
        + [jax.ShapeDtypeStruct(shape, BF16) for shape in shapes],
        scratch_shapes=[pltpu.VMEM((2, keys, rows), F32)]
        + [sem for plan in plans for sem in gather_sems(plan[1])],
        compiler_params=params(collective_id=number, has_side_effects=True),
        cost_estimate=pl.CostEstimate(
            flops=12 * rows * keys * cols, bytes_accessed=4 * keys * cols, transcendentals=rows * keys * cols // width
        ),
        name="attend_forward",
    )(q, k, v, *sources)


def sum_rows(target, at, left, left_at, right, right_at, rows, chunk=64):
    def one(i, carry):
        here = pl.multiple_of(i * chunk, chunk)
        value = left[pl.ds(left_at + here, chunk), :].astype(F32) + right[pl.ds(right_at + here, chunk), :].astype(F32)
        target[pl.ds(at + here, chunk), :] = value.astype(target.dtype)
        return carry

    lax.fori_loop(0, rows // chunk, one, 0)


class Axis:

    def __init__(self, name, count, sems):
        self.name, self.count, self.sems = name, count, sems
        self.me = lax.axis_index(name)

    def copy(self, d, source, target):
        return send(source(self.me ^ d, d), target(self.me, d), self.sems[0].at[d], self.sems[1].at[d], {self.name: self.me ^ d})

    def start(self, source, target):
        for d in range(1, self.count):
            self.copy(d, source, target).start()

    def wait(self, source, target):
        for d in range(1, self.count):
            self.copy(d, source, target).wait()


def axis_sems(*counts):
    return [pltpu.SemaphoreType.DMA((count,)) for count in counts for _ in range(2)]


def cross(source, target, sems, i):
    return send(source, target, sems[0].at[i], sems[1].at[i], {"tp": 1 - lax.axis_index("tp")})


class RowSum:

    def __init__(self, dw_send, dw_own, extra, received, total, blocks, tp_sems, ctx):
        self.dw_send, self.dw_own, self.extra = dw_send, dw_own, extra
        self.received, self.total, self.blocks = received, total, blocks
        self.tp_sems, self.ctx = tp_sems, ctx
        self.main, self.more = dw_own.shape[0], extra.shape[1]
        self.size = (self.main + self.more) // ctx.count

    def crossing(self):
        return [
            cross(self.dw_send, self.received.at[pl.ds(0, self.main), :], self.tp_sems, 0),
            cross(self.extra.at[1], self.received.at[pl.ds(self.main, self.more), :], self.tp_sems, 1),
        ]

    def start(self):
        for copy in self.crossing():
            copy.start()

    def source(self, peer, d):
        return self.total.at[pl.ds(pl.multiple_of(peer * self.size, 16), self.size), :]

    def target(self, me, d):
        return self.blocks.at[d]

    def spread(self):
        for copy in self.crossing():
            copy.wait()
        sum_rows(self.total, 0, self.dw_own, 0, self.received, 0, self.main)
        sum_rows(self.total, self.main, self.extra.at[0], 0, self.received, self.main, self.more)
        self.ctx.start(self.source, self.target)

    def finish(self, out):
        self.ctx.wait(self.source, self.target)
        count, size, width = out.shape
        value = self.total[pl.ds(pl.multiple_of(self.ctx.me * self.size, 16), self.size), :].astype(F32)
        for d in range(1, self.ctx.count):
            value += self.blocks[d].astype(F32)
        for j in range(count):
            out[j] = value[:, j * width : (j + 1) * width].astype(out.dtype)


class ShardSum:

    def __init__(self, parts, received, blocks, shard, ctx):
        self.parts, self.received, self.blocks, self.shard, self.ctx = parts, received, blocks, shard, ctx

    def source(self, peer, d):
        return self.parts.at[peer]

    def target(self, me, d):
        return self.received.at[d]

    def start(self):
        self.shard.start(self.source, self.target)

    def mine(self, peer, d):
        return self.blocks.at[self.ctx.me]

    def theirs(self, me, d):
        return self.blocks.at[me]

    def spread(self):
        self.shard.wait(self.source, self.target)
        value = self.parts[self.shard.me].astype(F32)
        for d in range(1, self.shard.count):
            value += self.received[d].astype(F32)
        self.blocks[self.ctx.me] = value.astype(BF16)
        self.ctx.start(self.mine, self.theirs)

    def finish(self):
        self.ctx.wait(self.mine, self.theirs)


class InputSum:

    def __init__(self, dn_send, dn_own, received, total, blocks, tp_sems, ctx):
        self.dn_send, self.dn_own, self.received = dn_send, dn_own, received
        self.total, self.blocks, self.tp_sems, self.ctx = total, blocks, tp_sems, ctx

    def crossing(self, d):
        return cross(self.dn_send(d), self.received.at[d], self.tp_sems, d)

    def source(self, peer, d):
        return self.total.at[d]

    def target(self, me, d):
        return self.blocks.at[d]

    def spread_one(self, d):
        self.crossing(d).wait()
        sum_rows(self.total.at[d], 0, self.dn_own(d), 0, self.received.at[d], 0, self.received.shape[1])
        self.ctx.copy(d, self.source, self.target).start()

    def finish(self):
        self.ctx.wait(self.source, self.target)

    def rows(self, own, at, size):
        value = own[pl.ds(at, size), :]
        for d in range(1, self.ctx.count):
            value += self.blocks[d, pl.ds(at, size), :].astype(F32)
        return value


def attend_back_step(refs, scratch, starts, width):
    qx_ref, k_ref, v_ref, go_ref, o_ref, n_ref, x_ref, w_ref = refs
    gx_all, dq_acc, dn_acc, dw_acc, db_ref, sums_ref = scratch
    i, j = pl.program_id(0), pl.program_id(1)
    last_block, last_pair = pl.num_programs(0) - 1, pl.num_programs(1) - 1
    rows, lanes = o_ref.shape
    keys = k_ref.shape[0]
    lane = lax.broadcasted_iota(jnp.int32, (rows, lanes), 1)
    lane_k = lax.broadcasted_iota(jnp.int32, (keys, lanes), 1)
    one = jnp.ones((), BF16)

    @pl.when(i == 0)
    def _():
        grad_out = go_ref[...].astype(F32)
        both = grad_out * o_ref[...].astype(F32)
        for h in range(2):
            inside = (lane < width) if h == 0 else (lane >= width)
            delta = jnp.sum(jnp.where(inside, both, 0.0), axis=1, keepdims=True)
            gx_all[j, h] = with_parts(lane, grad_out, -delta, width if h == 0 else 0, width).astype(BF16)
        dq_acc[j] = jnp.zeros(dq_acc.shape[1:], F32)
        dw_acc[j] = starts[0][j] if starts else jnp.zeros(dw_acc.shape[1:], F32)
        db_ref[j] = starts[1][j] if starts else jnp.zeros(db_ref.shape[1:], F32)

    @pl.when((i == 0) & (j == 0))
    def _():
        sums_ref[...] = starts[2][...] if starts else jnp.zeros_like(sums_ref)

    @pl.when(j == 0)
    def _():
        dn_acc[...] = jnp.zeros_like(dn_acc)

    grad_k, grad_v, grad_q = [], [], []
    for h in range(2):
        inside_k = (lane_k < width) if h == 0 else (lane_k >= width)
        kx = jnp.where(inside_k, k_ref[...], one)
        vx = jnp.where(inside_k, v_ref[...], one)
        qx = qx_ref[:, h * lanes : (h + 1) * lanes]
        gx = gx_all[j, h]
        prob = jnp.exp2(dot_nt(kx, qx))
        grad_v.append(dot_nn(prob.astype(BF16), gx))
        grad_score = (prob * dot_nt(vx, gx)).astype(BF16)
        grad_k.append(dot_nn(grad_score, qx))
        grad_q.append(dot_tn(kx, grad_score))
    dk = (jnp.where(lane_k < width, grad_k[0], grad_k[1]) * (1.0 / LOG2E)).astype(BF16)
    dv = jnp.where(lane_k < width, grad_v[0], grad_v[1]).astype(BF16)
    dq_acc[j] += jnp.concatenate([grad_q[0][:width], grad_q[1][width:]], axis=0)
    both = jnp.concatenate([dk, dv], axis=1)
    weights = jnp.concatenate([w_ref[0, 1], w_ref[0, 2]], axis=1)
    dn_acc[...] += dot_nt(both, weights)
    grad_w = dot_tn(both, n_ref[...])
    dw_acc[j, 1] += grad_w[:lanes]
    dw_acc[j, 2] += grad_w[lanes:]
    db_ref[j, 1:2] += column_sum(dv.astype(F32))

    @pl.when(i == last_block)
    def _():
        dq = (dq_acc[j].T * (1.0 / math.sqrt(width))).astype(BF16)
        dn_acc[:rows] += dot_nt(dq, w_ref[0, 0])
        dw_acc[j, 0] += dot_tn(dq, n_ref[:rows])
        db_ref[j, 0:1] += column_sum(dq.astype(F32))

    @pl.when(j == last_pair)
    def _():
        unit, _ = unit_norm(x_ref[...].astype(F32))
        sums_ref[0:1] += column_sum(dn_acc[...] * unit)
        sums_ref[1:2] += column_sum(dn_acc[...])


def attend_back_kernel(*refs, width, nc, ns, hosted, hosted_counts, started):
    i, j = pl.program_id(0), pl.program_id(1)
    last_pair = pl.num_programs(1) - 1
    n_in, n_out, n_scratch = hosted_counts
    at = 8
    base = refs[:at]
    starts = refs[at : at + 3] if started else ()
    at += 3 if started else 0
    extra_in, at = refs[at : at + n_in], at + n_in
    (dw_ref, db_ref, sums_ref, dn_done, dn_other), at = refs[at : at + 5], at + 5
    extra_out, at = refs[at : at + n_out], at + n_out
    gx_all, dq_acc, dn_acc, dw_acc, dn_sent, dn_received, dn_total, dn_blocks, tp_out, tp_in, ctx_out, ctx_in = refs[at : at + 12]
    extra_scratch = refs[at + 12 :]
    inputs = InputSum(
        lambda d: dn_sent.at[d, 1], lambda d: dn_sent.at[d, 0], dn_received, dn_total, dn_blocks,
        (tp_out, tp_in), Axis("ctx", nc, (ctx_out, ctx_in)),
    )
    guest = hosted(extra_in, extra_out, extra_scratch, nc, ns)

    @pl.when((i == 0) & (j == 0))
    def _():
        greet_first(guest.peers)

    @pl.when((i == 0) & (j == 1))
    def _():
        greet_wait(guest.peers)
        guest.begin()

    @pl.when((i == 1) & (j == 0))
    def _():
        guest.middle()

    for d in range(1, nc):

        @pl.when((i == nc - d) & (j == 0))
        def _(d=d):
            inputs.crossing(d).start()

        @pl.when((i == nc - d) & (j == 1))
        def _(d=d):
            inputs.spread_one(d)

    attend_back_step(
        base, (gx_all, dq_acc, dn_acc, dw_acc, db_ref, sums_ref), starts, width
    )

    half = dn_acc.shape[0] // 2

    @pl.when((j == last_pair) & (i < nc - 1))
    def _():
        for part in range(2):
            dn_sent[nc - 1 - i, part] = dn_acc[part * half : (part + 1) * half].astype(BF16)

    @pl.when((i == nc - 1) & (j == last_pair))
    def _():
        dw_ref[...] = dw_acc[...].astype(dw_ref.dtype)
        dn_other[...] = dn_acc[half:].astype(BF16)
        guest.end()
        inputs.finish()
        size = 64

        def one(r, carry):
            here = pl.multiple_of(r * size, size)
            dn_done[pl.ds(here, size), :] = inputs.rows(dn_acc, here, size)
            return carry

        lax.fori_loop(0, half // size, one, 0)


class HostRows:

    def __init__(self, ins, outs, scratch, nc, ns):
        dw_all, dw_own, extra, out_half = ins
        self.dw_out, whole = outs
        received, total, blocks, tp_out, tp_in, ctx_out, ctx_in, sems = scratch
        t = lax.axis_index("tp")
        self.rows = RowSum(
            dw_all.at[1], dw_own.at[0], extra, received, total, blocks, (tp_out, tp_in), Axis("ctx", nc, (ctx_out, ctx_in))
        )
        self.copies = lambda: [
            cross(out_half, whole.at[:, t], (sems, sems.at[pl.ds(1, 1)]), 0),
            pltpu.make_async_copy(out_half, whole.at[:, t], sems.at[2]),
        ]
        self.peers = [("tp", 2), ("ctx", nc)]

    def begin(self):
        self.rows.start()
        for copy in self.copies():
            copy.start()

    def middle(self):
        self.rows.spread()

    def end(self):
        self.rows.finish(self.dw_out)
        for copy in self.copies():
            copy.wait()


class HostShards:

    def __init__(self, ins, outs, scratch, nc, ns):
        (self.done,) = outs
        received, self.blocks, z_out, z_in, back_out, back_in = scratch
        self.sums = ShardSum(
            ins[0], received, self.blocks, Axis("shard", ns, (z_out, z_in)), Axis("ctx", nc, (back_out, back_in))
        )
        self.peers = [("tp", 2), ("ctx", nc), ("shard", ns)]

    def begin(self):
        self.sums.start()

    def middle(self):
        self.sums.spread()

    def end(self):
        self.sums.finish()
        self.done[...] = self.blocks[...]


def attend_back(
    hosted, entry, grad_mixed, x_all, weights, width, micro, starts, kind, ins, in_specs, outs, out_specs, scratch, number, ns, nc
):
    normed, k, v, qx, mixed = entry
    rows, cols = mixed.shape
    keys, features = normed.shape
    lanes = 2 * width
    pairs = cols // lanes
    size = keys // nc
    each = pairs // 2
    stack = (pairs, 3, lanes, features)
    block = pltpu.VMEM((nc, rows, features), BF16)

    def key_block(shape, column):
        return pl.BlockSpec(shape, lambda i, j: (nc - 1 - i, j if column else 0))

    return pl.pallas_call(
        functools.partial(
            attend_back_kernel, width=width, nc=nc, ns=ns, hosted=hosted,
            hosted_counts=(len(ins), len(outs), len(scratch)), started=bool(starts),
        ),
        grid=(nc, pairs),
        in_specs=[
            pl.BlockSpec((rows, 2 * lanes), lambda i, j: (0, j)),
            key_block((size, lanes), True),
            key_block((size, lanes), True),
            pl.BlockSpec((rows, lanes), lambda i, j: (micro, j)),
            pl.BlockSpec((rows, lanes), lambda i, j: (0, j)),
            key_block((size, features), False),
            key_block((size, features), False),
            pl.BlockSpec((1, 3, features, lanes), lambda i, j: (j // each, 0, 0, j % each)),
        ]
        + [once(value.shape) for value in starts]
        + in_specs,
        out_specs=[full_spec(stack), full_spec((pairs, 8, lanes)), full_spec((8, features))]
        + [full_spec((rows, features))] * 2
        + out_specs,
        out_shape=[
            jax.ShapeDtypeStruct(stack, kind),
            jax.ShapeDtypeStruct((pairs, 8, lanes), F32),
            jax.ShapeDtypeStruct((8, features), F32),
            jax.ShapeDtypeStruct((rows, features), F32),
            jax.ShapeDtypeStruct((rows, features), BF16),
        ]
        + outs,
        scratch_shapes=[
            pltpu.VMEM((pairs, 2, rows, lanes), BF16),
            pltpu.VMEM((pairs, lanes, rows), F32),
            pltpu.VMEM((size, features), F32),
            pltpu.VMEM(stack, F32),
            pltpu.VMEM((nc, 2, rows, features), BF16),
            block, block, block,
            *axis_sems(nc, nc),
        ]
        + scratch,
        compiler_params=params(collective_id=number, has_side_effects=True),
        cost_estimate=pl.CostEstimate(
            flops=30 * rows * keys * cols, bytes_accessed=8 * keys * cols, transcendentals=rows * keys * cols // width
        ),
        name="attend_back",
    )(qx, k, v, grad_mixed, mixed, normed, x_all, weights, *starts, *ins)


def attend_back_rows(entry, grad_mixed, x_all, weights, width, dw, extra, out, ns, nc):
    main, features = dw.shape[1:]
    rows = main + extra.shape[1]
    block = (nc, rows // nc, features)
    parts = (ns, rows // nc, features // ns)
    micros, half, _ = out.shape
    anywhere = pl.BlockSpec(memory_space=pl.ANY)
    return attend_back(
        HostRows, entry, grad_mixed, x_all, weights, width, 0, (), F32,
        [dw, dw, extra, out],
        [anywhere, once((1, main, features)), once(extra.shape), once(out.shape)],
        [jax.ShapeDtypeStruct(parts, BF16), jax.ShapeDtypeStruct((micros, 2, half, features), BF16)],
        [full_spec(parts), anywhere],
        [
            pltpu.VMEM((rows, features), BF16), pltpu.VMEM((rows, features), BF16), pltpu.VMEM(block, BF16),
            *axis_sems(2, nc), pltpu.SemaphoreType.DMA((3,)),
        ],
        3, ns, nc,
    )


def attend_back_shards(entry, grad_mixed, x_all, weights, width, starts, dw_parts, ns, nc):
    _, size, part = dw_parts.shape
    return attend_back(
        HostShards, entry, grad_mixed, x_all, weights, width, 1, starts, BF16,
        [dw_parts], [once(dw_parts.shape)],
        [jax.ShapeDtypeStruct((nc, size, part), BF16)], [full_spec((nc, size, part))],
        [pltpu.VMEM(dw_parts.shape, BF16), pltpu.VMEM((nc, size, part), BF16), *axis_sems(ns, nc)],
        4, ns, nc,
    )


def ffn_kernel(
    where_ref, x_ref, o0_ref, o1_ref, g_ref, w_out, up_first, up_rest, down_first, down_rest, bup_ref, vec_ref,
    out_ref, gm_ref, gx_ref, dw_ref, extra_ref, dw_acc, w_up, w_down, dup_ref, dvec_ref, extra, *, ns, up_part,
):
    step = pl.program_id(0)
    steps = pl.num_programs(0)
    b_out, b_down, gain, shift = (vec_ref[i : i + 1, :] for i in (0, 1, 4, 5))
    hw = w_out.shape[1]
    hidden = bup_ref.shape[2]

    @pl.when(step == 0)
    def _():
        split = up_first.shape[2]
        w_up[:, :, :split] = up_first[...]
        w_up[:, :, split:] = up_rest[...]
        split = down_first.shape[1]
        w_down[:, :split] = down_first[...]
        w_down[:, split:] = down_rest[...]
        dw_acc[...] = jnp.zeros_like(dw_acc)
        dup_ref[...] = jnp.zeros_like(dup_ref)
        dvec_ref[...] = jnp.zeros_like(dvec_ref)

    mixed = jnp.where(2 * step < steps, o0_ref[...], o1_ref[...])
    grad_b = g_ref[0, 0]
    grad = grad_b.astype(F32)
    attended = dot_nn(mixed[:, :hw], w_out[0]) + dot_nn(mixed[:, hw:], w_out[1])
    middle = x_ref[0, 0].astype(F32) + (attended + b_out)
    unit, inverse = unit_norm(middle)
    normed = (unit * gain + shift).astype(BF16)
    ffn_out = jnp.zeros_like(middle)
    grad_normed = jnp.zeros_like(middle)
    for part in range(2):
        pre = dot_nn(normed, w_up[part]) + bup_ref[part]
        gate = 0.5 + 0.5 * lax.erf(pre * math.sqrt(0.5))
        active = (pre * gate).astype(BF16)
        ffn_out += dot_nn(active, w_down[part])
        slope = gate + pre * jnp.exp(pre * pre * -0.5) * (1.0 / math.sqrt(2.0 * math.pi))
        grad_pre_f = dot_nt(grad_b, w_down[part]) * slope
        grad_pre = grad_pre_f.astype(BF16)
        dup_ref[part] += column_sum(grad_pre.astype(F32))
        grad_normed += dot_nt(grad_pre, w_up[part])
        dw_acc[part, hw : hw + hidden] += dot_tn(active, grad_b)
        dw_acc[part, hw + hidden :] += dot_tn(grad_pre, normed)
    out_ref[...] = (middle + (ffn_out + b_down)).astype(BF16)
    grad_middle = grad + norm_back(grad_normed, unit, inverse, gain)
    gm_ref[...] = grad_middle
    grad_att = grad_middle.astype(BF16)
    dvec_ref[0:1] += column_sum(grad_att.astype(F32))
    dvec_ref[1:2] += column_sum(grad)
    dvec_ref[2:3] += column_sum(grad_normed * unit)
    dvec_ref[3:4] += column_sum(grad_normed)
    for part in range(2):
        cols = slice(part * hw, (part + 1) * hw)
        gx_ref[:, cols] = dot_nt(grad_att, w_out[part]).astype(BF16)
        dw_acc[part, :hw] += dot_tn(mixed[:, cols], grad_att)

    @pl.when(step == steps - 1)
    def _():
        dw_ref[...] = dw_acc[...].astype(BF16)
        features = dvec_ref.shape[1]
        extra[...] = jnp.zeros_like(extra)
        for part in range(2):
            extra[part, 0:4] = dvec_ref[0:4]
            for r in range(hidden // features):
                extra[part, 4 + r : 5 + r] = spread_columns(dup_ref[part], r, up_part, ns, features)
        extra_ref[...] = extra[...].astype(BF16)


def spread_columns(row, r, size, ns, features):
    count = row.shape[1]
    width = features // ns
    column = lax.broadcasted_iota(jnp.int32, (1, features), 1)
    shard = column // width
    place = r * width + column % width
    source = (place // size) * (size * ns) + shard * size + place % size
    chosen = jnp.where(lax.broadcasted_iota(jnp.int32, (count, features), 0) == source, 1.0, 0.0).astype(BF16)
    return dot_nn(jnp.broadcast_to(row.astype(BF16), (16, count)), chosen)[0:1]


def feed_forward(tokens, mixed, cotangent, w_out, up_first, up_rest, down_first, down_rest, b_up, vectors, where, up_part, ns, nc):
    micros, _, length, features = tokens.shape
    block = 256
    half = length // 2
    each = half // block
    rows = micros * half
    hw, hidden = w_out.shape[1], b_up.shape[2]
    total = hw + 2 * hidden
    more = (2, 16 * nc, features)
    row_spec = pl.BlockSpec((block, features), lambda i, t: (i, 0))
    input_spec = pl.BlockSpec((1, 1, block, features), lambda i, t: (i // each, 0, t[0] * each + i % each, 0))
    return pl.pallas_call(
        functools.partial(ffn_kernel, ns=ns, up_part=up_part),
        grid_spec=pltpu.PrefetchScalarGridSpec(
            num_scalar_prefetch=1,
            grid=(rows // block,),
            in_specs=[
                input_spec,
                pl.BlockSpec((block, 2 * hw), lambda i, t: (jnp.minimum(i, each - 1), 0)),
                pl.BlockSpec((block, 2 * hw), lambda i, t: (jnp.maximum(i - each, 0), 0)),
                input_spec,
            ]
            + [once(w.shape) for w in (w_out, up_first, up_rest, down_first, down_rest)]
            + [once(b_up.shape), once(vectors.shape)],
            out_specs=[row_spec] * 3
            + [once((2, total, features)), full_spec(more)],
            scratch_shapes=[
                pltpu.VMEM((2, total, features), F32), pltpu.VMEM((2, features, hidden), BF16),
                pltpu.VMEM((2, hidden, features), BF16), pltpu.VMEM((2, 1, hidden), F32), pltpu.VMEM((8, features), F32),
                pltpu.VMEM(more, F32),
            ],
        ),
        out_shape=[
            jax.ShapeDtypeStruct((rows, features), BF16),
            jax.ShapeDtypeStruct((rows, features), F32),
            jax.ShapeDtypeStruct((rows, 2 * hw), BF16),
            jax.ShapeDtypeStruct((2, total, features), BF16),
            jax.ShapeDtypeStruct(more, BF16),
        ],
        compiler_params=params(),
        cost_estimate=pl.CostEstimate(
            flops=12 * rows * total * features, bytes_accessed=20 * total * features, transcendentals=4 * rows * hidden
        ),
        name="feed_forward",
    )(where, tokens, *mixed, cotangent, w_out, up_first, up_rest, down_first, down_rest, b_up, vectors)


def last_kernel(
    dw_ref, db_ref, sums_ref, dn0_ref, dn1_ref, other0_ref, other1_ref, x_ref, gm_ref, vec_ref,
    grad_ref, blocks_ref,
    extra, extra_ref, dn_received, w_received, w_total, w_blocks, z_parts, z_received,
    dn_out, dn_in, wtp_out, wtp_in, wctx_out, wctx_in, z_out, z_in, back_out, back_in, row_out, row_in, *, ns, nc, head_part,
):
    t = lax.axis_index("tp")
    half = grad_ref.shape[2]
    rows = RowSum(
        dw_ref.at[1], dw_ref.at[0], extra_ref, w_received, w_total, w_blocks, (wtp_out, wtp_in),
        Axis("ctx", nc, (wctx_out, wctx_in)),
    )
    weights = ShardSum(
        z_parts, z_received, blocks_ref, Axis("shard", ns, (z_out, z_in)), Axis("ctx", nc, (back_out, back_in))
    )

    def row(micro):
        return cross(grad_ref.at[micro, t], grad_ref.at[micro, t], (row_out, row_in), micro)

    others = [cross(ref, dn_received.at[m], (dn_out, dn_in), m) for m, ref in enumerate((other0_ref, other1_ref))]

    def finish_rows(micro, dn_ref):
        size = 64
        others[micro].wait()

        def one(i, carry):
            at = pl.multiple_of(i * size, size)
            unit, inverse = unit_norm(x_ref[micro, 0, pl.ds(t * half + at, size), :].astype(F32))
            value = gm_ref[micro, pl.ds(at, size), :] + norm_back(
                dn_ref[pl.ds(at, size), :] + dn_received[micro, pl.ds(at, size), :].astype(F32),
                unit, inverse, vec_ref[2:3],
            )
            grad_ref[micro, t, pl.ds(at, size), :] = value.astype(BF16)
            return carry

        lax.fori_loop(0, half // size, one, 0)
        row(micro).start()

    peers = [("tp", 2), ("ctx", nc), ("shard", ns)]
    greet_first(peers)
    features = sums_ref.shape[1]
    each = db_ref.shape[0] // 2
    extra[...] = jnp.zeros_like(extra)
    for part in range(2):
        extra[part, 0:2] = sums_ref[0:2]
        biases = [db_ref[part * each + i, kind : kind + 1] for kind in range(2) for i in range(each)]
        extra[part, 2:3] = spread_columns(jnp.concatenate(biases, axis=1), 0, head_part, ns, features)
    extra_ref[...] = extra[...].astype(BF16)
    greet_wait(peers)
    rows.start()
    for copy in others:
        copy.start()
    rows.spread()
    finish_rows(0, dn0_ref)
    rows.finish(z_parts)
    weights.start()
    finish_rows(1, dn1_ref)
    weights.spread()
    weights.finish()
    for micro in range(2):
        row(micro).wait()


def last_sums(dw, db, sums, dn, x, grad_middle, vectors, head_part, ns, nc):
    main, features = dw.shape[1:]
    more = (2, 16 * nc, features)
    rows = main + more[1]
    micros, half, _ = grad_middle.shape
    size, part = rows // nc, features // ns
    return pl.pallas_call(
        functools.partial(last_kernel, ns=ns, nc=nc, head_part=head_part),
        in_specs=[pl.BlockSpec(memory_space=pltpu.VMEM)] * 10,
        out_specs=[pl.BlockSpec(memory_space=pltpu.VMEM)] * 2,
        out_shape=[
            jax.ShapeDtypeStruct((micros, 2, half, features), BF16),
            jax.ShapeDtypeStruct((nc, size, part), BF16),
        ],
        scratch_shapes=[
            pltpu.VMEM(more, F32), pltpu.VMEM(more, BF16), pltpu.VMEM((micros, half, features), BF16),
            pltpu.VMEM((rows, features), BF16), pltpu.VMEM((rows, features), BF16), pltpu.VMEM((nc, size, features), BF16),
            pltpu.VMEM((ns, size, part), BF16), pltpu.VMEM((ns, size, part), BF16),
            *axis_sems(micros, 2, nc, ns, nc, micros),
        ],
        compiler_params=params(collective_id=5, has_side_effects=True),
        name="last_sums",
    )(dw, db, sums, *dn, x, grad_middle, vectors)


def results_kernel(out_ref, grad_ref, ffn_ref, attn_ref, *refs, heads, head_part, up_part):
    (out, grad_tokens, g_query, g_key, g_value, g_out, g_up, g_down, g_bq, g_bv, g_bup, *vectors) = refs
    out[...] = out_ref[...]
    grad_tokens[...] = grad_ref[...]
    width, lanes = g_out.shape
    hidden = g_down.shape[0]
    pair = 2 * width // heads

    def values(ref, at, size):
        return ref[at : at + size, :].astype(F32)

    @pl.when(pl.program_id(0) == 0)
    def _():
        g_out[...] = values(ffn_ref, 0, width)
        g_down[...] = values(ffn_ref, width, hidden)
        g_up[...] = values(ffn_ref, width + hidden, hidden).T
        for i in range(heads // 2):
            for kind, ref in enumerate((g_query, g_key, g_value)):
                ref[:, i * pair : (i + 1) * pair] = values(attn_ref, (3 * i + kind) * pair, pair).T
        tail = values(ffn_ref, width + 2 * hidden, 16)
        tail_attn = values(attn_ref, 3 * width, 16)
        rows = (tail[0], tail[1], tail_attn[0], tail_attn[1], tail[2], tail[3])
        for ref, row in zip(vectors, rows):
            ref[...] = row
        for h in range(heads):
            at = h * up_part
            g_bup[h : h + 1] = tail[4 + at // lanes : 5 + at // lanes, at % lanes : at % lanes + up_part]
            for start, ref in ((0, g_bq), (heads * head_part, g_bv)):
                at = start + h * head_part
                ref[h : h + 1] = tail_attn[2 + at // lanes : 3 + at // lanes, at % lanes : at % lanes + head_part]


def write_results(output, grad_tokens, done_ffn, done_attn, shapes, heads, head_part, up_part):
    micros, length, features = output.shape
    steps = 4
    rows = pl.BlockSpec((micros, length // steps, features), lambda i: (0, i, 0))
    return pl.pallas_call(
        functools.partial(results_kernel, heads=heads, head_part=head_part, up_part=up_part),
        grid=(steps,),
        in_specs=[rows, rows, once(done_ffn.shape), once(done_attn.shape)],
        out_specs=[rows, rows] + [full_spec(shape) for shape in shapes],
        out_shape=[jax.ShapeDtypeStruct(output.shape, BF16)] * 2 + [jax.ShapeDtypeStruct(shape, F32) for shape in shapes],
        compiler_params=params(),
        name="results",
    )(output, grad_tokens, done_ffn, done_attn)


def pad_rows(rows, multiple):
    extra = -rows.shape[0] % multiple
    return jnp.concatenate([rows, jnp.zeros((extra,) + rows.shape[1:], rows.dtype)]) if extra else rows


def body(
    tokens, cotangent, w_query, w_key, w_value, w_out, w_up, w_down,
    b_query, b_value, b_up, b_out, b_down, gain_attn, shift_attn, gain_ffn, shift_ffn,
):
    ns, nc = lax.axis_size("shard"), lax.axis_size("ctx")
    t = lax.axis_index("tp")
    micros, _, length, features = tokens.shape
    half = length // 2
    heads, head_part = b_query.shape
    head_width = head_part * ns
    up_part = b_up.shape[1]
    feature_part = b_out.shape[0]

    tables = [b_query, b_value, b_up] + [v[None] for v in (b_out, b_down, gain_attn, shift_attn, gain_ffn, shift_ffn)]
    keys = 2 * nc * half
    aligned = feature_part % 128 == 0
    column_place = place_columns if aligned else place_slot

    def column_shape(w, rows):
        return (2, rows, features) if aligned else (2, ns, rows, w.shape[1])

    def whole_columns(w):
        if not aligned:
            w = w.transpose(0, 2, 1, 3).reshape(2, w.shape[2], features)
        return w

    w_all, wo, small_all, x_first = gather_first(
        (w_query, w_key, w_value, w_out), tables, tokens, column_place, column_shape(w_out, w_out.shape[0]), ns, nc
    )

    def by_head(row, part):
        table = small_all[:, :, row : row + heads, :part].transpose(0, 2, 1, 3)
        return table.reshape(2, heads * part * ns)

    biases = jnp.stack([by_head(0, head_part).reshape(-1), by_head(heads, head_part).reshape(-1)])
    bup = by_head(2 * heads, up_part)[:, None]
    vectors = small_all[0, :, 3 * heads : 3 * heads + 6, :feature_part].transpose(1, 0, 2)
    vectors = vectors.reshape(6, features)
    ahead, up_ahead = w_down.shape[0] // 4, w_up.shape[1] // 4
    plans = [
        (("ctx", nc, place_distance, True, 0), ("shard", ns, place_rows, False, up_ahead)),
        (("shard", ns, column_place, False, ahead),),
    ]
    sources = [(tokens, w_up), (w_down,)]
    specs = [
        [once((1, 1, length, features), (1, 0, 0, 0)), once(w_up.shape)],
        [once(w_down.shape)],
    ]
    shapes = [
        ((nc, 2, half, features), (2, features, w_up.shape[1] - up_ahead)),
        (column_shape(w_down, w_down.shape[0] - ahead),),
    ]
    guests = [
        (w_up, up_ahead, (2, features, up_ahead), place_rows),
        (w_down, ahead, column_shape(w_down, ahead), column_place),
    ]
    x_alls = [x_first.reshape(keys, features), None]
    saved = []
    arrived = []
    for micro in range(micros):
        guest, guest_rows, guest_shape, guest_place = guests[micro]
        normed, k, v, q, early = front(
            x_alls[micro], w_all, vectors, biases, head_width, half, guest, guest_rows,
            guest_shape, ns, guest_place, 6 + micro,
        )
        mixed, qx, *more = attend_forward(
            q, k, v, head_width, plans[micro], sources[micro], specs[micro], shapes[micro], micro + 1
        )
        if micro == 0:
            x_alls[1] = more.pop(0).reshape(keys, features)
        arrived += [early] + more
        saved.append((normed, k, v, qx, mixed))
    up_first, up_rest, down_first, down_rest = arrived
    wo, down_first, down_rest = whole_columns(wo), whole_columns(down_first), whole_columns(down_rest)

    out, grad_middle, grad_mixed, dw, extra = feed_forward(
        tokens, [entry[4] for entry in saved], cotangent, wo, up_first, up_rest, down_first, down_rest, bup, vectors,
        jnp.full((1,), t, jnp.int32), up_part, ns, nc,
    )

    width = heads * head_width
    *starts, dn_first, other_first, dw_parts, output = attend_back_rows(
        saved[0], grad_mixed, x_alls[0], w_all, head_width, dw, extra, out.reshape(micros, half, features), ns, nc
    )
    dw_now, db_now, sums, dn_second, other_second, dw_done = attend_back_shards(
        saved[1], grad_mixed, x_alls[1], w_all, head_width, starts, dw_parts, ns, nc
    )

    grad_tokens, attn_done = last_sums(
        dw_now.reshape(2, 3 * width, features), db_now, sums,
        (dn_first, dn_second, other_first, other_second), tokens, grad_middle.reshape(micros, half, features), vectors, head_part, ns, nc,
    )

    if aligned:
        weights = (w_query, w_key, w_value, w_out, w_up, w_down, b_query, b_value, b_up)
        shapes = [v.shape for v in weights] + [(feature_part,)] * 6
        output, grad_tokens, *grads = write_results(
            output.reshape(micros, length, features), grad_tokens.reshape(micros, length, features),
            dw_done.reshape(-1, feature_part), attn_done.reshape(-1, feature_part), shapes, heads, head_part, up_part,
        )
        g_query, g_key, g_value, g_out, g_up, g_down, g_bq, g_bv, g_bup, *others = grads
        return (output[:, None], grad_tokens[:, None], g_query, g_key, g_value, g_out, g_up, g_down, g_bq, g_bv, g_bup, *others)
    output = output.reshape(micros, 1, length, features)
    grad_tokens = grad_tokens.reshape(micros, 1, length, features)
    done_ffn = dw_done.reshape(-1, feature_part).astype(F32)
    done_attn = attn_done.reshape(-1, feature_part).astype(F32)
    hidden = heads * up_part * ns
    g_out, g_down, g_up = done_ffn[:width], done_ffn[width : width + hidden], done_ffn[width + hidden : width + 2 * hidden]
    tail = done_ffn[width + 2 * hidden :]
    by_kind = done_attn[: 3 * width].reshape(-1, 3, 2 * head_width, feature_part)
    g_query, g_key, g_value = (by_kind[:, i].reshape(width, feature_part).T for i in range(3))
    tail_attn = done_attn[3 * width :]
    g_bup = tail[4:].reshape(-1)[: heads * up_part].reshape(heads, up_part)
    g_heads = tail_attn[2:].reshape(-1)
    g_bq = g_heads[: heads * head_part].reshape(heads, head_part)
    g_bv = g_heads[heads * head_part : 2 * heads * head_part].reshape(heads, head_part)
    return (
        output, grad_tokens, g_query, g_key, g_value, g_out, g_up.T, g_down, g_bq, g_bv, g_bup,
        tail[0], tail[1], tail_attn[0], tail_attn[1], tail[2], tail[3],
    )


def solution(mesh):
    wide, tall = P("shard", "tp"), P("tp", "shard")
    rows, vector = P(None, "shard", "ctx", None), P("shard")
    weights = (wide, wide, wide, tall, wide, tall)
    return jax.shard_map(
        body,
        mesh=mesh,
        in_specs=(rows, rows) + weights + (tall,) * 3 + (vector,) * 6,
        out_specs=(rows, rows) + weights + (tall,) * 3 + (vector,) * 6,
        check_vma=False,
    )
```

```python
import functools
import math

import jax
import jax.numpy as jnp
from jax import lax
from jax.experimental import pallas as pl
from jax.experimental.pallas import tpu as pltpu
from jax.sharding import PartitionSpec as P

F32 = jnp.float32
BF16 = jnp.bfloat16
MESH = pl.DeviceIdType.MESH
norm_eps = 1e-05
LOG2E = math.log2(math.e)
VMEM_LIMIT = 60 * 2**20


def dot_nn(left, right):
    return lax.dot_general(left, right, (((1,), (0,)), ((), ())), preferred_element_type=F32)


def dot_nt(left, right):
    return lax.dot_general(left, right, (((1,), (1,)), ((), ())), preferred_element_type=F32)


def dot_tn(left, right):
    return lax.dot_general(left, right, (((0,), (0,)), ((), ())), preferred_element_type=F32)


def unit_norm(values):
    average = jnp.mean(values, axis=-1, keepdims=True)
    centred = values - average
    variance = jnp.mean(centred * centred, axis=-1, keepdims=True)
    inverse = lax.rsqrt(variance + norm_eps)
    return centred * inverse, inverse


def norm_back(grad_normed, unit_vals, inverse, gain):
    scaled = grad_normed * gain
    return inverse * (
        scaled
        - jnp.mean(scaled, axis=-1, keepdims=True)
        - unit_vals * jnp.mean(scaled * unit_vals, axis=-1, keepdims=True)
    )


def column_sum(values):
    return jnp.sum(values, axis=0, keepdims=True)


def full_spec(shape):
    return pl.BlockSpec(shape, lambda *_: (0,) * len(shape))


def params(limit=VMEM_LIMIT, **others):
    return pltpu.CompilerParams(vmem_limit_bytes=limit, **others)


def once(shape, index=None):
    place = index or (0,) * len(shape)
    return pl.BlockSpec(shape, lambda *_: place, pipeline_mode=pl.Buffered(1))


def send(source, target, send_sem, recv_sem, where):
    return pltpu.make_async_remote_copy(
        src_ref=source, dst_ref=target, send_sem=send_sem, recv_sem=recv_sem, device_id=where, device_id_type=MESH
    )


def greet_first(counts):
    barrier = pltpu.get_barrier_semaphore()
    for name, count in counts:
        me = lax.axis_index(name)
        for d in range(1, count):
            pl.semaphore_signal(barrier, inc=1, device_id={name: me ^ d}, device_id_type=MESH)


def greet_wait(counts):
    pl.semaphore_wait(pltpu.get_barrier_semaphore(), sum(count - 1 for _, count in counts))


def greet(counts):
    greet_first(counts)
    greet_wait(counts)


class Gather:

    def __init__(self, name, count, source, theirs, target, place, sems):
        self.name, self.count, self.source, self.theirs = name, count, source, theirs
        self.target, self.place = target, place
        self.out_sem, self.in_sem, self.cross_out, self.cross_in, self.local = sems
        self.me = lax.axis_index(name)

    def first(self, d):
        where = {self.name: self.me ^ d}
        return send(self.source, self.place(self.target, 0, self.me, d), self.out_sem.at[d], self.in_sem.at[d], where)

    def cross(self, d):
        where = {"tp": 1 - lax.axis_index("tp")}
        owner = self.me ^ d
        source = self.place(self.target, 0, owner, d) if d else self.source
        return send(source, self.place(self.target, 1, owner, d), self.cross_out.at[d], self.cross_in.at[d], where)

    def locals(self):
        copies = [pltpu.make_async_copy(self.source, self.place(self.target, 0, self.me, 0), self.local.at[0])]
        if self.theirs is not None:
            copies.append(pltpu.make_async_copy(self.theirs, self.place(self.target, 1, self.me, 0), self.local.at[1]))
        return copies

    def crossed(self):
        return range(0 if self.theirs is None else 1, self.count)

    def start(self, late=0):
        for d in range(1, self.count - late):
            self.first(d).start()
        for copy in self.locals():
            copy.start()
        if self.theirs is None:
            self.cross(0).start()

    def forward(self, distances=None):
        for d in distances or range(1, self.count):
            self.first(d).wait_recv()
            self.cross(d).start()

    def relay(self, h):
        size = self.target.shape[2] // 2
        rows = pl.ds(h * size, size)
        i = (3, 0)[h]
        where = {self.name: self.me ^ (2 - h)}
        return send(
            self.target.at[1 + h, 0, rows, :], self.target.at[3, 0, rows, :], self.out_sem.at[i], self.in_sem.at[i], where
        )

    def forward_relayed(self):
        for h in range(2):
            self.relay(h).wait_recv()
        self.cross(3).start()

    def finish(self, relayed=False):
        for d in range(1, 3 if relayed else self.count):
            self.first(d).wait_send()
        for h in range(2 if relayed else 0):
            self.relay(h).wait_send()
        for d in self.crossed():
            self.cross(d).wait()
        for copy in self.locals():
            copy.wait()


def place_rows(ref, part, owner, d):
    size = ref.shape[1] // lax.axis_size("shard")
    return ref.at[part, pl.ds(pl.multiple_of(owner * size, size), size), :]


def place_columns(ref, part, owner, d):
    size = ref.shape[2] // lax.axis_size("shard")
    return ref.at[part, :, pl.ds(pl.multiple_of(owner * size, size), size)]


def place_slot(ref, part, owner, d):
    return ref.at[part, owner]


def place_distance(ref, part, owner, d):
    return ref.at[d, part]


def gather_sems(count):
    dma = pltpu.SemaphoreType.DMA
    return [dma((count,)), dma((count,)), dma((count,)), dma((count,)), dma((2,))]


def gather_kernel(ns, nc, wq_ref, wk_ref, wv_ref, x_block, *refs):
    tables, (w_out, small_out, x_out, small_ref), sems = refs[:-17], refs[-17:-13], refs[-13:]
    w_send, w_recv, s_send, s_recv, x_send, x_recv, wt_send, wt_recv, st_send, st_recv, xt_send, xt_recv, local = sems
    w_refs = (wq_ref, wk_ref, wv_ref)
    kinds = range(3)
    x_ref = x_block.at[0, 0]
    s = lax.axis_index("shard")
    c = lax.axis_index("ctx")
    t = lax.axis_index("tp")
    other = 1 - t
    depth = wq_ref.shape[0]
    half = x_ref.shape[0] // 2

    peers = [("tp", 2), ("ctx", nc), ("shard", ns)]
    greet_first(peers)
    small_ref[...] = jnp.zeros_like(small_ref)
    row = 0
    for table in tables:
        count, lanes = table.shape
        small_ref[row : row + count, :lanes] = table[...].astype(F32)
        row += count
    greet_wait(peers)

    def w_rows(part, kind, owner):
        return w_out.at[part, kind, pl.ds(pl.multiple_of(owner * depth, depth), depth), :]

    def x_rows(which):
        return x_ref.at[pl.ds(pl.multiple_of(which * half, half), half), :]

    def begin(source, target, send_sem, recv_sem, where):
        copy = send(source, target, send_sem, recv_sem, where)
        copy.start()
        return copy

    x_copies, w_copies, s_copies = {}, {}, {}
    size = half // 2

    def x_part(d, h):
        return x_out.at[d, 0, pl.ds(h * size, size), :]

    def x_begin(source, d, h, to):
        copy = begin(source, x_part(d, h), x_send.at[d, h], x_recv.at[d, h], {"ctx": c ^ to})
        x_copies[d, h] = copy

    relayed = nc == 4
    for h in range(2):
        for d in range(1, 3 if relayed else nc):
            part = h if d % 2 else 1 - h
            source = x_ref.at[pl.ds(pl.multiple_of(t * half + part * size, size), size), :]
            x_begin(source, d, part, d)
    for d in range(1, ns):
        for k in kinds:
            w_copies[d, k] = begin(
                w_refs[k], w_rows(0, k, s), w_send.at[k, d], w_recv.at[k, d], {"shard": s ^ d}
            )
        s_copies[d] = begin(small_ref, small_out.at[0, s], s_send.at[d], s_recv.at[d], {"shard": s ^ d})
    last = [begin(w_refs[k], w_rows(1, k, s), wt_send.at[k, 0], wt_recv.at[k, 0], {"tp": other}) for k in kinds]
    last.append(begin(small_ref, small_out.at[1, s], st_send.at[0], st_recv.at[0], {"tp": other}))
    locals_ = [pltpu.make_async_copy(w_refs[k], w_rows(0, k, s), local.at[k]) for k in kinds]
    locals_ += [
        pltpu.make_async_copy(small_ref, small_out.at[0, s], local.at[3]),
        pltpu.make_async_copy(x_rows(t), x_out.at[0, 0], local.at[4]),
        pltpu.make_async_copy(x_rows(other), x_out.at[0, 1], local.at[5]),
    ]
    for copy in locals_:
        copy.start()
    if relayed:
        x_copies[1, 0].wait_recv()
        x_begin(x_part(1, 0), 3, 0, 2)
        x_copies[2, 1].wait_recv()
        x_begin(x_part(2, 1), 3, 1, 1)
    waited = {(1, 0), (2, 1)} if relayed else set()
    for d in range(1, max(ns, nc)):
        if d < ns:
            for k in kinds:
                w_copies[d, k].wait_recv()
                last.append(
                    begin(
                        w_rows(0, k, s ^ d), w_rows(1, k, s ^ d), wt_send.at[k, d], wt_recv.at[k, d], {"tp": other}
                    )
                )
            s_copies[d].wait_recv()
            last.append(
                begin(small_out.at[0, s ^ d], small_out.at[1, s ^ d], st_send.at[d], st_recv.at[d], {"tp": other})
            )
        if d < nc:
            for h in range(2):
                if (d, h) not in waited:
                    x_copies[d, h].wait_recv()
            last.append(begin(x_out.at[d, 0], x_out.at[d, 1], xt_send.at[d], xt_recv.at[d], {"tp": other}))
    for copies in (x_copies, w_copies, s_copies):
        for copy in copies.values():
            copy.wait_send()
    for copy in last:
        copy.wait()
    for copy in locals_:
        copy.wait()


def gather_first(weights, tables, tokens, ns, nc):
    depth, width = weights[0].shape
    length, features = tokens.shape[2:]
    rows = -(-sum(table.shape[0] for table in tables) // 8) * 8
    lanes = -(-max(table.shape[1] for table in tables) // 128) * 128
    dma = pltpu.SemaphoreType.DMA
    vmem = pl.BlockSpec(memory_space=pltpu.VMEM)
    return pl.pallas_call(
        functools.partial(gather_kernel, ns, nc),
        grid=(1,),
        in_specs=[vmem] * 3 + [once((1, 1, length, features))] + [vmem] * len(tables),
        out_specs=[pl.BlockSpec(memory_space=pl.ANY)] * 3,
        out_shape=[
            jax.ShapeDtypeStruct((2, 3, ns * depth, width), BF16),
            jax.ShapeDtypeStruct((2, ns, rows, lanes), F32),
            jax.ShapeDtypeStruct((nc, 2, length // 2, features), BF16),
        ],
        scratch_shapes=[pltpu.VMEM((rows, lanes), F32)]
        + [dma((3, ns)), dma((3, ns)), dma((ns,)), dma((ns,)), dma((nc, 2)), dma((nc, 2))]
        + [dma((3, ns)), dma((3, ns)), dma((ns,)), dma((ns,)), dma((nc,)), dma((nc,)), dma((6,))],
        compiler_params=params(collective_id=0, has_side_effects=True),
        name="gather_first",
    )(*weights, tokens, *tables)


def project_rows(x, w_ref, vec_ref, bias_ref, n_ref, k_ref, v_ref):
    gain, shift = vec_ref[2:3], vec_ref[3:4]
    width = w_ref.shape[3]
    size = n_ref.shape[0] // 4
    for i in range(4):
        rows = slice(i * size, (i + 1) * size)
        unit, _ = unit_norm(x(i, size).astype(F32))
        normed = (unit * gain + shift).astype(BF16)
        n_ref[rows] = normed
        for part in range(2):
            cols = slice(part * width, (part + 1) * width)
            k_ref[rows, cols] = dot_nn(normed, w_ref[part, 1]).astype(BF16)
            v_ref[rows, cols] = (dot_nn(normed, w_ref[part, 2]) + bias_ref[1:2, cols]).astype(BF16)


def project_query(w_ref, bias_ref, n_ref, q_ref, q_scale):
    width = w_ref.shape[3]
    normed = n_ref[: q_ref.shape[0]]
    for part in range(2):
        cols = slice(part * width, (part + 1) * width)
        q_ref[:, cols] = ((dot_nn(normed, w_ref[part, 0]) + bias_ref[0:1, cols]) * q_scale).astype(BF16)


def front_kernel(
    x_ref, w_ref, vec_ref, bias_ref, guest_ref, n_ref, k_ref, v_ref, q_ref, guest_all, *sems, q_scale, ns, place, size
):
    step = pl.program_id(0)
    part = guest_ref.at[:, pl.ds(0, size)] if place is place_rows else guest_ref.at[pl.ds(0, size), :]
    gather = Gather("shard", ns, part, None, guest_all, place, sems)

    peers = [("tp", 2), ("shard", ns)]

    @pl.when(step == 0)
    def _():
        greet_first(peers)

    @pl.when(step == 1)
    def _():
        greet_wait(peers)
        gather.start()

    project_rows(lambda i, size: x_ref[i * size : (i + 1) * size], w_ref, vec_ref, bias_ref, n_ref, k_ref, v_ref)

    @pl.when(step == 0)
    def _():
        project_query(w_ref, bias_ref, n_ref, q_ref, q_scale)

    @pl.when(step == pl.num_programs(0) - 1)
    def _():
        gather.forward()
        gather.finish()


def front(x_all, weights, vectors, biases, head_width, half, guest, guest_rows, guest_shape, ns, place, number):
    keys, features = x_all.shape
    block = 2 * half
    width = 2 * weights.shape[3]
    scale = LOG2E / math.sqrt(head_width)
    return pl.pallas_call(
        functools.partial(front_kernel, q_scale=scale, ns=ns, place=place, size=guest_rows),
        grid=(keys // block,),
        in_specs=[
            pl.BlockSpec((block, features), lambda i: (i, 0)),
            once(weights.shape),
            once(vectors.shape),
            once(biases.shape),
            once(guest.shape),
        ],
        out_specs=[
            pl.BlockSpec((block, features), lambda i: (i, 0)),
            pl.BlockSpec((block, width), lambda i: (i, 0)),
            pl.BlockSpec((block, width), lambda i: (i, 0)),
            full_spec((half, width)),
            pl.BlockSpec(memory_space=pl.ANY),
        ],
        out_shape=[
            jax.ShapeDtypeStruct((keys, features), BF16),
            jax.ShapeDtypeStruct((keys, width), BF16),
            jax.ShapeDtypeStruct((keys, width), BF16),
            jax.ShapeDtypeStruct((half, width), BF16),
            jax.ShapeDtypeStruct(guest_shape, BF16),
        ],
        scratch_shapes=gather_sems(ns),
        compiler_params=params(collective_id=number, has_side_effects=True),
        cost_estimate=pl.CostEstimate(
            flops=4 * keys * features * width, bytes_accessed=8 * keys * features, transcendentals=keys
        ),
        name="front",
    )(x_all, weights, vectors, biases, guest)


def with_parts(lane, base, values, first, width):
    high = values.astype(BF16).astype(F32)
    rest = values - high
    middle = rest.astype(BF16).astype(F32)
    low = rest - middle
    extra = jnp.where(
        lane == first, high, jnp.where(lane == first + 1, middle, jnp.where(lane == first + 2, low, 0.0))
    )
    inside = (lane < width) if first else (lane >= width)
    return jnp.where(inside, base, extra)


def attend_kernel(*refs, kc, width, plans):
    count = len(plans)
    q_ref, k_ref, v_ref = refs[:3]
    sources = refs[3 : 3 + count]
    o_ref, qx_ref = refs[3 + count : 5 + count]
    targets = refs[5 + count : 5 + 2 * count]
    scores = refs[5 + 2 * count]
    sems = refs[6 + 2 * count :]
    step = pl.program_id(0)
    last = pl.num_programs(0) - 1
    t = lax.axis_index("tp")

    def gathers(wanted):
        found = []
        for i, (name, number, place, split, start) in enumerate(plans):
            if name != wanted:
                continue
            source, theirs = sources[i], None
            if split:
                source = source.at[0, 0]
                half = source.shape[0] // 2
                theirs = source.at[pl.ds(pl.multiple_of((1 - t) * half, half), half), :]
                source = source.at[pl.ds(pl.multiple_of(t * half, half), half), :]
            elif start and place is place_rows:
                source = source.at[:, pl.ds(start, source.shape[1] - start)]
            elif start:
                source = source.at[pl.ds(start, source.shape[0] - start), :]
            found.append(Gather(name, number, source, theirs, targets[i], place, sems[5 * i : 5 * i + 5]))
        return found

    counts = {name: number for name, number, *_ in plans}

    peers = [("tp", 2)] + list(counts.items())
    far = counts.get("ctx", 1) - 1
    relayed = far == 3

    @pl.when(step == 0)
    def _():
        greet_first(peers)


    rows, lanes = q_ref.shape
    keys = k_ref.shape[0]
    lane = lax.broadcasted_iota(jnp.int32, (rows, lanes), 1)
    lane_v = lax.broadcasted_iota(jnp.int32, (kc, lanes), 1)
    q = q_ref[...].astype(F32)
    tops = []
    for h in range(2):
        inside = (lane < width) if h == 0 else (lane >= width)
        q_head = jnp.where(inside, q, 0.0).astype(BF16)
        top = None
        for i in range(keys // kc):
            part = dot_nt(k_ref[i * kc : (i + 1) * kc], q_head)
            scores[h, i * kc : (i + 1) * kc] = part
            here = jnp.max(part.reshape(kc // 8, 8, rows), axis=0)
            top = here if top is None else jnp.maximum(top, here)
        tops.append(jnp.max(top, axis=0, keepdims=True))

    @pl.when(step == 0)
    def _():
        greet_wait(peers)
        for gather in gathers("shard"):
            gather.start()
        for gather in gathers("ctx"):
            gather.start(1)

    @pl.when(step == 2)
    def _():
        for gather in gathers("ctx"):
            if not relayed:
                gather.first(far).start()
            gather.forward(range(1, far))
            for h in range(2 if relayed else 0):
                gather.relay(h).start()

    def forward_last():
        for gather in gathers("shard"):
            gather.forward()
        for gather in gathers("ctx"):
            if relayed:
                gather.forward_relayed()
            else:
                gather.forward([far])

    if far:
        pl.when(step == last)(forward_last)

    outs = []
    for h in range(2):
        inside_v = (lane_v < width) if h == 0 else (lane_v >= width)
        total = jnp.zeros((lanes, rows), F32)
        for i in range(keys // kc):
            v_one = jnp.where(inside_v, v_ref[i * kc : (i + 1) * kc], jnp.ones((), BF16))
            exponent = jnp.exp2(scores[h, i * kc : (i + 1) * kc] - tops[h]).astype(BF16)
            total += dot_tn(v_one, exponent)
        first = width if h == 0 else 0
        log_total = tops[h] + jnp.log2(total[first : first + 1, :])
        total = total.T
        outs.append(total / pltpu.roll(total, width, 1))
        log_column = jnp.broadcast_to(log_total, (8, rows)).T[:, :1]
        qx_ref[:, h * lanes : (h + 1) * lanes] = with_parts(lane, q, -log_column, first, width).astype(BF16)
    o_ref[...] = jnp.where(lane < width, outs[0], outs[1]).astype(BF16)

    @pl.when(step == last)
    def _():
        if not far:
            forward_last()
        for name in counts:
            for gather in gathers(name):
                gather.finish(relayed and name == "ctx")


def attend_forward(q, k, v, width, plans, sources, source_specs, shapes, number):
    rows, cols = q.shape
    keys = k.shape[0]
    lanes = 2 * width
    kc = 512
    anywhere = pl.BlockSpec(memory_space=pl.ANY)
    return pl.pallas_call(
        functools.partial(attend_kernel, kc=kc, width=width, plans=plans),
        grid=(cols // lanes,),
        in_specs=[
            pl.BlockSpec((rows, lanes), lambda j: (0, j)),
            pl.BlockSpec((keys, lanes), lambda j: (0, j)),
            pl.BlockSpec((keys, lanes), lambda j: (0, j)),
        ]
        + source_specs,
        out_specs=[
            pl.BlockSpec((rows, lanes), lambda j: (0, j)),
            pl.BlockSpec((rows, 2 * lanes), lambda j: (0, j)),
        ]
        + [anywhere] * len(plans),
        out_shape=[
            jax.ShapeDtypeStruct((rows, cols), BF16),
            jax.ShapeDtypeStruct((rows, 2 * cols), BF16),
        ]
        + [jax.ShapeDtypeStruct(shape, BF16) for shape in shapes],
        scratch_shapes=[pltpu.VMEM((2, keys, rows), F32)]
        + [sem for plan in plans for sem in gather_sems(plan[1])],
        compiler_params=params(collective_id=number, has_side_effects=True),
        cost_estimate=pl.CostEstimate(
            flops=12 * rows * keys * cols, bytes_accessed=4 * keys * cols, transcendentals=rows * keys * cols // width
        ),
        name="attend_forward",
    )(q, k, v, *sources)


def sum_rows(target, at, left, left_at, right, right_at, rows, chunk=64):
    def one(i, carry):
        here = pl.multiple_of(i * chunk, chunk)
        target[pl.ds(at + here, chunk), :] = left[pl.ds(left_at + here, chunk), :] + right[pl.ds(right_at + here, chunk), :]
        return carry

    lax.fori_loop(0, rows // chunk, one, 0)


class Axis:

    def __init__(self, name, count, sems):
        self.name, self.count, self.sems = name, count, sems
        self.me = lax.axis_index(name)

    def copy(self, d, source, target):
        return send(source(self.me ^ d, d), target(self.me, d), self.sems[0].at[d], self.sems[1].at[d], {self.name: self.me ^ d})

    def start(self, source, target):
        for d in range(1, self.count):
            self.copy(d, source, target).start()

    def wait(self, source, target):
        for d in range(1, self.count):
            self.copy(d, source, target).wait()


def axis_sems(*counts):
    return [pltpu.SemaphoreType.DMA((count,)) for count in counts for _ in range(2)]


def cross(source, target, sems, i):
    return send(source, target, sems[0].at[i], sems[1].at[i], {"tp": 1 - lax.axis_index("tp")})


class RowSum:

    def __init__(self, dw_send, dw_own, extra, received, total, blocks, tp_sems, ctx):
        self.dw_send, self.dw_own, self.extra = dw_send, dw_own, extra
        self.received, self.total, self.blocks = received, total, blocks
        self.tp_sems, self.ctx = tp_sems, ctx
        self.main, self.more = dw_own.shape[0], extra.shape[1]
        self.size = (self.main + self.more) // ctx.count

    def crossing(self):
        return [
            cross(self.dw_send, self.received.at[pl.ds(0, self.main), :], self.tp_sems, 0),
            cross(self.extra.at[1], self.received.at[pl.ds(self.main, self.more), :], self.tp_sems, 1),
        ]

    def start(self):
        for copy in self.crossing():
            copy.start()

    def source(self, peer, d):
        return self.total.at[pl.ds(pl.multiple_of(peer * self.size, 16), self.size), :]

    def target(self, me, d):
        return self.blocks.at[d]

    def spread(self):
        for copy in self.crossing():
            copy.wait()
        sum_rows(self.total, 0, self.dw_own, 0, self.received, 0, self.main)
        sum_rows(self.total, self.main, self.extra.at[0], 0, self.received, self.main, self.more)
        self.ctx.start(self.source, self.target)

    def finish(self, out):
        self.ctx.wait(self.source, self.target)
        count, size, width = out.shape
        value = self.total[pl.ds(pl.multiple_of(self.ctx.me * self.size, 16), self.size), :].astype(F32)
        for d in range(1, self.ctx.count):
            value += self.blocks[d].astype(F32)
        for j in range(count):
            out[j] = value[:, j * width : (j + 1) * width].astype(out.dtype)


class ShardSum:

    def __init__(self, parts, received, blocks, shard, ctx):
        self.parts, self.received, self.blocks, self.shard, self.ctx = parts, received, blocks, shard, ctx

    def source(self, peer, d):
        return self.parts.at[peer]

    def target(self, me, d):
        return self.received.at[d]

    def start(self):
        self.shard.start(self.source, self.target)

    def mine(self, peer, d):
        return self.blocks.at[self.ctx.me]

    def theirs(self, me, d):
        return self.blocks.at[me]

    def spread(self):
        self.shard.wait(self.source, self.target)
        value = self.parts[self.shard.me].astype(F32)
        for d in range(1, self.shard.count):
            value += self.received[d].astype(F32)
        self.blocks[self.ctx.me] = value.astype(BF16)
        self.ctx.start(self.mine, self.theirs)

    def finish(self):
        self.ctx.wait(self.mine, self.theirs)


class InputSum:

    def __init__(self, dn_send, dn_own, received, total, blocks, tp_sems, ctx):
        self.dn_send, self.dn_own, self.received = dn_send, dn_own, received
        self.total, self.blocks, self.tp_sems, self.ctx = total, blocks, tp_sems, ctx

    def crossing(self, d):
        return cross(self.dn_send(d), self.received.at[d], self.tp_sems, d)

    def source(self, peer, d):
        return self.total.at[d]

    def target(self, me, d):
        return self.blocks.at[d]

    def spread_one(self, d):
        self.crossing(d).wait()
        sum_rows(self.total.at[d], 0, self.dn_own(d), 0, self.received.at[d], 0, self.received.shape[1])
        self.ctx.copy(d, self.source, self.target).start()

    def finish(self):
        self.ctx.wait(self.source, self.target)

    def rows(self, own, at, size):
        value = own[pl.ds(at, size), :]
        for d in range(1, self.ctx.count):
            value += self.blocks[d, pl.ds(at, size), :].astype(F32)
        return value


def attend_back_step(refs, scratch, starts, width):
    qx_ref, k_ref, v_ref, go_ref, o_ref, n_ref, x_ref, w_ref = refs
    gx_all, dq_acc, dn_acc, dw_acc, db_ref, sums_ref = scratch
    i, j = pl.program_id(0), pl.program_id(1)
    last_block, last_pair = pl.num_programs(0) - 1, pl.num_programs(1) - 1
    rows, lanes = o_ref.shape
    keys = k_ref.shape[0]
    lane = lax.broadcasted_iota(jnp.int32, (rows, lanes), 1)
    lane_k = lax.broadcasted_iota(jnp.int32, (keys, lanes), 1)
    one = jnp.ones((), BF16)

    @pl.when(i == 0)
    def _():
        grad_out = go_ref[...].astype(F32)
        both = grad_out * o_ref[...].astype(F32)
        for h in range(2):
            inside = (lane < width) if h == 0 else (lane >= width)
            delta = jnp.sum(jnp.where(inside, both, 0.0), axis=1, keepdims=True)
            gx_all[j, h] = with_parts(lane, grad_out, -delta, width if h == 0 else 0, width).astype(BF16)
        dq_acc[j] = jnp.zeros(dq_acc.shape[1:], F32)
        dw_acc[j] = starts[0][j] if starts else jnp.zeros(dw_acc.shape[1:], F32)
        db_ref[j] = starts[1][j] if starts else jnp.zeros(db_ref.shape[1:], F32)

    @pl.when((i == 0) & (j == 0))
    def _():
        sums_ref[...] = starts[2][...] if starts else jnp.zeros_like(sums_ref)

    @pl.when(j == 0)
    def _():
        dn_acc[...] = jnp.zeros_like(dn_acc)

    grad_k, grad_v, grad_q = [], [], []
    for h in range(2):
        inside_k = (lane_k < width) if h == 0 else (lane_k >= width)
        kx = jnp.where(inside_k, k_ref[...], one)
        vx = jnp.where(inside_k, v_ref[...], one)
        qx = qx_ref[:, h * lanes : (h + 1) * lanes]
        gx = gx_all[j, h]
        prob = jnp.exp2(dot_nt(kx, qx))
        grad_v.append(dot_nn(prob.astype(BF16), gx))
        grad_score = (prob * dot_nt(vx, gx)).astype(BF16)
        grad_k.append(dot_nn(grad_score, qx))
        grad_q.append(dot_tn(kx, grad_score))
    dk = (jnp.where(lane_k < width, grad_k[0], grad_k[1]) * (1.0 / LOG2E)).astype(BF16)
    dv = jnp.where(lane_k < width, grad_v[0], grad_v[1]).astype(BF16)
    dq_acc[j] += jnp.concatenate([grad_q[0][:width], grad_q[1][width:]], axis=0)
    both = jnp.concatenate([dk, dv], axis=1)
    weights = jnp.concatenate([w_ref[0, 1], w_ref[0, 2]], axis=1)
    dn_acc[...] += dot_nt(both, weights)
    grad_w = dot_tn(both, n_ref[...])
    dw_acc[j, 1] += grad_w[:lanes]
    dw_acc[j, 2] += grad_w[lanes:]
    db_ref[j, 1:2] += column_sum(dv.astype(F32))

    @pl.when(i == last_block)
    def _():
        dq = (dq_acc[j].T * (1.0 / math.sqrt(width))).astype(BF16)
        dn_acc[:rows] += dot_nt(dq, w_ref[0, 0])
        dw_acc[j, 0] += dot_tn(dq, n_ref[:rows])
        db_ref[j, 0:1] += column_sum(dq.astype(F32))

    @pl.when(j == last_pair)
    def _():
        unit, _ = unit_norm(x_ref[...].astype(F32))
        sums_ref[0:1] += column_sum(dn_acc[...] * unit)
        sums_ref[1:2] += column_sum(dn_acc[...])


def attend_back_kernel(*refs, width, nc, ns, hosted, hosted_counts, started):
    i, j = pl.program_id(0), pl.program_id(1)
    last_pair = pl.num_programs(1) - 1
    n_in, n_out, n_scratch = hosted_counts
    at = 8
    base = refs[:at]
    starts = refs[at : at + 3] if started else ()
    at += 3 if started else 0
    extra_in, at = refs[at : at + n_in], at + n_in
    (dw_ref, db_ref, sums_ref, dn_done, dn_other), at = refs[at : at + 5], at + 5
    extra_out, at = refs[at : at + n_out], at + n_out
    gx_all, dq_acc, dn_acc, dw_acc, dn_sent, dn_received, dn_total, dn_blocks, tp_out, tp_in, ctx_out, ctx_in = refs[at : at + 12]
    extra_scratch = refs[at + 12 :]
    inputs = InputSum(
        lambda d: dn_sent.at[d, 1], lambda d: dn_sent.at[d, 0], dn_received, dn_total, dn_blocks,
        (tp_out, tp_in), Axis("ctx", nc, (ctx_out, ctx_in)),
    )
    guest = hosted(extra_in, extra_out, extra_scratch, nc, ns)

    @pl.when((i == 0) & (j == 0))
    def _():
        greet_first(guest.peers)

    @pl.when((i == 0) & (j == 1))
    def _():
        greet_wait(guest.peers)
        guest.begin()

    @pl.when((i == 1) & (j == 0))
    def _():
        guest.middle()

    for d in range(1, nc):

        @pl.when((i == nc - d) & (j == 0))
        def _(d=d):
            inputs.crossing(d).start()

        @pl.when((i == nc - d) & (j == 1))
        def _(d=d):
            inputs.spread_one(d)

    attend_back_step(
        base, (gx_all, dq_acc, dn_acc, dw_acc, db_ref, sums_ref), starts, width
    )

    half = dn_acc.shape[0] // 2

    @pl.when((j == last_pair) & (i < nc - 1))
    def _():
        for part in range(2):
            dn_sent[nc - 1 - i, part] = dn_acc[part * half : (part + 1) * half].astype(BF16)

    @pl.when((i == nc - 1) & (j == last_pair))
    def _():
        dw_ref[...] = dw_acc[...].astype(dw_ref.dtype)
        dn_other[...] = dn_acc[half:].astype(BF16)
        guest.end()
        inputs.finish()
        size = 64

        def one(r, carry):
            here = pl.multiple_of(r * size, size)
            dn_done[pl.ds(here, size), :] = inputs.rows(dn_acc, here, size)
            return carry

        lax.fori_loop(0, half // size, one, 0)


class HostRows:

    def __init__(self, ins, outs, scratch, nc, ns):
        dw_all, dw_own, extra, out_half = ins
        self.dw_out, whole = outs
        received, total, blocks, tp_out, tp_in, ctx_out, ctx_in, sems = scratch
        t = lax.axis_index("tp")
        self.rows = RowSum(
            dw_all.at[1], dw_own.at[0], extra, received, total, blocks, (tp_out, tp_in), Axis("ctx", nc, (ctx_out, ctx_in))
        )
        self.copies = lambda: [
            cross(out_half, whole.at[:, t], (sems, sems.at[pl.ds(1, 1)]), 0),
            pltpu.make_async_copy(out_half, whole.at[:, t], sems.at[2]),
        ]
        self.peers = [("tp", 2), ("ctx", nc)]

    def begin(self):
        self.rows.start()
        for copy in self.copies():
            copy.start()

    def middle(self):
        self.rows.spread()

    def end(self):
        self.rows.finish(self.dw_out)
        for copy in self.copies():
            copy.wait()


class HostShards:

    def __init__(self, ins, outs, scratch, nc, ns):
        (self.done,) = outs
        received, self.blocks, z_out, z_in, back_out, back_in = scratch
        self.sums = ShardSum(
            ins[0], received, self.blocks, Axis("shard", ns, (z_out, z_in)), Axis("ctx", nc, (back_out, back_in))
        )
        self.peers = [("tp", 2), ("ctx", nc), ("shard", ns)]

    def begin(self):
        self.sums.start()

    def middle(self):
        self.sums.spread()

    def end(self):
        self.sums.finish()
        self.done[...] = self.blocks[...]


def attend_back(
    hosted, entry, grad_mixed, x_all, weights, width, micro, starts, kind, ins, in_specs, outs, out_specs, scratch, number, ns, nc
):
    normed, k, v, qx, mixed = entry
    rows, cols = mixed.shape
    keys, features = normed.shape
    lanes = 2 * width
    pairs = cols // lanes
    size = keys // nc
    each = pairs // 2
    stack = (pairs, 3, lanes, features)
    block = pltpu.VMEM((nc, rows, features), BF16)

    def key_block(shape, column):
        return pl.BlockSpec(shape, lambda i, j: (nc - 1 - i, j if column else 0))

    return pl.pallas_call(
        functools.partial(
            attend_back_kernel, width=width, nc=nc, ns=ns, hosted=hosted,
            hosted_counts=(len(ins), len(outs), len(scratch)), started=bool(starts),
        ),
        grid=(nc, pairs),
        in_specs=[
            pl.BlockSpec((rows, 2 * lanes), lambda i, j: (0, j)),
            key_block((size, lanes), True),
            key_block((size, lanes), True),
            pl.BlockSpec((rows, lanes), lambda i, j: (micro, j)),
            pl.BlockSpec((rows, lanes), lambda i, j: (0, j)),
            key_block((size, features), False),
            key_block((size, features), False),
            pl.BlockSpec((1, 3, features, lanes), lambda i, j: (j // each, 0, 0, j % each)),
        ]
        + [once(value.shape) for value in starts]
        + in_specs,
        out_specs=[full_spec(stack), full_spec((pairs, 8, lanes)), full_spec((8, features))]
        + [full_spec((rows, features))] * 2
        + out_specs,
        out_shape=[
            jax.ShapeDtypeStruct(stack, kind),
            jax.ShapeDtypeStruct((pairs, 8, lanes), F32),
            jax.ShapeDtypeStruct((8, features), F32),
            jax.ShapeDtypeStruct((rows, features), F32),
            jax.ShapeDtypeStruct((rows, features), BF16),
        ]
        + outs,
        scratch_shapes=[
            pltpu.VMEM((pairs, 2, rows, lanes), BF16),
            pltpu.VMEM((pairs, lanes, rows), F32),
            pltpu.VMEM((size, features), F32),
            pltpu.VMEM(stack, F32),
            pltpu.VMEM((nc, 2, rows, features), BF16),
            block, block, block,
            *axis_sems(nc, nc),
        ]
        + scratch,
        compiler_params=params(collective_id=number, has_side_effects=True),
        cost_estimate=pl.CostEstimate(
            flops=30 * rows * keys * cols, bytes_accessed=8 * keys * cols, transcendentals=rows * keys * cols // width
        ),
        name="attend_back",
    )(qx, k, v, grad_mixed, mixed, normed, x_all, weights, *starts, *ins)


def attend_back_rows(entry, grad_mixed, x_all, weights, width, dw, extra, out, ns, nc):
    main, features = dw.shape[1:]
    rows = main + extra.shape[1]
    block = (nc, rows // nc, features)
    parts = (ns, rows // nc, features // ns)
    micros, half, _ = out.shape
    anywhere = pl.BlockSpec(memory_space=pl.ANY)
    return attend_back(
        HostRows, entry, grad_mixed, x_all, weights, width, 0, (), F32,
        [dw, dw, extra, out],
        [anywhere, once((1, main, features)), once(extra.shape), once(out.shape)],
        [jax.ShapeDtypeStruct(parts, BF16), jax.ShapeDtypeStruct((micros, 2, half, features), BF16)],
        [full_spec(parts), anywhere],
        [
            pltpu.VMEM((rows, features), BF16), pltpu.VMEM((rows, features), BF16), pltpu.VMEM(block, BF16),
            *axis_sems(2, nc), pltpu.SemaphoreType.DMA((3,)),
        ],
        3, ns, nc,
    )


def attend_back_shards(entry, grad_mixed, x_all, weights, width, starts, dw_parts, ns, nc):
    _, size, part = dw_parts.shape
    return attend_back(
        HostShards, entry, grad_mixed, x_all, weights, width, 1, starts, BF16,
        [dw_parts], [once(dw_parts.shape)],
        [jax.ShapeDtypeStruct((nc, size, part), BF16)], [full_spec((nc, size, part))],
        [pltpu.VMEM(dw_parts.shape, BF16), pltpu.VMEM((nc, size, part), BF16), *axis_sems(ns, nc)],
        4, ns, nc,
    )


def ffn_kernel(
    where_ref, x_ref, o0_ref, o1_ref, g_ref, w_out, up_first, up_rest, w_down, bup_ref, vec_ref,
    out_ref, gm_ref, gx_ref, dw_ref, extra_ref, dw_acc, w_up, dup_ref, dvec_ref, extra, *, ns, up_part,
):
    step = pl.program_id(0)
    steps = pl.num_programs(0)
    b_out, b_down, gain, shift = (vec_ref[i : i + 1, :] for i in (0, 1, 4, 5))
    hw = w_out.shape[1]
    hidden = bup_ref.shape[2]

    @pl.when(step == 0)
    def _():
        split = up_first.shape[2]
        w_up[:, :, :split] = up_first[...]
        w_up[:, :, split:] = up_rest[...]
        dw_acc[...] = jnp.zeros_like(dw_acc)
        dup_ref[...] = jnp.zeros_like(dup_ref)
        dvec_ref[...] = jnp.zeros_like(dvec_ref)

    mixed = jnp.where(2 * step < steps, o0_ref[...], o1_ref[...])
    grad_b = g_ref[0, 0]
    grad = grad_b.astype(F32)
    attended = dot_nn(mixed[:, :hw], w_out[0]) + dot_nn(mixed[:, hw:], w_out[1])
    middle = x_ref[0, 0].astype(F32) + (attended + b_out)
    unit, inverse = unit_norm(middle)
    normed = (unit * gain + shift).astype(BF16)
    ffn_out = jnp.zeros_like(middle)
    grad_normed = jnp.zeros_like(middle)
    for part in range(2):
        pre = dot_nn(normed, w_up[part]) + bup_ref[part]
        gate = 0.5 + 0.5 * lax.erf(pre * math.sqrt(0.5))
        active = (pre * gate).astype(BF16)
        ffn_out += dot_nn(active, w_down[part])
        slope = gate + pre * jnp.exp(pre * pre * -0.5) * (1.0 / math.sqrt(2.0 * math.pi))
        grad_pre_f = dot_nt(grad_b, w_down[part]) * slope
        grad_pre = grad_pre_f.astype(BF16)
        dup_ref[part] += column_sum(grad_pre.astype(F32))
        grad_normed += dot_nt(grad_pre, w_up[part])
        dw_acc[part, hw : hw + hidden] += dot_tn(active, grad_b)
        dw_acc[part, hw + hidden :] += dot_tn(grad_pre, normed)
    out_ref[...] = (middle + (ffn_out + b_down)).astype(BF16)
    grad_middle = grad + norm_back(grad_normed, unit, inverse, gain)
    gm_ref[...] = grad_middle
    grad_att = grad_middle.astype(BF16)
    dvec_ref[0:1] += column_sum(grad_att.astype(F32))
    dvec_ref[1:2] += column_sum(grad)
    dvec_ref[2:3] += column_sum(grad_normed * unit)
    dvec_ref[3:4] += column_sum(grad_normed)
    for part in range(2):
        cols = slice(part * hw, (part + 1) * hw)
        gx_ref[:, cols] = dot_nt(grad_att, w_out[part]).astype(BF16)
        dw_acc[part, :hw] += dot_tn(mixed[:, cols], grad_att)

    @pl.when(step == steps - 1)
    def _():
        dw_ref[...] = dw_acc[...].astype(BF16)
        features = dvec_ref.shape[1]
        extra[...] = jnp.zeros_like(extra)
        for part in range(2):
            extra[part, 0:4] = dvec_ref[0:4]
            for r in range(hidden // features):
                extra[part, 4 + r : 5 + r] = spread_columns(dup_ref[part], r, up_part, ns, features)
        extra_ref[...] = extra[...].astype(BF16)


def spread_columns(row, r, size, ns, features):
    count = row.shape[1]
    width = features // ns
    column = lax.broadcasted_iota(jnp.int32, (1, features), 1)
    shard = column // width
    place = r * width + column % width
    source = (place // size) * (size * ns) + shard * size + place % size
    chosen = jnp.where(lax.broadcasted_iota(jnp.int32, (count, features), 0) == source, 1.0, 0.0).astype(BF16)
    return dot_nn(jnp.broadcast_to(row.astype(BF16), (16, count)), chosen)[0:1]


def feed_forward(tokens, mixed, cotangent, w_out, up_first, up_rest, w_down, b_up, vectors, where, up_part, ns, nc):
    micros, _, length, features = tokens.shape
    block = 256
    half = length // 2
    each = half // block
    rows = micros * half
    hw, hidden = w_out.shape[1], b_up.shape[2]
    total = hw + 2 * hidden
    more = (2, 16 * nc, features)
    row_spec = pl.BlockSpec((block, features), lambda i, t: (i, 0))
    input_spec = pl.BlockSpec((1, 1, block, features), lambda i, t: (i // each, 0, t[0] * each + i % each, 0))
    return pl.pallas_call(
        functools.partial(ffn_kernel, ns=ns, up_part=up_part),
        grid_spec=pltpu.PrefetchScalarGridSpec(
            num_scalar_prefetch=1,
            grid=(rows // block,),
            in_specs=[
                input_spec,
                pl.BlockSpec((block, 2 * hw), lambda i, t: (jnp.minimum(i, each - 1), 0)),
                pl.BlockSpec((block, 2 * hw), lambda i, t: (jnp.maximum(i - each, 0), 0)),
                input_spec,
            ]
            + [once(w.shape) for w in (w_out, up_first, up_rest, w_down)]
            + [once(b_up.shape), once(vectors.shape)],
            out_specs=[row_spec] * 3
            + [once((2, total, features)), full_spec(more)],
            scratch_shapes=[
                pltpu.VMEM((2, total, features), F32), pltpu.VMEM((2, features, hidden), BF16),
                pltpu.VMEM((2, 1, hidden), F32), pltpu.VMEM((8, features), F32),
                pltpu.VMEM(more, F32),
            ],
        ),
        out_shape=[
            jax.ShapeDtypeStruct((rows, features), BF16),
            jax.ShapeDtypeStruct((rows, features), F32),
            jax.ShapeDtypeStruct((rows, 2 * hw), BF16),
            jax.ShapeDtypeStruct((2, total, features), BF16),
            jax.ShapeDtypeStruct(more, BF16),
        ],
        compiler_params=params(),
        cost_estimate=pl.CostEstimate(
            flops=12 * rows * total * features, bytes_accessed=20 * total * features, transcendentals=4 * rows * hidden
        ),
        name="feed_forward",
    )(where, tokens, *mixed, cotangent, w_out, up_first, up_rest, w_down, b_up, vectors)


def last_kernel(
    dw_ref, db_ref, sums_ref, dn0_ref, dn1_ref, other0_ref, other1_ref, x_ref, gm_ref, vec_ref,
    grad_ref, blocks_ref,
    extra, extra_ref, x_rows, gm_rows, dn_received, w_received, w_total, w_blocks, z_parts, z_received,
    dn_out, dn_in, wtp_out, wtp_in, wctx_out, wctx_in, z_out, z_in, back_out, back_in, row_out, row_in, fetched, *, ns, nc, head_part,
):
    t = lax.axis_index("tp")
    half = grad_ref.shape[2]
    rows = RowSum(
        dw_ref.at[1], dw_ref.at[0], extra_ref, w_received, w_total, w_blocks, (wtp_out, wtp_in),
        Axis("ctx", nc, (wctx_out, wctx_in)),
    )
    weights = ShardSum(
        z_parts, z_received, blocks_ref, Axis("shard", ns, (z_out, z_in)), Axis("ctx", nc, (back_out, back_in))
    )

    def row(micro):
        return cross(grad_ref.at[micro, t], grad_ref.at[micro, t], (row_out, row_in), micro)

    others = [cross(ref, dn_received.at[m], (dn_out, dn_in), m) for m, ref in enumerate((other0_ref, other1_ref))]

    def finish_rows(micro, dn_ref):
        size = 64
        others[micro].wait()

        def one(i, carry):
            at = pl.multiple_of(i * size, size)
            unit, inverse = unit_norm(x_rows[micro, pl.ds(at, size), :].astype(F32))
            value = gm_rows[micro, pl.ds(at, size), :] + norm_back(
                dn_ref[pl.ds(at, size), :] + dn_received[micro, pl.ds(at, size), :].astype(F32),
                unit, inverse, vec_ref[2:3],
            )
            grad_ref[micro, t, pl.ds(at, size), :] = value.astype(BF16)
            return carry

        lax.fori_loop(0, half // size, one, 0)
        row(micro).start()

    peers = [("tp", 2), ("ctx", nc), ("shard", ns)]
    greet_first(peers)
    own = x_ref.at[:, 0, pl.ds(pl.multiple_of(t * half, half), half), :]
    fetches = [
        pltpu.make_async_copy(own, x_rows, fetched.at[0]), pltpu.make_async_copy(gm_ref, gm_rows, fetched.at[1])
    ]
    for copy in fetches:
        copy.start()
    features = sums_ref.shape[1]
    each = db_ref.shape[0] // 2
    extra[...] = jnp.zeros_like(extra)
    for part in range(2):
        extra[part, 0:2] = sums_ref[0:2]
        biases = [db_ref[part * each + i, kind : kind + 1] for kind in range(2) for i in range(each)]
        extra[part, 2:3] = spread_columns(jnp.concatenate(biases, axis=1), 0, head_part, ns, features)
    extra_ref[...] = extra[...].astype(BF16)
    greet_wait(peers)
    rows.start()
    for copy in others:
        copy.start()
    rows.spread()
    for copy in fetches:
        copy.wait()
    finish_rows(0, dn0_ref)
    rows.finish(z_parts)
    weights.start()
    finish_rows(1, dn1_ref)
    weights.spread()
    weights.finish()
    for micro in range(2):
        row(micro).wait()


def last_sums(dw, db, sums, dn, x, grad_middle, vectors, head_part, ns, nc):
    main, features = dw.shape[1:]
    more = (2, 16 * nc, features)
    rows = main + more[1]
    micros, half, _ = grad_middle.shape
    size, part = rows // nc, features // ns
    return pl.pallas_call(
        functools.partial(last_kernel, ns=ns, nc=nc, head_part=head_part),
        in_specs=[pl.BlockSpec(memory_space=pltpu.VMEM)] * 7
        + [pl.BlockSpec(memory_space=pl.ANY)] * 2
        + [pl.BlockSpec(memory_space=pltpu.VMEM)],
        out_specs=[pl.BlockSpec(memory_space=pltpu.VMEM)] * 2,
        out_shape=[
            jax.ShapeDtypeStruct((micros, 2, half, features), BF16),
            jax.ShapeDtypeStruct((nc, size, part), BF16),
        ],
        scratch_shapes=[
            pltpu.VMEM(more, F32), pltpu.VMEM(more, BF16),
            pltpu.VMEM((micros, half, features), BF16), pltpu.VMEM((micros, half, features), F32),
            pltpu.VMEM((micros, half, features), BF16),
            pltpu.VMEM((rows, features), BF16), pltpu.VMEM((rows, features), BF16), pltpu.VMEM((nc, size, features), BF16),
            pltpu.VMEM((ns, size, part), BF16), pltpu.VMEM((ns, size, part), BF16),
            *axis_sems(micros, 2, nc, ns, nc, micros), pltpu.SemaphoreType.DMA((2,)),
        ],
        compiler_params=params(collective_id=5, has_side_effects=True),
        name="last_sums",
    )(dw, db, sums, *dn, x, grad_middle, vectors)


def results_kernel(out_ref, grad_ref, ffn_ref, attn_ref, *refs, heads, head_part, up_part):
    (out, grad_tokens, g_query, g_key, g_value, g_out, g_up, g_down, g_bq, g_bv, g_bup, *vectors) = refs
    out[...] = out_ref[...]
    grad_tokens[...] = grad_ref[...]
    width, lanes = g_out.shape
    hidden = g_down.shape[0]
    pair = 2 * width // heads

    def values(ref, at, size):
        return ref[at : at + size, :].astype(F32)

    @pl.when(pl.program_id(0) == 0)
    def _():
        g_out[...] = values(ffn_ref, 0, width)
        g_down[...] = values(ffn_ref, width, hidden)
        g_up[...] = values(ffn_ref, width + hidden, hidden).T
        for i in range(heads // 2):
            for kind, ref in enumerate((g_query, g_key, g_value)):
                ref[:, i * pair : (i + 1) * pair] = values(attn_ref, (3 * i + kind) * pair, pair).T
        tail = values(ffn_ref, width + 2 * hidden, 16)
        tail_attn = values(attn_ref, 3 * width, 16)
        rows = (tail[0], tail[1], tail_attn[0], tail_attn[1], tail[2], tail[3])
        for ref, row in zip(vectors, rows):
            ref[...] = row
        for h in range(heads):
            at = h * up_part
            g_bup[h : h + 1] = tail[4 + at // lanes : 5 + at // lanes, at % lanes : at % lanes + up_part]
            for start, ref in ((0, g_bq), (heads * head_part, g_bv)):
                at = start + h * head_part
                ref[h : h + 1] = tail_attn[2 + at // lanes : 3 + at // lanes, at % lanes : at % lanes + head_part]


def write_results(output, grad_tokens, done_ffn, done_attn, shapes, heads, head_part, up_part):
    micros, length, features = output.shape
    steps = 4
    rows = pl.BlockSpec((micros, length // steps, features), lambda i: (0, i, 0))
    return pl.pallas_call(
        functools.partial(results_kernel, heads=heads, head_part=head_part, up_part=up_part),
        grid=(steps,),
        in_specs=[rows, rows, once(done_ffn.shape), once(done_attn.shape)],
        out_specs=[rows, rows] + [full_spec(shape) for shape in shapes],
        out_shape=[jax.ShapeDtypeStruct(output.shape, BF16)] * 2 + [jax.ShapeDtypeStruct(shape, F32) for shape in shapes],
        compiler_params=params(),
        name="results",
    )(output, grad_tokens, done_ffn, done_attn)


def pad_rows(rows, multiple):
    extra = -rows.shape[0] % multiple
    return jnp.concatenate([rows, jnp.zeros((extra,) + rows.shape[1:], rows.dtype)]) if extra else rows


def body(
    tokens, cotangent, w_query, w_key, w_value, w_out, w_up, w_down,
    b_query, b_value, b_up, b_out, b_down, gain_attn, shift_attn, gain_ffn, shift_ffn,
):
    ns, nc = lax.axis_size("shard"), lax.axis_size("ctx")
    t = lax.axis_index("tp")
    micros, _, length, features = tokens.shape
    half = length // 2
    heads, head_part = b_query.shape
    head_width = head_part * ns
    up_part = b_up.shape[1]
    feature_part = b_out.shape[0]

    tables = [b_query, b_value, b_up] + [v[None] for v in (b_out, b_down, gain_attn, shift_attn, gain_ffn, shift_ffn)]
    keys = 2 * nc * half
    aligned = feature_part % 128 == 0
    column_place = place_columns if aligned else place_slot

    def column_shape(w, rows):
        return (2, rows, features) if aligned else (2, ns, rows, w.shape[1])

    def whole_columns(w):
        if not aligned:
            w = w.transpose(0, 2, 1, 3).reshape(2, w.shape[2], features)
        return w

    w_all, small_all, x_first = gather_first((w_query, w_key, w_value), tables, tokens, ns, nc)

    def by_head(row, part):
        table = small_all[:, :, row : row + heads, :part].transpose(0, 2, 1, 3)
        return table.reshape(2, heads * part * ns)

    biases = jnp.stack([by_head(0, head_part).reshape(-1), by_head(heads, head_part).reshape(-1)])
    bup = by_head(2 * heads, up_part)[:, None]
    vectors = small_all[0, :, 3 * heads : 3 * heads + 6, :feature_part].transpose(1, 0, 2)
    vectors = vectors.reshape(6, features)
    up_ahead = w_up.shape[1] // 4
    plans = [
        (("ctx", nc, place_distance, True, 0), ("shard", ns, place_rows, False, up_ahead)),
        (("shard", ns, column_place, False, 0),),
    ]
    sources = [(tokens, w_up), (w_down,)]
    specs = [
        [once((1, 1, length, features), (1, 0, 0, 0)), once(w_up.shape)],
        [once(w_down.shape)],
    ]
    shapes = [
        ((nc, 2, half, features), (2, features, w_up.shape[1] - up_ahead)),
        (column_shape(w_down, w_down.shape[0]),),
    ]
    guests = [
        (w_up, up_ahead, (2, features, up_ahead), place_rows),
        (w_out, w_out.shape[0], column_shape(w_out, w_out.shape[0]), column_place),
    ]
    x_alls = [x_first.reshape(keys, features), None]
    saved = []
    arrived = []
    for micro in range(micros):
        guest, guest_rows, guest_shape, guest_place = guests[micro]
        normed, k, v, q, early = front(
            x_alls[micro], w_all, vectors, biases, head_width, half, guest, guest_rows,
            guest_shape, ns, guest_place, 6 + micro,
        )
        mixed, qx, *more = attend_forward(
            q, k, v, head_width, plans[micro], sources[micro], specs[micro], shapes[micro], micro + 1
        )
        if micro == 0:
            x_alls[1] = more.pop(0).reshape(keys, features)
        arrived += [early] + more
        saved.append((normed, k, v, qx, mixed))
    up_first, up_rest, wo, wd = arrived
    wo, wd = whole_columns(wo), whole_columns(wd)

    out, grad_middle, grad_mixed, dw, extra = feed_forward(
        tokens, [entry[4] for entry in saved], cotangent, wo, up_first, up_rest, wd, bup, vectors,
        jnp.full((1,), t, jnp.int32), up_part, ns, nc,
    )

    width = heads * head_width
    *starts, dn_first, other_first, dw_parts, output = attend_back_rows(
        saved[0], grad_mixed, x_alls[0], w_all, head_width, dw, extra, out.reshape(micros, half, features), ns, nc
    )
    dw_now, db_now, sums, dn_second, other_second, dw_done = attend_back_shards(
        saved[1], grad_mixed, x_alls[1], w_all, head_width, starts, dw_parts, ns, nc
    )

    grad_tokens, attn_done = last_sums(
        dw_now.reshape(2, 3 * width, features), db_now, sums,
        (dn_first, dn_second, other_first, other_second), tokens, grad_middle.reshape(micros, half, features), vectors, head_part, ns, nc,
    )

    if aligned:
        weights = (w_query, w_key, w_value, w_out, w_up, w_down, b_query, b_value, b_up)
        shapes = [v.shape for v in weights] + [(feature_part,)] * 6
        output, grad_tokens, *grads = write_results(
            output.reshape(micros, length, features), grad_tokens.reshape(micros, length, features),
            dw_done.reshape(-1, feature_part), attn_done.reshape(-1, feature_part), shapes, heads, head_part, up_part,
        )
        g_query, g_key, g_value, g_out, g_up, g_down, g_bq, g_bv, g_bup, *others = grads
        return (output[:, None], grad_tokens[:, None], g_query, g_key, g_value, g_out, g_up, g_down, g_bq, g_bv, g_bup, *others)
    output = output.reshape(micros, 1, length, features)
    grad_tokens = grad_tokens.reshape(micros, 1, length, features)
    done_ffn = dw_done.reshape(-1, feature_part).astype(F32)
    done_attn = attn_done.reshape(-1, feature_part).astype(F32)
    hidden = heads * up_part * ns
    g_out, g_down, g_up = done_ffn[:width], done_ffn[width : width + hidden], done_ffn[width + hidden : width + 2 * hidden]
    tail = done_ffn[width + 2 * hidden :]
    by_kind = done_attn[: 3 * width].reshape(-1, 3, 2 * head_width, feature_part)
    g_query, g_key, g_value = (by_kind[:, i].reshape(width, feature_part).T for i in range(3))
    tail_attn = done_attn[3 * width :]
    g_bup = tail[4:].reshape(-1)[: heads * up_part].reshape(heads, up_part)
    g_heads = tail_attn[2:].reshape(-1)
    g_bq = g_heads[: heads * head_part].reshape(heads, head_part)
    g_bv = g_heads[heads * head_part : 2 * heads * head_part].reshape(heads, head_part)
    return (
        output, grad_tokens, g_query, g_key, g_value, g_out, g_up.T, g_down, g_bq, g_bv, g_bup,
        tail[0], tail[1], tail_attn[0], tail_attn[1], tail[2], tail[3],
    )


def solution(mesh):
    wide, tall = P("shard", "tp"), P("tp", "shard")
    rows, vector = P(None, "shard", "ctx", None), P("shard")
    weights = (wide, wide, wide, tall, wide, tall)
    return jax.shard_map(
        body,
        mesh=mesh,
        in_specs=(rows, rows) + weights + (tall,) * 3 + (vector,) * 6,
        out_specs=(rows, rows) + weights + (tall,) * 3 + (vector,) * 6,
        check_vma=False,
    )
```

```python
import functools
import math

import jax
import jax.numpy as jnp
from jax import lax
from jax.experimental import pallas as pl
from jax.experimental.pallas import tpu as pltpu
from jax.sharding import PartitionSpec as P

F32 = jnp.float32
BF16 = jnp.bfloat16
MESH = pl.DeviceIdType.MESH
norm_eps = 1e-05
LOG2E = math.log2(math.e)
VMEM_LIMIT = 60 * 2**20


def dot_nn(left, right):
    return lax.dot_general(left, right, (((1,), (0,)), ((), ())), preferred_element_type=F32)


def dot_nt(left, right):
    return lax.dot_general(left, right, (((1,), (1,)), ((), ())), preferred_element_type=F32)


def dot_tn(left, right):
    return lax.dot_general(left, right, (((0,), (0,)), ((), ())), preferred_element_type=F32)


def unit_norm(values):
    average = jnp.mean(values, axis=-1, keepdims=True)
    centred = values - average
    variance = jnp.mean(centred * centred, axis=-1, keepdims=True)
    inverse = lax.rsqrt(variance + norm_eps)
    return centred * inverse, inverse


def norm_back(grad_normed, unit_vals, inverse, gain):
    scaled = grad_normed * gain
    return inverse * (
        scaled
        - jnp.mean(scaled, axis=-1, keepdims=True)
        - unit_vals * jnp.mean(scaled * unit_vals, axis=-1, keepdims=True)
    )


def column_sum(values):
    return jnp.sum(values, axis=0, keepdims=True)


def full_spec(shape):
    return pl.BlockSpec(shape, lambda *_: (0,) * len(shape))


def params(limit=VMEM_LIMIT, **others):
    return pltpu.CompilerParams(vmem_limit_bytes=limit, **others)


def once(shape, index=None):
    place = index or (0,) * len(shape)
    return pl.BlockSpec(shape, lambda *_: place, pipeline_mode=pl.Buffered(1))


def send(source, target, send_sem, recv_sem, where):
    return pltpu.make_async_remote_copy(
        src_ref=source, dst_ref=target, send_sem=send_sem, recv_sem=recv_sem, device_id=where, device_id_type=MESH
    )


def greet_first(counts):
    barrier = pltpu.get_barrier_semaphore()
    for name, count in counts:
        me = lax.axis_index(name)
        for d in range(1, count):
            pl.semaphore_signal(barrier, inc=1, device_id={name: me ^ d}, device_id_type=MESH)


def greet_wait(counts):
    pl.semaphore_wait(pltpu.get_barrier_semaphore(), sum(count - 1 for _, count in counts))


def greet(counts):
    greet_first(counts)
    greet_wait(counts)


class Gather:

    def __init__(self, name, count, source, theirs, target, place, sems):
        self.name, self.count, self.source, self.theirs = name, count, source, theirs
        self.target, self.place = target, place
        self.out_sem, self.in_sem, self.cross_out, self.cross_in, self.local = sems
        self.me = lax.axis_index(name)

    def first(self, d):
        where = {self.name: self.me ^ d}
        return send(self.source, self.place(self.target, 0, self.me, d), self.out_sem.at[d], self.in_sem.at[d], where)

    def cross(self, d):
        where = {"tp": 1 - lax.axis_index("tp")}
        owner = self.me ^ d
        source = self.place(self.target, 0, owner, d) if d else self.source
        return send(source, self.place(self.target, 1, owner, d), self.cross_out.at[d], self.cross_in.at[d], where)

    def locals(self):
        copies = [pltpu.make_async_copy(self.source, self.place(self.target, 0, self.me, 0), self.local.at[0])]
        if self.theirs is not None:
            copies.append(pltpu.make_async_copy(self.theirs, self.place(self.target, 1, self.me, 0), self.local.at[1]))
        return copies

    def crossed(self):
        return range(0 if self.theirs is None else 1, self.count)

    def start(self, late=0):
        for d in range(1, self.count - late):
            self.first(d).start()
        for copy in self.locals():
            copy.start()
        if self.theirs is None:
            self.cross(0).start()

    def forward(self, distances=None):
        for d in distances or range(1, self.count):
            self.first(d).wait_recv()
            self.cross(d).start()

    def half(self, d, h):
        size = self.source.shape[0] // 2
        rows = pl.ds(h * size, size)
        i = d + h * self.count
        return send(
            self.source.at[rows, :], self.target.at[d, 0, rows, :], self.out_sem.at[i], self.in_sem.at[i],
            {self.name: self.me ^ d},
        )

    def relay(self, h):
        size = self.source.shape[0] // 2
        rows = pl.ds(h * size, size)
        i = 3 + h * self.count
        return send(
            self.target.at[1 + h, 0, rows, :], self.target.at[3, 0, rows, :], self.out_sem.at[i], self.in_sem.at[i],
            {self.name: self.me ^ (2 - h)},
        )

    def start_relayed(self):
        for h in range(2):
            for d in (1, 2):
                self.half(d, h if d == 1 else 1 - h).start()
        for copy in self.locals():
            copy.start()

    def pass_on(self):
        for h in range(2):
            self.half(1 + h, h).wait_recv()
            self.relay(h).start()

    def forward_near(self):
        for d in (1, 2):
            self.half(d, 1 if d == 1 else 0).wait_recv()
            self.cross(d).start()

    def forward_relayed(self):
        for h in range(2):
            self.relay(h).wait_recv()
        self.cross(3).start()

    def finish(self, relayed=False):
        if relayed:
            for h in range(2):
                for d in (1, 2):
                    self.half(d, h).wait_send()
                self.relay(h).wait_send()
        else:
            for d in range(1, self.count):
                self.first(d).wait_send()
        for d in self.crossed():
            self.cross(d).wait()
        for copy in self.locals():
            copy.wait()


def place_rows(ref, part, owner, d):
    size = ref.shape[1] // lax.axis_size("shard")
    return ref.at[part, pl.ds(pl.multiple_of(owner * size, size), size), :]


def place_columns(ref, part, owner, d):
    size = ref.shape[2] // lax.axis_size("shard")
    return ref.at[part, :, pl.ds(pl.multiple_of(owner * size, size), size)]


def place_slot(ref, part, owner, d):
    return ref.at[part, owner]


def place_distance(ref, part, owner, d):
    return ref.at[d, part]


def gather_sems(count):
    dma = pltpu.SemaphoreType.DMA
    return [dma((2 * count,)), dma((2 * count,)), dma((count,)), dma((count,)), dma((2,))]


def gather_kernel(ns, nc, wq_ref, wk_ref, wv_ref, x_block, *refs):
    tables, (w_out, x_out, vec_out, bias_out, bup_out, small_ref, small_out), sems = refs[:-20], refs[-20:-13], refs[-13:]
    w_send, w_recv, s_send, s_recv, x_send, x_recv, wt_send, wt_recv, st_send, st_recv, xt_send, xt_recv, local = sems
    w_refs = (wq_ref, wk_ref, wv_ref)
    kinds = range(3)
    x_ref = x_block.at[0, 0]
    s = lax.axis_index("shard")
    c = lax.axis_index("ctx")
    t = lax.axis_index("tp")
    other = 1 - t
    depth = wq_ref.shape[0]
    half = x_ref.shape[0] // 2

    peers = [("tp", 2), ("ctx", nc), ("shard", ns)]
    greet_first(peers)
    small_ref[...] = jnp.zeros_like(small_ref)
    row = 0
    for table in tables:
        count, lanes = table.shape
        small_ref[row : row + count, :lanes] = table[...].astype(F32)
        row += count
    greet_wait(peers)

    def w_rows(part, kind, owner):
        return w_out.at[part, kind, pl.ds(pl.multiple_of(owner * depth, depth), depth), :]

    def x_rows(which):
        return x_ref.at[pl.ds(pl.multiple_of(which * half, half), half), :]

    def begin(source, target, send_sem, recv_sem, where):
        copy = send(source, target, send_sem, recv_sem, where)
        copy.start()
        return copy

    x_copies, w_copies, s_copies = {}, {}, {}
    size = half // 2

    def x_part(d, h):
        return x_out.at[d, 0, pl.ds(h * size, size), :]

    def x_begin(source, d, h, to):
        copy = begin(source, x_part(d, h), x_send.at[d, h], x_recv.at[d, h], {"ctx": c ^ to})
        x_copies[d, h] = copy

    relayed = nc == 4
    for h in range(2):
        for d in range(1, 3 if relayed else nc):
            part = h if d % 2 else 1 - h
            source = x_ref.at[pl.ds(pl.multiple_of(t * half + part * size, size), size), :]
            x_begin(source, d, part, d)
    for d in range(1, ns):
        for k in kinds:
            w_copies[d, k] = begin(
                w_refs[k], w_rows(0, k, s), w_send.at[k, d], w_recv.at[k, d], {"shard": s ^ d}
            )
        s_copies[d] = begin(small_ref, small_out.at[0, s], s_send.at[d], s_recv.at[d], {"shard": s ^ d})
    last = [begin(w_refs[k], w_rows(1, k, s), wt_send.at[k, 0], wt_recv.at[k, 0], {"tp": other}) for k in kinds]
    last.append(begin(small_ref, small_out.at[1, s], st_send.at[0], st_recv.at[0], {"tp": other}))
    locals_ = [pltpu.make_async_copy(w_refs[k], w_rows(0, k, s), local.at[k]) for k in kinds]
    locals_ += [
        pltpu.make_async_copy(small_ref, small_out.at[0, s], local.at[3]),
        pltpu.make_async_copy(x_rows(t), x_out.at[0, 0], local.at[4]),
        pltpu.make_async_copy(x_rows(other), x_out.at[0, 1], local.at[5]),
    ]
    for copy in locals_:
        copy.start()
    if relayed:
        x_copies[1, 0].wait_recv()
        x_begin(x_part(1, 0), 3, 0, 2)
        x_copies[2, 1].wait_recv()
        x_begin(x_part(2, 1), 3, 1, 1)
    waited = {(1, 0), (2, 1)} if relayed else set()
    for d in range(1, max(ns, nc)):
        if d < ns:
            for k in kinds:
                w_copies[d, k].wait_recv()
                last.append(
                    begin(
                        w_rows(0, k, s ^ d), w_rows(1, k, s ^ d), wt_send.at[k, d], wt_recv.at[k, d], {"tp": other}
                    )
                )
            s_copies[d].wait_recv()
            last.append(
                begin(small_out.at[0, s ^ d], small_out.at[1, s ^ d], st_send.at[d], st_recv.at[d], {"tp": other})
            )
        if d < nc:
            for h in range(2):
                if (d, h) not in waited:
                    x_copies[d, h].wait_recv()
            last.append(begin(x_out.at[d, 0], x_out.at[d, 1], xt_send.at[d], xt_recv.at[d], {"tp": other}))
    for copies in (x_copies, w_copies, s_copies):
        for copy in copies.values():
            copy.wait_send()
    for copy in last:
        copy.wait()
    for copy in locals_:
        copy.wait()
    heads = tables[0].shape[0]
    vec_out[...] = jnp.zeros_like(vec_out)
    bias_out[...] = jnp.zeros_like(bias_out)
    for shard in range(ns):
        width = tables[3].shape[1]
        for i in range(len(tables) - 3):
            row = small_out[0, shard, 3 * heads + i : 3 * heads + i + 1, :width]
            vec_out[i : i + 1, shard * width : (shard + 1) * width] = row
        for which in range(3):
            width = tables[which].shape[1]
            for part in range(2):
                for h in range(heads):
                    row = small_out[part, shard, which * heads + h : which * heads + h + 1, :width]
                    at = (h * ns + shard) * width
                    if which == 2:
                        bup_out[part, :, at : at + width] = row
                    else:
                        at += part * heads * ns * width
                        bias_out[which : which + 1, at : at + width] = row


def gather_first(weights, tables, tokens, ns, nc):
    depth, width = weights[0].shape
    length, features = tokens.shape[2:]
    rows = -(-sum(table.shape[0] for table in tables) // 8) * 8
    lanes = -(-max(table.shape[1] for table in tables) // 128) * 128
    finals = [(8, features), (8, 2 * tables[0].size * ns), (2, 1, tables[2].size * ns)]
    dma = pltpu.SemaphoreType.DMA
    vmem = pl.BlockSpec(memory_space=pltpu.VMEM)
    return pl.pallas_call(
        functools.partial(gather_kernel, ns, nc),
        grid=(1,),
        in_specs=[vmem] * 3 + [once((1, 1, length, features))] + [vmem] * len(tables),
        out_specs=[pl.BlockSpec(memory_space=pl.ANY)] * 2 + [full_spec(shape) for shape in finals],
        out_shape=[
            jax.ShapeDtypeStruct((2, 3, ns * depth, width), BF16),
            jax.ShapeDtypeStruct((nc, 2, length // 2, features), BF16),
        ]
        + [jax.ShapeDtypeStruct(shape, F32) for shape in finals],
        scratch_shapes=[pltpu.VMEM((rows, lanes), F32), pltpu.VMEM((2, ns, rows, lanes), F32)]
        + [dma((3, ns)), dma((3, ns)), dma((ns,)), dma((ns,)), dma((nc, 2)), dma((nc, 2))]
        + [dma((3, ns)), dma((3, ns)), dma((ns,)), dma((ns,)), dma((nc,)), dma((nc,)), dma((6,))],
        compiler_params=params(collective_id=0, has_side_effects=True),
        name="gather_first",
    )(*weights, tokens, *tables)


def project_rows(x, w_ref, vec_ref, bias_ref, n_ref, k_ref, v_ref):
    gain, shift = vec_ref[2:3], vec_ref[3:4]
    width = w_ref.shape[3]
    size = n_ref.shape[0] // 4
    for i in range(4):
        rows = slice(i * size, (i + 1) * size)
        unit, _ = unit_norm(x(i, size).astype(F32))
        normed = (unit * gain + shift).astype(BF16)
        n_ref[rows] = normed
        for part in range(2):
            cols = slice(part * width, (part + 1) * width)
            k_ref[rows, cols] = dot_nn(normed, w_ref[part, 1]).astype(BF16)
            v_ref[rows, cols] = (dot_nn(normed, w_ref[part, 2]) + bias_ref[1:2, cols]).astype(BF16)


def project_query(w_ref, bias_ref, n_ref, q_ref, q_scale):
    width = w_ref.shape[3]
    normed = n_ref[: q_ref.shape[0]]
    for part in range(2):
        cols = slice(part * width, (part + 1) * width)
        q_ref[:, cols] = ((dot_nn(normed, w_ref[part, 0]) + bias_ref[0:1, cols]) * q_scale).astype(BF16)


def front_kernel(
    x_ref, w_ref, vec_ref, bias_ref, guest_ref, n_ref, k_ref, v_ref, q_ref, guest_all, *sems, q_scale, ns, place, size
):
    step = pl.program_id(0)
    part = guest_ref.at[:, pl.ds(0, size)] if place is place_rows else guest_ref.at[pl.ds(0, size), :]
    gather = Gather("shard", ns, part, None, guest_all, place, sems)

    peers = [("tp", 2), ("shard", ns)]

    @pl.when(step == 0)
    def _():
        greet_first(peers)

    @pl.when(step == 1)
    def _():
        greet_wait(peers)
        gather.start()

    project_rows(lambda i, size: x_ref[i * size : (i + 1) * size], w_ref, vec_ref, bias_ref, n_ref, k_ref, v_ref)

    @pl.when(step == 0)
    def _():
        project_query(w_ref, bias_ref, n_ref, q_ref, q_scale)

    @pl.when(step == pl.num_programs(0) - 1)
    def _():
        gather.forward()
        gather.finish()


def front(x_all, weights, vectors, biases, head_width, half, guest, guest_rows, guest_shape, ns, place, number):
    keys, features = x_all.shape
    block = 2 * half
    width = 2 * weights.shape[3]
    scale = LOG2E / math.sqrt(head_width)
    return pl.pallas_call(
        functools.partial(front_kernel, q_scale=scale, ns=ns, place=place, size=guest_rows),
        grid=(keys // block,),
        in_specs=[
            pl.BlockSpec((block, features), lambda i: (i, 0)),
            once(weights.shape),
            once(vectors.shape),
            once(biases.shape),
            once(guest.shape),
        ],
        out_specs=[
            pl.BlockSpec((block, features), lambda i: (i, 0)),
            pl.BlockSpec((block, width), lambda i: (i, 0)),
            pl.BlockSpec((block, width), lambda i: (i, 0)),
            full_spec((half, width)),
            pl.BlockSpec(memory_space=pl.ANY),
        ],
        out_shape=[
            jax.ShapeDtypeStruct((keys, features), BF16),
            jax.ShapeDtypeStruct((keys, width), BF16),
            jax.ShapeDtypeStruct((keys, width), BF16),
            jax.ShapeDtypeStruct((half, width), BF16),
            jax.ShapeDtypeStruct(guest_shape, BF16),
        ],
        scratch_shapes=gather_sems(ns),
        compiler_params=params(collective_id=number, has_side_effects=True),
        cost_estimate=pl.CostEstimate(
            flops=4 * keys * features * width, bytes_accessed=8 * keys * features, transcendentals=keys
        ),
        name="front",
    )(x_all, weights, vectors, biases, guest)


def with_parts(lane, base, values, first, width):
    high = values.astype(BF16).astype(F32)
    rest = values - high
    middle = rest.astype(BF16).astype(F32)
    low = rest - middle
    extra = jnp.where(
        lane == first, high, jnp.where(lane == first + 1, middle, jnp.where(lane == first + 2, low, 0.0))
    )
    inside = (lane < width) if first else (lane >= width)
    return jnp.where(inside, base, extra)


def attend_kernel(*refs, kc, width, plans):
    count = len(plans)
    q_ref, k_ref, v_ref = refs[:3]
    sources = refs[3 : 3 + count]
    o_ref, qx_ref = refs[3 + count : 5 + count]
    targets = refs[5 + count : 5 + 2 * count]
    scores = refs[5 + 2 * count]
    sems = refs[6 + 2 * count :]
    step = pl.program_id(0)
    last = pl.num_programs(0) - 1
    t = lax.axis_index("tp")

    def gathers(wanted):
        found = []
        for i, (name, number, place, split, start) in enumerate(plans):
            if name != wanted:
                continue
            source, theirs = sources[i], None
            if split:
                source = source.at[0, 0]
                half = source.shape[0] // 2
                theirs = source.at[pl.ds(pl.multiple_of((1 - t) * half, half), half), :]
                source = source.at[pl.ds(pl.multiple_of(t * half, half), half), :]
            elif start and place is place_rows:
                source = source.at[:, pl.ds(start, source.shape[1] - start)]
            elif start:
                source = source.at[pl.ds(start, source.shape[0] - start), :]
            found.append(Gather(name, number, source, theirs, targets[i], place, sems[5 * i : 5 * i + 5]))
        return found

    counts = {name: number for name, number, *_ in plans}

    peers = [("tp", 2)] + list(counts.items())
    far = counts.get("ctx", 1) - 1
    relayed = far == 3

    @pl.when(step == 0)
    def _():
        greet_first(peers)


    rows, lanes = q_ref.shape
    keys = k_ref.shape[0]
    lane = lax.broadcasted_iota(jnp.int32, (rows, lanes), 1)
    lane_v = lax.broadcasted_iota(jnp.int32, (kc, lanes), 1)
    q = q_ref[...].astype(F32)
    tops = []
    for h in range(2):
        inside = (lane < width) if h == 0 else (lane >= width)
        q_head = jnp.where(inside, q, 0.0).astype(BF16)
        top = None
        for i in range(keys // kc):
            part = dot_nt(k_ref[i * kc : (i + 1) * kc], q_head)
            scores[h, i * kc : (i + 1) * kc] = part
            here = jnp.max(part.reshape(kc // 8, 8, rows), axis=0)
            top = here if top is None else jnp.maximum(top, here)
        tops.append(jnp.max(top, axis=0, keepdims=True))

    @pl.when(step == 0)
    def _():
        greet_wait(peers)
        for gather in gathers("shard"):
            gather.start()
        for gather in gathers("ctx"):
            if relayed:
                gather.start_relayed()
            else:
                gather.start(1)

    @pl.when(step == 1)
    def _():
        for gather in gathers("ctx"):
            if relayed:
                gather.pass_on()

    @pl.when(step == 2)
    def _():
        for gather in gathers("ctx"):
            if relayed:
                gather.forward_near()
            else:
                gather.first(far).start()
                gather.forward(range(1, far))

    def forward_last():
        for gather in gathers("shard"):
            gather.forward()
        for gather in gathers("ctx"):
            if relayed:
                gather.forward_relayed()
            else:
                gather.forward([far])

    if far:
        pl.when(step == last)(forward_last)

    outs = []
    for h in range(2):
        inside_v = (lane_v < width) if h == 0 else (lane_v >= width)
        total = jnp.zeros((lanes, rows), F32)
        for i in range(keys // kc):
            v_one = jnp.where(inside_v, v_ref[i * kc : (i + 1) * kc], jnp.ones((), BF16))
            exponent = jnp.exp2(scores[h, i * kc : (i + 1) * kc] - tops[h]).astype(BF16)
            total += dot_tn(v_one, exponent)
        first = width if h == 0 else 0
        log_total = tops[h] + jnp.log2(total[first : first + 1, :])
        total = total.T
        outs.append(total / pltpu.roll(total, width, 1))
        log_column = jnp.broadcast_to(log_total, (8, rows)).T[:, :1]
        qx_ref[:, h * lanes : (h + 1) * lanes] = with_parts(lane, q, -log_column, first, width).astype(BF16)
    o_ref[...] = jnp.where(lane < width, outs[0], outs[1]).astype(BF16)

    @pl.when(step == last)
    def _():
        if not far:
            forward_last()
        for name in counts:
            for gather in gathers(name):
                gather.finish(relayed and name == "ctx")


def attend_forward(q, k, v, width, plans, sources, source_specs, shapes, number):
    rows, cols = q.shape
    keys = k.shape[0]
    lanes = 2 * width
    kc = 512
    anywhere = pl.BlockSpec(memory_space=pl.ANY)
    return pl.pallas_call(
        functools.partial(attend_kernel, kc=kc, width=width, plans=plans),
        grid=(cols // lanes,),
        in_specs=[
            pl.BlockSpec((rows, lanes), lambda j: (0, j)),
            pl.BlockSpec((keys, lanes), lambda j: (0, j)),
            pl.BlockSpec((keys, lanes), lambda j: (0, j)),
        ]
        + source_specs,
        out_specs=[
            pl.BlockSpec((rows, lanes), lambda j: (0, j)),
            pl.BlockSpec((rows, 2 * lanes), lambda j: (0, j)),
        ]
        + [anywhere] * len(plans),
        out_shape=[
            jax.ShapeDtypeStruct((rows, cols), BF16),
            jax.ShapeDtypeStruct((rows, 2 * cols), BF16),
        ]
        + [jax.ShapeDtypeStruct(shape, BF16) for shape in shapes],
        scratch_shapes=[pltpu.VMEM((2, keys, rows), F32)]
        + [sem for plan in plans for sem in gather_sems(plan[1])],
        compiler_params=params(collective_id=number, has_side_effects=True),
        cost_estimate=pl.CostEstimate(
            flops=12 * rows * keys * cols, bytes_accessed=4 * keys * cols, transcendentals=rows * keys * cols // width
        ),
        name="attend_forward",
    )(q, k, v, *sources)


def sum_rows(target, at, left, left_at, right, right_at, rows, chunk=64):
    def one(i, carry):
        here = pl.multiple_of(i * chunk, chunk)
        target[pl.ds(at + here, chunk), :] = left[pl.ds(left_at + here, chunk), :] + right[pl.ds(right_at + here, chunk), :]
        return carry

    lax.fori_loop(0, rows // chunk, one, 0)


class Axis:

    def __init__(self, name, count, sems):
        self.name, self.count, self.sems = name, count, sems
        self.me = lax.axis_index(name)

    def copy(self, d, source, target):
        return send(source(self.me ^ d, d), target(self.me, d), self.sems[0].at[d], self.sems[1].at[d], {self.name: self.me ^ d})

    def start(self, source, target):
        for d in range(1, self.count):
            self.copy(d, source, target).start()

    def wait(self, source, target):
        for d in range(1, self.count):
            self.copy(d, source, target).wait()


def axis_sems(*counts):
    return [pltpu.SemaphoreType.DMA((count,)) for count in counts for _ in range(2)]


def cross(source, target, sems, i):
    return send(source, target, sems[0].at[i], sems[1].at[i], {"tp": 1 - lax.axis_index("tp")})


class RowSum:

    def __init__(self, dw_send, dw_own, extra, received, total, blocks, tp_sems, ctx):
        self.dw_send, self.dw_own, self.extra = dw_send, dw_own, extra
        self.received, self.total, self.blocks = received, total, blocks
        self.tp_sems, self.ctx = tp_sems, ctx
        self.main, self.more = dw_own.shape[0], extra.shape[1]
        self.size = (self.main + self.more) // ctx.count

    def crossing(self):
        return [
            cross(self.dw_send, self.received.at[pl.ds(0, self.main), :], self.tp_sems, 0),
            cross(self.extra.at[1], self.received.at[pl.ds(self.main, self.more), :], self.tp_sems, 1),
        ]

    def start(self):
        for copy in self.crossing():
            copy.start()

    def source(self, peer, d):
        return self.total.at[pl.ds(pl.multiple_of(peer * self.size, 16), self.size), :]

    def target(self, me, d):
        return self.blocks.at[d]

    def spread(self):
        for copy in self.crossing():
            copy.wait()
        sum_rows(self.total, 0, self.dw_own, 0, self.received, 0, self.main)
        sum_rows(self.total, self.main, self.extra.at[0], 0, self.received, self.main, self.more)
        self.ctx.start(self.source, self.target)

    def finish(self, out):
        self.ctx.wait(self.source, self.target)
        count, size, width = out.shape
        value = self.total[pl.ds(pl.multiple_of(self.ctx.me * self.size, 16), self.size), :].astype(F32)
        for d in range(1, self.ctx.count):
            value += self.blocks[d].astype(F32)
        for j in range(count):
            out[j] = value[:, j * width : (j + 1) * width].astype(out.dtype)


class ShardSum:

    def __init__(self, parts, received, blocks, shard, ctx):
        self.parts, self.received, self.blocks, self.shard, self.ctx = parts, received, blocks, shard, ctx

    def source(self, peer, d):
        return self.parts.at[peer]

    def target(self, me, d):
        return self.received.at[d]

    def start(self):
        self.shard.start(self.source, self.target)

    def mine(self, peer, d):
        return self.blocks.at[self.ctx.me]

    def theirs(self, me, d):
        return self.blocks.at[me]

    def spread(self):
        self.shard.wait(self.source, self.target)
        value = self.parts[self.shard.me].astype(F32)
        for d in range(1, self.shard.count):
            value += self.received[d].astype(F32)
        self.blocks[self.ctx.me] = value.astype(BF16)
        self.ctx.start(self.mine, self.theirs)

    def finish(self):
        self.ctx.wait(self.mine, self.theirs)


class InputSum:

    def __init__(self, dn_send, dn_own, received, total, blocks, tp_sems, ctx):
        self.dn_send, self.dn_own, self.received = dn_send, dn_own, received
        self.total, self.blocks, self.tp_sems, self.ctx = total, blocks, tp_sems, ctx

    def crossing(self, d):
        return cross(self.dn_send(d), self.received.at[d], self.tp_sems, d)

    def source(self, peer, d):
        return self.total.at[d]

    def target(self, me, d):
        return self.blocks.at[d]

    def spread_one(self, d):
        self.crossing(d).wait()
        sum_rows(self.total.at[d], 0, self.dn_own(d), 0, self.received.at[d], 0, self.received.shape[1])
        self.ctx.copy(d, self.source, self.target).start()

    def finish(self):
        self.ctx.wait(self.source, self.target)

    def rows(self, own, at, size):
        value = own[pl.ds(at, size), :]
        for d in range(1, self.ctx.count):
            value += self.blocks[d, pl.ds(at, size), :].astype(F32)
        return value


def attend_back_step(refs, scratch, starts, width):
    qx_ref, k_ref, v_ref, go_ref, o_ref, n_ref, x_ref, w_ref = refs
    gx_all, dq_acc, dn_acc, dw_acc, db_ref, sums_ref = scratch
    i, j = pl.program_id(0), pl.program_id(1)
    last_block, last_pair = pl.num_programs(0) - 1, pl.num_programs(1) - 1
    rows, lanes = o_ref.shape
    keys = k_ref.shape[0]
    lane = lax.broadcasted_iota(jnp.int32, (rows, lanes), 1)
    lane_k = lax.broadcasted_iota(jnp.int32, (keys, lanes), 1)
    one = jnp.ones((), BF16)

    @pl.when(i == 0)
    def _():
        grad_out = go_ref[...].astype(F32)
        both = grad_out * o_ref[...].astype(F32)
        for h in range(2):
            inside = (lane < width) if h == 0 else (lane >= width)
            delta = jnp.sum(jnp.where(inside, both, 0.0), axis=1, keepdims=True)
            gx_all[j, h] = with_parts(lane, grad_out, -delta, width if h == 0 else 0, width).astype(BF16)
        dq_acc[j] = jnp.zeros(dq_acc.shape[1:], F32)
        dw_acc[j] = starts[0][j] if starts else jnp.zeros(dw_acc.shape[1:], F32)
        db_ref[j] = starts[1][j] if starts else jnp.zeros(db_ref.shape[1:], F32)

    @pl.when((i == 0) & (j == 0))
    def _():
        sums_ref[...] = starts[2][...] if starts else jnp.zeros_like(sums_ref)

    @pl.when(j == 0)
    def _():
        dn_acc[...] = jnp.zeros_like(dn_acc)

    grad_k, grad_v, grad_q = [], [], []
    for h in range(2):
        inside_k = (lane_k < width) if h == 0 else (lane_k >= width)
        kx = jnp.where(inside_k, k_ref[...], one)
        vx = jnp.where(inside_k, v_ref[...], one)
        qx = qx_ref[:, h * lanes : (h + 1) * lanes]
        gx = gx_all[j, h]
        prob = jnp.exp2(dot_nt(kx, qx))
        grad_v.append(dot_nn(prob.astype(BF16), gx))
        grad_score = (prob * dot_nt(vx, gx)).astype(BF16)
        grad_k.append(dot_nn(grad_score, qx))
        grad_q.append(dot_tn(kx, grad_score))
    dk = (jnp.where(lane_k < width, grad_k[0], grad_k[1]) * (1.0 / LOG2E)).astype(BF16)
    dv = jnp.where(lane_k < width, grad_v[0], grad_v[1]).astype(BF16)
    dq_acc[j] += jnp.concatenate([grad_q[0][:width], grad_q[1][width:]], axis=0)
    both = jnp.concatenate([dk, dv], axis=1)
    weights = jnp.concatenate([w_ref[0, 1], w_ref[0, 2]], axis=1)
    dn_acc[...] += dot_nt(both, weights)
    grad_w = dot_tn(both, n_ref[...])
    dw_acc[j, 1] += grad_w[:lanes]
    dw_acc[j, 2] += grad_w[lanes:]
    db_ref[j, 1:2] += column_sum(dv.astype(F32))

    @pl.when(i == last_block)
    def _():
        dq = (dq_acc[j].T * (1.0 / math.sqrt(width))).astype(BF16)
        dn_acc[:rows] += dot_nt(dq, w_ref[0, 0])
        dw_acc[j, 0] += dot_tn(dq, n_ref[:rows])
        db_ref[j, 0:1] += column_sum(dq.astype(F32))

    @pl.when(j == last_pair)
    def _():
        unit, _ = unit_norm(x_ref[...].astype(F32))
        sums_ref[0:1] += column_sum(dn_acc[...] * unit)
        sums_ref[1:2] += column_sum(dn_acc[...])


def attend_back_kernel(*refs, width, nc, ns, hosted, hosted_counts, started):
    i, j = pl.program_id(0), pl.program_id(1)
    last_pair = pl.num_programs(1) - 1
    n_in, n_out, n_scratch = hosted_counts
    at = 8
    base = refs[:at]
    starts = refs[at : at + 3] if started else ()
    at += 3 if started else 0
    extra_in, at = refs[at : at + n_in], at + n_in
    (dw_ref, db_ref, sums_ref, dn_done, dn_other), at = refs[at : at + 5], at + 5
    extra_out, at = refs[at : at + n_out], at + n_out
    gx_all, dq_acc, dn_acc, dw_acc, dn_sent, dn_received, dn_total, dn_blocks, tp_out, tp_in, ctx_out, ctx_in = refs[at : at + 12]
    extra_scratch = refs[at + 12 :]
    inputs = InputSum(
        lambda d: dn_sent.at[d, 1], lambda d: dn_sent.at[d, 0], dn_received, dn_total, dn_blocks,
        (tp_out, tp_in), Axis("ctx", nc, (ctx_out, ctx_in)),
    )
    guest = hosted(extra_in, extra_out, extra_scratch, nc, ns)

    @pl.when((i == 0) & (j == 0))
    def _():
        greet_first(guest.peers)

    @pl.when((i == 0) & (j == 1))
    def _():
        greet_wait(guest.peers)
        guest.begin()

    @pl.when((i == 1) & (j == 0))
    def _():
        guest.middle()

    for d in range(1, nc):

        @pl.when((i == nc - d) & (j == 0))
        def _(d=d):
            inputs.crossing(d).start()

        @pl.when((i == nc - d) & (j == 1))
        def _(d=d):
            inputs.spread_one(d)

    attend_back_step(
        base, (gx_all, dq_acc, dn_acc, dw_acc, db_ref, sums_ref), starts, width
    )

    half = dn_acc.shape[0] // 2

    @pl.when((j == last_pair) & (i < nc - 1))
    def _():
        for part in range(2):
            dn_sent[nc - 1 - i, part] = dn_acc[part * half : (part + 1) * half].astype(BF16)

    @pl.when((i == nc - 1) & (j == last_pair))
    def _():
        dw_ref[...] = dw_acc[...].astype(dw_ref.dtype)
        dn_other[...] = dn_acc[half:].astype(BF16)
        guest.end()
        inputs.finish()
        size = 64

        def one(r, carry):
            here = pl.multiple_of(r * size, size)
            dn_done[pl.ds(here, size), :] = inputs.rows(dn_acc, here, size)
            return carry

        lax.fori_loop(0, half // size, one, 0)


class HostRows:

    def __init__(self, ins, outs, scratch, nc, ns):
        dw_all, dw_own, extra, out_half = ins
        self.dw_out, whole = outs
        received, total, blocks, tp_out, tp_in, ctx_out, ctx_in, sems = scratch
        t = lax.axis_index("tp")
        self.rows = RowSum(
            dw_all.at[1], dw_own.at[0], extra, received, total, blocks, (tp_out, tp_in), Axis("ctx", nc, (ctx_out, ctx_in))
        )
        self.copies = lambda: [
            cross(out_half, whole.at[:, t], (sems, sems.at[pl.ds(1, 1)]), 0),
            pltpu.make_async_copy(out_half, whole.at[:, t], sems.at[2]),
        ]
        self.peers = [("tp", 2), ("ctx", nc)]

    def begin(self):
        self.rows.start()
        for copy in self.copies():
            copy.start()

    def middle(self):
        self.rows.spread()

    def end(self):
        self.rows.finish(self.dw_out)
        for copy in self.copies():
            copy.wait()


class HostShards:

    def __init__(self, ins, outs, scratch, nc, ns):
        (self.done,) = outs
        received, self.blocks, z_out, z_in, back_out, back_in = scratch
        self.sums = ShardSum(
            ins[0], received, self.blocks, Axis("shard", ns, (z_out, z_in)), Axis("ctx", nc, (back_out, back_in))
        )
        self.peers = [("tp", 2), ("ctx", nc), ("shard", ns)]

    def begin(self):
        self.sums.start()

    def middle(self):
        self.sums.spread()

    def end(self):
        self.sums.finish()
        self.done[...] = self.blocks[...]


def attend_back(
    hosted, entry, grad_mixed, x_all, weights, width, micro, starts, kind, ins, in_specs, outs, out_specs, scratch, number, ns, nc
):
    normed, k, v, qx, mixed = entry
    rows, cols = mixed.shape
    keys, features = normed.shape
    lanes = 2 * width
    pairs = cols // lanes
    size = keys // nc
    each = pairs // 2
    stack = (pairs, 3, lanes, features)
    block = pltpu.VMEM((nc, rows, features), BF16)

    def key_block(shape, column):
        return pl.BlockSpec(shape, lambda i, j: (nc - 1 - i, j if column else 0))

    return pl.pallas_call(
        functools.partial(
            attend_back_kernel, width=width, nc=nc, ns=ns, hosted=hosted,
            hosted_counts=(len(ins), len(outs), len(scratch)), started=bool(starts),
        ),
        grid=(nc, pairs),
        in_specs=[
            pl.BlockSpec((rows, 2 * lanes), lambda i, j: (0, j)),
            key_block((size, lanes), True),
            key_block((size, lanes), True),
            pl.BlockSpec((rows, lanes), lambda i, j: (micro, j)),
            pl.BlockSpec((rows, lanes), lambda i, j: (0, j)),
            key_block((size, features), False),
            key_block((size, features), False),
            pl.BlockSpec((1, 3, features, lanes), lambda i, j: (j // each, 0, 0, j % each)),
        ]
        + [once(value.shape) for value in starts]
        + in_specs,
        out_specs=[full_spec(stack), full_spec((pairs, 8, lanes)), full_spec((8, features))]
        + [full_spec((rows, features))] * 2
        + out_specs,
        out_shape=[
            jax.ShapeDtypeStruct(stack, kind),
            jax.ShapeDtypeStruct((pairs, 8, lanes), F32),
            jax.ShapeDtypeStruct((8, features), F32),
            jax.ShapeDtypeStruct((rows, features), F32),
            jax.ShapeDtypeStruct((rows, features), BF16),
        ]
        + outs,
        scratch_shapes=[
            pltpu.VMEM((pairs, 2, rows, lanes), BF16),
            pltpu.VMEM((pairs, lanes, rows), F32),
            pltpu.VMEM((size, features), F32),
            pltpu.VMEM(stack, F32),
            pltpu.VMEM((nc, 2, rows, features), BF16),
            block, block, block,
            *axis_sems(nc, nc),
        ]
        + scratch,
        compiler_params=params(collective_id=number, has_side_effects=True),
        cost_estimate=pl.CostEstimate(
            flops=30 * rows * keys * cols, bytes_accessed=8 * keys * cols, transcendentals=rows * keys * cols // width
        ),
        name="attend_back",
    )(qx, k, v, grad_mixed, mixed, normed, x_all, weights, *starts, *ins)


def attend_back_rows(entry, grad_mixed, x_all, weights, width, dw, extra, out, ns, nc):
    main, features = dw.shape[1:]
    rows = main + extra.shape[1]
    block = (nc, rows // nc, features)
    parts = (ns, rows // nc, features // ns)
    micros, half, _ = out.shape
    anywhere = pl.BlockSpec(memory_space=pl.ANY)
    return attend_back(
        HostRows, entry, grad_mixed, x_all, weights, width, 0, (), F32,
        [dw, dw, extra, out],
        [anywhere, once((1, main, features)), once(extra.shape), once(out.shape)],
        [jax.ShapeDtypeStruct(parts, BF16), jax.ShapeDtypeStruct((micros, 2, half, features), BF16)],
        [full_spec(parts), anywhere],
        [
            pltpu.VMEM((rows, features), BF16), pltpu.VMEM((rows, features), BF16), pltpu.VMEM(block, BF16),
            *axis_sems(2, nc), pltpu.SemaphoreType.DMA((3,)),
        ],
        3, ns, nc,
    )


def attend_back_shards(entry, grad_mixed, x_all, weights, width, starts, dw_parts, ns, nc):
    _, size, part = dw_parts.shape
    return attend_back(
        HostShards, entry, grad_mixed, x_all, weights, width, 1, starts, BF16,
        [dw_parts], [once(dw_parts.shape)],
        [jax.ShapeDtypeStruct((nc, size, part), BF16)], [full_spec((nc, size, part))],
        [pltpu.VMEM(dw_parts.shape, BF16), pltpu.VMEM((nc, size, part), BF16), *axis_sems(ns, nc)],
        4, ns, nc,
    )


def ffn_kernel(
    where_ref, x_ref, o0_ref, o1_ref, g_ref, w_out, up_first, up_rest, w_down, bup_ref, vec_ref,
    out_ref, gm_ref, gx_ref, dw_ref, extra_ref, dw_acc, w_up, dup_ref, dvec_ref, extra, *, ns, up_part,
):
    step = pl.program_id(0)
    steps = pl.num_programs(0)
    b_out, b_down, gain, shift = (vec_ref[i : i + 1, :] for i in (0, 1, 4, 5))
    hw = w_out.shape[1]
    hidden = bup_ref.shape[2]

    @pl.when(step == 0)
    def _():
        split = up_first.shape[2]
        w_up[:, :, :split] = up_first[...]
        w_up[:, :, split:] = up_rest[...]
        dw_acc[...] = jnp.zeros_like(dw_acc)
        dup_ref[...] = jnp.zeros_like(dup_ref)
        dvec_ref[...] = jnp.zeros_like(dvec_ref)

    mixed = jnp.where(2 * step < steps, o0_ref[...], o1_ref[...])
    grad_b = g_ref[0, 0]
    grad = grad_b.astype(F32)
    attended = dot_nn(mixed[:, :hw], w_out[0]) + dot_nn(mixed[:, hw:], w_out[1])
    middle = x_ref[0, 0].astype(F32) + (attended + b_out)
    unit, inverse = unit_norm(middle)
    normed = (unit * gain + shift).astype(BF16)
    ffn_out = jnp.zeros_like(middle)
    grad_normed = jnp.zeros_like(middle)
    for part in range(2):
        pre = dot_nn(normed, w_up[part]) + bup_ref[part]
        gate = 0.5 + 0.5 * lax.erf(pre * math.sqrt(0.5))
        active = (pre * gate).astype(BF16)
        ffn_out += dot_nn(active, w_down[part])
        slope = gate + pre * jnp.exp(pre * pre * -0.5) * (1.0 / math.sqrt(2.0 * math.pi))
        grad_pre_f = dot_nt(grad_b, w_down[part]) * slope
        grad_pre = grad_pre_f.astype(BF16)
        dup_ref[part] += column_sum(grad_pre.astype(F32))
        grad_normed += dot_nt(grad_pre, w_up[part])
        dw_acc[part, hw : hw + hidden] += dot_tn(active, grad_b)
        dw_acc[part, hw + hidden :] += dot_tn(grad_pre, normed)
    out_ref[...] = (middle + (ffn_out + b_down)).astype(BF16)
    grad_middle = grad + norm_back(grad_normed, unit, inverse, gain)
    gm_ref[...] = grad_middle
    grad_att = grad_middle.astype(BF16)
    dvec_ref[0:1] += column_sum(grad_att.astype(F32))
    dvec_ref[1:2] += column_sum(grad)
    dvec_ref[2:3] += column_sum(grad_normed * unit)
    dvec_ref[3:4] += column_sum(grad_normed)
    for part in range(2):
        cols = slice(part * hw, (part + 1) * hw)
        gx_ref[:, cols] = dot_nt(grad_att, w_out[part]).astype(BF16)
        dw_acc[part, :hw] += dot_tn(mixed[:, cols], grad_att)

    @pl.when(step == steps - 1)
    def _():
        dw_ref[...] = dw_acc[...].astype(BF16)
        features = dvec_ref.shape[1]
        extra[...] = jnp.zeros_like(extra)
        for part in range(2):
            extra[part, 0:4] = dvec_ref[0:4]
            for r in range(hidden // features):
                extra[part, 4 + r : 5 + r] = spread_columns(dup_ref[part], r, up_part, ns, features)
        extra_ref[...] = extra[...].astype(BF16)


def spread_columns(row, r, size, ns, features):
    count = row.shape[1]
    width = features // ns
    column = lax.broadcasted_iota(jnp.int32, (1, features), 1)
    shard = column // width
    place = r * width + column % width
    source = (place // size) * (size * ns) + shard * size + place % size
    chosen = jnp.where(lax.broadcasted_iota(jnp.int32, (count, features), 0) == source, 1.0, 0.0).astype(BF16)
    return dot_nn(jnp.broadcast_to(row.astype(BF16), (16, count)), chosen)[0:1]


def feed_forward(tokens, mixed, cotangent, w_out, up_first, up_rest, w_down, b_up, vectors, where, up_part, ns, nc):
    micros, _, length, features = tokens.shape
    block = 256
    half = length // 2
    each = half // block
    rows = micros * half
    hw, hidden = w_out.shape[1], b_up.shape[2]
    total = hw + 2 * hidden
    more = (2, 16 * nc, features)
    row_spec = pl.BlockSpec((block, features), lambda i, t: (i, 0))
    input_spec = pl.BlockSpec((1, 1, block, features), lambda i, t: (i // each, 0, t[0] * each + i % each, 0))
    return pl.pallas_call(
        functools.partial(ffn_kernel, ns=ns, up_part=up_part),
        grid_spec=pltpu.PrefetchScalarGridSpec(
            num_scalar_prefetch=1,
            grid=(rows // block,),
            in_specs=[
                input_spec,
                pl.BlockSpec((block, 2 * hw), lambda i, t: (jnp.minimum(i, each - 1), 0)),
                pl.BlockSpec((block, 2 * hw), lambda i, t: (jnp.maximum(i - each, 0), 0)),
                input_spec,
            ]
            + [once(w.shape) for w in (w_out, up_first, up_rest, w_down)]
            + [once(b_up.shape), once(vectors.shape)],
            out_specs=[row_spec] * 3
            + [once((2, total, features)), full_spec(more)],
            scratch_shapes=[
                pltpu.VMEM((2, total, features), F32), pltpu.VMEM((2, features, hidden), BF16),
                pltpu.VMEM((2, 1, hidden), F32), pltpu.VMEM((8, features), F32),
                pltpu.VMEM(more, F32),
            ],
        ),
        out_shape=[
            jax.ShapeDtypeStruct((rows, features), BF16),
            jax.ShapeDtypeStruct((rows, features), F32),
            jax.ShapeDtypeStruct((rows, 2 * hw), BF16),
            jax.ShapeDtypeStruct((2, total, features), BF16),
            jax.ShapeDtypeStruct(more, BF16),
        ],
        compiler_params=params(),
        cost_estimate=pl.CostEstimate(
            flops=12 * rows * total * features, bytes_accessed=20 * total * features, transcendentals=4 * rows * hidden
        ),
        name="feed_forward",
    )(where, tokens, *mixed, cotangent, w_out, up_first, up_rest, w_down, b_up, vectors)


def last_kernel(
    dw_ref, db_ref, sums_ref, dn0_ref, dn1_ref, other0_ref, other1_ref, x_ref, gm_ref, vec_ref,
    grad_ref, blocks_ref,
    extra, extra_ref, x_rows, gm_rows, dn_received, w_received, w_total, w_blocks, z_parts, z_received,
    dn_out, dn_in, wtp_out, wtp_in, wctx_out, wctx_in, z_out, z_in, back_out, back_in, row_out, row_in, fetched, *, ns, nc, head_part,
):
    t = lax.axis_index("tp")
    half = grad_ref.shape[2]
    rows = RowSum(
        dw_ref.at[1], dw_ref.at[0], extra_ref, w_received, w_total, w_blocks, (wtp_out, wtp_in),
        Axis("ctx", nc, (wctx_out, wctx_in)),
    )
    weights = ShardSum(
        z_parts, z_received, blocks_ref, Axis("shard", ns, (z_out, z_in)), Axis("ctx", nc, (back_out, back_in))
    )

    def row(micro):
        return cross(grad_ref.at[micro, t], grad_ref.at[micro, t], (row_out, row_in), micro)

    others = [cross(ref, dn_received.at[m], (dn_out, dn_in), m) for m, ref in enumerate((other0_ref, other1_ref))]

    def finish_rows(micro, dn_ref):
        size = 64
        others[micro].wait()

        def one(i, carry):
            at = pl.multiple_of(i * size, size)
            unit, inverse = unit_norm(x_rows[micro, pl.ds(at, size), :].astype(F32))
            value = gm_rows[micro, pl.ds(at, size), :] + norm_back(
                dn_ref[pl.ds(at, size), :] + dn_received[micro, pl.ds(at, size), :].astype(F32),
                unit, inverse, vec_ref[2:3],
            )
            grad_ref[micro, t, pl.ds(at, size), :] = value.astype(BF16)
            return carry

        lax.fori_loop(0, half // size, one, 0)
        row(micro).start()

    peers = [("tp", 2), ("ctx", nc), ("shard", ns)]
    greet_first(peers)
    own = x_ref.at[:, 0, pl.ds(pl.multiple_of(t * half, half), half), :]
    fetches = [
        pltpu.make_async_copy(own, x_rows, fetched.at[0]), pltpu.make_async_copy(gm_ref, gm_rows, fetched.at[1])
    ]
    for copy in fetches:
        copy.start()
    features = sums_ref.shape[1]
    each = db_ref.shape[0] // 2
    extra[...] = jnp.zeros_like(extra)
    for part in range(2):
        extra[part, 0:2] = sums_ref[0:2]
        biases = [db_ref[part * each + i, kind : kind + 1] for kind in range(2) for i in range(each)]
        extra[part, 2:3] = spread_columns(jnp.concatenate(biases, axis=1), 0, head_part, ns, features)
    extra_ref[...] = extra[...].astype(BF16)
    greet_wait(peers)
    rows.start()
    for copy in others:
        copy.start()
    rows.spread()
    for copy in fetches:
        copy.wait()
    finish_rows(0, dn0_ref)
    rows.finish(z_parts)
    weights.start()
    finish_rows(1, dn1_ref)
    weights.spread()
    weights.finish()
    for micro in range(2):
        row(micro).wait()


def last_sums(dw, db, sums, dn, x, grad_middle, vectors, head_part, ns, nc):
    main, features = dw.shape[1:]
    more = (2, 16 * nc, features)
    rows = main + more[1]
    micros, half, _ = grad_middle.shape
    size, part = rows // nc, features // ns
    return pl.pallas_call(
        functools.partial(last_kernel, ns=ns, nc=nc, head_part=head_part),
        in_specs=[pl.BlockSpec(memory_space=pltpu.VMEM)] * 7
        + [pl.BlockSpec(memory_space=pl.ANY)] * 2
        + [pl.BlockSpec(memory_space=pltpu.VMEM)],
        out_specs=[pl.BlockSpec(memory_space=pltpu.VMEM)] * 2,
        out_shape=[
            jax.ShapeDtypeStruct((micros, 2, half, features), BF16),
            jax.ShapeDtypeStruct((nc, size, part), BF16),
        ],
        scratch_shapes=[
            pltpu.VMEM(more, F32), pltpu.VMEM(more, BF16),
            pltpu.VMEM((micros, half, features), BF16), pltpu.VMEM((micros, half, features), F32),
            pltpu.VMEM((micros, half, features), BF16),
            pltpu.VMEM((rows, features), BF16), pltpu.VMEM((rows, features), BF16), pltpu.VMEM((nc, size, features), BF16),
            pltpu.VMEM((ns, size, part), BF16), pltpu.VMEM((ns, size, part), BF16),
            *axis_sems(micros, 2, nc, ns, nc, micros), pltpu.SemaphoreType.DMA((2,)),
        ],
        compiler_params=params(collective_id=5, has_side_effects=True),
        name="last_sums",
    )(dw, db, sums, *dn, x, grad_middle, vectors)


def results_kernel(out_ref, grad_ref, ffn_ref, attn_ref, *refs, heads, head_part, up_part):
    (out, grad_tokens, g_query, g_key, g_value, g_out, g_up, g_down, g_bq, g_bv, g_bup, *vectors) = refs
    out[...] = out_ref[...]
    grad_tokens[...] = grad_ref[...]
    width, lanes = g_out.shape
    hidden = g_down.shape[0]
    pair = 2 * width // heads

    def values(ref, at, size):
        return ref[at : at + size, :].astype(F32)

    @pl.when(pl.program_id(0) == 0)
    def _():
        g_out[...] = values(ffn_ref, 0, width)
        g_down[...] = values(ffn_ref, width, hidden)
        g_up[...] = values(ffn_ref, width + hidden, hidden).T
        for i in range(heads // 2):
            for kind, ref in enumerate((g_query, g_key, g_value)):
                ref[:, i * pair : (i + 1) * pair] = values(attn_ref, (3 * i + kind) * pair, pair).T
        tail = values(ffn_ref, width + 2 * hidden, 16)
        tail_attn = values(attn_ref, 3 * width, 16)
        rows = (tail[0], tail[1], tail_attn[0], tail_attn[1], tail[2], tail[3])
        for ref, row in zip(vectors, rows):
            ref[...] = row
        for h in range(heads):
            at = h * up_part
            g_bup[h : h + 1] = tail[4 + at // lanes : 5 + at // lanes, at % lanes : at % lanes + up_part]
            for start, ref in ((0, g_bq), (heads * head_part, g_bv)):
                at = start + h * head_part
                ref[h : h + 1] = tail_attn[2 + at // lanes : 3 + at // lanes, at % lanes : at % lanes + head_part]


def write_results(output, grad_tokens, done_ffn, done_attn, shapes, heads, head_part, up_part):
    micros, length, features = output.shape
    steps = 4
    rows = pl.BlockSpec((micros, length // steps, features), lambda i: (0, i, 0))
    return pl.pallas_call(
        functools.partial(results_kernel, heads=heads, head_part=head_part, up_part=up_part),
        grid=(steps,),
        in_specs=[rows, rows, once(done_ffn.shape), once(done_attn.shape)],
        out_specs=[rows, rows] + [full_spec(shape) for shape in shapes],
        out_shape=[jax.ShapeDtypeStruct(output.shape, BF16)] * 2 + [jax.ShapeDtypeStruct(shape, F32) for shape in shapes],
        compiler_params=params(),
        name="results",
    )(output, grad_tokens, done_ffn, done_attn)


def pad_rows(rows, multiple):
    extra = -rows.shape[0] % multiple
    return jnp.concatenate([rows, jnp.zeros((extra,) + rows.shape[1:], rows.dtype)]) if extra else rows


def body(
    tokens, cotangent, w_query, w_key, w_value, w_out, w_up, w_down,
    b_query, b_value, b_up, b_out, b_down, gain_attn, shift_attn, gain_ffn, shift_ffn,
):
    ns, nc = lax.axis_size("shard"), lax.axis_size("ctx")
    t = lax.axis_index("tp")
    micros, _, length, features = tokens.shape
    half = length // 2
    heads, head_part = b_query.shape
    head_width = head_part * ns
    up_part = b_up.shape[1]
    feature_part = b_out.shape[0]

    tables = [b_query, b_value, b_up] + [v[None] for v in (b_out, b_down, gain_attn, shift_attn, gain_ffn, shift_ffn)]
    keys = 2 * nc * half
    aligned = feature_part % 128 == 0
    column_place = place_columns if aligned else place_slot

    def column_shape(w, rows):
        return (2, rows, features) if aligned else (2, ns, rows, w.shape[1])

    def whole_columns(w):
        if not aligned:
            w = w.transpose(0, 2, 1, 3).reshape(2, w.shape[2], features)
        return w

    w_all, x_first, vectors, biases, bup = gather_first((w_query, w_key, w_value), tables, tokens, ns, nc)

    up_ahead = w_up.shape[1] // 4
    plans = [
        (("ctx", nc, place_distance, True, 0), ("shard", ns, place_rows, False, up_ahead)),
        (("shard", ns, column_place, False, 0),),
    ]
    sources = [(tokens, w_up), (w_down,)]
    specs = [
        [once((1, 1, length, features), (1, 0, 0, 0)), once(w_up.shape)],
        [once(w_down.shape)],
    ]
    shapes = [
        ((nc, 2, half, features), (2, features, w_up.shape[1] - up_ahead)),
        (column_shape(w_down, w_down.shape[0]),),
    ]
    guests = [
        (w_up, up_ahead, (2, features, up_ahead), place_rows),
        (w_out, w_out.shape[0], column_shape(w_out, w_out.shape[0]), column_place),
    ]
    x_alls = [x_first.reshape(keys, features), None]
    saved = []
    arrived = []
    for micro in range(micros):
        guest, guest_rows, guest_shape, guest_place = guests[micro]
        normed, k, v, q, early = front(
            x_alls[micro], w_all, vectors, biases, head_width, half, guest, guest_rows,
            guest_shape, ns, guest_place, 6 + micro,
        )
        mixed, qx, *more = attend_forward(
            q, k, v, head_width, plans[micro], sources[micro], specs[micro], shapes[micro], micro + 1
        )
        if micro == 0:
            x_alls[1] = more.pop(0).reshape(keys, features)
        arrived += [early] + more
        saved.append((normed, k, v, qx, mixed))
    up_first, up_rest, wo, wd = arrived
    wo, wd = whole_columns(wo), whole_columns(wd)

    out, grad_middle, grad_mixed, dw, extra = feed_forward(
        tokens, [entry[4] for entry in saved], cotangent, wo, up_first, up_rest, wd, bup, vectors,
        jnp.full((1,), t, jnp.int32), up_part, ns, nc,
    )

    width = heads * head_width
    *starts, dn_first, other_first, dw_parts, output = attend_back_rows(
        saved[0], grad_mixed, x_alls[0], w_all, head_width, dw, extra, out.reshape(micros, half, features), ns, nc
    )
    dw_now, db_now, sums, dn_second, other_second, dw_done = attend_back_shards(
        saved[1], grad_mixed, x_alls[1], w_all, head_width, starts, dw_parts, ns, nc
    )

    grad_tokens, attn_done = last_sums(
        dw_now.reshape(2, 3 * width, features), db_now, sums,
        (dn_first, dn_second, other_first, other_second), tokens, grad_middle.reshape(micros, half, features), vectors, head_part, ns, nc,
    )

    if aligned:
        weights = (w_query, w_key, w_value, w_out, w_up, w_down, b_query, b_value, b_up)
        shapes = [v.shape for v in weights] + [(feature_part,)] * 6
        output, grad_tokens, *grads = write_results(
            output.reshape(micros, length, features), grad_tokens.reshape(micros, length, features),
            dw_done.reshape(-1, feature_part), attn_done.reshape(-1, feature_part), shapes, heads, head_part, up_part,
        )
        g_query, g_key, g_value, g_out, g_up, g_down, g_bq, g_bv, g_bup, *others = grads
        return (output[:, None], grad_tokens[:, None], g_query, g_key, g_value, g_out, g_up, g_down, g_bq, g_bv, g_bup, *others)
    output = output.reshape(micros, 1, length, features)
    grad_tokens = grad_tokens.reshape(micros, 1, length, features)
    done_ffn = dw_done.reshape(-1, feature_part).astype(F32)
    done_attn = attn_done.reshape(-1, feature_part).astype(F32)
    hidden = heads * up_part * ns
    g_out, g_down, g_up = done_ffn[:width], done_ffn[width : width + hidden], done_ffn[width + hidden : width + 2 * hidden]
    tail = done_ffn[width + 2 * hidden :]
    by_kind = done_attn[: 3 * width].reshape(-1, 3, 2 * head_width, feature_part)
    g_query, g_key, g_value = (by_kind[:, i].reshape(width, feature_part).T for i in range(3))
    tail_attn = done_attn[3 * width :]
    g_bup = tail[4:].reshape(-1)[: heads * up_part].reshape(heads, up_part)
    g_heads = tail_attn[2:].reshape(-1)
    g_bq = g_heads[: heads * head_part].reshape(heads, head_part)
    g_bv = g_heads[heads * head_part : 2 * heads * head_part].reshape(heads, head_part)
    return (
        output, grad_tokens, g_query, g_key, g_value, g_out, g_up.T, g_down, g_bq, g_bv, g_bup,
        tail[0], tail[1], tail_attn[0], tail_attn[1], tail[2], tail[3],
    )


def solution(mesh):
    wide, tall = P("shard", "tp"), P("tp", "shard")
    rows, vector = P(None, "shard", "ctx", None), P("shard")
    weights = (wide, wide, wide, tall, wide, tall)
    return jax.shard_map(
        body,
        mesh=mesh,
        in_specs=(rows, rows) + weights + (tall,) * 3 + (vector,) * 6,
        out_specs=(rows, rows) + weights + (tall,) * 3 + (vector,) * 6,
        check_vma=False,
    )
```

```python
import functools
import math

import jax
import jax.numpy as jnp
from jax import lax
from jax.experimental import pallas as pl
from jax.experimental.pallas import tpu as pltpu
from jax.sharding import PartitionSpec as P

F32 = jnp.float32
BF16 = jnp.bfloat16
MESH = pl.DeviceIdType.MESH
norm_eps = 1e-05
LOG2E = math.log2(math.e)
VMEM_LIMIT = 60 * 2**20


def dot_nn(left, right):
    return lax.dot_general(left, right, (((1,), (0,)), ((), ())), preferred_element_type=F32)


def dot_nt(left, right):
    return lax.dot_general(left, right, (((1,), (1,)), ((), ())), preferred_element_type=F32)


def dot_tn(left, right):
    return lax.dot_general(left, right, (((0,), (0,)), ((), ())), preferred_element_type=F32)


def unit_norm(values):
    average = jnp.mean(values, axis=-1, keepdims=True)
    centred = values - average
    variance = jnp.mean(centred * centred, axis=-1, keepdims=True)
    inverse = lax.rsqrt(variance + norm_eps)
    return centred * inverse, inverse


def norm_back(grad_normed, unit_vals, inverse, gain):
    scaled = grad_normed * gain
    return inverse * (
        scaled
        - jnp.mean(scaled, axis=-1, keepdims=True)
        - unit_vals * jnp.mean(scaled * unit_vals, axis=-1, keepdims=True)
    )


def column_sum(values):
    return jnp.sum(values, axis=0, keepdims=True)


def full_spec(shape):
    return pl.BlockSpec(shape, lambda *_: (0,) * len(shape))


def params(limit=VMEM_LIMIT, **others):
    return pltpu.CompilerParams(vmem_limit_bytes=limit, **others)


def once(shape, index=None):
    place = index or (0,) * len(shape)
    return pl.BlockSpec(shape, lambda *_: place, pipeline_mode=pl.Buffered(1))


def send(source, target, send_sem, recv_sem, where):
    return pltpu.make_async_remote_copy(
        src_ref=source, dst_ref=target, send_sem=send_sem, recv_sem=recv_sem, device_id=where, device_id_type=MESH
    )


def greet_first(counts):
    barrier = pltpu.get_barrier_semaphore()
    for name, count in counts:
        me = lax.axis_index(name)
        for d in range(1, count):
            pl.semaphore_signal(barrier, inc=1, device_id={name: me ^ d}, device_id_type=MESH)


def greet_wait(counts):
    pl.semaphore_wait(pltpu.get_barrier_semaphore(), sum(count - 1 for _, count in counts))


def greet(counts):
    greet_first(counts)
    greet_wait(counts)


class Gather:

    def __init__(self, name, count, source, theirs, target, place, sems):
        self.name, self.count, self.source, self.theirs = name, count, source, theirs
        self.target, self.place = target, place
        self.out_sem, self.in_sem, self.cross_out, self.cross_in, self.local = sems
        self.me = lax.axis_index(name)

    def first(self, d):
        where = {self.name: self.me ^ d}
        return send(self.source, self.place(self.target, 0, self.me, d), self.out_sem.at[d], self.in_sem.at[d], where)

    def cross(self, d):
        where = {"tp": 1 - lax.axis_index("tp")}
        owner = self.me ^ d
        source = self.place(self.target, 0, owner, d) if d else self.source
        return send(source, self.place(self.target, 1, owner, d), self.cross_out.at[d], self.cross_in.at[d], where)

    def locals(self):
        copies = [pltpu.make_async_copy(self.source, self.place(self.target, 0, self.me, 0), self.local.at[0])]
        if self.theirs is not None:
            copies.append(pltpu.make_async_copy(self.theirs, self.place(self.target, 1, self.me, 0), self.local.at[1]))
        return copies

    def crossed(self):
        return range(0 if self.theirs is None else 1, self.count)

    def start(self, late=0):
        for d in range(1, self.count - late):
            self.first(d).start()
        for copy in self.locals():
            copy.start()
        if self.theirs is None:
            self.cross(0).start()

    def forward(self, distances=None):
        for d in distances or range(1, self.count):
            self.first(d).wait_recv()
            self.cross(d).start()

    def half(self, d, h):
        size = self.source.shape[0] // 2
        rows = pl.ds(h * size, size)
        i = d + h * self.count
        return send(
            self.source.at[rows, :], self.target.at[d, 0, rows, :], self.out_sem.at[i], self.in_sem.at[i],
            {self.name: self.me ^ d},
        )

    def relay(self, h):
        size = self.source.shape[0] // 2
        rows = pl.ds(h * size, size)
        i = 3 + h * self.count
        return send(
            self.target.at[1 + h, 0, rows, :], self.target.at[3, 0, rows, :], self.out_sem.at[i], self.in_sem.at[i],
            {self.name: self.me ^ (2 - h)},
        )

    def start_relayed(self):
        for h in range(2):
            for d in (1, 2):
                self.half(d, h if d == 1 else 1 - h).start()
        for copy in self.locals():
            copy.start()

    def pass_on(self):
        for h in range(2):
            self.half(1 + h, h).wait_recv()
            self.relay(h).start()

    def forward_near(self):
        for d in (1, 2):
            self.half(d, 1 if d == 1 else 0).wait_recv()
            self.cross(d).start()

    def forward_relayed(self):
        for h in range(2):
            self.relay(h).wait_recv()
        self.cross(3).start()

    def finish(self, relayed=False):
        if relayed:
            for h in range(2):
                for d in (1, 2):
                    self.half(d, h).wait_send()
                self.relay(h).wait_send()
        else:
            for d in range(1, self.count):
                self.first(d).wait_send()
        for d in self.crossed():
            self.cross(d).wait()
        for copy in self.locals():
            copy.wait()


def place_rows(ref, part, owner, d):
    size = ref.shape[1] // lax.axis_size("shard")
    return ref.at[part, pl.ds(pl.multiple_of(owner * size, size), size), :]


def place_columns(ref, part, owner, d):
    size = ref.shape[2] // lax.axis_size("shard")
    return ref.at[part, :, pl.ds(pl.multiple_of(owner * size, size), size)]


def place_slot(ref, part, owner, d):
    return ref.at[part, owner]


def place_distance(ref, part, owner, d):
    return ref.at[d, part]


def gather_sems(count):
    dma = pltpu.SemaphoreType.DMA
    return [dma((2 * count,)), dma((2 * count,)), dma((count,)), dma((count,)), dma((2,))]


def gather_kernel(ns, nc, wq_ref, wk_ref, wv_ref, x_block, *refs):
    tables, (w_out, x_out, vec_out, bias_out, bup_out, small_ref, small_out), sems = refs[:-20], refs[-20:-13], refs[-13:]
    w_send, w_recv, s_send, s_recv, x_send, x_recv, wt_send, wt_recv, st_send, st_recv, xt_send, xt_recv, local = sems
    w_refs = (wq_ref, wk_ref, wv_ref)
    kinds = range(3)
    x_ref = x_block.at[0, 0]
    s = lax.axis_index("shard")
    c = lax.axis_index("ctx")
    t = lax.axis_index("tp")
    other = 1 - t
    depth = wq_ref.shape[0]
    half = x_ref.shape[0] // 2

    peers = [("tp", 2), ("ctx", nc), ("shard", ns)]
    greet_first(peers)
    small_ref[...] = jnp.zeros_like(small_ref)
    row = 0
    for table in tables:
        count, lanes = table.shape
        small_ref[row : row + count, :lanes] = table[...].astype(F32)
        row += count
    greet_wait(peers)

    def w_rows(part, kind, owner):
        return w_out.at[part, kind, pl.ds(pl.multiple_of(owner * depth, depth), depth), :]

    def x_rows(which):
        return x_ref.at[pl.ds(pl.multiple_of(which * half, half), half), :]

    def begin(source, target, send_sem, recv_sem, where):
        copy = send(source, target, send_sem, recv_sem, where)
        copy.start()
        return copy

    x_copies, w_copies, s_copies = {}, {}, {}
    size = half // 2

    def x_part(d, h):
        return x_out.at[d, 0, pl.ds(h * size, size), :]

    def x_begin(source, d, h, to):
        copy = begin(source, x_part(d, h), x_send.at[d, h], x_recv.at[d, h], {"ctx": c ^ to})
        x_copies[d, h] = copy

    relayed = nc == 4
    for h in range(2):
        for d in range(1, 3 if relayed else nc):
            part = h if d % 2 else 1 - h
            source = x_ref.at[pl.ds(pl.multiple_of(t * half + part * size, size), size), :]
            x_begin(source, d, part, d)
    for d in range(1, ns):
        for k in kinds:
            w_copies[d, k] = begin(
                w_refs[k], w_rows(0, k, s), w_send.at[k, d], w_recv.at[k, d], {"shard": s ^ d}
            )
        s_copies[d] = begin(small_ref, small_out.at[0, s], s_send.at[d], s_recv.at[d], {"shard": s ^ d})
    last = [begin(w_refs[k], w_rows(1, k, s), wt_send.at[k, 0], wt_recv.at[k, 0], {"tp": other}) for k in kinds]
    last.append(begin(small_ref, small_out.at[1, s], st_send.at[0], st_recv.at[0], {"tp": other}))
    locals_ = [pltpu.make_async_copy(w_refs[k], w_rows(0, k, s), local.at[k]) for k in kinds]
    locals_ += [
        pltpu.make_async_copy(small_ref, small_out.at[0, s], local.at[3]),
        pltpu.make_async_copy(x_rows(t), x_out.at[0, 0], local.at[4]),
        pltpu.make_async_copy(x_rows(other), x_out.at[0, 1], local.at[5]),
    ]
    for copy in locals_:
        copy.start()
    if relayed:
        x_copies[1, 0].wait_recv()
        x_begin(x_part(1, 0), 3, 0, 2)
        x_copies[2, 1].wait_recv()
        x_begin(x_part(2, 1), 3, 1, 1)
    waited = {(1, 0), (2, 1)} if relayed else set()
    for d in range(1, max(ns, nc)):
        if d < ns:
            for k in kinds:
                w_copies[d, k].wait_recv()
                last.append(
                    begin(
                        w_rows(0, k, s ^ d), w_rows(1, k, s ^ d), wt_send.at[k, d], wt_recv.at[k, d], {"tp": other}
                    )
                )
            s_copies[d].wait_recv()
            last.append(
                begin(small_out.at[0, s ^ d], small_out.at[1, s ^ d], st_send.at[d], st_recv.at[d], {"tp": other})
            )
        if d < nc:
            for h in range(2):
                if (d, h) not in waited:
                    x_copies[d, h].wait_recv()
            last.append(begin(x_out.at[d, 0], x_out.at[d, 1], xt_send.at[d], xt_recv.at[d], {"tp": other}))
    for copies in (x_copies, w_copies, s_copies):
        for copy in copies.values():
            copy.wait_send()
    for copy in last:
        copy.wait()
    for copy in locals_:
        copy.wait()
    heads = tables[0].shape[0]
    vec_out[...] = jnp.zeros_like(vec_out)
    bias_out[...] = jnp.zeros_like(bias_out)
    for shard in range(ns):
        width = tables[3].shape[1]
        for i in range(len(tables) - 3):
            row = small_out[0, shard, 3 * heads + i : 3 * heads + i + 1, :width]
            vec_out[i : i + 1, shard * width : (shard + 1) * width] = row
        for which in range(3):
            width = tables[which].shape[1]
            for part in range(2):
                for h in range(heads):
                    row = small_out[part, shard, which * heads + h : which * heads + h + 1, :width]
                    at = (h * ns + shard) * width
                    if which == 2:
                        bup_out[part, :, at : at + width] = row
                    else:
                        at += part * heads * ns * width
                        bias_out[which : which + 1, at : at + width] = row


def gather_first(weights, tables, tokens, ns, nc):
    depth, width = weights[0].shape
    length, features = tokens.shape[2:]
    rows = -(-sum(table.shape[0] for table in tables) // 8) * 8
    lanes = -(-max(table.shape[1] for table in tables) // 128) * 128
    finals = [(8, features), (8, 2 * tables[0].size * ns), (2, 1, tables[2].size * ns)]
    dma = pltpu.SemaphoreType.DMA
    vmem = pl.BlockSpec(memory_space=pltpu.VMEM)
    return pl.pallas_call(
        functools.partial(gather_kernel, ns, nc),
        grid=(1,),
        in_specs=[vmem] * 3 + [once((1, 1, length, features))] + [vmem] * len(tables),
        out_specs=[pl.BlockSpec(memory_space=pl.ANY)] * 2 + [full_spec(shape) for shape in finals],
        out_shape=[
            jax.ShapeDtypeStruct((2, 3, ns * depth, width), BF16),
            jax.ShapeDtypeStruct((nc, 2, length // 2, features), BF16),
        ]
        + [jax.ShapeDtypeStruct(shape, F32) for shape in finals],
        scratch_shapes=[pltpu.VMEM((rows, lanes), F32), pltpu.VMEM((2, ns, rows, lanes), F32)]
        + [dma((3, ns)), dma((3, ns)), dma((ns,)), dma((ns,)), dma((nc, 2)), dma((nc, 2))]
        + [dma((3, ns)), dma((3, ns)), dma((ns,)), dma((ns,)), dma((nc,)), dma((nc,)), dma((6,))],
        compiler_params=params(collective_id=0, has_side_effects=True),
        name="gather_first",
    )(*weights, tokens, *tables)


def project_rows(x, w_ref, vec_ref, bias_ref, n_ref, k_ref, v_ref):
    gain, shift = vec_ref[2:3], vec_ref[3:4]
    width = w_ref.shape[3]
    size = n_ref.shape[0] // 4
    for i in range(4):
        rows = slice(i * size, (i + 1) * size)
        unit, _ = unit_norm(x(i, size).astype(F32))
        normed = (unit * gain + shift).astype(BF16)
        n_ref[rows] = normed
        for part in range(2):
            cols = slice(part * width, (part + 1) * width)
            k_ref[rows, cols] = dot_nn(normed, w_ref[part, 1]).astype(BF16)
            v_ref[rows, cols] = (dot_nn(normed, w_ref[part, 2]) + bias_ref[1:2, cols]).astype(BF16)


def project_query(w_ref, bias_ref, n_ref, q_ref, q_scale):
    width = w_ref.shape[3]
    normed = n_ref[: q_ref.shape[0]]
    for part in range(2):
        cols = slice(part * width, (part + 1) * width)
        q_ref[:, cols] = ((dot_nn(normed, w_ref[part, 0]) + bias_ref[0:1, cols]) * q_scale).astype(BF16)


def front_kernel(
    x_ref, w_ref, vec_ref, bias_ref, guest_ref, n_ref, k_ref, v_ref, q_ref, guest_all, *sems, q_scale, ns, place, size
):
    step = pl.program_id(0)
    part = guest_ref.at[:, pl.ds(0, size)] if place is place_rows else guest_ref.at[pl.ds(0, size), :]
    gather = Gather("shard", ns, part, None, guest_all, place, sems)

    peers = [("tp", 2), ("shard", ns)]

    @pl.when(step == 0)
    def _():
        greet_first(peers)

    @pl.when(step == 1)
    def _():
        greet_wait(peers)
        gather.start()

    project_rows(lambda i, size: x_ref[i * size : (i + 1) * size], w_ref, vec_ref, bias_ref, n_ref, k_ref, v_ref)

    @pl.when(step == 0)
    def _():
        project_query(w_ref, bias_ref, n_ref, q_ref, q_scale)

    @pl.when(step == pl.num_programs(0) - 1)
    def _():
        gather.forward()
        gather.finish()


def front(x_all, weights, vectors, biases, head_width, half, guest, guest_rows, guest_shape, ns, place, number):
    keys, features = x_all.shape
    block = 2 * half
    width = 2 * weights.shape[3]
    scale = LOG2E / math.sqrt(head_width)
    return pl.pallas_call(
        functools.partial(front_kernel, q_scale=scale, ns=ns, place=place, size=guest_rows),
        grid=(keys // block,),
        in_specs=[
            pl.BlockSpec((block, features), lambda i: (i, 0)),
            once(weights.shape),
            once(vectors.shape),
            once(biases.shape),
            once(guest.shape),
        ],
        out_specs=[
            pl.BlockSpec((block, features), lambda i: (i, 0)),
            pl.BlockSpec((block, width), lambda i: (i, 0)),
            pl.BlockSpec((block, width), lambda i: (i, 0)),
            full_spec((half, width)),
            pl.BlockSpec(memory_space=pl.ANY),
        ],
        out_shape=[
            jax.ShapeDtypeStruct((keys, features), BF16),
            jax.ShapeDtypeStruct((keys, width), BF16),
            jax.ShapeDtypeStruct((keys, width), BF16),
            jax.ShapeDtypeStruct((half, width), BF16),
            jax.ShapeDtypeStruct(guest_shape, BF16),
        ],
        scratch_shapes=gather_sems(ns),
        compiler_params=params(collective_id=number, has_side_effects=True),
        cost_estimate=pl.CostEstimate(
            flops=4 * keys * features * width, bytes_accessed=8 * keys * features, transcendentals=keys
        ),
        name="front",
    )(x_all, weights, vectors, biases, guest)


def with_parts(lane, base, values, first, width):
    high = values.astype(BF16).astype(F32)
    rest = values - high
    middle = rest.astype(BF16).astype(F32)
    low = rest - middle
    extra = jnp.where(
        lane == first, high, jnp.where(lane == first + 1, middle, jnp.where(lane == first + 2, low, 0.0))
    )
    inside = (lane < width) if first else (lane >= width)
    return jnp.where(inside, base, extra)


def attend_kernel(*refs, kc, width, plans):
    count = len(plans)
    q_ref, k_ref, v_ref = refs[:3]
    sources = refs[3 : 3 + count]
    o_ref, qx_ref = refs[3 + count : 5 + count]
    targets = refs[5 + count : 5 + 2 * count]
    scores = refs[5 + 2 * count]
    sems = refs[6 + 2 * count :]
    step = pl.program_id(0)
    last = pl.num_programs(0) - 1
    t = lax.axis_index("tp")

    def gathers(wanted):
        found = []
        for i, (name, number, place, split, start) in enumerate(plans):
            if name != wanted:
                continue
            source, theirs = sources[i], None
            if split:
                source = source.at[0, 0]
                half = source.shape[0] // 2
                theirs = source.at[pl.ds(pl.multiple_of((1 - t) * half, half), half), :]
                source = source.at[pl.ds(pl.multiple_of(t * half, half), half), :]
            elif start and place is place_rows:
                source = source.at[:, pl.ds(start, source.shape[1] - start)]
            elif start:
                source = source.at[pl.ds(start, source.shape[0] - start), :]
            found.append(Gather(name, number, source, theirs, targets[i], place, sems[5 * i : 5 * i + 5]))
        return found

    counts = {name: number for name, number, *_ in plans}

    peers = [("tp", 2)] + list(counts.items())
    far = counts.get("ctx", 1) - 1
    relayed = far == 3

    @pl.when(step == 0)
    def _():
        greet_first(peers)


    rows, lanes = q_ref.shape
    keys = k_ref.shape[0]
    lane = lax.broadcasted_iota(jnp.int32, (rows, lanes), 1)
    lane_v = lax.broadcasted_iota(jnp.int32, (kc, lanes), 1)
    q = q_ref[...].astype(F32)
    tops = []
    for h in range(2):
        inside = (lane < width) if h == 0 else (lane >= width)
        q_head = jnp.where(inside, q, 0.0).astype(BF16)
        top = None
        for i in range(keys // kc):
            part = dot_nt(k_ref[i * kc : (i + 1) * kc], q_head)
            scores[h, i * kc : (i + 1) * kc] = part
            here = jnp.max(part.reshape(kc // 8, 8, rows), axis=0)
            top = here if top is None else jnp.maximum(top, here)
        tops.append(jnp.max(top, axis=0, keepdims=True))

    @pl.when(step == 0)
    def _():
        greet_wait(peers)
        for gather in gathers("shard"):
            gather.start()
        for gather in gathers("ctx"):
            if relayed:
                gather.start_relayed()
            else:
                gather.start(1)

    @pl.when(step == 1)
    def _():
        for gather in gathers("ctx"):
            if relayed:
                gather.pass_on()

    @pl.when(step == 2)
    def _():
        for gather in gathers("ctx"):
            if relayed:
                gather.forward_near()
            else:
                gather.first(far).start()
                gather.forward(range(1, far))

    def forward_last():
        for gather in gathers("shard"):
            gather.forward()
        for gather in gathers("ctx"):
            if relayed:
                gather.forward_relayed()
            else:
                gather.forward([far])

    if far:
        pl.when(step == last)(forward_last)

    outs = []
    for h in range(2):
        inside_v = (lane_v < width) if h == 0 else (lane_v >= width)
        total = jnp.zeros((lanes, rows), F32)
        for i in range(keys // kc):
            v_one = jnp.where(inside_v, v_ref[i * kc : (i + 1) * kc], jnp.ones((), BF16))
            exponent = jnp.exp2(scores[h, i * kc : (i + 1) * kc] - tops[h]).astype(BF16)
            total += dot_tn(v_one, exponent)
        first = width if h == 0 else 0
        log_total = tops[h] + jnp.log2(total[first : first + 1, :])
        total = total.T
        outs.append(total / pltpu.roll(total, width, 1))
        log_column = jnp.broadcast_to(log_total, (8, rows)).T[:, :1]
        qx_ref[:, h * lanes : (h + 1) * lanes] = with_parts(lane, q, -log_column, first, width).astype(BF16)
    o_ref[...] = jnp.where(lane < width, outs[0], outs[1]).astype(BF16)

    @pl.when(step == last)
    def _():
        if not far:
            forward_last()
        for name in counts:
            for gather in gathers(name):
                gather.finish(relayed and name == "ctx")


def attend_forward(q, k, v, width, plans, sources, source_specs, shapes, number):
    rows, cols = q.shape
    keys = k.shape[0]
    lanes = 2 * width
    kc = 512
    anywhere = pl.BlockSpec(memory_space=pl.ANY)
    return pl.pallas_call(
        functools.partial(attend_kernel, kc=kc, width=width, plans=plans),
        grid=(cols // lanes,),
        in_specs=[
            pl.BlockSpec((rows, lanes), lambda j: (0, j)),
            pl.BlockSpec((keys, lanes), lambda j: (0, j)),
            pl.BlockSpec((keys, lanes), lambda j: (0, j)),
        ]
        + source_specs,
        out_specs=[
            pl.BlockSpec((rows, lanes), lambda j: (0, j)),
            pl.BlockSpec((rows, 2 * lanes), lambda j: (0, j)),
        ]
        + [anywhere] * len(plans),
        out_shape=[
            jax.ShapeDtypeStruct((rows, cols), BF16),
            jax.ShapeDtypeStruct((rows, 2 * cols), BF16),
        ]
        + [jax.ShapeDtypeStruct(shape, BF16) for shape in shapes],
        scratch_shapes=[pltpu.VMEM((2, keys, rows), F32)]
        + [sem for plan in plans for sem in gather_sems(plan[1])],
        compiler_params=params(collective_id=number, has_side_effects=True),
        cost_estimate=pl.CostEstimate(
            flops=12 * rows * keys * cols, bytes_accessed=4 * keys * cols, transcendentals=rows * keys * cols // width
        ),
        name="attend_forward",
    )(q, k, v, *sources)


def sum_rows(target, at, left, left_at, right, right_at, rows, chunk=64):
    def one(i, carry):
        here = pl.multiple_of(i * chunk, chunk)
        target[pl.ds(at + here, chunk), :] = left[pl.ds(left_at + here, chunk), :] + right[pl.ds(right_at + here, chunk), :]
        return carry

    lax.fori_loop(0, rows // chunk, one, 0)


class Axis:

    def __init__(self, name, count, sems):
        self.name, self.count, self.sems = name, count, sems
        self.me = lax.axis_index(name)

    def copy(self, d, source, target):
        return send(source(self.me ^ d, d), target(self.me, d), self.sems[0].at[d], self.sems[1].at[d], {self.name: self.me ^ d})

    def start(self, source, target):
        for d in range(1, self.count):
            self.copy(d, source, target).start()

    def wait(self, source, target):
        for d in range(1, self.count):
            self.copy(d, source, target).wait()


def axis_sems(*counts):
    return [pltpu.SemaphoreType.DMA((count,)) for count in counts for _ in range(2)]


def cross(source, target, sems, i):
    return send(source, target, sems[0].at[i], sems[1].at[i], {"tp": 1 - lax.axis_index("tp")})


class RowSum:

    def __init__(self, dw_send, dw_own, extra, received, total, blocks, tp_sems, ctx):
        self.dw_send, self.dw_own, self.extra = dw_send, dw_own, extra
        self.received, self.total, self.blocks = received, total, blocks
        self.tp_sems, self.ctx = tp_sems, ctx
        self.main, self.more = dw_own.shape[0], extra.shape[1]
        self.size = (self.main + self.more) // ctx.count

    def crossing(self):
        return [
            cross(self.dw_send, self.received.at[pl.ds(0, self.main), :], self.tp_sems, 0),
            cross(self.extra.at[1], self.received.at[pl.ds(self.main, self.more), :], self.tp_sems, 1),
        ]

    def start(self):
        for copy in self.crossing():
            copy.start()

    def source(self, peer, d):
        return self.total.at[pl.ds(pl.multiple_of(peer * self.size, 16), self.size), :]

    def target(self, me, d):
        return self.blocks.at[d]

    def spread(self):
        for copy in self.crossing():
            copy.wait()
        sum_rows(self.total, 0, self.dw_own, 0, self.received, 0, self.main)
        sum_rows(self.total, self.main, self.extra.at[0], 0, self.received, self.main, self.more)
        self.ctx.start(self.source, self.target)

    def finish(self, out):
        self.ctx.wait(self.source, self.target)
        count, size, width = out.shape
        value = self.total[pl.ds(pl.multiple_of(self.ctx.me * self.size, 16), self.size), :].astype(F32)
        for d in range(1, self.ctx.count):
            value += self.blocks[d].astype(F32)
        for j in range(count):
            out[j] = value[:, j * width : (j + 1) * width].astype(out.dtype)


class ShardSum:

    def __init__(self, parts, received, blocks, shard, ctx):
        self.parts, self.received, self.blocks, self.shard, self.ctx = parts, received, blocks, shard, ctx

    def source(self, peer, d):
        return self.parts.at[peer]

    def target(self, me, d):
        return self.received.at[d]

    def start(self):
        self.shard.start(self.source, self.target)

    def mine(self, peer, d):
        return self.blocks.at[self.ctx.me]

    def theirs(self, me, d):
        return self.blocks.at[me]

    def spread(self):
        self.shard.wait(self.source, self.target)
        value = self.parts[self.shard.me].astype(F32)
        for d in range(1, self.shard.count):
            value += self.received[d].astype(F32)
        self.blocks[self.ctx.me] = value.astype(BF16)
        self.ctx.start(self.mine, self.theirs)

    def finish(self):
        self.ctx.wait(self.mine, self.theirs)


class InputSum:

    def __init__(self, dn_send, dn_own, received, total, blocks, tp_sems, ctx):
        self.dn_send, self.dn_own, self.received = dn_send, dn_own, received
        self.total, self.blocks, self.tp_sems, self.ctx = total, blocks, tp_sems, ctx

    def crossing(self, d):
        return cross(self.dn_send(d), self.received.at[d], self.tp_sems, d)

    def source(self, peer, d):
        return self.total.at[d]

    def target(self, me, d):
        return self.blocks.at[d]

    def spread_one(self, d):
        self.crossing(d).wait()
        sum_rows(self.total.at[d], 0, self.dn_own(d), 0, self.received.at[d], 0, self.received.shape[1])
        self.ctx.copy(d, self.source, self.target).start()

    def finish(self):
        self.ctx.wait(self.source, self.target)

    def rows(self, own, at, size):
        value = own[pl.ds(at, size), :]
        for d in range(1, self.ctx.count):
            value += self.blocks[d, pl.ds(at, size), :].astype(F32)
        return value


def attend_back_step(refs, scratch, starts, width):
    qx_ref, k_ref, v_ref, go_ref, o_ref, n_ref, x_ref, w_ref = refs
    gx_all, dq_acc, dn_acc, dw_acc, db_ref, sums_ref = scratch
    i, j = pl.program_id(0), pl.program_id(1)
    last_block, last_pair = pl.num_programs(0) - 1, pl.num_programs(1) - 1
    rows, lanes = o_ref.shape
    keys = k_ref.shape[0]
    lane = lax.broadcasted_iota(jnp.int32, (rows, lanes), 1)
    lane_k = lax.broadcasted_iota(jnp.int32, (keys, lanes), 1)
    one = jnp.ones((), BF16)

    @pl.when(i == 0)
    def _():
        grad_out = go_ref[...].astype(F32)
        both = grad_out * o_ref[...].astype(F32)
        for h in range(2):
            inside = (lane < width) if h == 0 else (lane >= width)
            delta = jnp.sum(jnp.where(inside, both, 0.0), axis=1, keepdims=True)
            gx_all[j, h] = with_parts(lane, grad_out, -delta, width if h == 0 else 0, width).astype(BF16)
        dq_acc[j] = jnp.zeros(dq_acc.shape[1:], F32)
        dw_acc[j] = starts[0][j] if starts else jnp.zeros(dw_acc.shape[1:], F32)
        db_ref[j] = starts[1][j] if starts else jnp.zeros(db_ref.shape[1:], F32)

    @pl.when((i == 0) & (j == 0))
    def _():
        sums_ref[...] = starts[2][...] if starts else jnp.zeros_like(sums_ref)

    @pl.when(j == 0)
    def _():
        dn_acc[...] = jnp.zeros_like(dn_acc)

    grad_k, grad_v, grad_q = [], [], []
    for h in range(2):
        inside_k = (lane_k < width) if h == 0 else (lane_k >= width)
        kx = jnp.where(inside_k, k_ref[...], one)
        vx = jnp.where(inside_k, v_ref[...], one)
        qx = qx_ref[:, h * lanes : (h + 1) * lanes]
        gx = gx_all[j, h]
        prob = jnp.exp2(dot_nt(kx, qx))
        grad_v.append(dot_nn(prob.astype(BF16), gx))
        grad_score = (prob * dot_nt(vx, gx)).astype(BF16)
        grad_k.append(dot_nn(grad_score, qx))
        grad_q.append(dot_tn(kx, grad_score))
    dk = (jnp.where(lane_k < width, grad_k[0], grad_k[1]) * (1.0 / LOG2E)).astype(BF16)
    dv = jnp.where(lane_k < width, grad_v[0], grad_v[1]).astype(BF16)
    dq_acc[j] += jnp.concatenate([grad_q[0][:width], grad_q[1][width:]], axis=0)
    both = jnp.concatenate([dk, dv], axis=1)
    weights = jnp.concatenate([w_ref[0, 1], w_ref[0, 2]], axis=1)
    dn_acc[...] += dot_nt(both, weights)
    grad_w = dot_tn(both, n_ref[...])
    dw_acc[j, 1] += grad_w[:lanes]
    dw_acc[j, 2] += grad_w[lanes:]
    db_ref[j, 1:2] += column_sum(dv.astype(F32))

    @pl.when(i == last_block)
    def _():
        dq = (dq_acc[j].T * (1.0 / math.sqrt(width))).astype(BF16)
        dn_acc[:rows] += dot_nt(dq, w_ref[0, 0])
        dw_acc[j, 0] += dot_tn(dq, n_ref[:rows])
        db_ref[j, 0:1] += column_sum(dq.astype(F32))

    @pl.when(j == last_pair)
    def _():
        unit, _ = unit_norm(x_ref[...].astype(F32))
        sums_ref[0:1] += column_sum(dn_acc[...] * unit)
        sums_ref[1:2] += column_sum(dn_acc[...])


def attend_back_kernel(*refs, width, nc, ns, hosted, hosted_counts, started):
    i, j = pl.program_id(0), pl.program_id(1)
    last_pair = pl.num_programs(1) - 1
    n_in, n_out, n_scratch = hosted_counts
    at = 8
    base = refs[:at]
    starts = refs[at : at + 3] if started else ()
    at += 3 if started else 0
    extra_in, at = refs[at : at + n_in], at + n_in
    (dw_ref, db_ref, sums_ref, dn_done, dn_other), at = refs[at : at + 5], at + 5
    extra_out, at = refs[at : at + n_out], at + n_out
    gx_all, dq_acc, dn_acc, dw_acc, dn_sent, dn_received, dn_total, dn_blocks, tp_out, tp_in, ctx_out, ctx_in = refs[at : at + 12]
    extra_scratch = refs[at + 12 :]
    inputs = InputSum(
        lambda d: dn_sent.at[d, 1], lambda d: dn_sent.at[d, 0], dn_received, dn_total, dn_blocks,
        (tp_out, tp_in), Axis("ctx", nc, (ctx_out, ctx_in)),
    )
    guest = hosted(extra_in, extra_out, extra_scratch, nc, ns)

    @pl.when((i == 0) & (j == 0))
    def _():
        greet_first(guest.peers)

    @pl.when((i == 0) & (j == 1))
    def _():
        greet_wait(guest.peers)
        guest.begin()

    @pl.when((i == 1) & (j == 2))
    def _():
        guest.middle()

    for d in range(1, nc):

        @pl.when((i == nc - d) & (j == 0))
        def _(d=d):
            inputs.crossing(d).start()

        @pl.when((i == nc - d) & (j == 1))
        def _(d=d):
            inputs.spread_one(d)

    attend_back_step(
        base, (gx_all, dq_acc, dn_acc, dw_acc, db_ref, sums_ref), starts, width
    )

    half = dn_acc.shape[0] // 2

    @pl.when((j == last_pair) & (i < nc - 1))
    def _():
        for part in range(2):
            dn_sent[nc - 1 - i, part] = dn_acc[part * half : (part + 1) * half].astype(BF16)

    @pl.when((i == nc - 1) & (j == last_pair))
    def _():
        dw_ref[...] = dw_acc[...].astype(dw_ref.dtype)
        dn_other[...] = dn_acc[half:].astype(BF16)
        guest.end()
        inputs.finish()
        size = 64

        def one(r, carry):
            here = pl.multiple_of(r * size, size)
            dn_done[pl.ds(here, size), :] = inputs.rows(dn_acc, here, size)
            return carry

        lax.fori_loop(0, half // size, one, 0)


class HostRows:

    def __init__(self, ins, outs, scratch, nc, ns):
        dw_all, dw_own, extra, out_half = ins
        self.dw_out, whole = outs
        received, total, blocks, tp_out, tp_in, ctx_out, ctx_in, sems = scratch
        t = lax.axis_index("tp")
        self.rows = RowSum(
            dw_all.at[1], dw_own.at[0], extra, received, total, blocks, (tp_out, tp_in), Axis("ctx", nc, (ctx_out, ctx_in))
        )
        self.copies = lambda: [
            cross(out_half, whole.at[:, t], (sems, sems.at[pl.ds(1, 1)]), 0),
            pltpu.make_async_copy(out_half, whole.at[:, t], sems.at[2]),
        ]
        self.peers = [("tp", 2), ("ctx", nc)]

    def begin(self):
        self.rows.start()
        for copy in self.copies():
            copy.start()

    def middle(self):
        self.rows.spread()

    def end(self):
        self.rows.finish(self.dw_out)
        for copy in self.copies():
            copy.wait()


class HostShards:

    def __init__(self, ins, outs, scratch, nc, ns):
        (self.done,) = outs
        received, self.blocks, z_out, z_in, back_out, back_in = scratch
        self.sums = ShardSum(
            ins[0], received, self.blocks, Axis("shard", ns, (z_out, z_in)), Axis("ctx", nc, (back_out, back_in))
        )
        self.peers = [("tp", 2), ("ctx", nc), ("shard", ns)]

    def begin(self):
        self.sums.start()

    def middle(self):
        self.sums.spread()

    def end(self):
        self.sums.finish()
        self.done[...] = self.blocks[...]


def attend_back(
    hosted, entry, grad_mixed, x_all, weights, width, micro, starts, kind, ins, in_specs, outs, out_specs, scratch, number, ns, nc
):
    normed, k, v, qx, mixed = entry
    rows, cols = mixed.shape
    keys, features = normed.shape
    lanes = 2 * width
    pairs = cols // lanes
    size = keys // nc
    each = pairs // 2
    stack = (pairs, 3, lanes, features)
    block = pltpu.VMEM((nc, rows, features), BF16)

    def key_block(shape, column):
        return pl.BlockSpec(shape, lambda i, j: (nc - 1 - i, j if column else 0))

    return pl.pallas_call(
        functools.partial(
            attend_back_kernel, width=width, nc=nc, ns=ns, hosted=hosted,
            hosted_counts=(len(ins), len(outs), len(scratch)), started=bool(starts),
        ),
        grid=(nc, pairs),
        in_specs=[
            pl.BlockSpec((rows, 2 * lanes), lambda i, j: (0, j)),
            key_block((size, lanes), True),
            key_block((size, lanes), True),
            pl.BlockSpec((rows, lanes), lambda i, j: (micro, j)),
            pl.BlockSpec((rows, lanes), lambda i, j: (0, j)),
            key_block((size, features), False),
            key_block((size, features), False),
            pl.BlockSpec((1, 3, features, lanes), lambda i, j: (j // each, 0, 0, j % each)),
        ]
        + [once(value.shape) for value in starts]
        + in_specs,
        out_specs=[full_spec(stack), full_spec((pairs, 8, lanes)), full_spec((8, features))]
        + [full_spec((rows, features))] * 2
        + out_specs,
        out_shape=[
            jax.ShapeDtypeStruct(stack, kind),
            jax.ShapeDtypeStruct((pairs, 8, lanes), F32),
            jax.ShapeDtypeStruct((8, features), F32),
            jax.ShapeDtypeStruct((rows, features), F32),
            jax.ShapeDtypeStruct((rows, features), BF16),
        ]
        + outs,
        scratch_shapes=[
            pltpu.VMEM((pairs, 2, rows, lanes), BF16),
            pltpu.VMEM((pairs, lanes, rows), F32),
            pltpu.VMEM((size, features), F32),
            pltpu.VMEM(stack, F32),
            pltpu.VMEM((nc, 2, rows, features), BF16),
            block, block, block,
            *axis_sems(nc, nc),
        ]
        + scratch,
        compiler_params=params(collective_id=number, has_side_effects=True),
        cost_estimate=pl.CostEstimate(
            flops=30 * rows * keys * cols, bytes_accessed=8 * keys * cols, transcendentals=rows * keys * cols // width
        ),
        name="attend_back",
    )(qx, k, v, grad_mixed, mixed, normed, x_all, weights, *starts, *ins)


def attend_back_rows(entry, grad_mixed, x_all, weights, width, dw, extra, out, ns, nc):
    main, features = dw.shape[1:]
    rows = main + extra.shape[1]
    block = (nc, rows // nc, features)
    parts = (ns, rows // nc, features // ns)
    micros, half, _ = out.shape
    anywhere = pl.BlockSpec(memory_space=pl.ANY)
    return attend_back(
        HostRows, entry, grad_mixed, x_all, weights, width, 0, (), F32,
        [dw, dw, extra, out],
        [anywhere, once((1, main, features)), once(extra.shape), once(out.shape)],
        [jax.ShapeDtypeStruct(parts, BF16), jax.ShapeDtypeStruct((micros, 2, half, features), BF16)],
        [full_spec(parts), anywhere],
        [
            pltpu.VMEM((rows, features), BF16), pltpu.VMEM((rows, features), BF16), pltpu.VMEM(block, BF16),
            *axis_sems(2, nc), pltpu.SemaphoreType.DMA((3,)),
        ],
        3, ns, nc,
    )


def attend_back_shards(entry, grad_mixed, x_all, weights, width, starts, dw_parts, ns, nc):
    _, size, part = dw_parts.shape
    return attend_back(
        HostShards, entry, grad_mixed, x_all, weights, width, 1, starts, BF16,
        [dw_parts], [once(dw_parts.shape)],
        [jax.ShapeDtypeStruct((nc, size, part), BF16)], [full_spec((nc, size, part))],
        [pltpu.VMEM(dw_parts.shape, BF16), pltpu.VMEM((nc, size, part), BF16), *axis_sems(ns, nc)],
        4, ns, nc,
    )


def ffn_kernel(
    where_ref, x_ref, o0_ref, o1_ref, g_ref, w_out, up_first, up_rest, w_down, bup_ref, vec_ref,
    out_ref, gm_ref, gx_ref, dw_ref, extra_ref, dw_acc, w_up, dup_ref, dvec_ref, extra, *, ns, up_part,
):
    step = pl.program_id(0)
    steps = pl.num_programs(0)
    b_out, b_down, gain, shift = (vec_ref[i : i + 1, :] for i in (0, 1, 4, 5))
    hw = w_out.shape[1]
    hidden = bup_ref.shape[2]

    @pl.when(step == 0)
    def _():
        split = up_first.shape[2]
        w_up[:, :, :split] = up_first[...]
        w_up[:, :, split:] = up_rest[...]
        dw_acc[...] = jnp.zeros_like(dw_acc)
        dup_ref[...] = jnp.zeros_like(dup_ref)
        dvec_ref[...] = jnp.zeros_like(dvec_ref)

    mixed = jnp.where(2 * step < steps, o0_ref[...], o1_ref[...])
    grad_b = g_ref[0, 0]
    grad = grad_b.astype(F32)
    attended = dot_nn(mixed[:, :hw], w_out[0]) + dot_nn(mixed[:, hw:], w_out[1])
    middle = x_ref[0, 0].astype(F32) + (attended + b_out)
    unit, inverse = unit_norm(middle)
    normed = (unit * gain + shift).astype(BF16)
    ffn_out = jnp.zeros_like(middle)
    grad_normed = jnp.zeros_like(middle)
    for part in range(2):
        pre = dot_nn(normed, w_up[part]) + bup_ref[part]
        gate = 0.5 + 0.5 * lax.erf(pre * math.sqrt(0.5))
        active = (pre * gate).astype(BF16)
        ffn_out += dot_nn(active, w_down[part])
        slope = gate + pre * jnp.exp(pre * pre * -0.5) * (1.0 / math.sqrt(2.0 * math.pi))
        grad_pre_f = dot_nt(grad_b, w_down[part]) * slope
        grad_pre = grad_pre_f.astype(BF16)
        dup_ref[part] += column_sum(grad_pre.astype(F32))
        grad_normed += dot_nt(grad_pre, w_up[part])
        dw_acc[part, hw : hw + hidden] += dot_tn(active, grad_b)
        dw_acc[part, hw + hidden :] += dot_tn(grad_pre, normed)
    out_ref[...] = (middle + (ffn_out + b_down)).astype(BF16)
    grad_middle = grad + norm_back(grad_normed, unit, inverse, gain)
    gm_ref[...] = grad_middle
    grad_att = grad_middle.astype(BF16)
    dvec_ref[0:1] += column_sum(grad_att.astype(F32))
    dvec_ref[1:2] += column_sum(grad)
    dvec_ref[2:3] += column_sum(grad_normed * unit)
    dvec_ref[3:4] += column_sum(grad_normed)
    for part in range(2):
        cols = slice(part * hw, (part + 1) * hw)
        gx_ref[:, cols] = dot_nt(grad_att, w_out[part]).astype(BF16)
        dw_acc[part, :hw] += dot_tn(mixed[:, cols], grad_att)

    @pl.when(step == steps - 1)
    def _():
        dw_ref[...] = dw_acc[...].astype(BF16)
        features = dvec_ref.shape[1]
        extra[...] = jnp.zeros_like(extra)
        for part in range(2):
            extra[part, 0:4] = dvec_ref[0:4]
            for r in range(hidden // features):
                extra[part, 4 + r : 5 + r] = spread_columns(dup_ref[part], r, up_part, ns, features)
        extra_ref[...] = extra[...].astype(BF16)


def spread_columns(row, r, size, ns, features):
    count = row.shape[1]
    width = features // ns
    column = lax.broadcasted_iota(jnp.int32, (1, features), 1)
    shard = column // width
    place = r * width + column % width
    source = (place // size) * (size * ns) + shard * size + place % size
    chosen = jnp.where(lax.broadcasted_iota(jnp.int32, (count, features), 0) == source, 1.0, 0.0).astype(BF16)
    return dot_nn(jnp.broadcast_to(row.astype(BF16), (16, count)), chosen)[0:1]


def feed_forward(tokens, mixed, cotangent, w_out, up_first, up_rest, w_down, b_up, vectors, where, up_part, ns, nc):
    micros, _, length, features = tokens.shape
    block = 256
    half = length // 2
    each = half // block
    rows = micros * half
    hw, hidden = w_out.shape[1], b_up.shape[2]
    total = hw + 2 * hidden
    more = (2, 16 * nc, features)
    row_spec = pl.BlockSpec((block, features), lambda i, t: (i, 0))
    input_spec = pl.BlockSpec((1, 1, block, features), lambda i, t: (i // each, 0, t[0] * each + i % each, 0))
    return pl.pallas_call(
        functools.partial(ffn_kernel, ns=ns, up_part=up_part),
        grid_spec=pltpu.PrefetchScalarGridSpec(
            num_scalar_prefetch=1,
            grid=(rows // block,),
            in_specs=[
                input_spec,
                pl.BlockSpec((block, 2 * hw), lambda i, t: (jnp.minimum(i, each - 1), 0)),
                pl.BlockSpec((block, 2 * hw), lambda i, t: (jnp.maximum(i - each, 0), 0)),
                input_spec,
            ]
            + [once(w.shape) for w in (w_out, up_first, up_rest, w_down)]
            + [once(b_up.shape), once(vectors.shape)],
            out_specs=[row_spec] * 3
            + [once((2, total, features)), full_spec(more)],
            scratch_shapes=[
                pltpu.VMEM((2, total, features), F32), pltpu.VMEM((2, features, hidden), BF16),
                pltpu.VMEM((2, 1, hidden), F32), pltpu.VMEM((8, features), F32),
                pltpu.VMEM(more, F32),
            ],
        ),
        out_shape=[
            jax.ShapeDtypeStruct((rows, features), BF16),
            jax.ShapeDtypeStruct((rows, features), F32),
            jax.ShapeDtypeStruct((rows, 2 * hw), BF16),
            jax.ShapeDtypeStruct((2, total, features), BF16),
            jax.ShapeDtypeStruct(more, BF16),
        ],
        compiler_params=params(),
        cost_estimate=pl.CostEstimate(
            flops=12 * rows * total * features, bytes_accessed=20 * total * features, transcendentals=4 * rows * hidden
        ),
        name="feed_forward",
    )(where, tokens, *mixed, cotangent, w_out, up_first, up_rest, w_down, b_up, vectors)


def last_kernel(
    dw_ref, db_ref, sums_ref, dn0_ref, dn1_ref, other0_ref, other1_ref, x_ref, gm_ref, vec_ref,
    grad_ref, blocks_ref,
    extra, extra_ref, x_rows, gm_rows, dn_received, w_received, w_total, w_blocks, z_parts, z_received,
    dn_out, dn_in, wtp_out, wtp_in, wctx_out, wctx_in, z_out, z_in, back_out, back_in, row_out, row_in, fetched, *, ns, nc, head_part,
):
    t = lax.axis_index("tp")
    half = grad_ref.shape[2]
    rows = RowSum(
        dw_ref.at[1], dw_ref.at[0], extra_ref, w_received, w_total, w_blocks, (wtp_out, wtp_in),
        Axis("ctx", nc, (wctx_out, wctx_in)),
    )
    weights = ShardSum(
        z_parts, z_received, blocks_ref, Axis("shard", ns, (z_out, z_in)), Axis("ctx", nc, (back_out, back_in))
    )

    def row(micro):
        return cross(grad_ref.at[micro, t], grad_ref.at[micro, t], (row_out, row_in), micro)

    others = [cross(ref, dn_received.at[m], (dn_out, dn_in), m) for m, ref in enumerate((other0_ref, other1_ref))]

    def finish_rows(micro, dn_ref):
        size = 64
        others[micro].wait()

        def one(i, carry):
            at = pl.multiple_of(i * size, size)
            unit, inverse = unit_norm(x_rows[micro, pl.ds(at, size), :].astype(F32))
            value = gm_rows[micro, pl.ds(at, size), :] + norm_back(
                dn_ref[pl.ds(at, size), :] + dn_received[micro, pl.ds(at, size), :].astype(F32),
                unit, inverse, vec_ref[2:3],
            )
            grad_ref[micro, t, pl.ds(at, size), :] = value.astype(BF16)
            return carry

        lax.fori_loop(0, half // size, one, 0)
        row(micro).start()

    peers = [("tp", 2), ("ctx", nc), ("shard", ns)]
    greet_first(peers)
    own = x_ref.at[:, 0, pl.ds(pl.multiple_of(t * half, half), half), :]
    fetches = [
        pltpu.make_async_copy(own, x_rows, fetched.at[0]), pltpu.make_async_copy(gm_ref, gm_rows, fetched.at[1])
    ]
    for copy in fetches:
        copy.start()
    features = sums_ref.shape[1]
    each = db_ref.shape[0] // 2
    extra[...] = jnp.zeros_like(extra)
    for part in range(2):
        extra[part, 0:2] = sums_ref[0:2]
        biases = [db_ref[part * each + i, kind : kind + 1] for kind in range(2) for i in range(each)]
        extra[part, 2:3] = spread_columns(jnp.concatenate(biases, axis=1), 0, head_part, ns, features)
    extra_ref[...] = extra[...].astype(BF16)
    greet_wait(peers)
    rows.start()
    for copy in others:
        copy.start()
    rows.spread()
    for copy in fetches:
        copy.wait()
    finish_rows(0, dn0_ref)
    rows.finish(z_parts)
    weights.start()
    finish_rows(1, dn1_ref)
    weights.spread()
    weights.finish()
    for micro in range(2):
        row(micro).wait()


def last_sums(dw, db, sums, dn, x, grad_middle, vectors, head_part, ns, nc):
    main, features = dw.shape[1:]
    more = (2, 16 * nc, features)
    rows = main + more[1]
    micros, half, _ = grad_middle.shape
    size, part = rows // nc, features // ns
    return pl.pallas_call(
        functools.partial(last_kernel, ns=ns, nc=nc, head_part=head_part),
        in_specs=[pl.BlockSpec(memory_space=pltpu.VMEM)] * 7
        + [pl.BlockSpec(memory_space=pl.ANY)] * 2
        + [pl.BlockSpec(memory_space=pltpu.VMEM)],
        out_specs=[pl.BlockSpec(memory_space=pltpu.VMEM)] * 2,
        out_shape=[
            jax.ShapeDtypeStruct((micros, 2, half, features), BF16),
            jax.ShapeDtypeStruct((nc, size, part), BF16),
        ],
        scratch_shapes=[
            pltpu.VMEM(more, F32), pltpu.VMEM(more, BF16),
            pltpu.VMEM((micros, half, features), BF16), pltpu.VMEM((micros, half, features), F32),
            pltpu.VMEM((micros, half, features), BF16),
            pltpu.VMEM((rows, features), BF16), pltpu.VMEM((rows, features), BF16), pltpu.VMEM((nc, size, features), BF16),
            pltpu.VMEM((ns, size, part), BF16), pltpu.VMEM((ns, size, part), BF16),
            *axis_sems(micros, 2, nc, ns, nc, micros), pltpu.SemaphoreType.DMA((2,)),
        ],
        compiler_params=params(collective_id=5, has_side_effects=True),
        name="last_sums",
    )(dw, db, sums, *dn, x, grad_middle, vectors)


def results_kernel(out_ref, grad_ref, ffn_ref, attn_ref, *refs, heads, head_part, up_part):
    (out, grad_tokens, g_query, g_key, g_value, g_out, g_up, g_down, g_bq, g_bv, g_bup, *vectors) = refs
    out[...] = out_ref[...]
    grad_tokens[...] = grad_ref[...]
    width, lanes = g_out.shape
    hidden = g_down.shape[0]
    pair = 2 * width // heads

    def values(ref, at, size):
        return ref[at : at + size, :].astype(F32)

    @pl.when(pl.program_id(0) == 0)
    def _():
        g_out[...] = values(ffn_ref, 0, width)
        g_down[...] = values(ffn_ref, width, hidden)
        g_up[...] = values(ffn_ref, width + hidden, hidden).T
        for i in range(heads // 2):
            for kind, ref in enumerate((g_query, g_key, g_value)):
                ref[:, i * pair : (i + 1) * pair] = values(attn_ref, (3 * i + kind) * pair, pair).T
        tail = values(ffn_ref, width + 2 * hidden, 16)
        tail_attn = values(attn_ref, 3 * width, 16)
        rows = (tail[0], tail[1], tail_attn[0], tail_attn[1], tail[2], tail[3])
        for ref, row in zip(vectors, rows):
            ref[...] = row
        for h in range(heads):
            at = h * up_part
            g_bup[h : h + 1] = tail[4 + at // lanes : 5 + at // lanes, at % lanes : at % lanes + up_part]
            for start, ref in ((0, g_bq), (heads * head_part, g_bv)):
                at = start + h * head_part
                ref[h : h + 1] = tail_attn[2 + at // lanes : 3 + at // lanes, at % lanes : at % lanes + head_part]


def write_results(output, grad_tokens, done_ffn, done_attn, shapes, heads, head_part, up_part):
    micros, length, features = output.shape
    steps = 4
    rows = pl.BlockSpec((micros, length // steps, features), lambda i: (0, i, 0))
    return pl.pallas_call(
        functools.partial(results_kernel, heads=heads, head_part=head_part, up_part=up_part),
        grid=(steps,),
        in_specs=[rows, rows, once(done_ffn.shape), once(done_attn.shape)],
        out_specs=[rows, rows] + [full_spec(shape) for shape in shapes],
        out_shape=[jax.ShapeDtypeStruct(output.shape, BF16)] * 2 + [jax.ShapeDtypeStruct(shape, F32) for shape in shapes],
        compiler_params=params(),
        name="results",
    )(output, grad_tokens, done_ffn, done_attn)


def pad_rows(rows, multiple):
    extra = -rows.shape[0] % multiple
    return jnp.concatenate([rows, jnp.zeros((extra,) + rows.shape[1:], rows.dtype)]) if extra else rows


def body(
    tokens, cotangent, w_query, w_key, w_value, w_out, w_up, w_down,
    b_query, b_value, b_up, b_out, b_down, gain_attn, shift_attn, gain_ffn, shift_ffn,
):
    ns, nc = lax.axis_size("shard"), lax.axis_size("ctx")
    t = lax.axis_index("tp")
    micros, _, length, features = tokens.shape
    half = length // 2
    heads, head_part = b_query.shape
    head_width = head_part * ns
    up_part = b_up.shape[1]
    feature_part = b_out.shape[0]

    tables = [b_query, b_value, b_up] + [v[None] for v in (b_out, b_down, gain_attn, shift_attn, gain_ffn, shift_ffn)]
    keys = 2 * nc * half
    aligned = feature_part % 128 == 0
    column_place = place_columns if aligned else place_slot

    def column_shape(w, rows):
        return (2, rows, features) if aligned else (2, ns, rows, w.shape[1])

    def whole_columns(w):
        if not aligned:
            w = w.transpose(0, 2, 1, 3).reshape(2, w.shape[2], features)
        return w

    w_all, x_first, vectors, biases, bup = gather_first((w_query, w_key, w_value), tables, tokens, ns, nc)

    up_ahead = w_up.shape[1] // 4
    plans = [
        (("ctx", nc, place_distance, True, 0), ("shard", ns, place_rows, False, up_ahead)),
        (("shard", ns, column_place, False, 0),),
    ]
    sources = [(tokens, w_up), (w_down,)]
    specs = [
        [once((1, 1, length, features), (1, 0, 0, 0)), once(w_up.shape)],
        [once(w_down.shape)],
    ]
    shapes = [
        ((nc, 2, half, features), (2, features, w_up.shape[1] - up_ahead)),
        (column_shape(w_down, w_down.shape[0]),),
    ]
    guests = [
        (w_up, up_ahead, (2, features, up_ahead), place_rows),
        (w_out, w_out.shape[0], column_shape(w_out, w_out.shape[0]), column_place),
    ]
    x_alls = [x_first.reshape(keys, features), None]
    saved = []
    arrived = []
    for micro in range(micros):
        guest, guest_rows, guest_shape, guest_place = guests[micro]
        normed, k, v, q, early = front(
            x_alls[micro], w_all, vectors, biases, head_width, half, guest, guest_rows,
            guest_shape, ns, guest_place, 6 + micro,
        )
        mixed, qx, *more = attend_forward(
            q, k, v, head_width, plans[micro], sources[micro], specs[micro], shapes[micro], micro + 1
        )
        if micro == 0:
            x_alls[1] = more.pop(0).reshape(keys, features)
        arrived += [early] + more
        saved.append((normed, k, v, qx, mixed))
    up_first, up_rest, wo, wd = arrived
    wo, wd = whole_columns(wo), whole_columns(wd)

    out, grad_middle, grad_mixed, dw, extra = feed_forward(
        tokens, [entry[4] for entry in saved], cotangent, wo, up_first, up_rest, wd, bup, vectors,
        jnp.full((1,), t, jnp.int32), up_part, ns, nc,
    )

    width = heads * head_width
    *starts, dn_first, other_first, dw_parts, output = attend_back_rows(
        saved[0], grad_mixed, x_alls[0], w_all, head_width, dw, extra, out.reshape(micros, half, features), ns, nc
    )
    dw_now, db_now, sums, dn_second, other_second, dw_done = attend_back_shards(
        saved[1], grad_mixed, x_alls[1], w_all, head_width, starts, dw_parts, ns, nc
    )

    grad_tokens, attn_done = last_sums(
        dw_now.reshape(2, 3 * width, features), db_now, sums,
        (dn_first, dn_second, other_first, other_second), tokens, grad_middle.reshape(micros, half, features), vectors, head_part, ns, nc,
    )

    if aligned:
        weights = (w_query, w_key, w_value, w_out, w_up, w_down, b_query, b_value, b_up)
        shapes = [v.shape for v in weights] + [(feature_part,)] * 6
        output, grad_tokens, *grads = write_results(
            output.reshape(micros, length, features), grad_tokens.reshape(micros, length, features),
            dw_done.reshape(-1, feature_part), attn_done.reshape(-1, feature_part), shapes, heads, head_part, up_part,
        )
        g_query, g_key, g_value, g_out, g_up, g_down, g_bq, g_bv, g_bup, *others = grads
        return (output[:, None], grad_tokens[:, None], g_query, g_key, g_value, g_out, g_up, g_down, g_bq, g_bv, g_bup, *others)
    output = output.reshape(micros, 1, length, features)
    grad_tokens = grad_tokens.reshape(micros, 1, length, features)
    done_ffn = dw_done.reshape(-1, feature_part).astype(F32)
    done_attn = attn_done.reshape(-1, feature_part).astype(F32)
    hidden = heads * up_part * ns
    g_out, g_down, g_up = done_ffn[:width], done_ffn[width : width + hidden], done_ffn[width + hidden : width + 2 * hidden]
    tail = done_ffn[width + 2 * hidden :]
    by_kind = done_attn[: 3 * width].reshape(-1, 3, 2 * head_width, feature_part)
    g_query, g_key, g_value = (by_kind[:, i].reshape(width, feature_part).T for i in range(3))
    tail_attn = done_attn[3 * width :]
    g_bup = tail[4:].reshape(-1)[: heads * up_part].reshape(heads, up_part)
    g_heads = tail_attn[2:].reshape(-1)
    g_bq = g_heads[: heads * head_part].reshape(heads, head_part)
    g_bv = g_heads[heads * head_part : 2 * heads * head_part].reshape(heads, head_part)
    return (
        output, grad_tokens, g_query, g_key, g_value, g_out, g_up.T, g_down, g_bq, g_bv, g_bup,
        tail[0], tail[1], tail_attn[0], tail_attn[1], tail[2], tail[3],
    )


def solution(mesh):
    wide, tall = P("shard", "tp"), P("tp", "shard")
    rows, vector = P(None, "shard", "ctx", None), P("shard")
    weights = (wide, wide, wide, tall, wide, tall)
    return jax.shard_map(
        body,
        mesh=mesh,
        in_specs=(rows, rows) + weights + (tall,) * 3 + (vector,) * 6,
        out_specs=(rows, rows) + weights + (tall,) * 3 + (vector,) * 6,
        check_vma=False,
    )
```
